32 devices in a mesh: fsdp: 32 (over z, y, x, core).
Axes of the slice: x: 2, y: 2, z: 4, core: 2. Of those that a mesh axis runs over, the one named last changes fastest.
Arguments:
- tokens: bfloat16 [4096, 1152], P('fsdp'), may hold values from -6 to 6
- segments: int32 [4096], replicated, may hold values from 0 to 4, never falling along the last dimension, each value on 1 to 2000 neighbouring positions
- routes: int32 [4096, 1], P('fsdp'), may hold values from 0 to 1
- norm_gain: bfloat16 [1152], P('fsdp'), may hold values from 0.25 to 1.75
- in_proj: bfloat16 [1152, 4608], P('fsdp'), may hold values from -0.1875 to 0.1875
- conv_taps: bfloat16 [4, 2304], P(None, 'fsdp'), may hold values from -3 to 3
- conv_bias: bfloat16 [2304], P('fsdp'), may hold values from -1.5 to 1.5
- select_proj: bfloat16 [2304, 104], P('fsdp'), may hold values from -0.25 to 0.25
- step_proj: bfloat16 [72, 2304], P(None, 'fsdp'), may hold values from -0.75 to 0.75
- step_bias: bfloat16 [2304], P('fsdp'), may hold values from -7 to -2
- decay_log: bfloat16 [16, 2304], P(None, 'fsdp'), may hold values from -2 to 2
- skip_gain: bfloat16 [2304], P('fsdp'), may hold values from 0.5 to 1.5
- out_proj: bfloat16 [2304, 1152], P('fsdp'), may hold values from -0.375 to 0.375
- moe_gain: bfloat16 [1152], P('fsdp'), may hold values from 0.25 to 1.75
- router: bfloat16 [1152, 2], P('fsdp'), may hold values from -0.125 to 0.125
- expert_up: bfloat16 [2, 1152, 3072], P(None, 'fsdp'), may hold values from -0.1875 to 0.1875
- expert_down: bfloat16 [2, 3072, 1152], P(None, 'fsdp'), may hold values from -0.3125 to 0.3125
- cotangent: bfloat16 [4096, 1152], P('fsdp'), may hold values from -6 to 6
Outputs:
- output: bfloat16 [4096, 1152], P('fsdp')
- grad_tokens: bfloat16 [4096, 1152], P('fsdp')
- grad_norm_gain: float32 [1152], P('fsdp')
- grad_in_proj: float32 [1152, 4608], P('fsdp')
- grad_conv_taps: float32 [4, 2304], P(None, 'fsdp')
- grad_conv_bias: float32 [2304], P('fsdp')
- grad_select_proj: float32 [2304, 104], P('fsdp')
- grad_step_proj: float32 [72, 2304], P(None, 'fsdp')
- grad_step_bias: float32 [2304], P('fsdp')
- grad_decay_log: float32 [16, 2304], P(None, 'fsdp')
- grad_skip_gain: float32 [2304], P('fsdp')
- grad_out_proj: float32 [2304, 1152], P('fsdp')
- grad_moe_gain: float32 [1152], P('fsdp')
- grad_router: float32 [1152, 2], P('fsdp')
- grad_expert_up: float32 [2, 1152, 3072], P(None, 'fsdp')
- grad_expert_down: float32 [2, 3072, 1152], P(None, 'fsdp')
The draws below stay inside these ranges and needn't reach their ends.
Inputs may be any that keep to these rules, and one draw needn't show every extreme that they name: `segments`: never falls along the stream; each document (run of equal ids) has 1 to 2000 tokens, and some document has exactly 2000.
All inputs are finite; a program needn't handle non-finite values.
Results may differ from the reference program's by a relative error of at most 0.014.
The reference program's roundings to bfloat16 on the way count: a program that leaves them out, or rounds other values in their place, can miss the bound.
Values may be sent and summed in bfloat16 or wider, within the bound.
A program may use at most 320 MiB of HBM per device.

```python
import math
import jax
import jax.numpy as jnp
import numpy as np
from jax import lax

D = 1152
DI = 2304
FF = 3072
RANK = 72
STATE = 16
EXPERTS = 2
DOC_MAX = 2000
TOK_DEV = 128
CAP = 68
TOKENS = 4096


def level_of(rng, shape, shards, smallest, largest):
    loudness, own = 1.0, jax.random.fold_in(rng, 6)
    for axis_at, parts in shards:
        steps = jnp.exp(jax.random.uniform(jax.random.fold_in(own, axis_at), (parts,), jnp.float32, smallest / len(shards), largest / len(shards)))
        loudness = loudness * jnp.repeat(steps, shape[axis_at] // parts).reshape([-1 if axis == axis_at else 1 for axis in range(len(shape))])
    return loudness


def choose_distinct(rng, rows, amount, top, lift):
    sequence = jax.random.permutation(jax.random.fold_in(rng, 1), amount)
    favour = sequence
    for power in range(3):
        favour = favour * favour // amount
    favour = favour * lift // amount
    tickets = jax.random.randint(jax.random.fold_in(rng, 2), (rows, amount), 0, 4096) + favour
    holders = jax.random.permutation(jax.random.fold_in(rng, 3), rows)[jnp.arange(amount) % rows]
    tickets = jnp.where(jnp.arange(rows)[:, None] == holders[None, :], 1 << 14, tickets)
    merit = tickets * amount + jnp.arange(amount)
    return lax.top_k(merit.astype(jnp.int32), top)[1].astype(jnp.int32)


def split_up(count, total, reach, skew):
    portions = [(1 << 20) // math.isqrt(grade ** skew) + 1 for grade in range(2, count + 1)]
    spare, given = total - reach - (count - 1), [1] * (count - 1)
    while spare > 0:
        candidates = [i for i in range(count - 1) if given[i] < reach]
        pool, left = sum([portions[i] for i in candidates]), spare
        for i in candidates:
            more = min(reach - given[i], max(1, left * portions[i] // pool), spare)
            given[i] = given[i] + more
            spare = spare - more
    return np.array([reach] + given)


def uneven(stream_key, number_of, total, limit, skew):
    if number_of == 2:
        one = jax.random.randint(stream_key, (), max(1, total - limit), min(limit, total - 1) + 1)
        return jnp.stack([one, total - one])
    lengths = jnp.asarray(split_up(number_of, total, limit, skew), jnp.int32)
    pairs = (number_of - 1) // 2
    donor, receiver = lengths[1:1 + 2 * pairs:2], lengths[2:2 + 2 * pairs:2]
    room = jnp.minimum(donor - 1, limit - receiver)
    passed = jax.random.randint(jax.random.fold_in(stream_key, 1), (pairs,), 0, 1 << 20) % (room + 1)
    lengths = lengths.at[1:1 + 2 * pairs:2].set(donor - passed).at[2:2 + 2 * pairs:2].set(receiver + passed)
    return lengths[jax.random.permutation(jax.random.fold_in(stream_key, 2), number_of)]


def bell_draw(rng, shape, scale, most, cuts=(), held_as=jnp.bfloat16):
    values = jax.random.normal(rng, shape, jnp.float32) * scale
    if len(cuts) > 0:
        values = level_of(rng, shape, cuts, -0.22, 0.18) * values
    return jnp.clip(values, min=-most, max=most).astype(held_as)


def setup_inputs(seed: int = 0) -> dict:
    key_of = jax.random.split(jax.random.key(seed), 19)
    return {
        "tokens": bell_draw(key_of[0], (TOKENS, D), 1.0, 6.0, ((0, 32),)),
        "segments": jnp.searchsorted(jnp.cumsum(uneven(key_of[1], TOKENS * 2 // DOC_MAX + 1, TOKENS, DOC_MAX, 1)), jnp.arange(TOKENS), side="right").astype(jnp.int32),
        "routes": choose_distinct(key_of[2], TOKENS, EXPERTS, 1, 4096),
        "norm_gain": jnp.clip(1.0 + 0.15 * jax.random.normal(key_of[3], (D,), jnp.float32), 0.25, 1.75).astype(jnp.bfloat16),
        "in_proj": bell_draw(key_of[4], (D, 2 * DI), D ** -0.5, 0.1875, ((0, 32),)),
        "conv_taps": bell_draw(key_of[5], (4, DI), 4 ** -0.5, 3.0, ((1, 32),)),
        "conv_bias": bell_draw(key_of[6], (DI,), 0.3, 1.5, ((0, 32),)),
        "select_proj": bell_draw(key_of[7], (DI, RANK + 2 * STATE), (DI // 4) ** -0.5, 0.25, ((0, 32),)),
        "step_proj": bell_draw(key_of[8], (RANK, DI), RANK ** -0.5, 0.75, ((1, 32),)),
        "step_bias": jnp.clip(-7.0 + 5.0 * jax.random.uniform(key_of[9], (DI,), jnp.float32) ** level_of(key_of[9], (DI,), ((0, 32),), -0.2, 0.2), -7.0, -2.0).astype(jnp.bfloat16),
        "decay_log": jnp.clip(jax.random.uniform(key_of[10], (STATE, DI), jnp.float32, -2.0, 2.0) * level_of(key_of[10], (STATE, DI), ((1, 32),), -0.4, 0.0), -2.0, 2.0).astype(jnp.bfloat16),
        "skip_gain": jnp.clip(0.5 + 1.0 * jax.random.uniform(key_of[11], (DI,), jnp.float32) ** level_of(key_of[11], (DI,), ((0, 32),), -0.2, 0.2), 0.5, 1.5).astype(jnp.bfloat16),
        "out_proj": bell_draw(key_of[12], (DI, D), (DI // 8) ** -0.5, 0.375, ((0, 32),)),
        "moe_gain": jnp.clip(1.0 + 0.15 * jax.random.normal(key_of[13], (D,), jnp.float32), 0.25, 1.75).astype(jnp.bfloat16),
        "router": bell_draw(key_of[14], (D, EXPERTS), (2 * D) ** -0.5, 0.125, ((0, 32),)),
        "expert_up": bell_draw(key_of[15], (EXPERTS, D, FF), D ** -0.5, 0.1875, ((1, 32),)),
        "expert_down": bell_draw(key_of[16], (EXPERTS, FF, D), (FF // 8) ** -0.5, 0.3125, ((1, 32),)),
        "cotangent": bell_draw(key_of[17], (TOKENS, D), 1.0, 6.0, ((0, 32),)),
    }


@jax.custom_vjp
def low(v):
    return lax.optimization_barrier(v.astype(jnp.bfloat16)).astype(jnp.float32)

@jax.custom_vjp
def low_back(v):
    return v

def low_keep(v):
    return (low(v), None)

def low_pass(kept, grad):
    return (grad,)

def back_keep(v):
    return (v, None)

def back_low(kept, grad):
    return (low(grad),)
low.defvjp(low_keep, low_pass)
low_back.defvjp(back_keep, back_low)
epsilon = 1e-05

def product(left, right):
    return jnp.dot(left, right, precision=lax.Precision.HIGHEST, preferred_element_type=jnp.float32)

def rms_norm(values, gain):
    return values * lax.rsqrt(lax.optimization_barrier(jnp.mean(values * values, axis=-1, keepdims=True)) + epsilon) * gain

def one_block(weights, carry, inputs):
    norm_gain, in_proj, conv_taps, conv_bias, select_proj, step_proj, step_bias, decay_log, skip_gain, out_proj, moe_gain, router, expert_up, expert_down = weights
    tail, state = carry
    stream, same, choose, kept = inputs
    count = stream.shape[0]
    normed = low(rms_norm(stream, norm_gain))
    joined = low_back(low(product(normed, in_proj)))
    inner = joined[:, :DI]
    gate_in = joined[:, DI:]
    padded = jnp.concatenate([tail, inner], axis=0)
    conv = conv_bias + conv_taps[0] * padded[0:count] * same[:, 0:1]
    for tap in range(1, 4):
        conv = conv + conv_taps[tap] * padded[tap:tap + count] * same[:, tap:tap + 1]
    signal = low(jax.nn.silu(conv))
    selected = low_back(low(product(signal, select_proj)))
    rank_part = selected[:, :RANK]
    input_mix = selected[:, RANK:RANK + STATE]
    output_mix = selected[:, RANK + STATE:]
    delta = jax.nn.softplus(low_back(product(rank_part, step_proj)) + step_bias)
    rate = -jnp.exp(decay_log)
    keep = same[:, 2]

    def advance(hidden, item):
        step_size, value, write, read, carry_on = item
        hidden = carry_on * jnp.exp(step_size[None, :] * rate) * hidden + write[:, None] * (step_size * value)[None, :]
        return (hidden, lax.optimization_barrier(jnp.sum(read[:, None] * hidden, axis=0)))
    state, scanned = lax.scan(advance, state, (delta, signal, input_mix, output_mix, keep))
    mixed = (scanned + skip_gain * signal) * jax.nn.silu(gate_in)
    branch = low_back(product(low(mixed), out_proj))
    middle = stream + branch
    routed = low(rms_norm(middle, moe_gain))
    probs = jax.nn.softmax(product(routed, router), axis=-1)
    gate = lax.optimization_barrier(jnp.sum(probs * choose, axis=-1))
    result = middle
    for expert in range(EXPERTS):
        hidden_units = low(jax.nn.gelu(low_back(product(routed, expert_up[expert]))))
        expert_out = low_back(product(hidden_units, expert_down[expert]))
        result = result + (choose[:, expert] * kept * gate)[:, None] * expert_out
    return ((inner[count - 3:], state), result)

def reference(tokens, segments, routes, norm_gain, in_proj, conv_taps, conv_bias, select_proj, step_proj, step_bias, decay_log, skip_gain, out_proj, moe_gain, router, expert_up, expert_down, cotangent):
    earlier = jnp.concatenate([jnp.full((3,), -1, jnp.int32), segments])
    same = jnp.stack([earlier[tap:tap + TOKENS] == segments for tap in range(4)], axis=1).astype(jnp.float32)
    picks = (routes[:, 0:1] == jnp.arange(EXPERTS, dtype=jnp.int32)[None, :]).astype(jnp.int32)
    places = jnp.cumsum(picks.reshape(TOKENS // TOK_DEV, TOK_DEV, EXPERTS), axis=1).reshape(TOKENS, EXPERTS)
    kept = lax.optimization_barrier(jnp.sum(picks * (places <= CAP).astype(jnp.int32), axis=1)).astype(jnp.float32)
    choose = picks.astype(jnp.float32)
    weights = tuple((weight.astype(jnp.float32) for weight in (norm_gain, in_proj, conv_taps, conv_bias, select_proj, step_proj, step_bias, decay_log, skip_gain, out_proj, moe_gain, router, expert_up, expert_down)))

    def forward(stream, params):

        def scan_block(carry, inputs):
            return one_block(params, carry, inputs)
        start = (jnp.zeros((3, DI), jnp.float32), jnp.zeros((STATE, DI), jnp.float32))
        blocks = (stream.reshape(-1, TOK_DEV, D), same.reshape(-1, TOK_DEV, 4), choose.reshape(-1, TOK_DEV, EXPERTS), kept.reshape(-1, TOK_DEV))
        finish, outputs = lax.scan(jax.checkpoint(scan_block), start, blocks)
        return outputs.reshape(TOKENS, D)
    result, pullback = jax.vjp(forward, tokens.astype(jnp.float32), weights)
    grad_stream, grads = pullback(cotangent.astype(jnp.float32))
    return (result.astype(jnp.bfloat16), grad_stream.astype(jnp.bfloat16), grads[0], grads[1], grads[2], grads[3], grads[4], grads[5], grads[6], grads[7], grads[8], grads[9], grads[10], grads[11], grads[12], grads[13])
```

```python
import functools

import jax
import jax.numpy as jnp
from jax import lax
from jax.experimental import pallas as pl
from jax.experimental.pallas import tpu as pltpu
from jax.sharding import Mesh, PartitionSpec as P

D = 1152
DI = 2304
FF = 3072
RANK = 72
STATE = 16
EXPERTS = 2
CAP = 68
SEL = RANK + 2 * STATE

PLANE = 8
CHIPS = PLANE // 2
WIDE = DI // PLANE
HID = FF // PLANE
BLK = 16
LOG2E = 1.4426950408889634
RESET = 1e5
epsilon = 1e-05

MESH = pl.DeviceIdType.MESH
ANY = pl.BlockSpec(memory_space=pl.ANY)
VM = pl.BlockSpec(memory_space=pltpu.VMEM)
bf16 = jnp.bfloat16
f32 = jnp.float32
DMA = pltpu.SemaphoreType.DMA


def params(cid=None, grid=None):
    extra = {} if cid is None else {"collective_id": cid, "has_side_effects": True}
    if grid is not None:
        extra["dimension_semantics"] = grid
    return pltpu.CompilerParams(vmem_limit_bytes=60 * 1024 * 1024, **extra)


def send(src, dst, ss, rs, to):
    copy = pltpu.make_async_remote_copy(
        src_ref=src, dst_ref=dst, send_sem=ss, recv_sem=rs, device_id=to, device_id_type=MESH
    )
    copy.start()
    return copy


def here():
    return lax.axis_index("z"), lax.axis_index("p")


def greet(plane=True, depth=0):
    z, p = here()
    barrier = pltpu.get_barrier_semaphore()
    count = 0
    if plane:
        for k in range(1, PLANE):
            pl.semaphore_signal(
                barrier, inc=1, device_id=(z, lax.rem(p + k, PLANE)), device_id_type=MESH
            )
            count += 1
    for k in range(1, depth):
        pl.semaphore_signal(barrier, inc=1, device_id=(lax.rem(z + k, depth), p), device_id_type=MESH)
        count += 1
    pl.semaphore_wait(barrier, count)


def share_start(x, out, ss, rs):
    z, p = here()
    core = lax.rem(p, 2)
    copies = [send(x, out.at[p], ss.at[0], rs.at[0], (z, p + 1 - 2 * core))]
    for k in range(1, CHIPS):
        copies.append(send(x, out.at[p], ss.at[k], rs.at[k], (z, lax.rem(p + 2 * k, PLANE))))
    return copies


def share_forward(out, copies, ss, rs):
    z, p = here()
    core = lax.rem(p, 2)
    onward = []
    for k in range(1, CHIPS):
        copies[k].wait_recv()
        src = lax.rem(p + PLANE - 2 * k, PLANE)
        onward.append(
            send(out.at[src], out.at[src], ss.at[CHIPS + k], rs.at[CHIPS + k], (z, p + 1 - 2 * core))
        )
    return onward


def share_finish(copies, onward):
    copies[0].wait_recv()
    for c in copies:
        c.wait_send()
    for c in onward:
        c.wait()


def share_kernel(count, *refs):
    xs, outs = refs[:count], refs[count : 2 * count]
    ss, rs, ls = refs[2 * count :]
    z, p = here()
    local = [pltpu.make_async_copy(x, o.at[p], ls.at[i]) for i, (x, o) in enumerate(zip(xs, outs))]
    for c in local:
        c.start()
    greet()
    first = [share_start(x, o, ss.at[i], rs.at[i]) for i, (x, o) in enumerate(zip(xs, outs))]
    second = [share_forward(o, first[i], ss.at[i], rs.at[i]) for i, o in enumerate(outs)]
    for c in local:
        c.wait()
    for a, b in zip(first, second):
        share_finish(a, b)


def plane_gather(cid, *xs):
    count = len(xs)
    return pl.pallas_call(
        functools.partial(share_kernel, count),
        out_shape=[jax.ShapeDtypeStruct((PLANE,) + x.shape, x.dtype) for x in xs],
        in_specs=[ANY] * count,
        out_specs=[ANY] * count,
        scratch_shapes=[DMA((count, PLANE)), DMA((count, PLANE)), DMA((count,))],
        compiler_params=params(cid),
        name="plane_gather",
    )(*xs)


def reduce_kernel(count, *refs):
    xs, outs = refs[:count], refs[count : 2 * count]
    sib, mix, far, ss, rs, ts, us = refs[2 * count :]
    z, p = here()
    core = lax.rem(p, 2)
    chip = lax.div(p, 2)
    twin = (z, p + 1 - 2 * core)
    greet()
    near = []
    for i in range(count):
        for k in (1, 2, 3, 0):
            q = lax.rem(chip + k, CHIPS)
            near.append(
                send(xs[i].at[2 * q + 1 - core], sib.at[i, k], ss.at[i, k], rs.at[i, k], twin)
            )
    away = []
    for i in range(count):
        for j, k in enumerate((1, 2, 3, 0)):
            q = lax.rem(chip + k, CHIPS)
            near[i * CHIPS + j].wait_recv()
            both = xs[i][2 * q + core].astype(f32) + sib[i, k].astype(f32)
            if k == 0:
                outs[i][...] = both
            else:
                mix[i, k] = both.astype(bf16)
                away.append(
                    send(mix.at[i, k], far.at[i, k], ts.at[i, k], us.at[i, k], (z, lax.rem(p + 2 * k, PLANE)))
                )
    for i in range(count):
        for k in range(1, CHIPS):
            away[i * (CHIPS - 1) + k - 1].wait_recv()
        outs[i][...] += far[i, 1].astype(f32) + far[i, 2].astype(f32) + far[i, 3].astype(f32)
    for c in near + away:
        c.wait_send()


def plane_reduce(cid, *xs):
    count = len(xs)
    rows, cols = xs[0].shape[1:]
    return pl.pallas_call(
        functools.partial(reduce_kernel, count),
        out_shape=[jax.ShapeDtypeStruct((rows, cols), f32) for _ in xs],
        in_specs=[VM] * count,
        out_specs=[VM] * count,
        scratch_shapes=[pltpu.VMEM((count, CHIPS, rows, cols), bf16)] * 3 + [DMA((count, CHIPS))] * 4,
        compiler_params=params(cid),
        name="plane_reduce",
    )(*xs)


def total_kernel(x, out, got, own, ss, rs, ts, us):
    z, p = here()
    greet()
    first = []
    for k in range(1, PLANE):
        q = lax.rem(p + k, PLANE)
        first.append(send(x.at[q], got.at[k], ss.at[k], rs.at[k], (z, q)))
    total = x[p]
    for k in range(1, PLANE):
        first[k - 1].wait_recv()
        total = total + got[k]
    own[...] = total.astype(bf16)
    second = []
    for k in range(1, PLANE):
        second.append(send(own, out.at[p], ts.at[k], us.at[k], (z, lax.rem(p + k, PLANE))))
    out[p] = own[...]
    for c in first:
        c.wait_send()
    for c in second:
        c.wait()


def plane_total(cid, x):
    return pl.pallas_call(
        total_kernel,
        out_shape=jax.ShapeDtypeStruct(x.shape, bf16),
        in_specs=[VM],
        out_specs=VM,
        scratch_shapes=[
            pltpu.VMEM(x.shape, f32),
            pltpu.VMEM(x.shape[1:], bf16),
        ]
        + [DMA((PLANE,))] * 4,
        compiler_params=params(cid),
        name="plane_total",
    )(x)


def column_kernel(depth, x, out, ss, rs, ls):
    z, p = here()
    local = pltpu.make_async_copy(x, out.at[z], ls)
    local.start()
    greet(False, depth)
    copies = [
        send(x, out.at[z], ss.at[k], rs.at[k], (lax.rem(z + k, depth), p)) for k in range(1, depth)
    ]
    local.wait()
    for c in copies:
        c.wait()


def column_gather(cid, depth, x):
    return pl.pallas_call(
        functools.partial(column_kernel, depth),
        out_shape=jax.ShapeDtypeStruct((depth,) + x.shape, x.dtype),
        in_specs=[VM],
        out_specs=VM,
        scratch_shapes=[DMA((depth,)), DMA((depth,)), DMA],
        compiler_params=params(cid),
        name="column_gather",
    )(x)


def opening_kernel(depth, tok, win, wup, pack, tok_all, win_all, up_all, pack_all, ss, rs, ws, wr, vs, vr, zs, zr, ls):
    z, p = here()
    local = [
        pltpu.make_async_copy(tok, tok_all.at[p], ls.at[0]),
        pltpu.make_async_copy(win.at[p], win_all.at[z, p], ls.at[1]),
        pltpu.make_async_copy(wup.at[p], up_all.at[p], ls.at[2]),
        pltpu.make_async_copy(pack, pack_all.at[z], ls.at[3]),
    ]
    for c in local:
        c.start()
    greet(True, depth)
    across = []
    for k in range(1, PLANE):
        q = lax.rem(p + k, PLANE)
        across.append(send(win.at[q], win_all.at[z, p], ws.at[k], wr.at[k], (z, q)))
    down = [
        send(pack, pack_all.at[z], zs.at[0, k], zr.at[0, k], (lax.rem(z + k, depth), p))
        for k in range(1, depth)
    ]
    first = share_start(tok, tok_all, ss, rs)
    local[1].wait()
    for c in across:
        c.wait_recv()
    down += [
        send(win_all.at[z], win_all.at[z], zs.at[1, k], zr.at[1, k], (lax.rem(z + k, depth), p))
        for k in range(1, depth)
    ]
    second = share_forward(tok_all, first, ss, rs)
    more = []
    for k in range(1, PLANE):
        q = lax.rem(p + k, PLANE)
        more.append(send(wup.at[q], up_all.at[p], vs.at[k], vr.at[k], (z, q)))
    share_finish(first, second)
    for c in across:
        c.wait_send()
    for c in more + down:
        c.wait()
    for c in (local[0], local[2], local[3]):
        c.wait()


def opening(cid, depth, tok, win, wup, pack):
    return pl.pallas_call(
        functools.partial(opening_kernel, depth),
        out_shape=[
            jax.ShapeDtypeStruct((PLANE,) + tok.shape, bf16),
            jax.ShapeDtypeStruct((depth,) + win.shape, bf16),
            jax.ShapeDtypeStruct(wup.shape, bf16),
            jax.ShapeDtypeStruct((depth,) + pack.shape, bf16),
        ],
        in_specs=[ANY] * 4,
        out_specs=[ANY] * 4,
        scratch_shapes=[DMA((PLANE,))] * 6 + [DMA((2, depth))] * 2 + [DMA((4,))],
        compiler_params=params(cid),
        name="opening",
    )(tok, win, wup, pack)


def closing_kernel(depth, gin, gpack, gup, in_out, pack_out, up_out, got, gotp, own, ss, rs, ps, pr, vs, vr, ls):
    z, p = here()
    local = pltpu.make_async_copy(gup.at[p], up_out.at[p], ls)
    local.start()
    greet(True, depth)
    down = []
    for k in range(1, depth):
        q = lax.rem(z + k, depth)
        down.append(send(gin.at[q], got.at[k], ss.at[0, k], rs.at[0, k], (q, p)))
    downp = []
    for k in range(1, depth):
        q = lax.rem(z + k, depth)
        downp.append(send(gpack.at[q], gotp.at[k], ss.at[1, k], rs.at[1, k], (q, p)))
    more = []
    for k in range(1, PLANE):
        q = lax.rem(p + k, PLANE)
        more.append(send(gup.at[q], up_out.at[p], vs.at[k], vr.at[k], (z, q)))
    for c in down:
        c.wait_recv()
    total = gin[z].astype(f32)
    for k in range(1, depth):
        total = total + got[k].astype(f32)
    own[...] = total.astype(bf16)
    across = []
    for k in range(1, PLANE):
        q = lax.rem(p + k, PLANE)
        across.append(send(own.at[q], in_out.at[p], ps.at[k], pr.at[k], (z, q)))
    in_out[p] = own[p]
    for c in downp:
        c.wait_recv()
    total = gpack[z].astype(f32)
    for k in range(1, depth):
        total = total + gotp[k].astype(f32)
    pack_out[...] = total
    for c in down + downp:
        c.wait_send()
    for c in across + more:
        c.wait()
    local.wait()


def closing(cid, depth, gin, gpack, gup):
    return pl.pallas_call(
        functools.partial(closing_kernel, depth),
        out_shape=[
            jax.ShapeDtypeStruct(gin.shape[1:], bf16),
            jax.ShapeDtypeStruct(gpack.shape[1:], f32),
            jax.ShapeDtypeStruct(gup.shape, bf16),
        ],
        in_specs=[VM] * 2 + [ANY],
        out_specs=[VM] * 2 + [ANY],
        scratch_shapes=[
            pltpu.VMEM(gin.shape, bf16),
            pltpu.VMEM(gpack.shape, bf16),
            pltpu.VMEM(gin.shape[1:], bf16),
        ]
        + [DMA((2, depth))] * 2
        + [DMA((PLANE,))] * 4
        + [DMA],
        compiler_params=params(cid),
        name="closing",
    )(gin, gpack, gup)


def ends_kernel(dk, push, sel, rate, end, total):
    slope = rate[...]

    def block(b, carry):
        hidden, acc = carry
        rows = pl.ds(pl.multiple_of(b * BLK, BLK), BLK)
        d, u, w = dk[rows, :], push[rows, :], sel[b, :STATE]
        for t in range(BLK):
            decay = jnp.exp2(d[t : t + 1] * slope)
            hidden = decay * hidden + w[:, t : t + 1] * u[t : t + 1]
        return hidden, acc + jnp.sum(d, axis=0, keepdims=True)

    zero = jnp.zeros(slope.shape, f32)
    hidden, acc = lax.fori_loop(0, dk.shape[0] // BLK, block, (zero, zero[:1]))
    end[...] = hidden
    total[...] = acc


def scan_ends(dk, push, sel, rate):
    return pl.pallas_call(
        ends_kernel,
        out_shape=[jax.ShapeDtypeStruct(rate.shape, f32), jax.ShapeDtypeStruct((1, rate.shape[1]), f32)],
        in_specs=[VM] * 4,
        out_specs=[VM] * 2,
        compiler_params=params(),
        name="scan_ends",
    )(dk, push, sel, rate)


def scan_kernel(dk, push, sel, rate, start, out, states, hold):
    @pl.when(pl.program_id(0) == 0)
    def _():
        hold[...] = start[...]

    slope = rate[...]

    def block(b, hidden):
        base = pl.multiple_of(b * BLK, BLK)
        rows = pl.ds(base, BLK)
        d, u, w, r = dk[rows, :], push[rows, :], sel[b, :STATE], sel[b, STATE:]
        lines = []
        for t in range(BLK):
            decay = jnp.exp2(d[t : t + 1] * slope)
            hidden = decay * hidden + w[:, t : t + 1] * u[t : t + 1]
            states[base + t] = hidden
            lines.append(jnp.sum(r[:, t : t + 1] * hidden, axis=0, keepdims=True))
        out[rows, :] = jnp.concatenate(lines, axis=0)
        return hidden

    hold[...] = lax.fori_loop(0, dk.shape[0] // BLK, block, hold[...])


def scan_forward(dk, push, sel, rate, start, tile):
    rows, wide = dk.shape
    per = tile // BLK
    return pl.pallas_call(
        scan_kernel,
        grid=(rows // tile,),
        out_shape=[
            jax.ShapeDtypeStruct((rows, wide), f32),
            jax.ShapeDtypeStruct((rows, STATE, wide), f32),
        ],
        in_specs=[
            pl.BlockSpec((tile, wide), lambda i: (i, 0)),
            pl.BlockSpec((tile, wide), lambda i: (i, 0)),
            pl.BlockSpec((per, 2 * STATE, BLK), lambda i: (i, 0, 0)),
            pl.BlockSpec((STATE, wide), lambda i: (0, 0)),
            pl.BlockSpec((STATE, wide), lambda i: (0, 0)),
        ],
        out_specs=[
            pl.BlockSpec((tile, wide), lambda i: (i, 0)),
            pl.BlockSpec((tile, STATE, wide), lambda i: (i, 0, 0)),
        ],
        scratch_shapes=[pltpu.VMEM((STATE, wide), f32)],
        compiler_params=params(grid=("arbitrary",)),
        name="scan_forward",
    )(dk, push, sel, rate, start)


def message_kernel(dk, grad, sel, rate, out):
    slope = rate[...]
    blocks = dk.shape[0] // BLK

    def block(i, message):
        b = blocks - 1 - i
        rows = pl.ds(pl.multiple_of(b * BLK, BLK), BLK)
        d, g, r = dk[rows, :], grad[rows, :], sel[b, STATE:]
        for t in reversed(range(BLK)):
            decay = jnp.exp2(d[t : t + 1] * slope)
            message = decay * (r[:, t : t + 1] * g[t : t + 1] + message)
        return message

    out[...] = lax.fori_loop(0, blocks, block, jnp.zeros(slope.shape, f32))


def scan_message(dk, grad, sel, rate):
    return pl.pallas_call(
        message_kernel,
        out_shape=jax.ShapeDtypeStruct(rate.shape, f32),
        in_specs=[VM] * 4,
        out_specs=VM,
        compiler_params=params(),
        name="scan_message",
    )(dk, grad, sel, rate)


def adjoint_kernel(dk, push, grad, sel, states, rate, arriving, g_push, g_step, g_sel, g_rate, hold):
    @pl.when(pl.program_id(0) == 0)
    def _():
        hold[...] = arriving[...]
        g_rate[...] = jnp.zeros_like(g_rate)

    slope = rate[...]
    blocks = dk.shape[0] // BLK
    lane = lax.broadcasted_iota(jnp.int32, (STATE, BLK), 1)

    def block(i, carry):
        message, acc = carry
        b = blocks - 1 - i
        base = pl.multiple_of(b * BLK, BLK)
        rows = pl.ds(base, BLK)
        d, u, g = dk[rows, :], push[rows, :], grad[rows, :]
        plain = jnp.where(d < RESET, d, 0.0)
        w, r = sel[b, :STATE], sel[b, STATE:]
        pushes, steps = [], []
        g_write = jnp.zeros((STATE, BLK), f32)
        g_read = jnp.zeros((STATE, BLK), f32)
        for t in reversed(range(BLK)):
            dt, ut, gt = d[t : t + 1], u[t : t + 1], g[t : t + 1]
            wt, rt = w[:, t : t + 1], r[:, t : t + 1]
            hidden = states[base + t]
            decay = jnp.exp2(dt * slope)
            total = rt * gt + message
            g_read = jnp.where(lane == t, jnp.sum(hidden * gt, axis=1, keepdims=True), g_read)
            g_write = jnp.where(lane == t, jnp.sum(total * ut, axis=1, keepdims=True), g_write)
            pushes.append(jnp.sum(total * wt, axis=0, keepdims=True))
            carried = total * (hidden - wt * ut)
            steps.append(jnp.sum(carried * slope, axis=0, keepdims=True))
            acc = acc + carried * plain[t : t + 1]
            message = decay * total
        g_push[rows, :] = jnp.concatenate(pushes[::-1], axis=0)
        g_step[rows, :] = jnp.concatenate(steps[::-1], axis=0)
        g_sel[b, :STATE] = g_write
        g_sel[b, STATE:] = g_read
        return message, acc

    message, acc = lax.fori_loop(0, blocks, block, (hold[...], g_rate[...]))
    hold[...] = message
    g_rate[...] = acc


def scan_adjoint(dk, push, grad, sel, states, rate, arriving, tile):
    rows, wide = dk.shape
    per, last = tile // BLK, rows // tile - 1
    line = pl.BlockSpec((tile, wide), lambda i: (last - i, 0))
    mix = pl.BlockSpec((per, 2 * STATE, BLK), lambda i: (last - i, 0, 0))
    flat = pl.BlockSpec((STATE, wide), lambda i: (0, 0))
    return pl.pallas_call(
        adjoint_kernel,
        grid=(rows // tile,),
        out_shape=[
            jax.ShapeDtypeStruct((rows, wide), f32),
            jax.ShapeDtypeStruct((rows, wide), f32),
            jax.ShapeDtypeStruct(sel.shape, f32),
            jax.ShapeDtypeStruct((STATE, wide), f32),
        ],
        in_specs=[line, line, line, mix, pl.BlockSpec((tile, STATE, wide), lambda i: (last - i, 0, 0)), flat, flat],
        out_specs=[line, line, mix, flat],
        scratch_shapes=[pltpu.VMEM((STATE, wide), f32)],
        compiler_params=params(grid=("arbitrary",)),
        name="scan_adjoint",
    )(dk, push, grad, sel, states, rate, arriving)


def norm_rows(values, gain):
    scale = lax.rsqrt(jnp.mean(values * values, axis=-1, keepdims=True) + epsilon)
    normed = values * scale
    return normed, scale, normed * gain


def norm_back(grad_out, normed, scale, gain):
    grad_normed = grad_out * gain
    grad_gain = jnp.sum(grad_out * normed, axis=0)
    inner_mean = jnp.mean(grad_normed * normed, axis=-1, keepdims=True)
    return scale * (grad_normed - normed * inner_mean), grad_gain


def mm(left, right):
    return jnp.dot(left, right, preferred_element_type=f32)


def contract_rows(left, right):
    return lax.dot_general(left, right, (((0,), (0,)), ((), ())), preferred_element_type=f32)


def contract_cols(left, right):
    return lax.dot_general(left, right, (((1,), (1,)), ((), ())), preferred_element_type=f32)


def body(
    depth,
    tokens,
    segments,
    routes,
    norm_gain,
    in_proj,
    conv_taps,
    conv_bias,
    select_proj,
    step_proj,
    step_bias,
    decay_log,
    skip_gain,
    out_proj,
    moe_gain,
    router,
    expert_up,
    expert_down,
    cotangent,
):
    count = tokens.shape[0]
    rows = PLANE * count
    rim = norm_gain.shape[0]
    ch = conv_bias.shape[0]
    fs = expert_down.shape[1]
    z, p = here()

    win = in_proj.reshape(rim, 2, depth, PLANE, ch).transpose(3, 0, 1, 2, 4).reshape(PLANE, rim, 2 * WIDE)
    small = jnp.concatenate([norm_gain[:, None], moe_gain[:, None], router], axis=1)
    win = jnp.concatenate([win, jnp.broadcast_to(small[None], (PLANE, rim, 4))], axis=2)
    wup = (
        expert_up.reshape(EXPERTS, rim, depth, PLANE, fs)
        .transpose(3, 1, 2, 0, 4)
        .reshape(PLANE, rim, EXPERTS * HID)
    )
    pack = jnp.concatenate(
        [
            out_proj,
            select_proj,
            step_proj.T,
            decay_log.T,
            conv_taps.T,
            conv_bias[:, None],
            step_bias[:, None],
            skip_gain[:, None],
        ],
        axis=1,
    )
    cot_all = lax.all_gather(cotangent, "p", axis=0, tiled=True)
    w_down = lax.all_gather(expert_down.reshape(EXPERTS * fs, D), "z", axis=0, tiled=True)
    tok_all, win_all, up_rows, pack_all = opening(1, depth, tokens, win, wup, pack)
    w_up = lax.all_gather(up_rows.reshape(PLANE * rim, EXPERTS * HID), "z", axis=0, tiled=True)
    tok_all = tok_all.reshape(rows, D)
    win_all = win_all.reshape(D, 2 * WIDE + 4)
    w_in = win_all[:, : 2 * WIDE]
    gain_norm = win_all[:, 2 * WIDE].astype(f32)
    gain_moe = win_all[:, 2 * WIDE + 1].astype(f32)
    w_router = win_all[:, 2 * WIDE + 2 :]
    pack_all = pack_all.reshape(WIDE, -1)
    w_out = pack_all[:, :D]
    w_sel = pack_all[:, D : D + SEL]
    w_step = pack_all[:, D + SEL : D + SEL + RANK]
    rest = pack_all[:, D + SEL + RANK :].astype(f32).T
    rate = -jnp.exp(rest[:STATE])
    taps = rest[STATE : STATE + 4]
    bias, step_off, skip = rest[STATE + 4], rest[STATE + 5], rest[STATE + 6]
    rate2 = rate * LOG2E

    earlier = jnp.concatenate([jnp.full((3,), -1, jnp.int32), segments])
    local_ids = lax.dynamic_slice_in_dim(earlier, z * rows, rows + 3)
    own_ids = local_ids[3:]
    same = jnp.stack([local_ids[k : k + rows] == own_ids for k in range(4)], axis=1).astype(f32)

    _, _, pre_one = norm_rows(tok_all.astype(f32), gain_norm)
    normed_in = pre_one.astype(bf16)
    joined = mm(normed_in, w_in).astype(bf16)
    inner = joined[:, :WIDE]
    gate_in = joined[:, WIDE:].astype(f32)
    later = [(i, i + 1) for i in range(depth - 1)]
    tail = lax.ppermute(inner[rows - 3 :], "z", later)
    padded = jnp.concatenate([tail, inner], axis=0).astype(f32)
    conv = bias + taps[0] * padded[0:rows] * same[:, 0:1]
    for k in range(1, 4):
        conv = conv + taps[k] * padded[k : k + rows] * same[:, k : k + 1]
    signal = jax.nn.silu(conv).astype(bf16)
    value = signal.astype(f32)
    part = jnp.pad(mm(signal, w_sel), ((0, 0), (0, 128 - SEL)))
    selected = plane_total(2, part.reshape(PLANE, count, 128)).reshape(rows, 128)[:, :SEL]
    rank_part = selected[:, :RANK]
    mixes = selected[:, RANK:].astype(f32).reshape(rows // BLK, BLK, 2 * STATE).transpose(0, 2, 1)
    step_pre = contract_cols(rank_part, w_step) + step_off
    delta = jax.nn.softplus(step_pre)
    dk = delta + (1.0 - same[:, 2:3]) * RESET
    push = delta * value
    end, total = scan_ends(dk, push, mixes, rate2)
    ends = column_gather(3, depth, jnp.concatenate([end, jnp.broadcast_to(total, (8, WIDE))], axis=0))
    spans = [jnp.exp2(ends[k, STATE : STATE + 1] * rate2) for k in range(depth)]
    entering = jnp.zeros((STATE, WIDE), f32)
    for k in range(depth - 1):
        entering = jnp.where(k < z, spans[k] * entering + ends[k, :STATE], entering)
    scanned, states = scan_forward(dk, push, mixes, rate2, entering, count)
    mixed_pre = scanned + skip * value
    gate_act = jax.nn.silu(gate_in)
    gated = (mixed_pre * gate_act).astype(bf16)
    (branch,) = plane_reduce(4, mm(gated, w_out).astype(bf16).reshape(PLANE, count, D))

    stream = tokens.astype(f32)
    middle = stream + branch
    normed_two, scale_two, pre_two = norm_rows(middle, gain_moe)
    routed = pre_two.astype(bf16)
    probs = jax.nn.softmax(mm(routed, w_router), axis=-1)
    choose = (routes == jnp.arange(EXPERTS, dtype=jnp.int32)[None, :]).astype(f32)
    order = lax.broadcasted_iota(jnp.int32, (count, count), 0) >= lax.broadcasted_iota(
        jnp.int32, (count, count), 1
    )
    places = mm(order.astype(bf16), choose.astype(bf16))
    slotted = choose * (places <= CAP).astype(f32)
    kept = jnp.sum(slotted, axis=1)
    gate = jnp.sum(probs * choose, axis=1)
    weight = gate * kept
    upstream = cotangent.astype(f32)
    marks = jnp.pad(jnp.concatenate([weight[:, None], slotted], axis=1), ((0, 0), (0, 125)))
    routed_all, marks_all = plane_gather(5, routed, marks)
    routed_all = routed_all.reshape(rows, D)
    marks_all = marks_all.reshape(rows, 128)
    first = (lax.broadcasted_iota(jnp.int32, (1, EXPERTS * HID), 1) // fs) % 2 == 0
    mask = jnp.where(first, marks_all[:, 1:2], marks_all[:, 2:3])
    slot_grad = (cot_all.astype(f32) * marks_all[:, 0:1]).astype(bf16)
    hidden_pre = mm(routed_all, w_up)
    hidden_units = (jax.nn.gelu(hidden_pre) * mask).astype(bf16)
    grad_hidden = contract_cols(slot_grad, w_down)
    grad_pre = (jax.vjp(jax.nn.gelu, hidden_pre)[1](grad_hidden)[0] * mask).astype(bf16)
    expert_part = mm(hidden_units, w_down).astype(bf16).reshape(PLANE, count, D)
    back_part = contract_cols(grad_pre, w_up).astype(bf16).reshape(PLANE, count, D)
    expert_tok, slot_back = plane_reduce(6, expert_part, back_part)
    grad_down = contract_rows(hidden_units, slot_grad).astype(bf16)
    grad_up = contract_rows(routed_all, grad_pre).astype(bf16)
    grad_down_own = lax.psum_scatter(grad_down, "z", scatter_dimension=0, tiled=True)
    grad_up_rows = lax.psum_scatter(grad_up, "z", scatter_dimension=0, tiled=True)

    output = (middle + weight[:, None] * expert_tok).astype(bf16)
    grad_gate = jnp.sum(upstream * expert_tok, axis=1) * kept
    grad_logits = (grad_gate * gate)[:, None] * (choose - probs)
    routed_value = routed.astype(f32)
    grad_router = lax.dot_general(
        routed_value, grad_logits, (((0,), (0,)), ((), ())), precision=lax.Precision.HIGHEST
    )
    grad_routed = slot_back + lax.dot_general(
        grad_logits, w_router.astype(f32), (((1,), (1,)), ((), ())), precision=lax.Precision.HIGHEST
    )
    grad_mid, grad_gain_two = norm_back(grad_routed, normed_two, scale_two, gain_moe)
    grad_mid = grad_mid + upstream
    (branch_all,) = plane_gather(7, grad_mid.astype(bf16))
    branch_all = branch_all.reshape(rows, D)
    grad_out_w = contract_rows(gated, branch_all)
    grad_gated = contract_cols(branch_all, w_out)
    grad_mixed = grad_gated * gate_act
    grad_gate_in = jax.vjp(jax.nn.silu, gate_in)[1](grad_gated * mixed_pre)[0]
    grad_skip = jnp.sum(grad_mixed * value, axis=0)
    message = scan_message(dk, grad_mixed, mixes, rate2)
    messages = column_gather(8, depth, message)
    arriving = jnp.zeros((STATE, WIDE), f32)
    for k in range(depth - 1, 0, -1):
        arriving = jnp.where(k > z, messages[k] + spans[k] * arriving, arriving)
    grad_push, grad_scaled, grad_mixes, grad_rate = scan_adjoint(
        dk, push, grad_mixed, mixes, states, rate2, arriving, count
    )
    grad_delta = grad_scaled * (1.0 / LOG2E) + grad_push * value
    grad_decay = grad_rate * rate
    grad_step_pre = grad_delta * jax.nn.sigmoid(step_pre)
    grad_step_bias = jnp.sum(grad_step_pre, axis=0)
    step_low = grad_step_pre.astype(bf16)
    grad_step_w = contract_rows(step_low, rank_part)
    grad_mixes = grad_mixes.transpose(0, 2, 1).reshape(rows, 2 * STATE)
    part = jnp.pad(
        jnp.concatenate([mm(step_low, w_step), grad_mixes], axis=1), ((0, 0), (0, 128 - SEL))
    )
    grad_selected = plane_total(9, part.reshape(PLANE, count, 128)).reshape(rows, 128)[:, :SEL]
    grad_select_w = contract_rows(signal, grad_selected)
    grad_signal = grad_mixed * skip + grad_push * delta + contract_cols(grad_selected, w_sel)
    grad_conv = jax.vjp(jax.nn.silu, conv)[1](grad_signal)[0]
    grad_conv_bias = jnp.sum(grad_conv, axis=0)
    grad_taps = jnp.stack(
        [jnp.sum(grad_conv * padded[k : k + rows] * same[:, k : k + 1], axis=0) for k in range(4)], axis=1
    )
    grad_padded = jnp.pad(grad_conv * taps[0] * same[:, 0:1], ((0, 3), (0, 0)))
    for k in range(1, 4):
        grad_padded = grad_padded + jnp.pad(
            grad_conv * taps[k] * same[:, k : k + 1], ((k, 3 - k), (0, 0))
        )
    returned = lax.ppermute(grad_padded[:3], "z", [(j, i) for i, j in later])
    grad_inner = grad_padded[3:] + jnp.pad(returned, ((rows - 3, 0), (0, 0)))
    grad_joined = jnp.concatenate([grad_inner, grad_gate_in], axis=1).astype(bf16)
    (grad_normed,) = plane_reduce(10, contract_cols(grad_joined, w_in).astype(bf16).reshape(PLANE, count, D))
    normed_one, scale_one, _ = norm_rows(stream, gain_norm)
    grad_stream, grad_gain_one = norm_back(grad_normed, normed_one, scale_one, gain_norm)
    grad_tokens = (grad_stream + grad_mid).astype(bf16)

    grad_in = jnp.concatenate(
        [contract_rows(normed_in, grad_joined), grad_gain_one[:, None], grad_gain_two[:, None], grad_router],
        axis=1,
    ).astype(bf16)
    grad_pack = jnp.concatenate(
        [
            grad_out_w,
            grad_select_w,
            grad_step_w,
            grad_decay.T,
            grad_taps,
            grad_conv_bias[:, None],
            grad_step_bias[:, None],
            grad_skip[:, None],
        ],
        axis=1,
    ).astype(bf16)
    in_cols, pack_own, up_cols = closing(
        11,
        depth,
        grad_in.reshape(depth, PLANE, rim, 2 * WIDE + 4),
        grad_pack.reshape(depth, ch, -1),
        grad_up_rows.reshape(PLANE, rim, EXPERTS * HID),
    )
    in_cols = in_cols.astype(f32)
    up_cols = up_cols.astype(f32)
    ours = jnp.sum(in_cols[:, :, 2 * WIDE :], axis=0)
    grad_in_own = (
        in_cols[:, :, : 2 * WIDE]
        .reshape(PLANE, rim, 2, depth, ch)
        .transpose(1, 2, 3, 0, 4)
        .reshape(rim, 2 * DI)
    )
    grad_up_own = (
        up_cols.reshape(PLANE, rim, depth, EXPERTS, fs).transpose(3, 1, 2, 0, 4).reshape(EXPERTS, rim, FF)
    )
    side = pack_own[:, D + SEL + RANK :].T
    return (
        output,
        grad_tokens,
        ours[:, 0],
        grad_in_own,
        side[STATE : STATE + 4],
        side[STATE + 4],
        pack_own[:, D : D + SEL],
        pack_own[:, D + SEL : D + SEL + RANK].T,
        side[STATE + 5],
        side[:STATE],
        side[STATE + 6],
        pack_own[:, :D],
        ours[:, 1],
        ours[:, 2:],
        grad_up_own,
        grad_down_own.astype(f32).reshape(EXPERTS, fs, D),
    )


def solution(mesh):
    planes = Mesh(mesh.devices.reshape(-1, PLANE), ("z", "p"))
    every = ("z", "p")
    rows, flat, cols, third = P(every, None), P(every), P(None, every), P(None, every, None)
    return jax.shard_map(
        functools.partial(body, planes.shape["z"]),
        mesh=planes,
        in_specs=(
            rows, P(), rows, flat, rows, cols, flat, rows, cols,
            flat, cols, flat, rows, flat, rows, third, third, rows,
        ),
        out_specs=(
            rows, rows, flat, rows, cols, flat, rows, cols,
            flat, cols, flat, rows, flat, rows, third, third,
        ),
        check_vma=False,
    )
```

```python
import functools

import jax
import jax.numpy as jnp
from jax import lax
from jax.experimental import pallas as pl
from jax.experimental.pallas import tpu as pltpu
from jax.sharding import Mesh, PartitionSpec as P

D = 1152
DI = 2304
FF = 3072
RANK = 72
STATE = 16
EXPERTS = 2
CAP = 68
SEL = RANK + 2 * STATE

PLANE = 8
CHIPS = PLANE // 2
WIDE = DI // PLANE
PAD = -WIDE % 128
HID = FF // PLANE
BLK = 16
LOG2E = 1.4426950408889634
GELU = 0.7978845608028654
RESET = 1e5
epsilon = 1e-05

MESH = pl.DeviceIdType.MESH
ANY = pl.BlockSpec(memory_space=pl.ANY)
VM = pl.BlockSpec(memory_space=pltpu.VMEM)
bf16 = jnp.bfloat16
f32 = jnp.float32
DMA = pltpu.SemaphoreType.DMA


def params(cid=None, grid=None):
    extra = {} if cid is None else {"collective_id": cid, "has_side_effects": True}
    if grid is not None:
        extra["dimension_semantics"] = grid
    return pltpu.CompilerParams(vmem_limit_bytes=60 * 1024 * 1024, **extra)


def cost(us):
    return pl.CostEstimate(flops=int(us * 1e9), bytes_accessed=int(us * 3e6), transcendentals=0)


def send(src, dst, ss, rs, to):
    copy = pltpu.make_async_remote_copy(
        src_ref=src, dst_ref=dst, send_sem=ss, recv_sem=rs, device_id=to, device_id_type=MESH
    )
    copy.start()
    return copy


def here():
    return lax.axis_index("z"), lax.axis_index("p")


def greet(plane=True, depth=0):
    z, p = here()
    barrier = pltpu.get_barrier_semaphore()
    count = 0
    if plane:
        for k in range(1, PLANE):
            pl.semaphore_signal(
                barrier, inc=1, device_id=(z, lax.rem(p + k, PLANE)), device_id_type=MESH
            )
            count += 1
    for k in range(1, depth):
        pl.semaphore_signal(barrier, inc=1, device_id=(lax.rem(z + k, depth), p), device_id_type=MESH)
        count += 1
    pl.semaphore_wait(barrier, count)


def share_start(x, out, ss, rs):
    z, p = here()
    core = lax.rem(p, 2)
    copies = [send(x, out.at[p], ss.at[0], rs.at[0], (z, p + 1 - 2 * core))]
    for k in range(1, CHIPS):
        copies.append(send(x, out.at[p], ss.at[k], rs.at[k], (z, lax.rem(p + 2 * k, PLANE))))
    return copies


def share_forward(out, copies, ss, rs):
    z, p = here()
    core = lax.rem(p, 2)
    onward = []
    for k in range(1, CHIPS):
        copies[k].wait_recv()
        src = lax.rem(p + PLANE - 2 * k, PLANE)
        onward.append(
            send(out.at[src], out.at[src], ss.at[CHIPS + k], rs.at[CHIPS + k], (z, p + 1 - 2 * core))
        )
    return onward


def share_finish(copies, onward):
    copies[0].wait_recv()
    for c in copies:
        c.wait_send()
    for c in onward:
        c.wait()


def share_kernel(count, *refs):
    xs, outs = refs[:count], refs[count : 2 * count]
    ss, rs, ls = refs[2 * count :]
    z, p = here()
    local = [pltpu.make_async_copy(x, o.at[p], ls.at[i]) for i, (x, o) in enumerate(zip(xs, outs))]
    for c in local:
        c.start()
    greet()
    first = [share_start(x, o, ss.at[i], rs.at[i]) for i, (x, o) in enumerate(zip(xs, outs))]
    second = [share_forward(o, first[i], ss.at[i], rs.at[i]) for i, o in enumerate(outs)]
    for c in local:
        c.wait()
    for a, b in zip(first, second):
        share_finish(a, b)


def plane_gather(cid, *xs):
    count = len(xs)
    return pl.pallas_call(
        functools.partial(share_kernel, count),
        out_shape=[jax.ShapeDtypeStruct((PLANE,) + x.shape, x.dtype) for x in xs],
        in_specs=[ANY] * count,
        out_specs=[ANY] * count,
        scratch_shapes=[DMA((count, PLANE)), DMA((count, PLANE)), DMA((count,))],
        compiler_params=params(cid),
        cost_estimate=cost(18),
        name="plane_gather",
    )(*xs)


def reduce_kernel(count, *refs):
    xs, outs = refs[:count], refs[count : 2 * count]
    sib, mix, far, ss, rs, ts, us = refs[2 * count :]
    z, p = here()
    core = lax.rem(p, 2)
    chip = lax.div(p, 2)
    twin = (z, p + 1 - 2 * core)
    greet()
    near = []
    for i in range(count):
        for k in (1, 2, 3, 0):
            q = lax.rem(chip + k, CHIPS)
            near.append(
                send(xs[i].at[2 * q + 1 - core], sib.at[i, k], ss.at[i, k], rs.at[i, k], twin)
            )
    away = []
    for i in range(count):
        for j, k in enumerate((1, 2, 3, 0)):
            q = lax.rem(chip + k, CHIPS)
            near[i * CHIPS + j].wait_recv()
            both = xs[i][2 * q + core].astype(f32) + sib[i, k].astype(f32)
            if k == 0:
                outs[i][...] = both
            else:
                mix[i, k] = both.astype(bf16)
                away.append(
                    send(mix.at[i, k], far.at[i, k], ts.at[i, k], us.at[i, k], (z, lax.rem(p + 2 * k, PLANE)))
                )
    for i in range(count):
        for k in range(1, CHIPS):
            away[i * (CHIPS - 1) + k - 1].wait_recv()
        outs[i][...] += far[i, 1].astype(f32) + far[i, 2].astype(f32) + far[i, 3].astype(f32)
    for c in near + away:
        c.wait_send()


def plane_reduce(cid, *xs):
    count = len(xs)
    rows, cols = xs[0].shape[1:]
    return pl.pallas_call(
        functools.partial(reduce_kernel, count),
        out_shape=[jax.ShapeDtypeStruct((rows, cols), f32) for _ in xs],
        in_specs=[VM] * count,
        out_specs=[VM] * count,
        scratch_shapes=[pltpu.VMEM((count, CHIPS, rows, cols), bf16)] * 3 + [DMA((count, CHIPS))] * 4,
        compiler_params=params(cid),
        cost_estimate=cost(20),
        name="plane_reduce",
    )(*xs)


def total_kernel(x, out, got, own, ss, rs, ts, us):
    z, p = here()
    greet()
    first = []
    for k in range(1, PLANE):
        q = lax.rem(p + k, PLANE)
        first.append(send(x.at[q], got.at[k], ss.at[k], rs.at[k], (z, q)))
    total = x[p]
    for k in range(1, PLANE):
        first[k - 1].wait_recv()
        total = total + got[k]
    own[...] = total.astype(bf16)
    second = []
    for k in range(1, PLANE):
        second.append(send(own, out.at[p], ts.at[k], us.at[k], (z, lax.rem(p + k, PLANE))))
    out[p] = own[...]
    for c in first:
        c.wait_send()
    for c in second:
        c.wait()


def plane_total(cid, x):
    return pl.pallas_call(
        total_kernel,
        out_shape=jax.ShapeDtypeStruct(x.shape, bf16),
        in_specs=[VM],
        out_specs=VM,
        scratch_shapes=[
            pltpu.VMEM(x.shape, f32),
            pltpu.VMEM(x.shape[1:], bf16),
        ]
        + [DMA((PLANE,))] * 4,
        compiler_params=params(cid),
        cost_estimate=cost(14),
        name="plane_total",
    )(x)


def column_kernel(depth, x, out, ss, rs, ls):
    z, p = here()
    local = pltpu.make_async_copy(x, out.at[z], ls)
    local.start()
    greet(False, depth)
    copies = [
        send(x, out.at[z], ss.at[k], rs.at[k], (lax.rem(z + k, depth), p)) for k in range(1, depth)
    ]
    local.wait()
    for c in copies:
        c.wait()


def column_gather(cid, depth, x):
    return pl.pallas_call(
        functools.partial(column_kernel, depth),
        out_shape=jax.ShapeDtypeStruct((depth,) + x.shape, x.dtype),
        in_specs=[VM],
        out_specs=VM,
        scratch_shapes=[DMA((depth,)), DMA((depth,)), DMA],
        compiler_params=params(cid),
        cost_estimate=cost(9),
        name="column_gather",
    )(x)


def opening_kernel(depth, tok, win, wup, pack, tok_all, win_all, up_all, pack_all, ss, rs, ws, wr, vs, vr, zs, zr, ls):
    z, p = here()
    local = [
        pltpu.make_async_copy(tok, tok_all.at[p], ls.at[0]),
        pltpu.make_async_copy(win.at[p], win_all.at[z, p], ls.at[1]),
        pltpu.make_async_copy(wup.at[p], up_all.at[p], ls.at[2]),
        pltpu.make_async_copy(pack, pack_all.at[z], ls.at[3]),
    ]
    for c in local:
        c.start()
    greet(True, depth)
    across = []
    for k in range(1, PLANE):
        q = lax.rem(p + k, PLANE)
        across.append(send(win.at[q], win_all.at[z, p], ws.at[k], wr.at[k], (z, q)))
    down = [
        send(pack, pack_all.at[z], zs.at[0, k], zr.at[0, k], (lax.rem(z + k, depth), p))
        for k in range(1, depth)
    ]
    first = share_start(tok, tok_all, ss, rs)
    local[1].wait()
    for c in across:
        c.wait_recv()
    down += [
        send(win_all.at[z], win_all.at[z], zs.at[1, k], zr.at[1, k], (lax.rem(z + k, depth), p))
        for k in range(1, depth)
    ]
    second = share_forward(tok_all, first, ss, rs)
    more = []
    for k in range(1, PLANE):
        q = lax.rem(p + k, PLANE)
        more.append(send(wup.at[q], up_all.at[p], vs.at[k], vr.at[k], (z, q)))
    share_finish(first, second)
    for c in across:
        c.wait_send()
    for c in more + down:
        c.wait()
    for c in (local[0], local[2], local[3]):
        c.wait()


def opening(cid, depth, tok, win, wup, pack):
    return pl.pallas_call(
        functools.partial(opening_kernel, depth),
        out_shape=[
            jax.ShapeDtypeStruct((PLANE,) + tok.shape, bf16),
            jax.ShapeDtypeStruct((depth,) + win.shape, bf16),
            jax.ShapeDtypeStruct(wup.shape, bf16),
            jax.ShapeDtypeStruct((depth,) + pack.shape, bf16),
        ],
        in_specs=[ANY] * 4,
        out_specs=[ANY] * 4,
        scratch_shapes=[DMA((PLANE,))] * 6 + [DMA((2, depth))] * 2 + [DMA((4,))],
        compiler_params=params(cid),
        cost_estimate=cost(40),
        name="opening",
    )(tok, win, wup, pack)


def closing_kernel(depth, gin, gpack, gup, in_out, pack_out, up_out, got, gotp, own, ss, rs, ps, pr, vs, vr, ls):
    z, p = here()
    local = pltpu.make_async_copy(gup.at[p], up_out.at[p], ls)
    local.start()
    greet(True, depth)
    down = []
    for k in range(1, depth):
        q = lax.rem(z + k, depth)
        down.append(send(gin.at[q], got.at[k], ss.at[0, k], rs.at[0, k], (q, p)))
    downp = []
    for k in range(1, depth):
        q = lax.rem(z + k, depth)
        downp.append(send(gpack.at[q], gotp.at[k], ss.at[1, k], rs.at[1, k], (q, p)))
    more = []
    for k in range(1, PLANE):
        q = lax.rem(p + k, PLANE)
        more.append(send(gup.at[q], up_out.at[p], vs.at[k], vr.at[k], (z, q)))
    for c in down:
        c.wait_recv()
    total = gin[z].astype(f32)
    for k in range(1, depth):
        total = total + got[k].astype(f32)
    own[...] = total.astype(bf16)
    across = []
    for k in range(1, PLANE):
        q = lax.rem(p + k, PLANE)
        across.append(send(own.at[q], in_out.at[p], ps.at[k], pr.at[k], (z, q)))
    in_out[p] = own[p]
    for c in downp:
        c.wait_recv()
    total = gpack[z].astype(f32)
    for k in range(1, depth):
        total = total + gotp[k].astype(f32)
    pack_out[...] = total
    for c in down + downp:
        c.wait_send()
    for c in across + more:
        c.wait()
    local.wait()


def closing(cid, depth, gin, gpack, gup):
    return pl.pallas_call(
        functools.partial(closing_kernel, depth),
        out_shape=[
            jax.ShapeDtypeStruct(gin.shape[1:], bf16),
            jax.ShapeDtypeStruct(gpack.shape[1:], f32),
            jax.ShapeDtypeStruct(gup.shape, bf16),
        ],
        in_specs=[VM] * 2 + [ANY],
        out_specs=[VM] * 2 + [ANY],
        scratch_shapes=[
            pltpu.VMEM(gin.shape, bf16),
            pltpu.VMEM(gpack.shape, bf16),
            pltpu.VMEM(gin.shape[1:], bf16),
        ]
        + [DMA((2, depth))] * 2
        + [DMA((PLANE,))] * 4
        + [DMA],
        compiler_params=params(cid),
        cost_estimate=cost(45),
        name="closing",
    )(gin, gpack, gup)


def middle_kernel(
    fs,
    scanned, signal, gate_in, skip, w_out, tok, cot_all, w_up, w_down, w_router, rows_in, picks,
    output, grad_mid, mixed_grad, gate_grad, grad_out, grad_up, grad_down, sums,
    gated, mixed, part, sib, mix, far, routed_all, marks_all, hidden_all, pre_all, slot_all, back_all, flip,
    near_s, near_r, away_s, away_r, gs, gr,
):
    z, p = here()
    core = lax.rem(p, 2)
    chip = lax.div(p, 2)
    twin = (z, p + 1 - 2 * core)
    count = tok.shape[0]
    pair = 2 * count

    def chip_at(k):
        return lax.rem(chip + k, CHIPS)

    def rows_of(q):
        return pl.ds(pl.multiple_of(q * pair, pair), pair)

    def pass_near(i, k):
        return send(part.at[i, k, 1 - core], sib.at[i, k], near_s.at[i, k], near_r.at[i, k], twin)

    def pass_away(i, k, copy):
        copy.wait_recv()
        mix[i, k] = (part[i, k, core].astype(f32) + sib[i, k].astype(f32)).astype(bf16)
        return send(
            mix.at[i, k], far.at[i, k], away_s.at[i, k], away_r.at[i, k], (z, lax.rem(p + 2 * k, PLANE))
        )

    def gathered(i, near, away):
        near.wait_recv()
        total = part[i, 0, core].astype(f32) + sib[i, 0].astype(f32)
        for k in range(1, CHIPS):
            away[k - 1].wait_recv()
            total = total + far[i, k].astype(f32)
        return total

    greet()
    sent = []
    near = {}
    for k in (1, 2, 3, 0):
        q = chip_at(k)
        at = rows_of(q)
        pre = scanned[at, :WIDE] + skip[0:1] * signal[at, :].astype(f32)
        mixed[at, :] = pre
        inward = gate_in[at, :].astype(f32)
        gated[at, :] = (pre * (inward * jax.nn.sigmoid(inward))).astype(bf16)
        part[0, k] = mm(gated[at, :], w_out[...]).astype(bf16).reshape(2, count, D)
        near[k] = pass_near(0, k)
    away = [pass_away(0, k, near[k]) for k in range(1, CHIPS)]
    branch = gathered(0, near[0], away)
    sent += list(near.values()) + away

    gain, router0, router1 = rows_in[0:1], rows_in[1:2], rows_in[2:3]
    middle = tok[...].astype(f32) + branch
    scale = lax.rsqrt(jnp.mean(middle * middle, axis=-1, keepdims=True) + epsilon)
    normed = middle * scale
    routed = (normed * gain).astype(bf16)
    routed_all[p] = routed
    logits = mm(routed, w_router[...])
    l0, l1 = logits[:, 0:1], logits[:, 1:2]
    top = jnp.maximum(l0, l1)
    e0, e1 = jnp.exp(l0 - top), jnp.exp(l1 - top)
    p0, p1 = e0 / (e0 + e1), e1 / (e0 + e1)
    c0, c1, s0, s1 = (picks[:, k : k + 1] for k in range(4))
    gate = p0 * c0 + p1 * c1
    kept = s0 + s1
    weight = gate * kept
    lane = lax.broadcasted_iota(jnp.int32, (count, 128), 1)
    marks_all[p] = jnp.where(lane == 0, weight, jnp.where(lane == 1, s0, s1))
    first = share_start(routed_all.at[p], routed_all, gs.at[0], gr.at[0])
    firstm = share_start(marks_all.at[p], marks_all, gs.at[1], gr.at[1])

    odd = (lax.div(lax.broadcasted_iota(jnp.int32, (1, EXPERTS * HID), 1), fs) % 2) == 1
    onward, onwardm, near1, near2, away1, away2 = [], [], {}, {}, [], []
    for k in range(CHIPS):
        q = chip_at(k)
        if k == 0:
            first[0].wait_recv()
            firstm[0].wait_recv()
        else:
            src = lax.rem(p + PLANE - 2 * (CHIPS - k), PLANE)
            for copies, ref, after, i in ((first, routed_all, onward, 0), (firstm, marks_all, onwardm, 1)):
                copies[CHIPS - k].wait_recv()
                after.append(
                    send(ref.at[src], ref.at[src], gs.at[i, CHIPS + k], gr.at[i, CHIPS + k], twin)
                )
            onward[-1].wait_recv()
            onwardm[-1].wait_recv()
        both = pl.ds(2 * q, 2)
        marks = marks_all[both].reshape(pair, 128)
        mask = jnp.where(odd, marks[:, 2:3], marks[:, 1:2])
        hidden = mm(routed_all[both].reshape(pair, D), w_up[...])
        slot = (cot_all[rows_of(q), :].astype(f32) * marks[:, 0:1]).astype(bf16)
        slot_all[q] = slot
        square = hidden * hidden
        bend = jnp.tanh(GELU * hidden * (1.0 + 0.044715 * square))
        units = (0.5 * hidden * (1.0 + bend) * mask).astype(bf16)
        hidden_all[q] = units
        slope = 0.5 * (1.0 + bend) + 0.5 * GELU * hidden * (1.0 - bend * bend) * (1.0 + 3 * 0.044715 * square)
        grad = (slope * contract_cols(slot, w_down[...]) * mask).astype(bf16)
        pre_all[q] = grad
        part[1, k] = mm(units, w_down[...]).astype(bf16).reshape(2, count, D)
        near1[k] = pass_near(1, k)
        part[2, k] = contract_cols(grad, w_up[...]).astype(bf16).reshape(2, count, D)
        near2[k] = pass_near(2, k)
        if k > 1:
            away1.append(pass_away(1, k - 1, near1[k - 1]))
            away2.append(pass_away(2, k - 1, near2[k - 1]))
    away1.append(pass_away(1, CHIPS - 1, near1[CHIPS - 1]))
    away2.append(pass_away(2, CHIPS - 1, near2[CHIPS - 1]))
    every = CHIPS * pair
    flip[...] = hidden_all[...].reshape(every, EXPERTS * HID).T
    for c in range(0, D, 384):
        grad_down[:, c : c + 384] = mm(flip[...], slot_all[:, :, c : c + 384].reshape(every, 384)).astype(bf16)
    expert_tok = gathered(1, near1[0], away1)
    slot_back = gathered(2, near2[0], away2)
    sent += list(near1.values()) + list(near2.values()) + away1 + away2

    up = cot_all[pl.ds(pl.multiple_of(p * count, count), count), :].astype(f32)
    output[...] = (middle + weight * expert_tok).astype(bf16)
    pull = jnp.sum(up * expert_tok, axis=-1, keepdims=True) * kept * gate
    g0, g1 = pull * (c0 - p0), pull * (c1 - p1)
    grad_routed = slot_back + g0 * router0 + g1 * router1
    routed = routed.astype(f32)
    sums[0:1] = jnp.sum(grad_routed * normed, axis=0, keepdims=True)
    sums[1:2] = jnp.sum(routed * g0, axis=0, keepdims=True)
    sums[2:3] = jnp.sum(routed * g1, axis=0, keepdims=True)
    grad_normed = grad_routed * gain
    inner = jnp.mean(grad_normed * normed, axis=-1, keepdims=True)
    total = scale * (grad_normed - normed * inner) + up
    grad_mid[...] = total
    back_all[p] = total.astype(bf16)
    last = share_start(back_all.at[p], back_all, gs.at[2], gr.at[2])
    flip[...] = pre_all[...].reshape(every, EXPERTS * HID).T
    for c in range(0, D, 384):
        grad_up[:, c : c + 384] = mm(flip[...], routed_all[:, :, c : c + 384].reshape(every, 384)).astype(bf16)

    skips = jnp.zeros((1, WIDE), f32)
    onwardb = []
    for k in range(CHIPS):
        q = chip_at(k)
        if k == 0:
            last[0].wait_recv()
        else:
            src = lax.rem(p + PLANE - 2 * (CHIPS - k), PLANE)
            last[CHIPS - k].wait_recv()
            onwardb.append(
                send(back_all.at[src], back_all.at[src], gs.at[2, CHIPS + k], gr.at[2, CHIPS + k], twin)
            )
            onwardb[-1].wait_recv()
        at = rows_of(q)
        grad = contract_cols(back_all[pl.ds(2 * q, 2)].reshape(pair, D), w_out[...])
        inward = gate_in[at, :].astype(f32)
        sig = jax.nn.sigmoid(inward)
        act = inward * sig
        through = grad * act
        skips = skips + jnp.sum(through * signal[at, :].astype(f32), axis=0, keepdims=True)
        mixed_grad[at, :WIDE] = through
        mixed_grad[at, WIDE:] = jnp.zeros((pair, PAD), f32)
        gate_grad[at, :] = (grad * mixed[at, :] * (sig * (1.0 + inward * (1.0 - sig)))).astype(bf16)
    sums[3:4] = jnp.concatenate([skips, jnp.zeros((1, D - WIDE), f32)], axis=1)
    for c in range(0, D, 384):
        grad_out[:, c : c + 384] = contract_rows(
            gated[...], back_all[:, :, c : c + 384].reshape(every, 384)
        ).astype(bf16)
    for c in sent:
        c.wait_send()
    for copies, after in ((first, onward), (firstm, onwardm), (last, onwardb)):
        for c in copies + after:
            c.wait_send()


def middle_part(cid, fs, scanned, signal, gate_in, skip, w_out, tok, cot_all, w_up, w_down, w_router, rows_in, picks):
    count, rows = tok.shape[0], cot_all.shape[0]
    wide = EXPERTS * HID
    block = (CHIPS, count, D)
    return pl.pallas_call(
        functools.partial(middle_kernel, fs),
        out_shape=[
            jax.ShapeDtypeStruct((count, D), bf16),
            jax.ShapeDtypeStruct((count, D), f32),
            jax.ShapeDtypeStruct((rows, WIDE + PAD), f32),
            jax.ShapeDtypeStruct((rows, WIDE), bf16),
            jax.ShapeDtypeStruct((WIDE, D), bf16),
            jax.ShapeDtypeStruct((wide, D), bf16),
            jax.ShapeDtypeStruct((wide, D), bf16),
            jax.ShapeDtypeStruct((8, D), f32),
        ],
        in_specs=[VM] * 12,
        out_specs=[VM] * 8,
        scratch_shapes=[
            pltpu.VMEM((rows, WIDE), bf16),
            pltpu.VMEM((rows, WIDE), f32),
            pltpu.VMEM((3, CHIPS, 2, count, D), bf16),
            pltpu.VMEM((3,) + block, bf16),
            pltpu.VMEM((3,) + block, bf16),
            pltpu.VMEM((3,) + block, bf16),
            pltpu.VMEM((PLANE, count, D), bf16),
            pltpu.VMEM((PLANE, count, 128), f32),
            pltpu.VMEM((CHIPS, 2 * count, wide), bf16),
            pltpu.VMEM((CHIPS, 2 * count, wide), bf16),
            pltpu.VMEM((CHIPS, 2 * count, D), bf16),
            pltpu.VMEM((PLANE, count, D), bf16),
            pltpu.VMEM((wide, rows), bf16),
        ]
        + [DMA((3, CHIPS))] * 4
        + [DMA((3, PLANE))] * 2,
        compiler_params=params(cid),
        cost_estimate=cost(75),
        name="middle_part",
    )(scanned, signal, gate_in, skip, w_out, tok, cot_all, w_up, w_down, w_router, rows_in, picks)


def tree(parts):
    row = lax.broadcasted_iota(jnp.int32, parts[0].shape, 0)
    for step in (1, 2, 4):
        low = (row // step) % 2 == 0
        parts = [
            jnp.where(low, a, b) + pltpu.roll(jnp.where(low, b, a), step, 0)
            for a, b in zip(parts[::2], parts[1::2])
        ]
    return parts[0]


def lane_tiles(x):
    total = x[:, :128]
    for k in range(128, x.shape[1], 128):
        total = total + x[:, k : k + 128]
    return total


def spread(ref, i):
    return jnp.broadcast_to(ref[pl.ds(i, 1), :], (8, ref.shape[1]))


HALVES = (slice(0, 8), slice(8, 16))


def ends_kernel(dk, push, sel, rate, end, total):
    slope = [rate[h, :] for h in HALVES]

    def block(b, carry):
        hidden, acc = list(carry[:2]), carry[2]
        base = pl.multiple_of(b * BLK, BLK)
        w = sel[b, :STATE]
        for t in range(BLK):
            d, u = spread(dk, base + t), spread(push, base + t)
            for k, h in enumerate(HALVES):
                hidden[k] = jnp.exp2(d * slope[k]) * hidden[k] + w[h, t : t + 1] * u
            acc = acc + d
        return hidden[0], hidden[1], acc

    zero = jnp.zeros((8, rate.shape[1]), f32)
    first, second, acc = lax.fori_loop(0, dk.shape[0] // BLK, block, (zero, zero, zero))
    end[:8], end[8:] = first, second
    total[...] = acc


def scan_ends(dk, push, sel, rate):
    return pl.pallas_call(
        ends_kernel,
        out_shape=[jax.ShapeDtypeStruct(rate.shape, f32), jax.ShapeDtypeStruct((8, rate.shape[1]), f32)],
        in_specs=[VM] * 4,
        out_specs=[VM] * 2,
        compiler_params=params(),
        cost_estimate=cost(12),
        name="scan_ends",
    )(dk, push, sel, rate)


def scan_kernel(dk, push, sel, rate, start, out, states, hold):
    @pl.when(pl.program_id(0) == 0)
    def _():
        hold[...] = start[...]

    slope = [rate[h, :] for h in HALVES]

    def block(b, carry):
        hidden = list(carry)
        base = pl.multiple_of(b * BLK, BLK)
        w, r = sel[b, :STATE], sel[b, STATE:]
        parts = []
        for t in range(BLK):
            d, u = spread(dk, base + t), spread(push, base + t)
            line = None
            for k, h in enumerate(HALVES):
                hidden[k] = jnp.exp2(d * slope[k]) * hidden[k] + w[h, t : t + 1] * u
                states[base + t, h] = hidden[k]
                y = r[h, t : t + 1] * hidden[k]
                line = y if line is None else line + y
            parts.append(line)
            if len(parts) == 8:
                out[pl.ds(pl.multiple_of(base + t - 7, 8), 8), :] = tree(parts)
                parts = []
        return tuple(hidden)

    first, second = lax.fori_loop(0, dk.shape[0] // BLK, block, (hold[:8], hold[8:]))
    hold[:8], hold[8:] = first, second


def scan_forward(dk, push, sel, rate, start, tile):
    rows, wide = dk.shape
    per = tile // BLK
    return pl.pallas_call(
        scan_kernel,
        grid=(rows // tile,),
        out_shape=[
            jax.ShapeDtypeStruct((rows, wide), f32),
            jax.ShapeDtypeStruct((rows, STATE, wide), f32),
        ],
        in_specs=[
            pl.BlockSpec((tile, wide), lambda i: (i, 0)),
            pl.BlockSpec((tile, wide), lambda i: (i, 0)),
            pl.BlockSpec((per, 2 * STATE, BLK), lambda i: (i, 0, 0)),
            pl.BlockSpec((STATE, wide), lambda i: (0, 0)),
            pl.BlockSpec((STATE, wide), lambda i: (0, 0)),
        ],
        out_specs=[
            pl.BlockSpec((tile, wide), lambda i: (i, 0)),
            pl.BlockSpec((tile, STATE, wide), lambda i: (i, 0, 0)),
        ],
        scratch_shapes=[pltpu.VMEM((STATE, wide), f32)],
        compiler_params=params(grid=("arbitrary",)),
        cost_estimate=cost(18),
        name="scan_forward",
    )(dk, push, sel, rate, start)


def message_kernel(dk, grad, sel, rate, out):
    slope = [rate[h, :] for h in HALVES]
    blocks = dk.shape[0] // BLK

    def block(i, carry):
        message = list(carry)
        b = blocks - 1 - i
        base = pl.multiple_of(b * BLK, BLK)
        r = sel[b, STATE:]
        for t in reversed(range(BLK)):
            d, g = spread(dk, base + t), spread(grad, base + t)
            for k, h in enumerate(HALVES):
                message[k] = jnp.exp2(d * slope[k]) * (r[h, t : t + 1] * g + message[k])
        return tuple(message)

    zero = jnp.zeros((8, rate.shape[1]), f32)
    first, second = lax.fori_loop(0, blocks, block, (zero, zero))
    out[:8], out[8:] = first, second


def scan_message(dk, grad, sel, rate):
    return pl.pallas_call(
        message_kernel,
        out_shape=jax.ShapeDtypeStruct(rate.shape, f32),
        in_specs=[VM] * 4,
        out_specs=VM,
        compiler_params=params(),
        cost_estimate=cost(12),
        name="scan_message",
    )(dk, grad, sel, rate)


def adjoint_kernel(dk, push, grad, sel, states, rate, arriving, g_push, g_step, g_sel, g_rate, hold):
    @pl.when(pl.program_id(0) == 0)
    def _():
        hold[...] = arriving[...]
        g_rate[...] = jnp.zeros_like(g_rate)

    slope = [rate[h, :] for h in HALVES]
    blocks = dk.shape[0] // BLK
    lane = lax.broadcasted_iota(jnp.int32, (STATE, 128), 1)
    ones = jnp.ones((128, 128), bf16)

    def block(i, carry):
        message, acc = list(carry[:2]), list(carry[2:])
        b = blocks - 1 - i
        base = pl.multiple_of(b * BLK, BLK)
        w, r = sel[b, :STATE], sel[b, STATE:]
        pushes, steps = [], []
        reads, writes = [None] * (2 * BLK), [None] * (2 * BLK)
        for t in reversed(range(BLK)):
            d, u, g = spread(dk, base + t), spread(push, base + t), spread(grad, base + t)
            plain = jnp.where(d < RESET, d, 0.0)
            to_push = to_step = None
            for k, h in enumerate(HALVES):
                wt = w[h, t : t + 1]
                hidden = states[base + t, h]
                total = r[h, t : t + 1] * g + message[k]
                reads[2 * t + k] = lane_tiles(hidden * g)
                writes[2 * t + k] = lane_tiles(total * u)
                x = total * wt
                carried = total * (hidden - wt * u)
                y = carried * slope[k]
                to_push = x if k == 0 else to_push + x
                to_step = y if k == 0 else to_step + y
                acc[k] = acc[k] + carried * plain
                message[k] = jnp.exp2(d * slope[k]) * total
            pushes.insert(0, to_push)
            steps.insert(0, to_step)
            if len(pushes) == 8:
                at = pl.ds(pl.multiple_of(base + t, 8), 8)
                g_push[at, :] = tree(pushes)
                g_step[at, :] = tree(steps)
                pushes, steps = [], []
        for j, quantity in enumerate((writes, reads)):
            x = jnp.concatenate(quantity, axis=0)
            high = x.astype(bf16)
            low = (x - high.astype(f32)).astype(bf16)
            sums = jnp.dot(high, ones, preferred_element_type=f32)
            sums = sums + jnp.dot(low, ones, preferred_element_type=f32)
            kept = jnp.zeros((STATE, 128), f32)
            for t in range(BLK):
                kept = jnp.where(lane == t, sums[STATE * t : STATE * t + STATE], kept)
            g_sel[b, STATE * j : STATE * j + STATE] = kept[:, :BLK]
        return message[0], message[1], acc[0], acc[1]

    done = lax.fori_loop(0, blocks, block, (hold[:8], hold[8:], g_rate[:8], g_rate[8:]))
    hold[:8], hold[8:], g_rate[:8], g_rate[8:] = done


def scan_adjoint(dk, push, grad, sel, states, rate, arriving, tile):
    rows, wide = dk.shape
    per, last = tile // BLK, rows // tile - 1
    line = pl.BlockSpec((tile, wide), lambda i: (last - i, 0))
    mix = pl.BlockSpec((per, 2 * STATE, BLK), lambda i: (last - i, 0, 0))
    flat = pl.BlockSpec((STATE, wide), lambda i: (0, 0))
    return pl.pallas_call(
        adjoint_kernel,
        grid=(rows // tile,),
        out_shape=[
            jax.ShapeDtypeStruct((rows, wide), f32),
            jax.ShapeDtypeStruct((rows, wide), f32),
            jax.ShapeDtypeStruct(sel.shape, f32),
            jax.ShapeDtypeStruct((STATE, wide), f32),
        ],
        in_specs=[line, line, line, mix, pl.BlockSpec((tile, STATE, wide), lambda i: (last - i, 0, 0)), flat, flat],
        out_specs=[line, line, mix, flat],
        scratch_shapes=[pltpu.VMEM((STATE, wide), f32)],
        compiler_params=params(grid=("arbitrary",)),
        cost_estimate=cost(38),
        name="scan_adjoint",
    )(dk, push, grad, sel, states, rate, arriving)


def norm_rows(values, gain):
    scale = lax.rsqrt(jnp.mean(values * values, axis=-1, keepdims=True) + epsilon)
    normed = values * scale
    return normed, scale, normed * gain


def norm_back(grad_out, normed, scale, gain):
    grad_normed = grad_out * gain
    grad_gain = jnp.sum(grad_out * normed, axis=0)
    inner_mean = jnp.mean(grad_normed * normed, axis=-1, keepdims=True)
    return scale * (grad_normed - normed * inner_mean), grad_gain


def mm(left, right):
    return jnp.dot(left, right, preferred_element_type=f32)


def contract_rows(left, right):
    return lax.dot_general(left, right, (((0,), (0,)), ((), ())), preferred_element_type=f32)


def contract_cols(left, right):
    return lax.dot_general(left, right, (((1,), (1,)), ((), ())), preferred_element_type=f32)


def body(
    depth,
    tokens,
    segments,
    routes,
    norm_gain,
    in_proj,
    conv_taps,
    conv_bias,
    select_proj,
    step_proj,
    step_bias,
    decay_log,
    skip_gain,
    out_proj,
    moe_gain,
    router,
    expert_up,
    expert_down,
    cotangent,
):
    count = tokens.shape[0]
    rows = PLANE * count
    rim = norm_gain.shape[0]
    ch = conv_bias.shape[0]
    fs = expert_down.shape[1]
    z, p = here()

    win = in_proj.reshape(rim, 2, depth, PLANE, ch).transpose(3, 0, 1, 2, 4).reshape(PLANE, rim, 2 * WIDE)
    small = jnp.concatenate([norm_gain[:, None], moe_gain[:, None], router], axis=1)
    win = jnp.concatenate([win, jnp.broadcast_to(small[None], (PLANE, rim, 4))], axis=2)
    wup = (
        expert_up.reshape(EXPERTS, rim, depth, PLANE, fs)
        .transpose(3, 1, 2, 0, 4)
        .reshape(PLANE, rim, EXPERTS * HID)
    )
    pack = jnp.concatenate(
        [
            select_proj,
            step_proj.T,
            decay_log.T,
            conv_taps.T,
            conv_bias[:, None],
            step_bias[:, None],
            skip_gain[:, None],
        ],
        axis=1,
    )
    cot_all = lax.all_gather(cotangent, "p", axis=0, tiled=True)
    lower = lax.all_gather(
        jnp.concatenate([expert_down.reshape(EXPERTS * fs, D), out_proj], axis=0), "z", axis=0, tiled=False
    )
    w_down = lower[:, : EXPERTS * fs].reshape(EXPERTS * HID, D)
    w_out = lower[:, EXPERTS * fs :].reshape(WIDE, D)
    tok_all, win_all, up_rows, pack_all = opening(1, depth, tokens, win, wup, pack)
    w_up = lax.all_gather(up_rows.reshape(PLANE * rim, EXPERTS * HID), "z", axis=0, tiled=True)
    tok_all = tok_all.reshape(rows, D)
    win_all = win_all.reshape(D, 2 * WIDE + 4)
    w_in = win_all[:, : 2 * WIDE]
    gain_norm = win_all[:, 2 * WIDE].astype(f32)
    w_router = win_all[:, 2 * WIDE + 2 :]
    small_all = win_all[:, 2 * WIDE :].T
    pack_all = pack_all.reshape(WIDE, -1)
    w_sel = pack_all[:, :SEL]
    w_step = pack_all[:, SEL : SEL + RANK]
    rest = pack_all[:, SEL + RANK :].astype(f32).T
    rate = -jnp.exp(rest[:STATE])
    taps = rest[STATE : STATE + 4]
    bias, step_off, skip = rest[STATE + 4], rest[STATE + 5], rest[STATE + 6]
    rate2 = jnp.pad(rate * LOG2E, ((0, 0), (0, PAD)))

    earlier = jnp.concatenate([jnp.full((3,), -1, jnp.int32), segments])
    local_ids = lax.dynamic_slice_in_dim(earlier, z * rows, rows + 3)
    own_ids = local_ids[3:]
    same = jnp.stack([local_ids[k : k + rows] == own_ids for k in range(4)], axis=1).astype(f32)

    _, _, pre_one = norm_rows(tok_all.astype(f32), gain_norm)
    normed_in = pre_one.astype(bf16)
    joined = mm(normed_in, w_in).astype(bf16)
    inner = joined[:, :WIDE]
    gate_in = joined[:, WIDE:]
    later = [(i, i + 1) for i in range(depth - 1)]
    tail = lax.ppermute(inner[rows - 3 :], "z", later)
    padded = jnp.concatenate([tail, inner], axis=0).astype(f32)
    conv = bias + taps[0] * padded[0:rows] * same[:, 0:1]
    for k in range(1, 4):
        conv = conv + taps[k] * padded[k : k + rows] * same[:, k : k + 1]
    signal = jax.nn.silu(conv).astype(bf16)
    value = signal.astype(f32)
    part = jnp.pad(mm(signal, w_sel), ((0, 0), (0, 128 - SEL)))
    selected = plane_total(2, part.reshape(PLANE, count, 128)).reshape(rows, 128)[:, :SEL]
    rank_part = selected[:, :RANK]
    mixes = selected[:, RANK:].astype(f32).reshape(rows // BLK, BLK, 2 * STATE).transpose(0, 2, 1)
    step_pre = contract_cols(rank_part, w_step) + step_off
    delta = jax.nn.softplus(step_pre)
    dk = delta + (1.0 - same[:, 2:3]) * RESET
    push = delta * value
    dk_wide = jnp.pad(dk, ((0, 0), (0, PAD)))
    push_wide = jnp.pad(push, ((0, 0), (0, PAD)))
    end, total = scan_ends(dk_wide, push_wide, mixes, rate2)
    ends = column_gather(3, depth, jnp.concatenate([end, total], axis=0))
    spans = [jnp.exp2(ends[k, STATE : STATE + 1] * rate2) for k in range(depth)]
    entering = jnp.zeros((STATE, WIDE + PAD), f32)
    for k in range(depth - 1):
        entering = jnp.where(k < z, spans[k] * entering + ends[k, :STATE], entering)
    scanned, states = scan_forward(dk_wide, push_wide, mixes, rate2, entering, count)
    choose = (routes == jnp.arange(EXPERTS, dtype=jnp.int32)[None, :]).astype(f32)
    order = lax.broadcasted_iota(jnp.int32, (count, count), 0) >= lax.broadcasted_iota(
        jnp.int32, (count, count), 1
    )
    places = mm(order.astype(bf16), choose.astype(bf16))
    slotted = choose * (places <= CAP).astype(f32)
    picks = jnp.pad(jnp.concatenate([choose, slotted], axis=1), ((0, 0), (0, 124)))
    output, grad_mid, mixed_wide, grad_gate_in, grad_out_w, grad_up, grad_down, sums = middle_part(
        4,
        fs,
        scanned,
        signal,
        gate_in,
        jnp.broadcast_to(skip[None], (8, WIDE)),
        w_out,
        tokens,
        cot_all,
        w_up,
        w_down,
        jnp.pad(w_router, ((0, 0), (0, 126))),
        jnp.pad(small_all[1:].astype(f32), ((0, 5), (0, 0))),
        picks,
    )
    grad_out_own = lax.psum_scatter(grad_out_w, "z", scatter_dimension=0, tiled=True).astype(f32)
    grad_down_own = lax.psum_scatter(grad_down, "z", scatter_dimension=0, tiled=True)
    grad_up_rows = lax.psum_scatter(grad_up.T, "z", scatter_dimension=0, tiled=True)
    grad_mixed = mixed_wide[:, :WIDE]
    grad_skip = sums[3, :WIDE]
    stream = tokens.astype(f32)
    message = scan_message(dk_wide, mixed_wide, mixes, rate2)
    messages = column_gather(8, depth, message)
    arriving = jnp.zeros((STATE, WIDE + PAD), f32)
    for k in range(depth - 1, 0, -1):
        arriving = jnp.where(k > z, messages[k] + spans[k] * arriving, arriving)
    grad_push, grad_scaled, grad_mixes, grad_rate = scan_adjoint(
        dk_wide, push_wide, mixed_wide, mixes, states, rate2, arriving, count
    )
    grad_push, grad_scaled, grad_rate = grad_push[:, :WIDE], grad_scaled[:, :WIDE], grad_rate[:, :WIDE]
    grad_delta = grad_scaled * (1.0 / LOG2E) + grad_push * value
    grad_decay = grad_rate * rate
    grad_step_pre = grad_delta * jax.nn.sigmoid(step_pre)
    grad_step_bias = jnp.sum(grad_step_pre, axis=0)
    step_low = grad_step_pre.astype(bf16)
    grad_step_w = contract_rows(step_low, rank_part)
    grad_mixes = grad_mixes.transpose(0, 2, 1).reshape(rows, 2 * STATE)
    part = jnp.pad(
        jnp.concatenate([mm(step_low, w_step), grad_mixes], axis=1), ((0, 0), (0, 128 - SEL))
    )
    grad_selected = plane_total(9, part.reshape(PLANE, count, 128)).reshape(rows, 128)[:, :SEL]
    grad_select_w = contract_rows(signal, grad_selected)
    grad_signal = grad_mixed * skip + grad_push * delta + contract_cols(grad_selected, w_sel)
    grad_conv = jax.vjp(jax.nn.silu, conv)[1](grad_signal)[0]
    grad_conv_bias = jnp.sum(grad_conv, axis=0)
    grad_taps = jnp.stack(
        [jnp.sum(grad_conv * padded[k : k + rows] * same[:, k : k + 1], axis=0) for k in range(4)], axis=1
    )
    grad_padded = jnp.pad(grad_conv * taps[0] * same[:, 0:1], ((0, 3), (0, 0)))
    for k in range(1, 4):
        grad_padded = grad_padded + jnp.pad(
            grad_conv * taps[k] * same[:, k : k + 1], ((k, 3 - k), (0, 0))
        )
    returned = lax.ppermute(grad_padded[:3], "z", [(j, i) for i, j in later])
    grad_inner = grad_padded[3:] + jnp.pad(returned, ((rows - 3, 0), (0, 0)))
    grad_joined = jnp.concatenate([grad_inner.astype(bf16), grad_gate_in], axis=1)
    (grad_normed,) = plane_reduce(10, contract_cols(grad_joined, w_in).astype(bf16).reshape(PLANE, count, D))
    normed_one, scale_one, _ = norm_rows(stream, gain_norm)
    grad_stream, grad_gain_one = norm_back(grad_normed, normed_one, scale_one, gain_norm)
    grad_tokens = (grad_stream + grad_mid).astype(bf16)

    grad_in = jnp.concatenate(
        [contract_rows(normed_in, grad_joined), grad_gain_one[:, None], sums[:3].T],
        axis=1,
    ).astype(bf16)
    grad_pack = jnp.concatenate(
        [
            grad_select_w,
            grad_step_w,
            grad_decay.T,
            grad_taps,
            grad_conv_bias[:, None],
            grad_step_bias[:, None],
            grad_skip[:, None],
        ],
        axis=1,
    ).astype(bf16)
    in_cols, pack_own, up_cols = closing(
        11,
        depth,
        grad_in.reshape(depth, PLANE, rim, 2 * WIDE + 4),
        grad_pack.reshape(depth, ch, -1),
        grad_up_rows.reshape(PLANE, rim, EXPERTS * HID),
    )
    in_cols = in_cols.astype(f32)
    up_cols = up_cols.astype(f32)
    ours = jnp.sum(in_cols[:, :, 2 * WIDE :], axis=0)
    grad_in_own = (
        in_cols[:, :, : 2 * WIDE]
        .reshape(PLANE, rim, 2, depth, ch)
        .transpose(1, 2, 3, 0, 4)
        .reshape(rim, 2 * DI)
    )
    grad_up_own = (
        up_cols.reshape(PLANE, rim, depth, EXPERTS, fs).transpose(3, 1, 2, 0, 4).reshape(EXPERTS, rim, FF)
    )
    side = pack_own[:, SEL + RANK :].T
    return (
        output,
        grad_tokens,
        ours[:, 0],
        grad_in_own,
        side[STATE : STATE + 4],
        side[STATE + 4],
        pack_own[:, :SEL],
        pack_own[:, SEL : SEL + RANK].T,
        side[STATE + 5],
        side[:STATE],
        side[STATE + 6],
        grad_out_own,
        ours[:, 1],
        ours[:, 2:],
        grad_up_own,
        grad_down_own.astype(f32).reshape(EXPERTS, fs, D),
    )


def solution(mesh):
    planes = Mesh(mesh.devices.reshape(-1, PLANE), ("z", "p"))
    every = ("z", "p")
    rows, flat, cols, third = P(every, None), P(every), P(None, every), P(None, every, None)
    return jax.shard_map(
        functools.partial(body, planes.shape["z"]),
        mesh=planes,
        in_specs=(
            rows, P(), rows, flat, rows, cols, flat, rows, cols,
            flat, cols, flat, rows, flat, rows, third, third, rows,
        ),
        out_specs=(
            rows, rows, flat, rows, cols, flat, rows, cols,
            flat, cols, flat, rows, flat, rows, third, third,
        ),
        check_vma=False,
    )
```

```python
import functools

import jax
import jax.numpy as jnp
from jax import lax
from jax.experimental import pallas as pl
from jax.experimental.pallas import tpu as pltpu
from jax.sharding import Mesh, PartitionSpec as P

D = 1152
DI = 2304
FF = 3072
RANK = 72
STATE = 16
EXPERTS = 2
CAP = 68
SEL = RANK + 2 * STATE

PLANE = 8
CHIPS = PLANE // 2
WIDE = DI // PLANE
PAD = -WIDE % 128
HID = FF // PLANE
BLK = 16
LOG2E = 1.4426950408889634
GELU = 0.7978845608028654
RESET = 1e5
epsilon = 1e-05

MESH = pl.DeviceIdType.MESH
ANY = pl.BlockSpec(memory_space=pl.ANY)
VM = pl.BlockSpec(memory_space=pltpu.VMEM)
bf16 = jnp.bfloat16
f32 = jnp.float32
DMA = pltpu.SemaphoreType.DMA


def params(cid=None, grid=None):
    extra = {} if cid is None else {"collective_id": cid, "has_side_effects": True}
    if grid is not None:
        extra["dimension_semantics"] = grid
    return pltpu.CompilerParams(vmem_limit_bytes=60 * 1024 * 1024, **extra)


def cost(us):
    return pl.CostEstimate(flops=int(us * 1e9), bytes_accessed=int(us * 3e6), transcendentals=0)


def mm(left, right):
    return jnp.dot(left, right, preferred_element_type=f32)


def contract_rows(left, right):
    return lax.dot_general(left, right, (((0,), (0,)), ((), ())), preferred_element_type=f32)


def contract_cols(left, right):
    return lax.dot_general(left, right, (((1,), (1,)), ((), ())), preferred_element_type=f32)


def send(src, dst, ss, rs, to):
    copy = pltpu.make_async_remote_copy(
        src_ref=src, dst_ref=dst, send_sem=ss, recv_sem=rs, device_id=to, device_id_type=MESH
    )
    copy.start()
    return copy


def here():
    return lax.axis_index("z"), lax.axis_index("p")


def greet(plane=True, depth=0):
    z, p = here()
    barrier = pltpu.get_barrier_semaphore()
    count = 0
    if plane:
        for k in range(1, PLANE):
            pl.semaphore_signal(
                barrier, inc=1, device_id=(z, lax.rem(p + k, PLANE)), device_id_type=MESH
            )
            count += 1
    for k in range(1, depth):
        pl.semaphore_signal(barrier, inc=1, device_id=(lax.rem(z + k, depth), p), device_id_type=MESH)
        count += 1
    pl.semaphore_wait(barrier, count)


def share_start(x, out, ss, rs):
    z, p = here()
    core = lax.rem(p, 2)
    copies = [send(x, out.at[p], ss.at[0], rs.at[0], (z, p + 1 - 2 * core))]
    for k in range(1, CHIPS):
        copies.append(send(x, out.at[p], ss.at[k], rs.at[k], (z, lax.rem(p + 2 * k, PLANE))))
    return copies


def share_forward(out, copies, ss, rs):
    z, p = here()
    core = lax.rem(p, 2)
    onward = []
    for k in range(1, CHIPS):
        copies[k].wait_recv()
        src = lax.rem(p + PLANE - 2 * k, PLANE)
        onward.append(
            send(out.at[src], out.at[src], ss.at[CHIPS + k], rs.at[CHIPS + k], (z, p + 1 - 2 * core))
        )
    return onward


def share_finish(copies, onward):
    copies[0].wait_recv()
    for c in copies:
        c.wait_send()
    for c in onward:
        c.wait()


def column_kernel(depth, x, out, ss, rs, ls):
    z, p = here()
    local = pltpu.make_async_copy(x, out.at[z], ls)
    local.start()
    greet(False, depth)
    copies = [
        send(x, out.at[z], ss.at[k], rs.at[k], (lax.rem(z + k, depth), p)) for k in range(1, depth)
    ]
    local.wait()
    for c in copies:
        c.wait()


def column_gather(cid, depth, x):
    return pl.pallas_call(
        functools.partial(column_kernel, depth),
        out_shape=jax.ShapeDtypeStruct((depth,) + x.shape, x.dtype),
        in_specs=[VM],
        out_specs=VM,
        scratch_shapes=[DMA((depth,)), DMA((depth,)), DMA],
        compiler_params=params(cid),
        cost_estimate=cost(9),
        name="column_gather",
    )(x)


def opening_kernel(depth, tok, win, wup, pack, tok_all, win_all, up_all, pack_all, ss, rs, ws, wr, vs, vr, zs, zr, ls):
    z, p = here()
    local = [
        pltpu.make_async_copy(tok, tok_all.at[p], ls.at[0]),
        pltpu.make_async_copy(win.at[p], win_all.at[z, p], ls.at[1]),
        pltpu.make_async_copy(wup.at[p], up_all.at[p], ls.at[2]),
        pltpu.make_async_copy(pack, pack_all.at[z], ls.at[3]),
    ]
    for c in local:
        c.start()
    greet(True, depth)
    across = []
    for k in range(1, PLANE):
        q = lax.rem(p + k, PLANE)
        across.append(send(win.at[q], win_all.at[z, p], ws.at[k], wr.at[k], (z, q)))
    down = [
        send(pack, pack_all.at[z], zs.at[0, k], zr.at[0, k], (lax.rem(z + k, depth), p))
        for k in range(1, depth)
    ]
    first = share_start(tok, tok_all, ss, rs)
    local[1].wait()
    for c in across:
        c.wait_recv()
    down += [
        send(win_all.at[z], win_all.at[z], zs.at[1, k], zr.at[1, k], (lax.rem(z + k, depth), p))
        for k in range(1, depth)
    ]
    second = share_forward(tok_all, first, ss, rs)
    more = []
    for k in range(1, PLANE):
        q = lax.rem(p + k, PLANE)
        more.append(send(wup.at[q], up_all.at[p], vs.at[k], vr.at[k], (z, q)))
    share_finish(first, second)
    for c in across:
        c.wait_send()
    for c in more + down:
        c.wait()
    for c in (local[0], local[2], local[3]):
        c.wait()


def opening(cid, depth, tok, win, wup, pack):
    return pl.pallas_call(
        functools.partial(opening_kernel, depth),
        out_shape=[
            jax.ShapeDtypeStruct((PLANE,) + tok.shape, bf16),
            jax.ShapeDtypeStruct((depth,) + win.shape, bf16),
            jax.ShapeDtypeStruct(wup.shape, bf16),
            jax.ShapeDtypeStruct((depth,) + pack.shape, bf16),
        ],
        in_specs=[ANY] * 4,
        out_specs=[ANY] * 4,
        scratch_shapes=[DMA((PLANE,))] * 6 + [DMA((2, depth))] * 2 + [DMA((4,))],
        compiler_params=params(cid),
        cost_estimate=cost(40),
        name="opening",
    )(tok, win, wup, pack)


def softplus(x):
    return jnp.maximum(x, 0.0) + jnp.log1p(jnp.exp(-jnp.abs(x)))


def total_start(x, got, ss, rs):
    z, p = here()
    copies = []
    for k in range(1, PLANE):
        q = lax.rem(p + k, PLANE)
        copies.append(send(x.at[q], got.at[k], ss.at[k], rs.at[k], (z, q)))
    return copies


def total_share(x, got, copies, out, ts, us):
    z, p = here()
    total = x[p]
    for k in range(1, PLANE):
        copies[k - 1].wait_recv()
        total = total + got[k]
    out[p] = total.astype(bf16)
    after = [
        send(out.at[p], out.at[p], ts.at[k], us.at[k], (z, lax.rem(p + k, PLANE))) for k in range(1, PLANE)
    ]
    for c in copies:
        c.wait_send()
    return after


def front_kernel(
    depth,
    tok_all, w_in, gain, same, vecs, w_sel, w_step,
    normed_in, inner, gate_in, conv, signal, selected, mixes, step_pre, dk, push,
    near, halo, x, got, sel_all, hs, ss, rs, ts, us,
):
    z, p = here()
    count = tok_all.shape[1]
    pair = 2 * count
    rows = PLANE * count
    greet(True, depth)
    for b in (3, 0, 1, 2):
        at = slice(pair * b, pair * b + pair)
        values = tok_all[2 * b : 2 * b + 2].reshape(pair, D).astype(f32)
        scale = lax.rsqrt(jnp.mean(values * values, axis=-1, keepdims=True) + epsilon)
        normed = (values * scale * gain[0:1]).astype(bf16)
        normed_in[at, :] = normed
        joined = mm(normed, w_in[...]).astype(bf16)
        near[BLK + pair * b : BLK + pair * b + pair, :] = joined[:, :WIDE].astype(f32)
        gate_in[at, :] = joined[:, WIDE:]
        if b == 3:
            edge = send(near.at[pl.ds(rows, BLK)], halo, hs.at[0], hs.at[1], (lax.rem(z + 1, depth), p))
    for b in (1, 2, 3, 0):
        if b == 0:
            edge.wait()
            near[:BLK, :] = halo[...]
        base = pair * b
        at = slice(base, base + pair)
        total = vecs[4:5] + vecs[0:1] * near[base + 13 : base + 13 + pair, :] * same[at, 0:1]
        for k in range(1, 4):
            total = total + vecs[k : k + 1] * near[base + 13 + k : base + 13 + k + pair, :] * same[at, k : k + 1]
        conv[at, :] = total
        value = (total * jax.nn.sigmoid(total)).astype(bf16)
        signal[at, :] = value
        x[2 * b : 2 * b + 2] = mm(value, w_sel[...]).reshape(2, count, 128)
    first = total_start(x, got, ss, rs)
    inner[...] = near[...].astype(bf16)
    second = total_share(x, got, first, sel_all, ts, us)
    for c in second:
        c.wait()
    for b in range(CHIPS):
        at = slice(pair * b, pair * b + pair)
        chosen = sel_all[2 * b : 2 * b + 2].reshape(pair, 128)
        selected[at, :] = chosen
        step = contract_cols(chosen, w_step[...]) + vecs[5:6]
        step_pre[at, :] = step
        delta = softplus(step)
        dk[at, :WIDE] = delta + (1.0 - same[at, 2:3]) * RESET
        push[at, :WIDE] = delta * signal[at, :].astype(f32)
        dk[at, WIDE:] = jnp.zeros((pair, PAD), f32)
        push[at, WIDE:] = jnp.zeros((pair, PAD), f32)
        wide = chosen.astype(f32)
        for i in range(pair // BLK):
            flipped = wide[i * BLK : i * BLK + BLK].T
            mixes[b * (pair // BLK) + i] = flipped[RANK:SEL]


def front_part(cid, depth, tok_all, w_in, gain, same, vecs, w_sel, w_step):
    count = tok_all.shape[1]
    rows = PLANE * count

    def made(*shape, dtype=f32):
        return jax.ShapeDtypeStruct(shape, dtype)

    return pl.pallas_call(
        functools.partial(front_kernel, depth),
        out_shape=[
            made(rows, D, dtype=bf16),
            made(rows + BLK, WIDE, dtype=bf16),
            made(rows, WIDE, dtype=bf16),
            made(rows, WIDE),
            made(rows, WIDE, dtype=bf16),
            made(rows, 128, dtype=bf16),
            made(rows // BLK, 2 * STATE, BLK),
            made(rows, WIDE),
            made(rows, WIDE + PAD),
            made(rows, WIDE + PAD),
        ],
        in_specs=[VM] * 7,
        out_specs=[VM] * 10,
        scratch_shapes=[
            pltpu.VMEM((BLK + rows, WIDE), f32),
            pltpu.VMEM((BLK, WIDE), f32),
            pltpu.VMEM((PLANE, count, 128), f32),
            pltpu.VMEM((PLANE, count, 128), f32),
            pltpu.VMEM((PLANE, count, 128), bf16),
            DMA((2,)),
        ]
        + [DMA((PLANE,))] * 4,
        compiler_params=params(cid),
        cost_estimate=cost(30),
        name="front_part",
    )(tok_all, w_in, gain, same, vecs, w_sel, w_step)


def back_kernel(
    depth,
    g_push, g_step, g_mixes, g_rate, step_pre, signal, conv, inner, same, vecs, rate, selected, w_sel, w_step,
    mixed_grad, gate_grad, w_in, normed_in, tok, gain, grad_mid, sums, gup,
    tokens_out, in_out, up_out, pack_out, small_out,
    x, got, gsel, low, gc, halo, nearf, gj, part, sib, mix, far, gin, gin_got, own, pack, pack_got, row, row_got, sml, sml_got,
    hs, ss, rs, ts, us, near_s, near_r, away_s, away_r, zs, zr, cs, cr, ups, upr, ls,
):
    z, p = here()
    core = lax.rem(p, 2)
    chip = lax.div(p, 2)
    twin = (z, p + 1 - 2 * core)
    count = tok.shape[0]
    pair = 2 * count
    rows = PLANE * count
    ch = pack_out.shape[0]
    rim = in_out.shape[1]
    sent = []

    def down(i, src, dst):
        copies = []
        for k in range(1, depth):
            q = lax.rem(z + k, depth)
            copies.append(send(src.at[q], dst.at[k], zs.at[i, k], zr.at[i, k], (q, p)))
        return copies

    keep = pltpu.make_async_copy(gup.at[p], up_out.at[p], ls)
    keep.start()
    greet(True, depth)
    bias = jnp.zeros((1, WIDE), f32)
    for b in range(CHIPS):
        at = slice(pair * b, pair * b + pair)
        value = signal[at, :].astype(f32)
        grad = g_step[at, :WIDE] * (1.0 / LOG2E) + g_push[at, :WIDE] * value
        grad = grad * jax.nn.sigmoid(step_pre[at, :])
        bias = bias + jnp.sum(grad, axis=0, keepdims=True)
        low[at, :] = grad.astype(bf16)
        ranks = mm(low[at, :], w_step[...])
        for i in range(pair // BLK):
            block = g_mixes[b * (pair // BLK) + i]
            wide = jnp.concatenate(
                [jnp.zeros((RANK, BLK), f32), block, jnp.zeros((128 - SEL, BLK), f32)], axis=0
            ).T
            t = i * BLK
            x[2 * b + t // count, t % count : t % count + BLK, :] = ranks[t : t + BLK] + wide
    first = total_start(x, got, ss, rs)
    ups_sent = []
    for k in range(1, PLANE):
        q = lax.rem(p + k, PLANE)
        ups_sent.append(send(gup.at[q], up_out.at[p], ups.at[k], upr.at[k], (z, q)))
    grad_step_w = contract_rows(low[...], selected[...])
    nearf[...] = inner[...].astype(f32)
    second = total_share(x, got, first, gsel, ts, us)
    for c in second:
        c.wait()
    taps = [jnp.zeros((1, WIDE), f32)] * 4
    conv_bias = jnp.zeros((1, WIDE), f32)
    for b in range(CHIPS):
        base = pair * b
        at = slice(base, base + pair)
        delta = softplus(step_pre[at, :])
        grad = mixed_grad[at, :WIDE] * vecs[6:7] + g_push[at, :WIDE] * delta
        grad = grad + contract_cols(gsel[2 * b : 2 * b + 2].reshape(pair, 128), w_sel[...])
        c = conv[at, :]
        sig = jax.nn.sigmoid(c)
        grad = grad * (sig * (1.0 + c * (1.0 - sig)))
        gc[at, :] = grad
        if b == 0:
            edge = send(gc.at[pl.ds(0, BLK)], halo, hs.at[0], hs.at[1], (lax.rem(z + depth - 1, depth), p))
        conv_bias = conv_bias + jnp.sum(grad, axis=0, keepdims=True)
        for k in range(4):
            taps[k] = taps[k] + jnp.sum(
                grad * nearf[base + 13 + k : base + 13 + k + pair, :] * same[at, k : k + 1], axis=0, keepdims=True
            )
    for b in range(CHIPS):
        base = pair * b
        if b == CHIPS - 1:
            edge.wait()
            gc[rows : rows + BLK, :] = halo[...]
        total = jnp.zeros((pair, WIDE), f32)
        for k in range(4):
            off = slice(base + 3 - k, base + 3 - k + pair)
            total = total + gc[off, :] * vecs[k : k + 1] * same[off, k : k + 1]
        gj[base : base + pair, :WIDE] = total.astype(bf16)
        gj[base : base + pair, WIDE:] = gate_grad[base : base + pair, :]
    block = D // depth
    for q in range(depth):
        gin[q] = contract_rows(normed_in[:, q * block : q * block + block], gj[...]).astype(bf16)
    in_sent = down(0, gin, gin_got)
    near = {}
    for k in (1, 2, 3, 0):
        q = lax.rem(chip + k, CHIPS)
        at = pl.ds(pl.multiple_of(q * pair, pair), pair)
        part[k] = contract_cols(gj[at, :], w_in[...]).astype(bf16).reshape(2, count, D)
        near[k] = send(part.at[k, 1 - core], sib.at[k], near_s.at[k], near_r.at[k], twin)
    away = []
    for k in range(1, CHIPS):
        near[k].wait_recv()
        mix[k] = (part[k, core].astype(f32) + sib[k].astype(f32)).astype(bf16)
        away.append(
            send(mix.at[k], far.at[k], away_s.at[k], away_r.at[k], (z, lax.rem(p + 2 * k, PLANE)))
        )
    row[...] = jnp.zeros_like(row)
    row[0:STATE, :] = g_rate[...] * rate[...]
    for k in range(4):
        row[STATE + k : STATE + k + 1, :WIDE] = taps[k]
    row[STATE + 4 : STATE + 5, :WIDE] = conv_bias
    row[STATE + 5 : STATE + 6, :WIDE] = bias
    row[STATE + 6 : STATE + 7, :WIDE] = sums[3:4, :WIDE]
    side = row[...].T
    grad_sel_w = contract_rows(signal[...], gsel[...].reshape(rows, 128))
    for q in range(depth):
        cut = slice(q * ch, q * ch + ch)
        pack[q, :, :128] = grad_sel_w[cut].astype(bf16)
        pack[q, :, 128:256] = grad_step_w[cut].astype(bf16)
        pack[q, :, 256:] = side[cut].astype(bf16)
    pack_sent = down(1, pack, pack_got)
    near[0].wait_recv()
    total = part[0, core].astype(f32) + sib[0].astype(f32)
    for k in range(1, CHIPS):
        away[k - 1].wait_recv()
        total = total + far[k].astype(f32)
    values = tok[...].astype(f32)
    scale = lax.rsqrt(jnp.mean(values * values, axis=-1, keepdims=True) + epsilon)
    normed = values * scale
    grad_normed = total * gain[0:1]
    mean = jnp.mean(grad_normed * normed, axis=-1, keepdims=True)
    tokens_out[...] = (scale * (grad_normed - normed * mean) + grad_mid[...]).astype(bf16)
    ours = jnp.concatenate(
        [jnp.sum(total * normed, axis=0, keepdims=True), sums[0:3, :], jnp.zeros((4, D), f32)], axis=0
    )
    for q in range(depth):
        sml[q] = ours[:, q * block : q * block + block]
    sml_sent = down(2, sml, sml_got)
    for c in in_sent:
        c.wait_recv()
    total = gin[z].astype(f32)
    for k in range(1, depth):
        total = total + gin_got[k].astype(f32)
    for q in range(PLANE):
        own[q] = total[q * rim : q * rim + rim].astype(bf16)
    across = []
    for k in range(1, PLANE):
        q = lax.rem(p + k, PLANE)
        across.append(send(own.at[q], in_out.at[p], cs.at[0, k], cr.at[0, k], (z, q)))
    in_out[p] = own[p]
    for c in sml_sent:
        c.wait_recv()
    total = sml[z]
    for k in range(1, depth):
        total = total + sml_got[k]
    sml_got[0] = total
    for k in range(1, PLANE):
        q = lax.rem(p + k, PLANE)
        across.append(send(sml_got.at[0], row_got.at[k], cs.at[1, k], cr.at[1, k], (z, q)))
    for c in pack_sent:
        c.wait_recv()
    total = pack[z].astype(f32)
    for k in range(1, depth):
        total = total + pack_got[k].astype(f32)
    pack_out[...] = total
    for c in across:
        c.wait()
    total = sml_got[0]
    for k in range(1, PLANE):
        total = total + row_got[k]
    small_out[...] = total
    for c in list(near.values()) + away + in_sent + pack_sent + sml_sent:
        c.wait_send()
    for c in ups_sent:
        c.wait()
    keep.wait()


def back_part(cid, depth, rim, ch, *args):
    count = args[18].shape[0]
    rows = PLANE * count
    block = D // depth

    def made(*shape, dtype=f32):
        return jax.ShapeDtypeStruct(shape, dtype)

    return pl.pallas_call(
        functools.partial(back_kernel, depth),
        out_shape=[
            made(count, D, dtype=bf16),
            made(PLANE, rim, 2 * WIDE, dtype=bf16),
            made(PLANE, rim, EXPERTS * HID, dtype=bf16),
            made(ch, 288),
            made(8, block),
        ],
        in_specs=[VM] * 22 + [ANY],
        out_specs=[VM, VM, ANY, VM, VM],
        scratch_shapes=[
            pltpu.VMEM((PLANE, count, 128), f32),
            pltpu.VMEM((PLANE, count, 128), f32),
            pltpu.VMEM((PLANE, count, 128), bf16),
            pltpu.VMEM((rows, WIDE), bf16),
            pltpu.VMEM((rows + BLK, WIDE), f32),
            pltpu.VMEM((BLK, WIDE), f32),
            pltpu.VMEM((rows + BLK, WIDE), f32),
            pltpu.VMEM((rows, 2 * WIDE), bf16),
            pltpu.VMEM((CHIPS, 2, count, D), bf16),
            pltpu.VMEM((CHIPS, count, D), bf16),
            pltpu.VMEM((CHIPS, count, D), bf16),
            pltpu.VMEM((CHIPS, count, D), bf16),
            pltpu.VMEM((depth, block, 2 * WIDE), bf16),
            pltpu.VMEM((depth, block, 2 * WIDE), bf16),
            pltpu.VMEM((PLANE, rim, 2 * WIDE), bf16),
            pltpu.VMEM((depth, ch, 288), bf16),
            pltpu.VMEM((depth, ch, 288), bf16),
            pltpu.VMEM((2 * STATE, WIDE + PAD), f32),
            pltpu.VMEM((PLANE, 8, block), f32),
            pltpu.VMEM((depth, 8, block), f32),
            pltpu.VMEM((depth, 8, block), f32),
            DMA((2,)),
        ]
        + [DMA((PLANE,))] * 4
        + [DMA((CHIPS,))] * 4
        + [DMA((3, depth))] * 2
        + [DMA((2, PLANE))] * 2
        + [DMA((PLANE,))] * 2
        + [DMA],
        compiler_params=params(cid),
        cost_estimate=cost(70),
        name="back_part",
    )(*args)


def middle_kernel(
    fs,
    scanned, signal, gate_in, skip, w_out, tok, cot_all, w_up, w_down, w_router, rows_in, picks,
    output, grad_mid, mixed_grad, gate_grad, grad_out, grad_up, grad_down, sums,
    gated, mixed, part, sib, mix, far, routed_all, marks_all, hidden_all, pre_all, slot_all, back_all, flip,
    near_s, near_r, away_s, away_r, gs, gr,
):
    z, p = here()
    core = lax.rem(p, 2)
    chip = lax.div(p, 2)
    twin = (z, p + 1 - 2 * core)
    count = tok.shape[0]
    pair = 2 * count

    def chip_at(k):
        return lax.rem(chip + k, CHIPS)

    def rows_of(q):
        return pl.ds(pl.multiple_of(q * pair, pair), pair)

    def pass_near(i, k):
        return send(part.at[i, k, 1 - core], sib.at[i, k], near_s.at[i, k], near_r.at[i, k], twin)

    def pass_away(i, k, copy):
        copy.wait_recv()
        mix[i, k] = (part[i, k, core].astype(f32) + sib[i, k].astype(f32)).astype(bf16)
        return send(
            mix.at[i, k], far.at[i, k], away_s.at[i, k], away_r.at[i, k], (z, lax.rem(p + 2 * k, PLANE))
        )

    def gathered(i, near, away):
        near.wait_recv()
        total = part[i, 0, core].astype(f32) + sib[i, 0].astype(f32)
        for k in range(1, CHIPS):
            away[k - 1].wait_recv()
            total = total + far[i, k].astype(f32)
        return total

    greet()
    sent = []
    near = {}
    for k in (1, 2, 3, 0):
        q = chip_at(k)
        at = rows_of(q)
        pre = scanned[at, :WIDE] + skip[0:1] * signal[at, :].astype(f32)
        mixed[at, :] = pre
        inward = gate_in[at, :].astype(f32)
        gated[at, :] = (pre * (inward * jax.nn.sigmoid(inward))).astype(bf16)
        part[0, k] = mm(gated[at, :], w_out[...]).astype(bf16).reshape(2, count, D)
        near[k] = pass_near(0, k)
    away = [pass_away(0, k, near[k]) for k in range(1, CHIPS)]
    branch = gathered(0, near[0], away)
    sent += list(near.values()) + away

    gain, router0, router1 = rows_in[0:1], rows_in[1:2], rows_in[2:3]
    middle = tok[...].astype(f32) + branch
    scale = lax.rsqrt(jnp.mean(middle * middle, axis=-1, keepdims=True) + epsilon)
    normed = middle * scale
    routed = (normed * gain).astype(bf16)
    routed_all[p] = routed
    logits = mm(routed, w_router[...])
    l0, l1 = logits[:, 0:1], logits[:, 1:2]
    top = jnp.maximum(l0, l1)
    e0, e1 = jnp.exp(l0 - top), jnp.exp(l1 - top)
    p0, p1 = e0 / (e0 + e1), e1 / (e0 + e1)
    c0, c1, s0, s1 = (picks[:, k : k + 1] for k in range(4))
    gate = p0 * c0 + p1 * c1
    kept = s0 + s1
    weight = gate * kept
    lane = lax.broadcasted_iota(jnp.int32, (count, 128), 1)
    marks_all[p] = jnp.where(lane == 0, weight, jnp.where(lane == 1, s0, s1))
    first = share_start(routed_all.at[p], routed_all, gs.at[0], gr.at[0])
    firstm = share_start(marks_all.at[p], marks_all, gs.at[1], gr.at[1])

    odd = (lax.div(lax.broadcasted_iota(jnp.int32, (1, EXPERTS * HID), 1), fs) % 2) == 1
    onward, onwardm, near1, near2, away1, away2 = [], [], {}, {}, [], []
    for k in range(CHIPS):
        q = chip_at(k)
        if k == 0:
            first[0].wait_recv()
            firstm[0].wait_recv()
        else:
            src = lax.rem(p + PLANE - 2 * (CHIPS - k), PLANE)
            for copies, ref, after, i in ((first, routed_all, onward, 0), (firstm, marks_all, onwardm, 1)):
                copies[CHIPS - k].wait_recv()
                after.append(
                    send(ref.at[src], ref.at[src], gs.at[i, CHIPS + k], gr.at[i, CHIPS + k], twin)
                )
            onward[-1].wait_recv()
            onwardm[-1].wait_recv()
        both = pl.ds(2 * q, 2)
        marks = marks_all[both].reshape(pair, 128)
        mask = jnp.where(odd, marks[:, 2:3], marks[:, 1:2])
        hidden = mm(routed_all[both].reshape(pair, D), w_up[...])
        slot = (cot_all[rows_of(q), :].astype(f32) * marks[:, 0:1]).astype(bf16)
        slot_all[q] = slot
        square = hidden * hidden
        bend = jnp.tanh(GELU * hidden * (1.0 + 0.044715 * square))
        units = (0.5 * hidden * (1.0 + bend) * mask).astype(bf16)
        hidden_all[q] = units
        slope = 0.5 * (1.0 + bend) + 0.5 * GELU * hidden * (1.0 - bend * bend) * (1.0 + 3 * 0.044715 * square)
        grad = (slope * contract_cols(slot, w_down[...]) * mask).astype(bf16)
        pre_all[q] = grad
        part[1, k] = mm(units, w_down[...]).astype(bf16).reshape(2, count, D)
        near1[k] = pass_near(1, k)
        part[2, k] = contract_cols(grad, w_up[...]).astype(bf16).reshape(2, count, D)
        near2[k] = pass_near(2, k)
        if k > 1:
            away1.append(pass_away(1, k - 1, near1[k - 1]))
            away2.append(pass_away(2, k - 1, near2[k - 1]))
    away1.append(pass_away(1, CHIPS - 1, near1[CHIPS - 1]))
    away2.append(pass_away(2, CHIPS - 1, near2[CHIPS - 1]))
    every = CHIPS * pair
    flip[...] = hidden_all[...].reshape(every, EXPERTS * HID).T
    for c in range(0, D, 384):
        grad_down[:, c : c + 384] = mm(flip[...], slot_all[:, :, c : c + 384].reshape(every, 384)).astype(bf16)
    expert_tok = gathered(1, near1[0], away1)
    slot_back = gathered(2, near2[0], away2)
    sent += list(near1.values()) + list(near2.values()) + away1 + away2

    up = cot_all[pl.ds(pl.multiple_of(p * count, count), count), :].astype(f32)
    output[...] = (middle + weight * expert_tok).astype(bf16)
    pull = jnp.sum(up * expert_tok, axis=-1, keepdims=True) * kept * gate
    g0, g1 = pull * (c0 - p0), pull * (c1 - p1)
    grad_routed = slot_back + g0 * router0 + g1 * router1
    routed = routed.astype(f32)
    sums[0:1] = jnp.sum(grad_routed * normed, axis=0, keepdims=True)
    sums[1:2] = jnp.sum(routed * g0, axis=0, keepdims=True)
    sums[2:3] = jnp.sum(routed * g1, axis=0, keepdims=True)
    grad_normed = grad_routed * gain
    inner = jnp.mean(grad_normed * normed, axis=-1, keepdims=True)
    total = scale * (grad_normed - normed * inner) + up
    grad_mid[...] = total
    back_all[p] = total.astype(bf16)
    last = share_start(back_all.at[p], back_all, gs.at[2], gr.at[2])
    flip[...] = pre_all[...].reshape(every, EXPERTS * HID).T
    for c in range(0, D, 384):
        grad_up[:, c : c + 384] = mm(flip[...], routed_all[:, :, c : c + 384].reshape(every, 384)).astype(bf16)

    skips = jnp.zeros((1, WIDE), f32)
    onwardb = []
    for k in range(CHIPS):
        q = chip_at(k)
        if k == 0:
            last[0].wait_recv()
        else:
            src = lax.rem(p + PLANE - 2 * (CHIPS - k), PLANE)
            last[CHIPS - k].wait_recv()
            onwardb.append(
                send(back_all.at[src], back_all.at[src], gs.at[2, CHIPS + k], gr.at[2, CHIPS + k], twin)
            )
            onwardb[-1].wait_recv()
        at = rows_of(q)
        grad = contract_cols(back_all[pl.ds(2 * q, 2)].reshape(pair, D), w_out[...])
        inward = gate_in[at, :].astype(f32)
        sig = jax.nn.sigmoid(inward)
        act = inward * sig
        through = grad * act
        skips = skips + jnp.sum(through * signal[at, :].astype(f32), axis=0, keepdims=True)
        mixed_grad[at, :WIDE] = through
        mixed_grad[at, WIDE:] = jnp.zeros((pair, PAD), f32)
        gate_grad[at, :] = (grad * mixed[at, :] * (sig * (1.0 + inward * (1.0 - sig)))).astype(bf16)
    sums[3:4] = jnp.concatenate([skips, jnp.zeros((1, D - WIDE), f32)], axis=1)
    for c in range(0, D, 384):
        grad_out[:, c : c + 384] = contract_rows(
            gated[...], back_all[:, :, c : c + 384].reshape(every, 384)
        ).astype(bf16)
    for c in sent:
        c.wait_send()
    for copies, after in ((first, onward), (firstm, onwardm), (last, onwardb)):
        for c in copies + after:
            c.wait_send()


def middle_part(cid, fs, scanned, signal, gate_in, skip, w_out, tok, cot_all, w_up, w_down, w_router, rows_in, picks):
    count, rows = tok.shape[0], cot_all.shape[0]
    wide = EXPERTS * HID
    block = (CHIPS, count, D)
    return pl.pallas_call(
        functools.partial(middle_kernel, fs),
        out_shape=[
            jax.ShapeDtypeStruct((count, D), bf16),
            jax.ShapeDtypeStruct((count, D), f32),
            jax.ShapeDtypeStruct((rows, WIDE + PAD), f32),
            jax.ShapeDtypeStruct((rows, WIDE), bf16),
            jax.ShapeDtypeStruct((WIDE, D), bf16),
            jax.ShapeDtypeStruct((wide, D), bf16),
            jax.ShapeDtypeStruct((wide, D), bf16),
            jax.ShapeDtypeStruct((8, D), f32),
        ],
        in_specs=[VM] * 12,
        out_specs=[VM] * 8,
        scratch_shapes=[
            pltpu.VMEM((rows, WIDE), bf16),
            pltpu.VMEM((rows, WIDE), f32),
            pltpu.VMEM((3, CHIPS, 2, count, D), bf16),
            pltpu.VMEM((3,) + block, bf16),
            pltpu.VMEM((3,) + block, bf16),
            pltpu.VMEM((3,) + block, bf16),
            pltpu.VMEM((PLANE, count, D), bf16),
            pltpu.VMEM((PLANE, count, 128), f32),
            pltpu.VMEM((CHIPS, 2 * count, wide), bf16),
            pltpu.VMEM((CHIPS, 2 * count, wide), bf16),
            pltpu.VMEM((CHIPS, 2 * count, D), bf16),
            pltpu.VMEM((PLANE, count, D), bf16),
            pltpu.VMEM((wide, rows), bf16),
        ]
        + [DMA((3, CHIPS))] * 4
        + [DMA((3, PLANE))] * 2,
        compiler_params=params(cid),
        cost_estimate=cost(75),
        name="middle_part",
    )(scanned, signal, gate_in, skip, w_out, tok, cot_all, w_up, w_down, w_router, rows_in, picks)


def tree(parts):
    row = lax.broadcasted_iota(jnp.int32, parts[0].shape, 0)
    for step in (1, 2, 4):
        low = (row // step) % 2 == 0
        parts = [
            jnp.where(low, a, b) + pltpu.roll(jnp.where(low, b, a), step, 0)
            for a, b in zip(parts[::2], parts[1::2])
        ]
    return parts[0]


def lane_tiles(x):
    total = x[:, :128]
    for k in range(128, x.shape[1], 128):
        total = total + x[:, k : k + 128]
    return total


def spread(ref, i):
    return jnp.broadcast_to(ref[pl.ds(i, 1), :], (8, ref.shape[1]))


HALVES = (slice(0, 8), slice(8, 16))


def ends_kernel(dk, push, sel, rate, end, total):
    slope = [rate[h, :] for h in HALVES]

    def block(b, carry):
        hidden, acc = list(carry[:2]), carry[2]
        base = pl.multiple_of(b * BLK, BLK)
        w = sel[b, :STATE]
        for t in range(BLK):
            d, u = spread(dk, base + t), spread(push, base + t)
            for k, h in enumerate(HALVES):
                hidden[k] = jnp.exp2(d * slope[k]) * hidden[k] + w[h, t : t + 1] * u
            acc = acc + d
        return hidden[0], hidden[1], acc

    zero = jnp.zeros((8, rate.shape[1]), f32)
    first, second, acc = lax.fori_loop(0, dk.shape[0] // BLK, block, (zero, zero, zero))
    end[:8], end[8:] = first, second
    total[...] = acc


def scan_ends(dk, push, sel, rate):
    return pl.pallas_call(
        ends_kernel,
        out_shape=[jax.ShapeDtypeStruct(rate.shape, f32), jax.ShapeDtypeStruct((8, rate.shape[1]), f32)],
        in_specs=[VM] * 4,
        out_specs=[VM] * 2,
        compiler_params=params(),
        cost_estimate=cost(12),
        name="scan_ends",
    )(dk, push, sel, rate)


def scan_kernel(dk, push, sel, rate, start, out, states, hold):
    @pl.when(pl.program_id(0) == 0)
    def _():
        hold[...] = start[...]

    slope = [rate[h, :] for h in HALVES]

    def block(b, carry):
        hidden = list(carry)
        base = pl.multiple_of(b * BLK, BLK)
        w, r = sel[b, :STATE], sel[b, STATE:]
        parts = []
        for t in range(BLK):
            d, u = spread(dk, base + t), spread(push, base + t)
            line = None
            for k, h in enumerate(HALVES):
                hidden[k] = jnp.exp2(d * slope[k]) * hidden[k] + w[h, t : t + 1] * u
                states[base + t, h] = hidden[k]
                y = r[h, t : t + 1] * hidden[k]
                line = y if line is None else line + y
            parts.append(line)
            if len(parts) == 8:
                out[pl.ds(pl.multiple_of(base + t - 7, 8), 8), :] = tree(parts)
                parts = []
        return tuple(hidden)

    first, second = lax.fori_loop(0, dk.shape[0] // BLK, block, (hold[:8], hold[8:]))
    hold[:8], hold[8:] = first, second


def scan_forward(dk, push, sel, rate, start, tile):
    rows, wide = dk.shape
    per = tile // BLK
    return pl.pallas_call(
        scan_kernel,
        grid=(rows // tile,),
        out_shape=[
            jax.ShapeDtypeStruct((rows, wide), f32),
            jax.ShapeDtypeStruct((rows, STATE, wide), f32),
        ],
        in_specs=[
            pl.BlockSpec((tile, wide), lambda i: (i, 0)),
            pl.BlockSpec((tile, wide), lambda i: (i, 0)),
            pl.BlockSpec((per, 2 * STATE, BLK), lambda i: (i, 0, 0)),
            pl.BlockSpec((STATE, wide), lambda i: (0, 0)),
            pl.BlockSpec((STATE, wide), lambda i: (0, 0)),
        ],
        out_specs=[
            pl.BlockSpec((tile, wide), lambda i: (i, 0)),
            pl.BlockSpec((tile, STATE, wide), lambda i: (i, 0, 0)),
        ],
        scratch_shapes=[pltpu.VMEM((STATE, wide), f32)],
        compiler_params=params(grid=("arbitrary",)),
        cost_estimate=cost(18),
        name="scan_forward",
    )(dk, push, sel, rate, start)


def message_kernel(dk, grad, sel, rate, out):
    slope = [rate[h, :] for h in HALVES]
    blocks = dk.shape[0] // BLK

    def block(i, carry):
        message = list(carry)
        b = blocks - 1 - i
        base = pl.multiple_of(b * BLK, BLK)
        r = sel[b, STATE:]
        for t in reversed(range(BLK)):
            d, g = spread(dk, base + t), spread(grad, base + t)
            for k, h in enumerate(HALVES):
                message[k] = jnp.exp2(d * slope[k]) * (r[h, t : t + 1] * g + message[k])
        return tuple(message)

    zero = jnp.zeros((8, rate.shape[1]), f32)
    first, second = lax.fori_loop(0, blocks, block, (zero, zero))
    out[:8], out[8:] = first, second


def scan_message(dk, grad, sel, rate):
    return pl.pallas_call(
        message_kernel,
        out_shape=jax.ShapeDtypeStruct(rate.shape, f32),
        in_specs=[VM] * 4,
        out_specs=VM,
        compiler_params=params(),
        cost_estimate=cost(12),
        name="scan_message",
    )(dk, grad, sel, rate)


def adjoint_kernel(dk, push, grad, sel, states, rate, arriving, g_push, g_step, g_sel, g_rate, hold):
    @pl.when(pl.program_id(0) == 0)
    def _():
        hold[...] = arriving[...]
        g_rate[...] = jnp.zeros_like(g_rate)

    slope = [rate[h, :] for h in HALVES]
    blocks = dk.shape[0] // BLK
    lane = lax.broadcasted_iota(jnp.int32, (STATE, 128), 1)
    ones = jnp.ones((128, 128), bf16)

    def block(i, carry):
        message, acc = list(carry[:2]), list(carry[2:])
        b = blocks - 1 - i
        base = pl.multiple_of(b * BLK, BLK)
        w, r = sel[b, :STATE], sel[b, STATE:]
        pushes, steps = [], []
        reads, writes = [None] * (2 * BLK), [None] * (2 * BLK)
        for t in reversed(range(BLK)):
            d, u, g = spread(dk, base + t), spread(push, base + t), spread(grad, base + t)
            plain = jnp.where(d < RESET, d, 0.0)
            to_push = to_step = None
            for k, h in enumerate(HALVES):
                wt = w[h, t : t + 1]
                hidden = states[base + t, h]
                total = r[h, t : t + 1] * g + message[k]
                reads[2 * t + k] = lane_tiles(hidden * g)
                writes[2 * t + k] = lane_tiles(total * u)
                x = total * wt
                carried = total * (hidden - wt * u)
                y = carried * slope[k]
                to_push = x if k == 0 else to_push + x
                to_step = y if k == 0 else to_step + y
                acc[k] = acc[k] + carried * plain
                message[k] = jnp.exp2(d * slope[k]) * total
            pushes.insert(0, to_push)
            steps.insert(0, to_step)
            if len(pushes) == 8:
                at = pl.ds(pl.multiple_of(base + t, 8), 8)
                g_push[at, :] = tree(pushes)
                g_step[at, :] = tree(steps)
                pushes, steps = [], []
        for j, quantity in enumerate((writes, reads)):
            x = jnp.concatenate(quantity, axis=0)
            high = x.astype(bf16)
            low = (x - high.astype(f32)).astype(bf16)
            sums = jnp.dot(high, ones, preferred_element_type=f32)
            sums = sums + jnp.dot(low, ones, preferred_element_type=f32)
            kept = jnp.zeros((STATE, 128), f32)
            for t in range(BLK):
                kept = jnp.where(lane == t, sums[STATE * t : STATE * t + STATE], kept)
            g_sel[b, STATE * j : STATE * j + STATE] = kept[:, :BLK]
        return message[0], message[1], acc[0], acc[1]

    done = lax.fori_loop(0, blocks, block, (hold[:8], hold[8:], g_rate[:8], g_rate[8:]))
    hold[:8], hold[8:], g_rate[:8], g_rate[8:] = done


def scan_adjoint(dk, push, grad, sel, states, rate, arriving, tile):
    rows, wide = dk.shape
    per, last = tile // BLK, rows // tile - 1
    line = pl.BlockSpec((tile, wide), lambda i: (last - i, 0))
    mix = pl.BlockSpec((per, 2 * STATE, BLK), lambda i: (last - i, 0, 0))
    flat = pl.BlockSpec((STATE, wide), lambda i: (0, 0))
    return pl.pallas_call(
        adjoint_kernel,
        grid=(rows // tile,),
        out_shape=[
            jax.ShapeDtypeStruct((rows, wide), f32),
            jax.ShapeDtypeStruct((rows, wide), f32),
            jax.ShapeDtypeStruct(sel.shape, f32),
            jax.ShapeDtypeStruct((STATE, wide), f32),
        ],
        in_specs=[line, line, line, mix, pl.BlockSpec((tile, STATE, wide), lambda i: (last - i, 0, 0)), flat, flat],
        out_specs=[line, line, mix, flat],
        scratch_shapes=[pltpu.VMEM((STATE, wide), f32)],
        compiler_params=params(grid=("arbitrary",)),
        cost_estimate=cost(38),
        name="scan_adjoint",
    )(dk, push, grad, sel, states, rate, arriving)


def body(
    depth,
    tokens,
    segments,
    routes,
    norm_gain,
    in_proj,
    conv_taps,
    conv_bias,
    select_proj,
    step_proj,
    step_bias,
    decay_log,
    skip_gain,
    out_proj,
    moe_gain,
    router,
    expert_up,
    expert_down,
    cotangent,
):
    count = tokens.shape[0]
    rows = PLANE * count
    rim = norm_gain.shape[0]
    ch = conv_bias.shape[0]
    fs = expert_down.shape[1]
    z, p = here()

    win = in_proj.reshape(rim, 2, depth, PLANE, ch).transpose(3, 0, 1, 2, 4).reshape(PLANE, rim, 2 * WIDE)
    small = jnp.concatenate([norm_gain[:, None], moe_gain[:, None], router], axis=1)
    win = jnp.concatenate([win, jnp.broadcast_to(small[None], (PLANE, rim, 4))], axis=2)
    wup = (
        expert_up.reshape(EXPERTS, rim, depth, PLANE, fs)
        .transpose(3, 1, 2, 0, 4)
        .reshape(PLANE, rim, EXPERTS * HID)
    )
    pack = jnp.concatenate(
        [
            select_proj,
            step_proj.T,
            decay_log.T,
            conv_taps.T,
            conv_bias[:, None],
            step_bias[:, None],
            skip_gain[:, None],
        ],
        axis=1,
    )
    cot_all = lax.all_gather(cotangent, "p", axis=0, tiled=True)
    lower = lax.all_gather(
        jnp.concatenate([expert_down.reshape(EXPERTS * fs, D), out_proj], axis=0), "z", axis=0, tiled=False
    )
    w_down = lower[:, : EXPERTS * fs].reshape(EXPERTS * HID, D)
    w_out = lower[:, EXPERTS * fs :].reshape(WIDE, D)
    tok_all, win_all, up_rows, pack_all = opening(1, depth, tokens, win, wup, pack)
    w_up = lax.all_gather(up_rows.reshape(PLANE * rim, EXPERTS * HID), "z", axis=0, tiled=True)
    win_all = win_all.reshape(D, 2 * WIDE + 4)
    w_in = win_all[:, : 2 * WIDE]
    small_all = win_all[:, 2 * WIDE :].T
    gain_rows = jnp.pad(small_all[:1].astype(f32), ((0, 7), (0, 0)))
    w_router = win_all[:, 2 * WIDE + 2 :]
    pack_all = pack_all.reshape(WIDE, -1)
    w_sel = jnp.pad(pack_all[:, :SEL], ((0, 0), (0, 128 - SEL)))
    w_step = jnp.pad(pack_all[:, SEL : SEL + RANK], ((0, 0), (0, 128 - RANK)))
    rest = pack_all[:, SEL + RANK :].astype(f32).T
    rate = jnp.pad(-jnp.exp(rest[:STATE]), ((0, 0), (0, PAD)))
    rate2 = rate * LOG2E
    vecs = jnp.pad(rest[STATE:], ((0, 1), (0, 0)))

    ids = jnp.concatenate([jnp.full((3,), -1, jnp.int32), segments, jnp.full((BLK,), -2, jnp.int32)])
    local_ids = lax.dynamic_slice_in_dim(ids, z * rows, rows + 3 + BLK)
    own_ids = local_ids[3:]
    inside = own_ids >= 0
    same = jnp.stack(
        [(local_ids[k : k + rows + BLK] == own_ids) & inside for k in range(4)], axis=1
    ).astype(f32)
    same = jnp.pad(same, ((0, 0), (0, 124)))
    normed_in, inner, gate_in, conv, signal, selected, mixes, step_pre, dk_wide, push_wide = front_part(
        2, depth, tok_all, w_in, gain_rows, same, vecs, w_sel, w_step
    )
    end, total = scan_ends(dk_wide, push_wide, mixes, rate2)
    ends = column_gather(3, depth, jnp.concatenate([end, total], axis=0))
    spans = [jnp.exp2(ends[k, STATE : STATE + 1] * rate2) for k in range(depth)]
    entering = jnp.zeros((STATE, WIDE + PAD), f32)
    for k in range(depth - 1):
        entering = jnp.where(k < z, spans[k] * entering + ends[k, :STATE], entering)
    scanned, states = scan_forward(dk_wide, push_wide, mixes, rate2, entering, count)
    choose = (routes == jnp.arange(EXPERTS, dtype=jnp.int32)[None, :]).astype(f32)
    order = lax.broadcasted_iota(jnp.int32, (count, count), 0) >= lax.broadcasted_iota(
        jnp.int32, (count, count), 1
    )
    places = mm(order.astype(bf16), choose.astype(bf16))
    slotted = choose * (places <= CAP).astype(f32)
    picks = jnp.pad(jnp.concatenate([choose, slotted], axis=1), ((0, 0), (0, 124)))
    output, grad_mid, mixed_wide, grad_gate_in, grad_out_w, grad_up, grad_down, sums = middle_part(
        4,
        fs,
        scanned,
        signal,
        gate_in,
        jnp.broadcast_to(vecs[6:7], (8, WIDE)),
        w_out,
        tokens,
        cot_all,
        w_up,
        w_down,
        jnp.pad(w_router, ((0, 0), (0, 126))),
        jnp.pad(small_all[1:].astype(f32), ((0, 5), (0, 0))),
        picks,
    )
    grad_out_own = lax.psum_scatter(grad_out_w, "z", scatter_dimension=0, tiled=True).astype(f32)
    grad_down_own = lax.psum_scatter(grad_down, "z", scatter_dimension=0, tiled=True)
    grad_up_rows = lax.psum_scatter(grad_up.T, "z", scatter_dimension=0, tiled=True)
    message = scan_message(dk_wide, mixed_wide, mixes, rate2)
    messages = column_gather(8, depth, message)
    arriving = jnp.zeros((STATE, WIDE + PAD), f32)
    for k in range(depth - 1, 0, -1):
        arriving = jnp.where(k > z, messages[k] + spans[k] * arriving, arriving)
    grad_push, grad_scaled, grad_mixes, grad_rate = scan_adjoint(
        dk_wide, push_wide, mixed_wide, mixes, states, rate2, arriving, count
    )
    grad_tokens, in_cols, up_cols, pack_own, small_own = back_part(
        9,
        depth,
        rim,
        ch,
        grad_push,
        grad_scaled,
        grad_mixes,
        grad_rate,
        step_pre,
        signal,
        conv,
        inner,
        same,
        vecs,
        rate,
        selected,
        w_sel,
        w_step,
        mixed_wide,
        grad_gate_in,
        w_in,
        normed_in,
        tokens,
        gain_rows,
        grad_mid,
        sums,
        grad_up_rows.reshape(PLANE, rim, EXPERTS * HID),
    )
    in_cols = in_cols.astype(f32)
    up_cols = up_cols.astype(f32)
    ours = lax.dynamic_slice_in_dim(small_own, p * rim, rim, axis=1)
    grad_in_own = (
        in_cols.reshape(PLANE, rim, 2, depth, ch)
        .transpose(1, 2, 3, 0, 4)
        .reshape(rim, 2 * DI)
    )
    grad_up_own = (
        up_cols.reshape(PLANE, rim, depth, EXPERTS, fs).transpose(3, 1, 2, 0, 4).reshape(EXPERTS, rim, FF)
    )
    side = pack_own[:, 256:].T
    return (
        output,
        grad_tokens,
        ours[0],
        grad_in_own,
        side[STATE : STATE + 4],
        side[STATE + 4],
        pack_own[:, :SEL],
        pack_own[:, 128 : 128 + RANK].T,
        side[STATE + 5],
        side[:STATE],
        side[STATE + 6],
        grad_out_own,
        ours[1],
        ours[2:4].T,
        grad_up_own,
        grad_down_own.astype(f32).reshape(EXPERTS, fs, D),
    )


def solution(mesh):
    planes = Mesh(mesh.devices.reshape(-1, PLANE), ("z", "p"))
    every = ("z", "p")
    rows, flat, cols, third = P(every, None), P(every), P(None, every), P(None, every, None)
    return jax.shard_map(
        functools.partial(body, planes.shape["z"]),
        mesh=planes,
        in_specs=(
            rows, P(), rows, flat, rows, cols, flat, rows, cols,
            flat, cols, flat, rows, flat, rows, third, third, rows,
        ),
        out_specs=(
            rows, rows, flat, rows, cols, flat, rows, cols,
            flat, cols, flat, rows, flat, rows, third, third,
        ),
        check_vma=False,
    )
```

```python
import functools

import jax
import jax.numpy as jnp
from jax import lax
from jax.experimental import pallas as pl
from jax.experimental.pallas import tpu as pltpu
from jax.sharding import Mesh, PartitionSpec as P

D = 1152
DI = 2304
FF = 3072
RANK = 72
STATE = 16
EXPERTS = 2
CAP = 68
SEL = RANK + 2 * STATE

PLANE = 8
CHIPS = PLANE // 2
WIDE = DI // PLANE
PAD = -WIDE % 128
HID = FF // PLANE
BLK = 16
LOG2E = 1.4426950408889634
GELU = 0.7978845608028654
RESET = 1e5
EARLY, LATE = slice(0, 2), slice(2, PLANE)
epsilon = 1e-05

MESH = pl.DeviceIdType.MESH
ANY = pl.BlockSpec(memory_space=pl.ANY)
VM = pl.BlockSpec(memory_space=pltpu.VMEM)
bf16 = jnp.bfloat16
f32 = jnp.float32
DMA = pltpu.SemaphoreType.DMA


def params(cid=None, grid=None):
    extra = {} if cid is None else {"collective_id": cid, "has_side_effects": True}
    if grid is not None:
        extra["dimension_semantics"] = grid
    return pltpu.CompilerParams(vmem_limit_bytes=60 * 1024 * 1024, **extra)


def cost(us):
    return pl.CostEstimate(flops=int(us * 1e9), bytes_accessed=int(us * 3e6), transcendentals=0)


def mm(left, right):
    return jnp.dot(left, right, preferred_element_type=f32)


def contract_rows(left, right):
    return lax.dot_general(left, right, (((0,), (0,)), ((), ())), preferred_element_type=f32)


def contract_cols(left, right):
    return lax.dot_general(left, right, (((1,), (1,)), ((), ())), preferred_element_type=f32)


def send(src, dst, ss, rs, to):
    copy = pltpu.make_async_remote_copy(
        src_ref=src, dst_ref=dst, send_sem=ss, recv_sem=rs, device_id=to, device_id_type=MESH
    )
    copy.start()
    return copy


def here():
    return lax.axis_index("z"), lax.axis_index("p")


def greet(plane=True, depth=0):
    z, p = here()
    barrier = pltpu.get_barrier_semaphore()
    count = 0
    if plane:
        for k in range(1, PLANE):
            pl.semaphore_signal(
                barrier, inc=1, device_id=(z, lax.rem(p + k, PLANE)), device_id_type=MESH
            )
            count += 1
    for k in range(1, depth):
        pl.semaphore_signal(barrier, inc=1, device_id=(lax.rem(z + k, depth), p), device_id_type=MESH)
        count += 1
    pl.semaphore_wait(barrier, count)


def share_start(x, out, ss, rs):
    z, p = here()
    core = lax.rem(p, 2)
    copies = [send(x, out.at[p], ss.at[0], rs.at[0], (z, p + 1 - 2 * core))]
    for k in range(1, CHIPS):
        copies.append(send(x, out.at[p], ss.at[k], rs.at[k], (z, lax.rem(p + 2 * k, PLANE))))
    return copies


def share_forward(out, copies, ss, rs):
    z, p = here()
    core = lax.rem(p, 2)
    onward = []
    for k in range(1, CHIPS):
        copies[k].wait_recv()
        src = lax.rem(p + PLANE - 2 * k, PLANE)
        onward.append(
            send(out.at[src], out.at[src], ss.at[CHIPS + k], rs.at[CHIPS + k], (z, p + 1 - 2 * core))
        )
    return onward


def share_finish(copies, onward):
    copies[0].wait_recv()
    for c in copies:
        c.wait_send()
    for c in onward:
        c.wait()


def column_copy(src, out, ss, rs, frm, to, part=None):
    dst = out.at[frm] if part is None else out.at[frm, part]
    return pltpu.make_async_remote_copy(
        src_ref=dst if src is None else src,
        dst_ref=dst,
        send_sem=ss.at[to],
        recv_sem=rs.at[frm],
        device_id=(to, lax.axis_index("p")),
        device_id_type=MESH,
    )


def column_each(depth, act):
    z = lax.axis_index("z")
    for t in range(depth):
        far = abs(t - z) == depth - 1 if depth == 4 else t == z
        pl.when(jnp.logical_not((t == z) | far))(functools.partial(act, t))


def column_start(depth, src, out, ss, rs, part=None):
    z = lax.axis_index("z")
    column_each(depth, lambda t: column_copy(src, out, ss, rs, z, t, part).start())


def column_forward(depth, out, ss, rs, part=None):
    if depth != 4:
        return
    z = lax.axis_index("z")
    for me, frm, to in ((2, 0, 3), (1, 3, 0)):

        @pl.when(z == me)
        def _():
            copy = column_copy(None, out, ss, rs, frm, to, part)
            copy.wait_recv()
            copy.start()


def column_finish(depth, src, out, ss, rs, part=None):
    z = lax.axis_index("z")
    for s in range(depth):
        ahead = ((z == 2) & (s == 0)) | ((z == 1) & (s == 3)) if depth == 4 else s == z

        @pl.when(jnp.logical_not((s == z) | ahead))
        def _():
            column_copy(src, out, ss, rs, s, s, part).wait_recv()

    column_each(depth, lambda t: column_copy(src, out, ss, rs, z, t, part).wait_send())
    if depth == 4:
        for me, frm, to in ((2, 0, 3), (1, 3, 0)):

            @pl.when(z == me)
            def _():
                column_copy(None, out, ss, rs, frm, to, part).wait_send()


def softplus(x):
    return jnp.maximum(x, 0.0) + jnp.log1p(jnp.exp(-jnp.abs(x)))


def total_start(x, got, ss, rs):
    z, p = here()
    copies = []
    for k in range(1, PLANE):
        q = lax.rem(p + k, PLANE)
        copies.append(send(x.at[q], got.at[k], ss.at[k], rs.at[k], (z, q)))
    return copies


def total_share(x, got, copies, out, ts, us):
    z, p = here()
    total = x[p]
    for k in range(1, PLANE):
        copies[k - 1].wait_recv()
        total = total + got[k]
    out[p] = total.astype(bf16)
    after = [
        send(out.at[p], out.at[p], ts.at[k], us.at[k], (z, lax.rem(p + k, PLANE))) for k in range(1, PLANE)
    ]
    for c in copies:
        c.wait_send()
    return after


def front_kernel(
    depth,
    tok, win, wup, pack, w_down, w_out, same,
    normed_in, w_in, w_route, small, w_sel, w_step, vecs, rate, inner, gate_in, conv, signal, selected, mixes,
    step_pre, dk, push, up_rows, down_all, out_all,
    tok_all, win_all, pack_all, wide, thin, near, halo, x, got, sel_all,
    gs, gr, ws, wr, vs, vr, zs, zr, hs, ss, rs, ts, us, ls,
):
    z, p = here()
    count = tok.shape[0]
    rim = win.shape[1]
    ch = pack.shape[0]
    pair = 2 * count
    rows = PLANE * count
    local = [
        pltpu.make_async_copy(tok, tok_all.at[p], ls.at[0]),
        pltpu.make_async_copy(win.at[p], win_all.at[z, p], ls.at[1]),
        pltpu.make_async_copy(wup.at[p], up_rows.at[p], ls.at[2]),
        pltpu.make_async_copy(pack, pack_all.at[z], ls.at[3]),
        pltpu.make_async_copy(w_down, down_all.at[z], ls.at[4]),
        pltpu.make_async_copy(w_out, out_all.at[z], ls.at[5]),
    ]
    for c in local:
        c.start()
    greet(True, depth)
    across = []
    for k in range(1, PLANE):
        q = lax.rem(p + k, PLANE)
        across.append(send(win.at[q], win_all.at[z, p], ws.at[k], wr.at[k], (z, q)))
    column_start(depth, pack, pack_all, zs.at[0], zr.at[0])
    first = share_start(tok, tok_all, gs, gr)
    local[1].wait()
    for c in across:
        c.wait_recv()
    column_start(depth, win_all.at[z], win_all, zs.at[1], zr.at[1])
    second = share_forward(tok_all, first, gs, gr)
    more = []
    for k in range(1, PLANE):
        q = lax.rem(p + k, PLANE)
        more.append(send(wup.at[q], up_rows.at[p], vs.at[k], vr.at[k], (z, q)))
    local[3].wait()
    column_forward(depth, pack_all, zs.at[0], zr.at[0])
    column_finish(depth, pack, pack_all, zs.at[0], zr.at[0])
    for k in range(depth):
        thin[k * ch : k * ch + ch, :] = pack_all[k].astype(f32)
    w_sel[...] = thin[:, :128].astype(bf16)
    w_step[...] = thin[:, 128:256].astype(bf16)
    side = thin[:, 256:].T
    rate[:, :WIDE] = -jnp.exp(side[:STATE])
    rate[:, WIDE:] = jnp.zeros((STATE, PAD), f32)
    vecs[...] = side[STATE : STATE + 8]
    column_forward(depth, win_all, zs.at[1], zr.at[1])
    local[0].wait()
    share_finish(first, second)
    column_finish(depth, win_all.at[z], win_all, zs.at[1], zr.at[1])
    for k in range(depth):
        for q in range(PLANE):
            at = (k * PLANE + q) * rim
            wide[at : at + rim, :] = win_all[k, q].astype(f32)
    w_in[...] = wide[:, : 2 * WIDE].astype(bf16)
    w_route[...] = wide[:, 512:].astype(bf16)
    small[...] = wide[:, 512:].T[64:72]
    gain = small[0:1]
    for b in (3, 0, 1, 2):
        at = slice(pair * b, pair * b + pair)
        values = tok_all[2 * b : 2 * b + 2].reshape(pair, D).astype(f32)
        scale = lax.rsqrt(jnp.mean(values * values, axis=-1, keepdims=True) + epsilon)
        normed = (values * scale * gain).astype(bf16)
        normed_in[at, :] = normed
        joined = mm(normed, w_in[...]).astype(bf16)
        near[BLK + pair * b : BLK + pair * b + pair, :] = joined[:, :WIDE].astype(f32)
        gate_in[at, :] = joined[:, WIDE:]
        if b == 3:
            edge = send(near.at[pl.ds(rows, BLK)], halo, hs.at[0], hs.at[1], (lax.rem(z + 1, depth), p))
            column_start(depth, w_out, out_all, zs.at[2], zr.at[2])
            column_start(depth, w_down, down_all, zs.at[3], zr.at[3])
    for b in (1, 2, 3, 0):
        if b == 0:
            edge.wait()
            near[:BLK, :] = halo[...]
        base = pair * b
        at = slice(base, base + pair)
        total = vecs[4:5] + vecs[0:1] * near[base + 13 : base + 13 + pair, :] * same[at, 0:1]
        for k in range(1, 4):
            total = total + vecs[k : k + 1] * near[base + 13 + k : base + 13 + k + pair, :] * same[at, k : k + 1]
        conv[at, :] = total
        value = (total * jax.nn.sigmoid(total)).astype(bf16)
        signal[at, :] = value
        x[2 * b : 2 * b + 2] = mm(value, w_sel[...]).reshape(2, count, 128)
    third = total_start(x, got, ss, rs)
    inner[...] = near[...].astype(bf16)
    fourth = total_share(x, got, third, sel_all, ts, us)
    local[5].wait()
    column_forward(depth, out_all, zs.at[2], zr.at[2])
    for c in fourth:
        c.wait()
    for b in range(CHIPS):
        at = slice(pair * b, pair * b + pair)
        chosen = sel_all[2 * b : 2 * b + 2].reshape(pair, 128)
        selected[at, :] = chosen
        step = contract_cols(chosen, w_step[...]) + vecs[5:6]
        step_pre[at, :] = step
        delta = softplus(step)
        dk[at, :WIDE] = delta + (1.0 - same[at, 2:3]) * RESET
        push[at, :WIDE] = delta * signal[at, :].astype(f32)
        dk[at, WIDE:] = jnp.zeros((pair, PAD), f32)
        push[at, WIDE:] = jnp.zeros((pair, PAD), f32)
        full = chosen.astype(f32)
        for i in range(pair // BLK):
            flipped = full[i * BLK : i * BLK + BLK].T
            mixes[b * (pair // BLK) + i] = flipped[RANK:SEL]
    local[4].wait()
    column_forward(depth, down_all, zs.at[3], zr.at[3])
    column_finish(depth, w_out, out_all, zs.at[2], zr.at[2])
    column_finish(depth, w_down, down_all, zs.at[3], zr.at[3])
    local[2].wait()
    for c in across:
        c.wait_send()
    for c in more:
        c.wait()


def front_part(cid, depth, tok, win, wup, pack, w_down, w_out, same):
    count, rim, ch, low = tok.shape[0], win.shape[1], pack.shape[0], w_down.shape[0]
    rows = PLANE * count

    def made(*shape, dtype=f32):
        return jax.ShapeDtypeStruct(shape, dtype)

    return pl.pallas_call(
        functools.partial(front_kernel, depth),
        out_shape=[
            made(rows, D, dtype=bf16),
            made(D, 2 * WIDE, dtype=bf16),
            made(D, 128, dtype=bf16),
            made(8, D),
            made(WIDE, 128, dtype=bf16),
            made(WIDE, 128, dtype=bf16),
            made(8, WIDE),
            made(STATE, WIDE + PAD),
            made(rows + BLK, WIDE, dtype=bf16),
            made(rows, WIDE, dtype=bf16),
            made(rows, WIDE),
            made(rows, WIDE, dtype=bf16),
            made(rows, 128, dtype=bf16),
            made(rows // BLK, 2 * STATE, BLK),
            made(rows, WIDE),
            made(rows, WIDE + PAD),
            made(rows, WIDE + PAD),
            made(PLANE, rim, EXPERTS * HID, dtype=bf16),
            made(depth, low, D, dtype=bf16),
            made(depth, ch, D, dtype=bf16),
        ],
        in_specs=[VM] * 7,
        out_specs=[VM] * 18 + [ANY] * 2,
        scratch_shapes=[
            pltpu.VMEM((PLANE, count, D), bf16),
            pltpu.VMEM((depth,) + win.shape, bf16),
            pltpu.VMEM((depth,) + pack.shape, bf16),
            pltpu.VMEM((D, win.shape[2]), f32),
            pltpu.VMEM((WIDE, pack.shape[1]), f32),
            pltpu.VMEM((BLK + rows, WIDE), f32),
            pltpu.VMEM((BLK, WIDE), f32),
            pltpu.VMEM((PLANE, count, 128), f32),
            pltpu.VMEM((PLANE, count, 128), f32),
            pltpu.VMEM((PLANE, count, 128), bf16),
        ]
        + [DMA((PLANE,))] * 6
        + [DMA((4, depth))] * 2
        + [DMA((2,))]
        + [DMA((PLANE,))] * 4
        + [DMA((6,))],
        compiler_params=params(cid),
        cost_estimate=cost(80),
        name="front_part",
    )(tok, win, wup, pack, w_down, w_out, same)


def back_kernel(
    depth,
    g_push, g_step, g_mixes, g_rate, step_pre, signal, conv, inner, same, vecs, rate, selected, w_sel, w_step,
    mixed_grad, gate_grad, w_in, normed_in, tok, gain, grad_mid, sums, gup,
    tokens_out, in_out, up_out, pack_out, small_out,
    x, got, gsel, low, gc, halo, nearf, gj, part, sib, mix, far, gin, gin_got, own, pack, pack_got, row, row_got, sml, sml_got,
    hs, ss, rs, ts, us, near_s, near_r, away_s, away_r, zs, zr, cs, cr, ups, upr, ls,
):
    z, p = here()
    core = lax.rem(p, 2)
    chip = lax.div(p, 2)
    twin = (z, p + 1 - 2 * core)
    count = tok.shape[0]
    pair = 2 * count
    rows = PLANE * count
    ch = pack_out.shape[0]
    rim = in_out.shape[1]
    sent = []

    def down(i, src, dst):
        copies = []
        for k in range(1, depth):
            q = lax.rem(z + k, depth)
            copies.append(send(src.at[q], dst.at[k], zs.at[i, k], zr.at[i, k], (q, p)))
        return copies

    keep = pltpu.make_async_copy(gup.at[p], up_out.at[p], ls)
    keep.start()
    greet(True, depth)
    bias = jnp.zeros((1, WIDE), f32)
    for b in range(CHIPS):
        at = slice(pair * b, pair * b + pair)
        value = signal[at, :].astype(f32)
        grad = g_step[at, :WIDE] * (1.0 / LOG2E) + g_push[at, :WIDE] * value
        grad = grad * jax.nn.sigmoid(step_pre[at, :])
        bias = bias + jnp.sum(grad, axis=0, keepdims=True)
        low[at, :] = grad.astype(bf16)
        ranks = mm(low[at, :], w_step[...])
        for i in range(pair // BLK):
            block = g_mixes[b * (pair // BLK) + i]
            wide = jnp.concatenate(
                [jnp.zeros((RANK, BLK), f32), block, jnp.zeros((128 - SEL, BLK), f32)], axis=0
            ).T
            t = i * BLK
            x[2 * b + t // count, t % count : t % count + BLK, :] = ranks[t : t + BLK] + wide
    first = total_start(x, got, ss, rs)
    grad_step_w = contract_rows(low[...], selected[...])
    nearf[...] = inner[...].astype(f32)
    second = total_share(x, got, first, gsel, ts, us)
    ups_sent = []
    for k in range(1, PLANE):
        q = lax.rem(p + k, PLANE)
        ups_sent.append(send(gup.at[q], up_out.at[p], ups.at[k], upr.at[k], (z, q)))
    for c in second:
        c.wait()
    taps = [jnp.zeros((1, WIDE), f32)] * 4
    conv_bias = jnp.zeros((1, WIDE), f32)
    for b in range(CHIPS):
        base = pair * b
        at = slice(base, base + pair)
        delta = softplus(step_pre[at, :])
        grad = mixed_grad[at, :WIDE] * vecs[6:7] + g_push[at, :WIDE] * delta
        grad = grad + contract_cols(gsel[2 * b : 2 * b + 2].reshape(pair, 128), w_sel[...])
        c = conv[at, :]
        sig = jax.nn.sigmoid(c)
        grad = grad * (sig * (1.0 + c * (1.0 - sig)))
        gc[at, :] = grad
        if b == 0:
            edge = send(gc.at[pl.ds(0, BLK)], halo, hs.at[0], hs.at[1], (lax.rem(z + depth - 1, depth), p))
        conv_bias = conv_bias + jnp.sum(grad, axis=0, keepdims=True)
        for k in range(4):
            taps[k] = taps[k] + jnp.sum(
                grad * nearf[base + 13 + k : base + 13 + k + pair, :] * same[at, k : k + 1], axis=0, keepdims=True
            )
    for b in range(CHIPS):
        base = pair * b
        if b == CHIPS - 1:
            edge.wait()
            gc[rows : rows + BLK, :] = halo[...]
        total = jnp.zeros((pair, WIDE), f32)
        for k in range(4):
            off = slice(base + 3 - k, base + 3 - k + pair)
            total = total + gc[off, :] * vecs[k : k + 1] * same[off, k : k + 1]
        gj[base : base + pair, :WIDE] = total.astype(bf16)
        gj[base : base + pair, WIDE:] = gate_grad[base : base + pair, :]
    block = D // depth
    for q in range(depth):
        gin[q] = contract_rows(normed_in[:, q * block : q * block + block], gj[...]).astype(bf16)
    in_sent = down(0, gin, gin_got)
    near = {}
    for k in (1, 2, 3, 0):
        q = lax.rem(chip + k, CHIPS)
        at = pl.ds(pl.multiple_of(q * pair, pair), pair)
        part[k] = contract_cols(gj[at, :], w_in[...]).astype(bf16).reshape(2, count, D)
        near[k] = send(part.at[k, 1 - core], sib.at[k], near_s.at[k], near_r.at[k], twin)
    away = []
    for k in range(1, CHIPS):
        near[k].wait_recv()
        mix[k] = (part[k, core].astype(f32) + sib[k].astype(f32)).astype(bf16)
        away.append(
            send(mix.at[k], far.at[k], away_s.at[k], away_r.at[k], (z, lax.rem(p + 2 * k, PLANE)))
        )
    row[...] = jnp.zeros_like(row)
    row[0:STATE, :] = g_rate[...] * rate[...]
    for k in range(4):
        row[STATE + k : STATE + k + 1, :WIDE] = taps[k]
    row[STATE + 4 : STATE + 5, :WIDE] = conv_bias
    row[STATE + 5 : STATE + 6, :WIDE] = bias
    row[STATE + 6 : STATE + 7, :WIDE] = sums[3:4, :WIDE]
    side = row[...].T
    grad_sel_w = contract_rows(signal[...], gsel[...].reshape(rows, 128))
    for q in range(depth):
        cut = slice(q * ch, q * ch + ch)
        pack[q, :, :128] = grad_sel_w[cut].astype(bf16)
        pack[q, :, 128:256] = grad_step_w[cut].astype(bf16)
        pack[q, :, 256:] = side[cut].astype(bf16)
    pack_sent = down(1, pack, pack_got)
    near[0].wait_recv()
    total = part[0, core].astype(f32) + sib[0].astype(f32)
    for k in range(1, CHIPS):
        away[k - 1].wait_recv()
        total = total + far[k].astype(f32)
    values = tok[...].astype(f32)
    scale = lax.rsqrt(jnp.mean(values * values, axis=-1, keepdims=True) + epsilon)
    normed = values * scale
    grad_normed = total * gain[0:1]
    mean = jnp.mean(grad_normed * normed, axis=-1, keepdims=True)
    tokens_out[...] = (scale * (grad_normed - normed * mean) + grad_mid[...]).astype(bf16)
    ours = jnp.concatenate(
        [jnp.sum(total * normed, axis=0, keepdims=True), sums[0:3, :], jnp.zeros((4, D), f32)], axis=0
    )
    for q in range(depth):
        sml[q] = ours[:, q * block : q * block + block]
    sml_sent = down(2, sml, sml_got)
    for c in in_sent:
        c.wait_recv()
    total = gin[z].astype(f32)
    for k in range(1, depth):
        total = total + gin_got[k].astype(f32)
    for q in range(PLANE):
        own[q] = total[q * rim : q * rim + rim].astype(bf16)
    across = []
    for k in range(1, PLANE):
        q = lax.rem(p + k, PLANE)
        across.append(send(own.at[q], in_out.at[p], cs.at[0, k], cr.at[0, k], (z, q)))
    in_out[p] = own[p]
    for c in sml_sent:
        c.wait_recv()
    total = sml[z]
    for k in range(1, depth):
        total = total + sml_got[k]
    sml_got[0] = total
    for k in range(1, PLANE):
        q = lax.rem(p + k, PLANE)
        across.append(send(sml_got.at[0], row_got.at[k], cs.at[1, k], cr.at[1, k], (z, q)))
    for c in pack_sent:
        c.wait_recv()
    total = pack[z].astype(f32)
    for k in range(1, depth):
        total = total + pack_got[k].astype(f32)
    pack_out[...] = total
    for c in across:
        c.wait()
    total = sml_got[0]
    for k in range(1, PLANE):
        total = total + row_got[k]
    small_out[...] = total
    for c in list(near.values()) + away + in_sent + pack_sent + sml_sent:
        c.wait_send()
    for c in ups_sent:
        c.wait()
    keep.wait()


def back_part(cid, depth, rim, ch, *args):
    count = args[18].shape[0]
    rows = PLANE * count
    block = D // depth

    def made(*shape, dtype=f32):
        return jax.ShapeDtypeStruct(shape, dtype)

    return pl.pallas_call(
        functools.partial(back_kernel, depth),
        out_shape=[
            made(count, D, dtype=bf16),
            made(PLANE, rim, 2 * WIDE, dtype=bf16),
            made(PLANE, rim, EXPERTS * HID, dtype=bf16),
            made(ch, 288),
            made(8, block),
        ],
        in_specs=[VM] * 23,
        out_specs=[VM] * 5,
        scratch_shapes=[
            pltpu.VMEM((PLANE, count, 128), f32),
            pltpu.VMEM((PLANE, count, 128), f32),
            pltpu.VMEM((PLANE, count, 128), bf16),
            pltpu.VMEM((rows, WIDE), bf16),
            pltpu.VMEM((rows + BLK, WIDE), f32),
            pltpu.VMEM((BLK, WIDE), f32),
            pltpu.VMEM((rows + BLK, WIDE), f32),
            pltpu.VMEM((rows, 2 * WIDE), bf16),
            pltpu.VMEM((CHIPS, 2, count, D), bf16),
            pltpu.VMEM((CHIPS, count, D), bf16),
            pltpu.VMEM((CHIPS, count, D), bf16),
            pltpu.VMEM((CHIPS, count, D), bf16),
            pltpu.VMEM((depth, block, 2 * WIDE), bf16),
            pltpu.VMEM((depth, block, 2 * WIDE), bf16),
            pltpu.VMEM((PLANE, rim, 2 * WIDE), bf16),
            pltpu.VMEM((depth, ch, 288), bf16),
            pltpu.VMEM((depth, ch, 288), bf16),
            pltpu.VMEM((2 * STATE, WIDE + PAD), f32),
            pltpu.VMEM((PLANE, 8, block), f32),
            pltpu.VMEM((depth, 8, block), f32),
            pltpu.VMEM((depth, 8, block), f32),
            DMA((2,)),
        ]
        + [DMA((PLANE,))] * 4
        + [DMA((CHIPS,))] * 4
        + [DMA((4, depth))] * 2
        + [DMA((2, PLANE))] * 2
        + [DMA((PLANE,))] * 2
        + [DMA],
        compiler_params=params(cid),
        cost_estimate=cost(70),
        name="back_part",
    )(*args)


def middle_kernel(
    depth,
    scanned, signal, gate_in, skip, w_out, tok, cot_all, up_early, up_rows, down0, down1, w_router, rows_in, picks,
    output, grad_mid, mixed_grad, gate_grad, grad_out, grad_up, down_own, sums,
    gated, mixed, part, sib, mix, far, routed_all, marks_all, hidden_all, pre_all, slot_all, back_all,
    up_late, w_up, wide, grad_down, down_got,
    near_s, near_r, away_s, away_r, gs, gr, zs, zr, ds, dr, ls,
):
    z, p = here()
    core = lax.rem(p, 2)
    chip = lax.div(p, 2)
    twin = (z, p + 1 - 2 * core)
    count = tok.shape[0]
    pair = 2 * count

    def chip_at(k):
        return lax.rem(chip + k, CHIPS)

    def rows_of(q):
        return pl.ds(pl.multiple_of(q * pair, pair), pair)

    def pass_near(i, k):
        return send(part.at[i, k, 1 - core], sib.at[i, k], near_s.at[i, k], near_r.at[i, k], twin)

    def pass_away(i, k, copy):
        copy.wait_recv()
        mix[i, k] = (part[i, k, core].astype(f32) + sib[i, k].astype(f32)).astype(bf16)
        return send(
            mix.at[i, k], far.at[i, k], away_s.at[i, k], away_r.at[i, k], (z, lax.rem(p + 2 * k, PLANE))
        )

    def gathered(i, near, away):
        near.wait_recv()
        total = part[i, 0, core].astype(f32) + sib[i, 0].astype(f32)
        for k in range(1, CHIPS):
            away[k - 1].wait_recv()
            total = total + far[i, k].astype(f32)
        return total

    local = pltpu.make_async_copy(up_rows.at[LATE], up_late.at[z], ls)
    local.start()
    greet(True, depth)
    column_start(depth, up_rows.at[LATE], up_late, zs, zr)
    sent = []
    near = {}
    for k in (1, 2, 3, 0):
        q = chip_at(k)
        at = rows_of(q)
        pre = scanned[at, :WIDE] + skip[0:1] * signal[at, :].astype(f32)
        mixed[at, :] = pre
        inward = gate_in[at, :].astype(f32)
        gated[at, :] = (pre * (inward * jax.nn.sigmoid(inward))).astype(bf16)
        part[0, k] = mm(gated[at, :], w_out[...]).astype(bf16).reshape(2, count, D)
        near[k] = pass_near(0, k)
    away = [pass_away(0, k, near[k]) for k in range(1, CHIPS)]
    branch = gathered(0, near[0], away)
    sent += list(near.values()) + away

    gain, router0, router1 = rows_in[1:2], rows_in[2:3], rows_in[3:4]
    middle = tok[...].astype(f32) + branch
    scale = lax.rsqrt(jnp.mean(middle * middle, axis=-1, keepdims=True) + epsilon)
    normed = middle * scale
    routed = (normed * gain).astype(bf16)
    routed_all[p] = routed
    logits = mm(routed, w_router[...])
    l0, l1 = logits[:, 66:67], logits[:, 67:68]
    top = jnp.maximum(l0, l1)
    e0, e1 = jnp.exp(l0 - top), jnp.exp(l1 - top)
    p0, p1 = e0 / (e0 + e1), e1 / (e0 + e1)
    c0, c1, s0, s1 = (picks[:, k : k + 1] for k in range(4))
    gate = p0 * c0 + p1 * c1
    kept = s0 + s1
    weight = gate * kept
    lane = lax.broadcasted_iota(jnp.int32, (count, 128), 1)
    marks_all[p] = jnp.where(lane == 0, weight, jnp.where(lane == 1, s0, s1))
    first = share_start(routed_all.at[p], routed_all, gs.at[0], gr.at[0])
    firstm = share_start(marks_all.at[p], marks_all, gs.at[1], gr.at[1])
    local.wait()
    column_forward(depth, up_late, zs, zr)
    column_finish(depth, up_rows.at[LATE], up_late, zs, zr)
    rim = up_rows.shape[1]
    block = PLANE * rim
    for k in range(depth):
        for q in range(PLANE):
            source = up_early[k, q] if q < EARLY.stop else up_late[k, q - EARLY.stop]
            wide[q * rim : q * rim + rim, :] = source.astype(f32)
        w_up[k * block : k * block + block, :] = wide[...].astype(bf16)

    odd = lax.broadcasted_iota(jnp.int32, (1, EXPERTS * HID), 1) >= HID
    onward, onwardm, near1, near2, away1, away2 = [], [], {}, {}, [], []
    for k in range(CHIPS):
        q = chip_at(k)
        if k == 0:
            first[0].wait_recv()
            firstm[0].wait_recv()
        else:
            src = lax.rem(p + PLANE - 2 * (CHIPS - k), PLANE)
            for copies, ref, after, i in ((first, routed_all, onward, 0), (firstm, marks_all, onwardm, 1)):
                copies[CHIPS - k].wait_recv()
                after.append(
                    send(ref.at[src], ref.at[src], gs.at[i, CHIPS + k], gr.at[i, CHIPS + k], twin)
                )
            onward[-1].wait_recv()
            onwardm[-1].wait_recv()
        both = pl.ds(2 * q, 2)
        marks = marks_all[both].reshape(pair, 128)
        mask = jnp.where(odd, marks[:, 2:3], marks[:, 1:2])
        hidden = mm(routed_all[both].reshape(pair, D), w_up[...])
        slot = (cot_all[rows_of(q), :].astype(f32) * marks[:, 0:1]).astype(bf16)
        slot_all[q] = slot
        square = hidden * hidden
        bend = jnp.tanh(GELU * hidden * (1.0 + 0.044715 * square))
        units = (0.5 * hidden * (1.0 + bend) * mask).astype(bf16)
        hidden_all[q] = units
        slope = 0.5 * (1.0 + bend) + 0.5 * GELU * hidden * (1.0 - bend * bend) * (1.0 + 3 * 0.044715 * square)
        grad = jnp.concatenate([contract_cols(slot, down0[...]), contract_cols(slot, down1[...])], axis=1)
        grad = (slope * grad * mask).astype(bf16)
        pre_all[q] = grad
        made = mm(units[:, :HID], down0[...]) + mm(units[:, HID:], down1[...])
        part[1, k] = made.astype(bf16).reshape(2, count, D)
        near1[k] = pass_near(1, k)
        part[2, k] = contract_cols(grad, w_up[...]).astype(bf16).reshape(2, count, D)
        near2[k] = pass_near(2, k)
        if k > 1:
            away1.append(pass_away(1, k - 1, near1[k - 1]))
            away2.append(pass_away(2, k - 1, near2[k - 1]))
    away1.append(pass_away(1, CHIPS - 1, near1[CHIPS - 1]))
    away2.append(pass_away(2, CHIPS - 1, near2[CHIPS - 1]))
    every = CHIPS * pair
    fs = HID // depth
    for c in range(0, D, 384):
        for e in range(EXPERTS):
            made = contract_rows(
                hidden_all[:, :, e * HID : e * HID + HID].reshape(every, HID),
                slot_all[:, :, c : c + 384].reshape(every, 384),
            )
            for k in range(depth):
                grad_down[k, e, :, c : c + 384] = made[k * fs : k * fs + fs].astype(bf16)
    down = []
    for k in range(1, depth):
        q = lax.rem(z + k, depth)
        down.append(send(grad_down.at[q], down_got.at[k], ds.at[k], dr.at[k], (q, p)))
    expert_tok = gathered(1, near1[0], away1)
    slot_back = gathered(2, near2[0], away2)
    sent += list(near1.values()) + list(near2.values()) + away1 + away2

    up = cot_all[pl.ds(pl.multiple_of(p * count, count), count), :].astype(f32)
    output[...] = (middle + weight * expert_tok).astype(bf16)
    pull = jnp.sum(up * expert_tok, axis=-1, keepdims=True) * kept * gate
    g0, g1 = pull * (c0 - p0), pull * (c1 - p1)
    grad_routed = slot_back + g0 * router0 + g1 * router1
    routed = routed.astype(f32)
    sums[0:1] = jnp.sum(grad_routed * normed, axis=0, keepdims=True)
    sums[1:2] = jnp.sum(routed * g0, axis=0, keepdims=True)
    sums[2:3] = jnp.sum(routed * g1, axis=0, keepdims=True)
    grad_normed = grad_routed * gain
    inner = jnp.mean(grad_normed * normed, axis=-1, keepdims=True)
    total = scale * (grad_normed - normed * inner) + up
    grad_mid[...] = total
    back_all[p] = total.astype(bf16)
    last = share_start(back_all.at[p], back_all, gs.at[2], gr.at[2])
    for c in range(0, D, 384):
        grad_up[c : c + 384, :] = contract_rows(
            routed_all[:, :, c : c + 384].reshape(every, 384), pre_all[...].reshape(every, EXPERTS * HID)
        ).astype(bf16)

    skips = jnp.zeros((1, WIDE), f32)
    onwardb = []
    for k in range(CHIPS):
        q = chip_at(k)
        if k == 0:
            last[0].wait_recv()
        else:
            src = lax.rem(p + PLANE - 2 * (CHIPS - k), PLANE)
            last[CHIPS - k].wait_recv()
            onwardb.append(
                send(back_all.at[src], back_all.at[src], gs.at[2, CHIPS + k], gr.at[2, CHIPS + k], twin)
            )
            onwardb[-1].wait_recv()
        at = rows_of(q)
        grad = contract_cols(back_all[pl.ds(2 * q, 2)].reshape(pair, D), w_out[...])
        inward = gate_in[at, :].astype(f32)
        sig = jax.nn.sigmoid(inward)
        act = inward * sig
        through = grad * act
        skips = skips + jnp.sum(through * signal[at, :].astype(f32), axis=0, keepdims=True)
        mixed_grad[at, :WIDE] = through
        mixed_grad[at, WIDE:] = jnp.zeros((pair, PAD), f32)
        gate_grad[at, :] = (grad * mixed[at, :] * (sig * (1.0 + inward * (1.0 - sig)))).astype(bf16)
    sums[3:4] = jnp.concatenate([skips, jnp.zeros((1, D - WIDE), f32)], axis=1)
    for c in range(0, D, 384):
        grad_out[:, c : c + 384] = contract_rows(
            gated[...], back_all[:, :, c : c + 384].reshape(every, 384)
        ).astype(bf16)
    for c in down:
        c.wait_recv()
    total = grad_down[z].astype(f32)
    for k in range(1, depth):
        total = total + down_got[k].astype(f32)
    down_own[...] = total
    for c in sent + down:
        c.wait_send()
    for copies, after in ((first, onward), (firstm, onwardm), (last, onwardb)):
        for c in copies + after:
            c.wait_send()


def middle_part(cid, depth, *args):
    tok, cot_all, up_rows = args[5], args[6], args[8]
    count, rows, rim = tok.shape[0], cot_all.shape[0], up_rows.shape[1]
    wide = EXPERTS * HID
    block = (CHIPS, count, D)
    return pl.pallas_call(
        functools.partial(middle_kernel, depth),
        out_shape=[
            jax.ShapeDtypeStruct((count, D), bf16),
            jax.ShapeDtypeStruct((count, D), f32),
            jax.ShapeDtypeStruct((rows, WIDE + PAD), f32),
            jax.ShapeDtypeStruct((rows, WIDE), bf16),
            jax.ShapeDtypeStruct((WIDE, D), bf16),
            jax.ShapeDtypeStruct((D, wide), bf16),
            jax.ShapeDtypeStruct((EXPERTS, HID // depth, D), f32),
            jax.ShapeDtypeStruct((8, D), f32),
        ],
        in_specs=[VM] * 14,
        out_specs=[VM] * 8,
        scratch_shapes=[
            pltpu.VMEM((rows, WIDE), bf16),
            pltpu.VMEM((rows, WIDE), f32),
            pltpu.VMEM((3, CHIPS, 2, count, D), bf16),
            pltpu.VMEM((3,) + block, bf16),
            pltpu.VMEM((3,) + block, bf16),
            pltpu.VMEM((3,) + block, bf16),
            pltpu.VMEM((PLANE, count, D), bf16),
            pltpu.VMEM((PLANE, count, 128), f32),
            pltpu.VMEM((CHIPS, 2 * count, wide), bf16),
            pltpu.VMEM((CHIPS, 2 * count, wide), bf16),
            pltpu.VMEM((CHIPS, 2 * count, D), bf16),
            pltpu.VMEM((PLANE, count, D), bf16),
            pltpu.VMEM((depth, LATE.stop - LATE.start, rim, wide), bf16),
            pltpu.VMEM((D, wide), bf16),
            pltpu.VMEM((PLANE * rim, wide), f32),
            pltpu.VMEM((depth, EXPERTS, HID // depth, D), bf16),
            pltpu.VMEM((depth, EXPERTS, HID // depth, D), bf16),
        ]
        + [DMA((3, CHIPS))] * 4
        + [DMA((3, PLANE))] * 2
        + [DMA((depth,))] * 4
        + [DMA],
        compiler_params=params(cid),
        cost_estimate=cost(75),
        name="middle_part",
    )(*args)


def tree(parts):
    row = lax.broadcasted_iota(jnp.int32, parts[0].shape, 0)
    for step in (1, 2, 4):
        low = (row // step) % 2 == 0
        parts = [
            jnp.where(low, a, b) + pltpu.roll(jnp.where(low, b, a), step, 0)
            for a, b in zip(parts[::2], parts[1::2])
        ]
    return parts[0]


def lane_tiles(x):
    total = x[:, :128]
    for k in range(128, x.shape[1], 128):
        total = total + x[:, k : k + 128]
    return total


def spread(ref, i):
    return jnp.broadcast_to(ref[pl.ds(i, 1), :], (8, ref.shape[1]))


HALVES = (slice(0, 8), slice(8, 16))


def ends_loop(dk, push, sel, slope):
    def block(b, carry):
        hidden, acc = list(carry[:2]), carry[2]
        base = pl.multiple_of(b * BLK, BLK)
        w = sel[b, :STATE]
        for t in range(BLK):
            d, u = spread(dk, base + t), spread(push, base + t)
            for k, h in enumerate(HALVES):
                hidden[k] = jnp.exp2(d * slope[k]) * hidden[k] + w[h, t : t + 1] * u
            acc = acc + d
        return hidden[0], hidden[1], acc

    zero = jnp.zeros(slope[0].shape, f32)
    return lax.fori_loop(0, dk.shape[0] // BLK, block, (zero, zero, zero))


def scan_kernel(
    depth,
    dk, push, sel, rate, up_rows, cot, w_down,
    out, states, ends, up_all, cot_all, down_all,
    slots, gs, gr, es, er, zs, zr, ks, ls,
):
    z, p = here()
    tile = slots.shape[1]
    tiles = dk.shape[0] // tile
    local = [
        pltpu.make_async_copy(up_rows.at[EARLY], up_all.at[z], ls.at[0]),
        pltpu.make_async_copy(cot, cot_all.at[p], ls.at[1]),
        pltpu.make_async_copy(w_down, down_all.at[z], ls.at[2]),
    ]
    for c in local:
        c.start()
    greet(True, depth)
    column_start(depth, up_rows.at[EARLY], up_all, zs.at[0], zr.at[0])
    first = share_start(cot, cot_all, gs, gr)
    slope = [rate[h, :] * LOG2E for h in HALVES]
    one, two, acc = ends_loop(dk, push, sel, slope)
    ends[z, :8], ends[z, 8:16], ends[z, 16:] = one, two, acc
    mine = []
    for k in range(1, depth):
        mine.append(send(ends.at[z], ends.at[z], es.at[k], er.at[k], (lax.rem(z + k, depth), p)))
    column_start(depth, w_down, down_all, zs.at[1], zr.at[1])
    second = share_forward(cot_all, first, gs, gr)
    for c in local:
        c.wait()
    column_forward(depth, up_all, zs.at[0], zr.at[0])
    for c in mine:
        c.wait_recv()
    hidden = [jnp.zeros(slope[0].shape, f32)] * 2
    for k in range(depth - 1):
        for i, h in enumerate(HALVES):
            hidden[i] = jnp.where(k < z, jnp.exp2(ends[k, 16:] * slope[i]) * hidden[i] + ends[k, h], hidden[i])

    def stored(i, slot):
        return pltpu.make_async_copy(
            slots.at[slot], states.at[pl.ds(pl.multiple_of(i * tile, tile), tile)], ks.at[slot]
        )

    def piece(i, carry):
        slot = lax.rem(i, 2)

        @pl.when(i >= 2)
        def _():
            stored(i - 2, slot).wait()

        def block(j, carry):
            hidden = list(carry)
            b = i * (tile // BLK) + j
            base = pl.multiple_of(b * BLK, BLK)
            inside = j * BLK
            w, r = sel[b, :STATE], sel[b, STATE:]
            parts = []
            for t in range(BLK):
                d, u = spread(dk, base + t), spread(push, base + t)
                line = None
                for k, h in enumerate(HALVES):
                    hidden[k] = jnp.exp2(d * slope[k]) * hidden[k] + w[h, t : t + 1] * u
                    slots[slot, inside + t, h] = hidden[k]
                    y = r[h, t : t + 1] * hidden[k]
                    line = y if line is None else line + y
                parts.append(line)
                if len(parts) == 8:
                    out[pl.ds(pl.multiple_of(base + t - 7, 8), 8), :] = tree(parts)
                    parts = []
            return tuple(hidden)

        carry = lax.fori_loop(0, tile // BLK, block, carry)
        stored(i, slot).start()
        return carry

    carry = lax.fori_loop(0, tiles - 2, piece, tuple(hidden))
    column_forward(depth, down_all, zs.at[1], zr.at[1])
    lax.fori_loop(tiles - 2, tiles, piece, carry)
    for i in (tiles - 2, tiles - 1):
        stored(i, i % 2).wait()
    share_finish(first, second)
    column_finish(depth, up_rows.at[EARLY], up_all, zs.at[0], zr.at[0])
    column_finish(depth, w_down, down_all, zs.at[1], zr.at[1])
    for c in mine:
        c.wait_send()


def scan_part(cid, depth, dk, push, sel, rate, up_rows, cot, w_down):
    rows, wide = dk.shape
    tile = cot.shape[0]
    return pl.pallas_call(
        functools.partial(scan_kernel, depth),
        out_shape=[
            jax.ShapeDtypeStruct((rows, wide), f32),
            jax.ShapeDtypeStruct((rows, STATE, wide), f32),
            jax.ShapeDtypeStruct((depth, STATE + 8, wide), f32),
            jax.ShapeDtypeStruct((depth, EARLY.stop) + up_rows.shape[1:], bf16),
            jax.ShapeDtypeStruct((PLANE,) + cot.shape, bf16),
            jax.ShapeDtypeStruct((depth,) + w_down.shape, bf16),
        ],
        in_specs=[VM] * 7,
        out_specs=[VM, ANY, VM, ANY, ANY, ANY],
        scratch_shapes=[pltpu.VMEM((2, tile, STATE, wide), f32)]
        + [DMA((PLANE,))] * 2
        + [DMA((depth,))] * 2
        + [DMA((2, depth))] * 2
        + [DMA((2,)), DMA((3,))],
        compiler_params=params(cid),
        cost_estimate=cost(40),
        name="scan_part",
    )(dk, push, sel, rate, up_rows, cot, w_down)


def message_loop(dk, grad, sel, slope):
    blocks = dk.shape[0] // BLK

    def block(i, carry):
        message = list(carry)
        b = blocks - 1 - i
        base = pl.multiple_of(b * BLK, BLK)
        r = sel[b, STATE:]
        for t in reversed(range(BLK)):
            d, g = spread(dk, base + t), spread(grad, base + t)
            for k, h in enumerate(HALVES):
                message[k] = jnp.exp2(d * slope[k]) * (r[h, t : t + 1] * g + message[k])
        return tuple(message)

    zero = jnp.zeros(slope[0].shape, f32)
    return lax.fori_loop(0, blocks, block, (zero, zero))


def adjoint_kernel(
    depth,
    dk, push, grad, sel, states, rate, ends, gup, gout,
    g_push, g_step, g_sel, g_rate, up_own, out_own,
    slots, notes, up_got, out_got, es, er, zs, zr, ks,
):
    z, p = here()
    tile = slots.shape[1]
    tiles = dk.shape[0] // tile
    per = tile // BLK

    def fetch(i, slot):
        return pltpu.make_async_copy(
            states.at[pl.ds(pl.multiple_of(i * tile, tile), tile)], slots.at[slot], ks.at[slot]
        )

    fetch(tiles - 1, 0).start()
    fetch(tiles - 2, 1).start()
    greet(False, depth)
    down = []
    for k in range(1, depth):
        q = lax.rem(z + k, depth)
        down.append(send(gout.at[q], out_got.at[k], zs.at[1, k], zr.at[1, k], (q, p)))
    slope = [rate[h, :] * LOG2E for h in HALVES]
    notes[z, :8], notes[z, 8:] = message_loop(dk, grad, sel, slope)
    mine = []
    for k in range(1, depth):
        mine.append(send(notes.at[z], notes.at[z], es.at[k], er.at[k], (lax.rem(z + k, depth), p)))
    for k in range(1, depth):
        q = lax.rem(z + k, depth)
        down.append(send(gup.at[q], up_got.at[k], zs.at[0, k], zr.at[0, k], (q, p)))
    for c in mine:
        c.wait_recv()
    message = [jnp.zeros(slope[0].shape, f32)] * 2
    for k in range(depth - 1, 0, -1):
        for i, h in enumerate(HALVES):
            message[i] = jnp.where(k > z, notes[k, h] + jnp.exp2(ends[k, 16:] * slope[i]) * message[i], message[i])
    lane = lax.broadcasted_iota(jnp.int32, (STATE, 128), 1)
    ones = jnp.ones((128, 128), bf16)

    def piece(n, carry):
        i = tiles - 1 - n
        slot = lax.rem(n, 2)
        fetch(i, slot).wait()

        def block(m, carry):
            message, acc = list(carry[:2]), list(carry[2:])
            j = per - 1 - m
            b = i * per + j
            base = pl.multiple_of(b * BLK, BLK)
            inside = j * BLK
            w, r = sel[b, :STATE], sel[b, STATE:]
            pushes, steps = [], []
            reads, writes = [None] * (2 * BLK), [None] * (2 * BLK)
            for t in reversed(range(BLK)):
                d, u, g = spread(dk, base + t), spread(push, base + t), spread(grad, base + t)
                plain = jnp.where(d < RESET, d, 0.0)
                to_push = to_step = None
                for k, h in enumerate(HALVES):
                    wt = w[h, t : t + 1]
                    hidden = slots[slot, inside + t, h]
                    total = r[h, t : t + 1] * g + message[k]
                    reads[2 * t + k] = lane_tiles(hidden * g)
                    writes[2 * t + k] = lane_tiles(total * u)
                    x = total * wt
                    carried = total * (hidden - wt * u)
                    y = carried * slope[k]
                    to_push = x if k == 0 else to_push + x
                    to_step = y if k == 0 else to_step + y
                    acc[k] = acc[k] + carried * plain
                    message[k] = jnp.exp2(d * slope[k]) * total
                pushes.insert(0, to_push)
                steps.insert(0, to_step)
                if len(pushes) == 8:
                    at = pl.ds(pl.multiple_of(base + t, 8), 8)
                    g_push[at, :] = tree(pushes)
                    g_step[at, :] = tree(steps)
                    pushes, steps = [], []
            for j2, quantity in enumerate((writes, reads)):
                x = jnp.concatenate(quantity, axis=0)
                high = x.astype(bf16)
                low = (x - high.astype(f32)).astype(bf16)
                sums = jnp.dot(high, ones, preferred_element_type=f32)
                sums = sums + jnp.dot(low, ones, preferred_element_type=f32)
                kept = jnp.zeros((STATE, 128), f32)
                for t in range(BLK):
                    kept = jnp.where(lane == t, sums[STATE * t : STATE * t + STATE], kept)
                g_sel[b, STATE * j2 : STATE * j2 + STATE] = kept[:, :BLK]
            return message[0], message[1], acc[0], acc[1]

        carry = lax.fori_loop(0, per, block, carry)

        @pl.when(n + 2 < tiles)
        def _():
            fetch(i - 2, slot).start()

        return carry

    zero = jnp.zeros(slope[0].shape, f32)
    done = lax.fori_loop(0, tiles, piece, (message[0], message[1], zero, zero))
    g_rate[:8], g_rate[8:] = done[2], done[3]
    for c in down:
        c.wait_recv()
    total = gup[z].astype(f32)
    for k in range(1, depth):
        total = total + up_got[k].astype(f32)
    rim = up_own.shape[1]
    for q in range(PLANE):
        up_own[q] = total[q * rim : q * rim + rim].astype(bf16)
    total = gout[z].astype(f32)
    for k in range(1, depth):
        total = total + out_got[k].astype(f32)
    out_own[...] = total
    for c in mine + down:
        c.wait_send()


def adjoint_part(cid, depth, tile, dk, push, grad, sel, states, rate, ends, gup, gout):
    rows, wide = dk.shape
    rim = gup.shape[1] // PLANE
    return pl.pallas_call(
        functools.partial(adjoint_kernel, depth),
        out_shape=[
            jax.ShapeDtypeStruct((rows, wide), f32),
            jax.ShapeDtypeStruct((rows, wide), f32),
            jax.ShapeDtypeStruct(sel.shape, f32),
            jax.ShapeDtypeStruct((STATE, wide), f32),
            jax.ShapeDtypeStruct((PLANE, rim, gup.shape[2]), bf16),
            jax.ShapeDtypeStruct(gout.shape[1:], f32),
        ],
        in_specs=[VM] * 4 + [ANY] + [VM] * 4,
        out_specs=[VM] * 6,
        scratch_shapes=[
            pltpu.VMEM((2, tile, STATE, wide), f32),
            pltpu.VMEM((depth, STATE, wide), f32),
            pltpu.VMEM(gup.shape, bf16),
            pltpu.VMEM(gout.shape, bf16),
        ]
        + [DMA((depth,))] * 2
        + [DMA((2, depth))] * 2
        + [DMA((2,))],
        compiler_params=params(cid),
        cost_estimate=cost(60),
        name="adjoint_part",
    )(dk, push, grad, sel, states, rate, ends, gup, gout)


def body(
    depth,
    tokens,
    segments,
    routes,
    norm_gain,
    in_proj,
    conv_taps,
    conv_bias,
    select_proj,
    step_proj,
    step_bias,
    decay_log,
    skip_gain,
    out_proj,
    moe_gain,
    router,
    expert_up,
    expert_down,
    cotangent,
):
    count = tokens.shape[0]
    rows = PLANE * count
    rim = norm_gain.shape[0]
    ch = conv_bias.shape[0]
    fs = expert_down.shape[1]
    z, p = here()

    win = in_proj.reshape(rim, 2, depth, PLANE, ch).transpose(3, 0, 1, 2, 4).reshape(PLANE, rim, 2 * WIDE)
    small = jnp.concatenate([norm_gain[:, None], moe_gain[:, None], router], axis=1)
    small = jnp.pad(small, ((0, 0), (0, 640 - 2 * WIDE - 4)))
    win = jnp.concatenate([win, jnp.broadcast_to(small[None], (PLANE, rim, 640 - 2 * WIDE))], axis=2)
    wup = (
        expert_up.reshape(EXPERTS, rim, depth, PLANE, fs)
        .transpose(3, 1, 0, 2, 4)
        .reshape(PLANE, rim, EXPERTS * HID)
    )
    side = jnp.concatenate(
        [decay_log.T, conv_taps.T, conv_bias[:, None], step_bias[:, None], skip_gain[:, None]], axis=1
    )
    pack = jnp.concatenate(
        [
            jnp.pad(select_proj, ((0, 0), (0, 128 - SEL))),
            jnp.pad(step_proj.T, ((0, 0), (0, 128 - RANK))),
            jnp.pad(side, ((0, 0), (0, 128 - side.shape[1]))),
        ],
        axis=1,
    )
    ids = jnp.concatenate([jnp.full((3,), -1, jnp.int32), segments, jnp.full((BLK,), -2, jnp.int32)])
    local_ids = lax.dynamic_slice_in_dim(ids, z * rows, rows + 3 + BLK)
    own_ids = local_ids[3:]
    inside = own_ids >= 0
    same = jnp.stack(
        [(local_ids[k : k + rows + BLK] == own_ids) & inside for k in range(4)], axis=1
    ).astype(f32)
    same = jnp.pad(same, ((0, 0), (0, 124)))
    (
        normed_in,
        w_in,
        w_route,
        small,
        w_sel,
        w_step,
        vecs,
        rate,
        inner,
        gate_in,
        conv,
        signal,
        selected,
        mixes,
        step_pre,
        dk,
        push,
        up_rows,
        down0,
        out_all,
    ) = front_part(1, depth, tokens, win, wup, pack, expert_down[0], out_proj, same)
    scanned, states, ends, up_early, cot_all, down1 = scan_part(
        2, depth, dk, push, mixes, rate, up_rows, cotangent, expert_down[1]
    )
    w_out = out_all.reshape(WIDE, D)
    choose = (routes == jnp.arange(EXPERTS, dtype=jnp.int32)[None, :]).astype(f32)
    order = lax.broadcasted_iota(jnp.int32, (count, count), 0) >= lax.broadcasted_iota(
        jnp.int32, (count, count), 1
    )
    places = mm(order.astype(bf16), choose.astype(bf16))
    slotted = choose * (places <= CAP).astype(f32)
    picks = jnp.pad(jnp.concatenate([choose, slotted], axis=1), ((0, 0), (0, 124)))
    output, grad_mid, mixed_wide, grad_gate_in, grad_out_w, grad_up, grad_down_own, sums = middle_part(
        3,
        depth,
        scanned,
        signal,
        gate_in,
        jnp.broadcast_to(vecs[6:7], (8, WIDE)),
        w_out,
        tokens,
        cot_all.reshape(rows, D),
        up_early,
        up_rows,
        down0.reshape(HID, D),
        down1.reshape(HID, D),
        w_route,
        small,
        picks,
    )
    grad_push, grad_scaled, grad_mixes, grad_rate, grad_up_rows, grad_out_own = adjoint_part(
        4,
        depth,
        count,
        dk,
        push,
        mixed_wide,
        mixes,
        states,
        rate,
        ends,
        grad_up.reshape(depth, D // depth, EXPERTS * HID),
        grad_out_w.reshape(depth, ch, D),
    )
    grad_tokens, in_cols, up_cols, pack_own, small_own = back_part(
        5,
        depth,
        rim,
        ch,
        grad_push,
        grad_scaled,
        grad_mixes,
        grad_rate,
        step_pre,
        signal,
        conv,
        inner,
        same,
        vecs,
        rate,
        selected,
        w_sel,
        w_step,
        mixed_wide,
        grad_gate_in,
        w_in,
        normed_in,
        tokens,
        small,
        grad_mid,
        sums,
        grad_up_rows,
    )
    in_cols = in_cols.astype(f32)
    up_cols = up_cols.astype(f32)
    ours = lax.dynamic_slice_in_dim(small_own, p * rim, rim, axis=1)
    grad_in_own = (
        in_cols.reshape(PLANE, rim, 2, depth, ch)
        .transpose(1, 2, 3, 0, 4)
        .reshape(rim, 2 * DI)
    )
    grad_up_own = (
        up_cols.reshape(PLANE, rim, EXPERTS, depth, fs).transpose(2, 1, 3, 0, 4).reshape(EXPERTS, rim, FF)
    )
    side = pack_own[:, 256:].T
    return (
        output,
        grad_tokens,
        ours[0],
        grad_in_own,
        side[STATE : STATE + 4],
        side[STATE + 4],
        pack_own[:, :SEL],
        pack_own[:, 128 : 128 + RANK].T,
        side[STATE + 5],
        side[:STATE],
        side[STATE + 6],
        grad_out_own,
        ours[1],
        ours[2:4].T,
        grad_up_own,
        grad_down_own,
    )


def solution(mesh):
    planes = Mesh(mesh.devices.reshape(-1, PLANE), ("z", "p"))
    every = ("z", "p")
    rows, flat, cols, third = P(every, None), P(every), P(None, every), P(None, every, None)
    return jax.shard_map(
        functools.partial(body, planes.shape["z"]),
        mesh=planes,
        in_specs=(
            rows, P(), rows, flat, rows, cols, flat, rows, cols,
            flat, cols, flat, rows, flat, rows, third, third, rows,
        ),
        out_specs=(
            rows, rows, flat, rows, cols, flat, rows, cols,
            flat, cols, flat, rows, flat, rows, third, third,
        ),
        check_vma=False,
    )
```

```python
import functools

import jax
import jax.numpy as jnp
from jax import lax
from jax.experimental import pallas as pl
from jax.experimental.pallas import tpu as pltpu
from jax.sharding import Mesh, PartitionSpec as P

D = 1152
DI = 2304
FF = 3072
RANK = 72
STATE = 16
EXPERTS = 2
CAP = 68
SEL = RANK + 2 * STATE

PLANE = 8
CHIPS = PLANE // 2
WIDE = DI // PLANE
PAD = -WIDE % 128
HID = FF // PLANE
BLK = 16
LOG2E = 1.4426950408889634
GELU = 0.7978845608028654
RESET = 1e5
EARLY, LATE = slice(0, 2), slice(2, PLANE)
epsilon = 1e-05

MESH = pl.DeviceIdType.MESH
ANY = pl.BlockSpec(memory_space=pl.ANY)
VM = pl.BlockSpec(memory_space=pltpu.VMEM)
bf16 = jnp.bfloat16
f32 = jnp.float32
DMA = pltpu.SemaphoreType.DMA


def params(cid=None, grid=None):
    extra = {} if cid is None else {"collective_id": cid, "has_side_effects": True}
    if grid is not None:
        extra["dimension_semantics"] = grid
    return pltpu.CompilerParams(vmem_limit_bytes=60 * 1024 * 1024, **extra)


def cost(us):
    return pl.CostEstimate(flops=int(us * 1e9), bytes_accessed=int(us * 3e6), transcendentals=0)


def mm(left, right):
    return jnp.dot(left, right, preferred_element_type=f32)


def contract_rows(left, right):
    return lax.dot_general(left, right, (((0,), (0,)), ((), ())), preferred_element_type=f32)


def contract_cols(left, right):
    return lax.dot_general(left, right, (((1,), (1,)), ((), ())), preferred_element_type=f32)


class Stage:
    def __init__(self, fetches, flushes):
        self.fetches, self.flushes, self.going = fetches, flushes, []
        for copy in fetches.values():
            copy.start()

    def need(self, *names):
        for name in names:
            self.fetches.pop(name).wait()

    def done(self, *names):
        for name in names:
            self.flushes[name].start()
            self.going.append(self.flushes[name])

    def end(self):
        self.need(*tuple(self.fetches))
        for copy in self.going:
            copy.wait()


def staged_call(kernel, name, cid, us, ins, outs, scratch, late=(), early=(), away=(), raw=()):
    inside = [n for n in outs if n not in away]
    early = [n for n in inside if n in early]

    def body(*refs):
        refs = list(refs)
        take = lambda names: dict(zip(names, [refs.pop(0) for _ in names]))
        source, target = take(ins), take(outs)
        buffers, results = take(late), take(early)
        in_sem, out_sem = refs.pop(0), refs.pop(0)
        stage = Stage(
            {n: pltpu.make_async_copy(source[n], buffers[n], in_sem.at[i]) for i, n in enumerate(late)},
            {n: pltpu.make_async_copy(results[n], target[n], out_sem.at[i]) for i, n in enumerate(early)},
        )
        kernel(
            stage,
            *[buffers.get(n, source[n]) for n in ins],
            *[results.get(n, target[n]) for n in outs],
            *refs,
        )
        stage.end()

    return pl.pallas_call(
        body,
        out_shape=list(outs.values()),
        in_specs=[ANY if n in late or n in raw else VM for n in ins],
        out_specs=[ANY if n in early or n in away else VM for n in outs],
        scratch_shapes=[pltpu.VMEM(ins[n].shape, ins[n].dtype) for n in late]
        + [pltpu.VMEM(outs[n].shape, outs[n].dtype) for n in early]
        + [DMA((max(len(late), 1),)), DMA((max(len(early), 1),))]
        + scratch,
        compiler_params=params(cid),
        cost_estimate=cost(us),
        name=name,
    )(*ins.values())


def made(*shape, dtype=None):
    return jax.ShapeDtypeStruct(shape, dtype or f32)


def remote(src, dst, ss, rs, to):
    return pltpu.make_async_remote_copy(
        src_ref=src, dst_ref=dst, send_sem=ss, recv_sem=rs, device_id=to, device_id_type=MESH
    )


def send(src, dst, ss, rs, to):
    copy = remote(src, dst, ss, rs, to)
    copy.start()
    return copy


def here():
    return lax.axis_index("z"), lax.axis_index("p")


def greet(plane=True, depth=0):
    z, p = here()
    barrier = pltpu.get_barrier_semaphore()
    count = 0
    if plane:
        for k in range(1, PLANE):
            pl.semaphore_signal(
                barrier, inc=1, device_id=(z, lax.rem(p + k, PLANE)), device_id_type=MESH
            )
            count += 1
    for k in range(1, depth):
        pl.semaphore_signal(barrier, inc=1, device_id=(lax.rem(z + k, depth), p), device_id_type=MESH)
        count += 1
    pl.semaphore_wait(barrier, count)


def share_start(x, out, ss, rs):
    z, p = here()
    core = lax.rem(p, 2)
    copies = [send(x, out.at[p], ss.at[0], rs.at[0], (z, p + 1 - 2 * core))]
    for k in range(1, CHIPS):
        copies.append(send(x, out.at[p], ss.at[k], rs.at[k], (z, lax.rem(p + 2 * k, PLANE))))
    return copies


def share_forward(out, copies, ss, rs):
    z, p = here()
    core = lax.rem(p, 2)
    onward = []
    for k in range(1, CHIPS):
        copies[k].wait_recv()
        src = lax.rem(p + PLANE - 2 * k, PLANE)
        onward.append(
            send(out.at[src], out.at[src], ss.at[CHIPS + k], rs.at[CHIPS + k], (z, p + 1 - 2 * core))
        )
    return onward


def share_finish(copies, onward):
    copies[0].wait_recv()
    for c in copies:
        c.wait_send()
    for c in onward:
        c.wait()


def column_copy(src, out, ss, rs, frm, to, part=None):
    dst = out.at[frm] if part is None else out.at[frm, part]
    return pltpu.make_async_remote_copy(
        src_ref=dst if src is None else src,
        dst_ref=dst,
        send_sem=ss.at[to],
        recv_sem=rs.at[frm],
        device_id=(to, lax.axis_index("p")),
        device_id_type=MESH,
    )


def column_each(depth, act):
    z = lax.axis_index("z")
    for t in range(depth):
        far = abs(t - z) == depth - 1 if depth == 4 else t == z
        pl.when(jnp.logical_not((t == z) | far))(functools.partial(act, t))


def column_start(depth, src, out, ss, rs, part=None):
    z = lax.axis_index("z")
    column_each(depth, lambda t: column_copy(src, out, ss, rs, z, t, part).start())


def column_forward(depth, out, ss, rs, part=None):
    if depth != 4:
        return
    z = lax.axis_index("z")
    for me, frm, to in ((2, 0, 3), (1, 3, 0)):

        @pl.when(z == me)
        def _():
            copy = column_copy(None, out, ss, rs, frm, to, part)
            copy.wait_recv()
            copy.start()


def column_finish(depth, src, out, ss, rs, part=None):
    z = lax.axis_index("z")
    for s in range(depth):
        ahead = ((z == 2) & (s == 0)) | ((z == 1) & (s == 3)) if depth == 4 else s == z

        @pl.when(jnp.logical_not((s == z) | ahead))
        def _():
            column_copy(src, out, ss, rs, s, s, part).wait_recv()

    column_each(depth, lambda t: column_copy(src, out, ss, rs, z, t, part).wait_send())
    if depth == 4:
        for me, frm, to in ((2, 0, 3), (1, 3, 0)):

            @pl.when(z == me)
            def _():
                column_copy(None, out, ss, rs, frm, to, part).wait_send()


def softplus(x):
    return jnp.maximum(x, 0.0) + jnp.log1p(jnp.exp(-jnp.abs(x)))


def total_start(x, got, ss, rs):
    z, p = here()
    copies = []
    for k in range(1, PLANE):
        q = lax.rem(p + k, PLANE)
        copies.append(send(x.at[q], got.at[k], ss.at[k], rs.at[k], (z, q)))
    return copies


def total_share(x, got, copies, out, ts, us):
    z, p = here()
    total = x[p]
    for k in range(1, PLANE):
        copies[k - 1].wait_recv()
        total = total + got[k]
    out[p] = total.astype(bf16)
    after = [
        send(out.at[p], out.at[p], ts.at[k], us.at[k], (z, lax.rem(p + k, PLANE))) for k in range(1, PLANE)
    ]
    for c in copies:
        c.wait_send()
    return after


def front_kernel(
    depth, stage,
    tok, in_proj, norm_gain, moe_gain, router, expert_up, select, step, decay, taps, bias, offset, skip,
    w_down, w_out, same,
    normed_in, w_in, w_route, small, w_sel, w_step, vecs, rate, inner, gate_in, conv, signal, selected, mixes,
    step_pre, dk, push, up_rows, down_all, out_all,
    tok_all, win_all, pack_all, wide, thin, near, halo, x, got, sel_all, win, wup, pack, square,
    gs, gr, ws, wr, vs, vr, zs, zr, hs, ss, rs, ts, us, ls,
):
    z, p = here()
    count = tok.shape[0]
    rim = in_proj.shape[0]
    ch = select.shape[0]
    pair = 2 * count
    rows = PLANE * count
    fs = expert_up.shape[2] // (depth * PLANE)
    local = [
        pltpu.make_async_copy(tok, tok_all.at[p], ls.at[0]),
        pltpu.make_async_copy(win.at[p], win_all.at[z, p], ls.at[1]),
        pltpu.make_async_copy(wup.at[p], up_rows.at[p], ls.at[2]),
        pltpu.make_async_copy(pack, pack_all.at[z], ls.at[3]),
        pltpu.make_async_copy(w_down.at[0], down_all.at[z], ls.at[4]),
        pltpu.make_async_copy(w_out, out_all.at[z], ls.at[5]),
    ]
    for i in (0, 4, 5):
        local[i].start()
    square[...] = jnp.zeros_like(square)
    square[0:1, :rim] = norm_gain[...].astype(f32)
    square[1:2, :rim] = moe_gain[...].astype(f32)
    square[2:4, :rim] = router[...].astype(f32)
    columns = square[...].T
    square[...] = columns
    for q in range(PLANE):
        for i in range(2 * depth):
            start = (i // depth) * DI + ((i % depth) * PLANE + q) * ch
            win[q, :, i * ch : i * ch + ch] = in_proj[:, start : start + ch]
        win[q, :, 2 * WIDE :] = square[:rim, :64].astype(bf16)
    local[1].start()
    greet(True, depth)
    across = []
    for k in range(1, PLANE):
        q = lax.rem(p + k, PLANE)
        across.append(send(win.at[q], win_all.at[z, p], ws.at[k], wr.at[k], (z, q)))
    first = share_start(tok, tok_all, gs, gr)
    square[...] = jnp.zeros_like(square)
    square[0:STATE, :ch] = decay[...].astype(f32)
    square[STATE : STATE + 4, :ch] = taps[...].astype(f32)
    for i, ref in enumerate((bias, offset, skip)):
        square[STATE + 4 + i : STATE + 5 + i, :ch] = ref[...].astype(f32)
    columns = square[...].T
    pack[:, 256:] = columns[:ch].astype(bf16)
    square[...] = jnp.zeros_like(square)
    square[:RANK, :ch] = step[...].astype(f32)
    columns = square[...].T
    pack[:, 128:256] = columns[:ch].astype(bf16)
    pack[:, :128] = jnp.zeros((ch, 128), bf16)
    pack[:, :SEL] = select[...]
    column_start(depth, pack, pack_all, zs.at[0], zr.at[0])
    local[3].start()
    for q in range(PLANE):
        for i in range(EXPERTS * depth):
            start = ((i % depth) * PLANE + q) * fs
            wup[q, :, i * fs : i * fs + fs] = expert_up[:, i // depth, start : start + fs]
    local[2].start()
    local[1].wait()
    for c in across:
        c.wait_recv()
    column_start(depth, win_all.at[z], win_all, zs.at[1], zr.at[1])
    second = share_forward(tok_all, first, gs, gr)
    more = []
    for k in range(1, PLANE):
        q = lax.rem(p + k, PLANE)
        more.append(send(wup.at[q], up_rows.at[p], vs.at[k], vr.at[k], (z, q)))
    local[3].wait()
    column_forward(depth, pack_all, zs.at[0], zr.at[0])
    column_finish(depth, pack, pack_all, zs.at[0], zr.at[0])
    for k in range(depth):
        thin[k * ch : k * ch + ch, :] = pack_all[k].astype(f32)
    w_sel[...] = thin[:, :128].astype(bf16)
    w_step[...] = thin[:, 128:256].astype(bf16)
    side = thin[:, 256:].T
    rate[:, :WIDE] = -jnp.exp(side[:STATE])
    rate[:, WIDE:] = jnp.zeros((STATE, PAD), f32)
    vecs[...] = side[STATE : STATE + 8]
    column_forward(depth, win_all, zs.at[1], zr.at[1])
    local[0].wait()
    share_finish(first, second)
    column_finish(depth, win_all.at[z], win_all, zs.at[1], zr.at[1])
    for k in range(depth):
        for q in range(PLANE):
            at = (k * PLANE + q) * rim
            wide[at : at + rim, :] = win_all[k, q].astype(f32)
    w_in[...] = wide[:, : 2 * WIDE].astype(bf16)
    w_route[...] = wide[:, 512:].astype(bf16)
    small[...] = wide[:, 512:].T[64:72]
    gain = small[0:1]
    for b in (3, 0, 1, 2):
        at = slice(pair * b, pair * b + pair)
        values = tok_all[2 * b : 2 * b + 2].reshape(pair, D).astype(f32)
        scale = lax.rsqrt(jnp.mean(values * values, axis=-1, keepdims=True) + epsilon)
        normed = (values * scale * gain).astype(bf16)
        normed_in[at, :] = normed
        joined = mm(normed, w_in[...]).astype(bf16)
        near[BLK + pair * b : BLK + pair * b + pair, :] = joined[:, :WIDE].astype(f32)
        gate_in[at, :] = joined[:, WIDE:]
        if b == 3:
            edge = send(near.at[pl.ds(rows, BLK)], halo, hs.at[0], hs.at[1], (lax.rem(z + 1, depth), p))
            column_start(depth, w_out, out_all, zs.at[2], zr.at[2])
            column_start(depth, w_down.at[0], down_all, zs.at[3], zr.at[3])
    stage.done("w_in", "normed_in", "gate_in")
    stage.need("same")
    for b in (1, 2, 3, 0):
        if b == 0:
            edge.wait()
            near[:BLK, :] = halo[...]
        base = pair * b
        at = slice(base, base + pair)
        total = vecs[4:5] + vecs[0:1] * near[base + 13 : base + 13 + pair, :] * same[at, 0:1]
        for k in range(1, 4):
            total = total + vecs[k : k + 1] * near[base + 13 + k : base + 13 + k + pair, :] * same[at, k : k + 1]
        conv[at, :] = total
        value = (total * jax.nn.sigmoid(total)).astype(bf16)
        signal[at, :] = value
        x[2 * b : 2 * b + 2] = mm(value, w_sel[...]).reshape(2, count, 128)
    third = total_start(x, got, ss, rs)
    inner[...] = near[...].astype(bf16)
    stage.done("conv", "signal", "inner")
    fourth = total_share(x, got, third, sel_all, ts, us)
    local[5].wait()
    column_forward(depth, out_all, zs.at[2], zr.at[2])
    for c in fourth:
        c.wait()
    for b in range(CHIPS):
        at = slice(pair * b, pair * b + pair)
        chosen = sel_all[2 * b : 2 * b + 2].reshape(pair, 128)
        selected[at, :] = chosen
        step = contract_cols(chosen, w_step[...]) + vecs[5:6]
        step_pre[at, :] = step
        delta = softplus(step)
        dk[at, :WIDE] = delta + (1.0 - same[at, 2:3]) * RESET
        push[at, :WIDE] = delta * signal[at, :].astype(f32)
        dk[at, WIDE:] = jnp.zeros((pair, PAD), f32)
        push[at, WIDE:] = jnp.zeros((pair, PAD), f32)
        full = chosen.astype(f32)
        for i in range(pair // BLK):
            flipped = full[i * BLK : i * BLK + BLK].T
            mixes[b * (pair // BLK) + i] = flipped[RANK:SEL]
    stage.done("dk", "push", "step_pre", "mixes", "selected")
    local[4].wait()
    column_forward(depth, down_all, zs.at[3], zr.at[3])
    column_finish(depth, w_out, out_all, zs.at[2], zr.at[2])
    column_finish(depth, w_down.at[0], down_all, zs.at[3], zr.at[3])
    local[2].wait()
    for c in across:
        c.wait_send()
    for c in more:
        c.wait()


def front_part(cid, depth, **ins):
    count, rim, ch = ins["tok"].shape[0], ins["in_proj"].shape[0], ins["select"].shape[0]
    low = ins["w_down"].shape[1]
    rows = PLANE * count
    outs = dict(
        normed_in=made(rows, D, dtype=bf16),
        w_in=made(D, 2 * WIDE, dtype=bf16),
        w_route=made(D, 128, dtype=bf16),
        small=made(8, D),
        w_sel=made(WIDE, 128, dtype=bf16),
        w_step=made(WIDE, 128, dtype=bf16),
        vecs=made(8, WIDE),
        rate=made(STATE, WIDE + PAD),
        inner=made(rows + BLK, WIDE, dtype=bf16),
        gate_in=made(rows, WIDE, dtype=bf16),
        conv=made(rows, WIDE),
        signal=made(rows, WIDE, dtype=bf16),
        selected=made(rows, 128, dtype=bf16),
        mixes=made(rows // BLK, 2 * STATE, BLK),
        step_pre=made(rows, WIDE),
        dk=made(rows, WIDE + PAD),
        push=made(rows, WIDE + PAD),
        up_rows=made(PLANE, rim, EXPERTS * HID, dtype=bf16),
        down_all=made(depth, low, D, dtype=bf16),
        out_all=made(depth, ch, D, dtype=bf16),
    )
    scratch = (
        [
            pltpu.VMEM((PLANE, count, D), bf16),
            pltpu.VMEM((depth, PLANE, rim, 640), bf16),
            pltpu.VMEM((depth, ch, 384), bf16),
            pltpu.VMEM((D, 640), f32),
            pltpu.VMEM((WIDE, 384), f32),
            pltpu.VMEM((BLK + rows, WIDE), f32),
            pltpu.VMEM((BLK, WIDE), f32),
            pltpu.VMEM((PLANE, count, 128), f32),
            pltpu.VMEM((PLANE, count, 128), f32),
            pltpu.VMEM((PLANE, count, 128), bf16),
            pltpu.VMEM((PLANE, rim, 640), bf16),
            pltpu.VMEM((PLANE, rim, EXPERTS * HID), bf16),
            pltpu.VMEM((ch, 384), bf16),
            pltpu.VMEM((128, 128), f32),
        ]
        + [DMA((PLANE,))] * 6
        + [DMA((4, depth))] * 2
        + [DMA((2,))]
        + [DMA((PLANE,))] * 4
        + [DMA((6,))]
    )
    early = (
        "normed_in", "w_in", "inner", "gate_in", "conv", "signal", "selected", "mixes", "step_pre", "dk", "push",
    )
    return staged_call(
        functools.partial(front_kernel, depth), "front_part", cid, 80, ins, outs, scratch,
        late=("same",), early=early, away=("down_all", "out_all"),
    )


def back_kernel(
    depth, stage,
    g_push, g_step, g_mixes, g_rate, step_pre, signal, conv, inner, same, vecs, rate, selected, w_sel, w_step,
    mixed_grad, gate_grad, w_in, normed_in, tok, gain, grad_mid, sums, gup,
    tokens_out, in_own, up_own, sel_own, step_own, decay_own, taps_own, bias_own, offset_own, skip_own,
    norm_own, moe_own, router_own,
    in_out, up_out, pack_out, x, got, gsel, low, gc, halo, nearf, gj, part, sib, mix, far, gin, gin_got, own, pack, pack_got, row, row_got, sml, sml_got,
    hs, ss, rs, ts, us, near_s, near_r, away_s, away_r, zs, zr, cs, cr, ups, upr, ls,
):
    z, p = here()
    core = lax.rem(p, 2)
    chip = lax.div(p, 2)
    twin = (z, p + 1 - 2 * core)
    count = tok.shape[0]
    pair = 2 * count
    rows = PLANE * count
    ch = sel_own.shape[0]
    rim = in_own.shape[0]
    fs = up_own.shape[2] // (depth * PLANE)
    sent = []

    def down(i, src, dst):
        copies = []
        for k in range(1, depth):
            q = lax.rem(z + k, depth)
            copies.append(send(src.at[q], dst.at[k], zs.at[i, k], zr.at[i, k], (q, p)))
        return copies

    greet(True, depth)
    block = D // depth
    stage.need("normed_in", "gate_grad")
    for q in range(depth):
        gin[1, q] = contract_rows(normed_in[:, q * block : q * block + block], gate_grad[...]).astype(bf16)
    gate_sent = down(3, gin.at[1], gin_got.at[1])
    stage.need("g_mixes", "w_step", "g_step", "g_push", "signal", "step_pre")
    bias = jnp.zeros((1, WIDE), f32)
    for b in range(CHIPS):
        at = slice(pair * b, pair * b + pair)
        value = signal[at, :].astype(f32)
        grad = g_step[at, :WIDE] * (1.0 / LOG2E) + g_push[at, :WIDE] * value
        grad = grad * jax.nn.sigmoid(step_pre[at, :])
        bias = bias + jnp.sum(grad, axis=0, keepdims=True)
        low[at, :] = grad.astype(bf16)
        ranks = mm(low[at, :], w_step[...])
        for i in range(pair // BLK):
            mixed = g_mixes[b * (pair // BLK) + i]
            wide = jnp.concatenate(
                [jnp.zeros((RANK, BLK), f32), mixed, jnp.zeros((128 - SEL, BLK), f32)], axis=0
            ).T
            t = i * BLK
            x[2 * b + t // count, t % count : t % count + BLK, :] = ranks[t : t + BLK] + wide
    first = total_start(x, got, ss, rs)
    stage.need("selected", "inner", "gup")
    keep = pltpu.make_async_copy(gup.at[p], up_out.at[p], ls)
    keep.start()
    grad_step_w = contract_rows(low[...], selected[...])
    nearf[...] = inner[...].astype(f32)
    second = total_share(x, got, first, gsel, ts, us)
    ups_sent = []
    for k in range(1, PLANE):
        q = lax.rem(p + k, PLANE)
        ups_sent.append(send(gup.at[q], up_out.at[p], ups.at[k], upr.at[k], (z, q)))
    for c in second:
        c.wait()
    stage.need("mixed_grad", "conv", "same", "w_sel")
    taps = [jnp.zeros((1, WIDE), f32)] * 4
    conv_bias = jnp.zeros((1, WIDE), f32)
    for b in range(CHIPS):
        base = pair * b
        at = slice(base, base + pair)
        delta = softplus(step_pre[at, :])
        grad = mixed_grad[at, :WIDE] * vecs[6:7] + g_push[at, :WIDE] * delta
        grad = grad + contract_cols(gsel[2 * b : 2 * b + 2].reshape(pair, 128), w_sel[...])
        c = conv[at, :]
        sig = jax.nn.sigmoid(c)
        grad = grad * (sig * (1.0 + c * (1.0 - sig)))
        gc[at, :] = grad
        if b == 0:
            edge = send(gc.at[pl.ds(0, BLK)], halo, hs.at[0], hs.at[1], (lax.rem(z + depth - 1, depth), p))
        conv_bias = conv_bias + jnp.sum(grad, axis=0, keepdims=True)
        for k in range(4):
            taps[k] = taps[k] + jnp.sum(
                grad * nearf[base + 13 + k : base + 13 + k + pair, :] * same[at, k : k + 1], axis=0, keepdims=True
            )
    stage.need("w_in", "tok", "grad_mid")
    for b in range(CHIPS):
        base = pair * b
        if b == CHIPS - 1:
            edge.wait()
            gc[rows : rows + BLK, :] = halo[...]
        total = jnp.zeros((pair, WIDE), f32)
        for k in range(4):
            off = slice(base + 3 - k, base + 3 - k + pair)
            total = total + gc[off, :] * vecs[k : k + 1] * same[off, k : k + 1]
        gj[base : base + pair, :WIDE] = total.astype(bf16)
        gj[base : base + pair, WIDE:] = gate_grad[base : base + pair, :]
    for q in range(depth):
        gin[0, q] = contract_rows(normed_in[:, q * block : q * block + block], gj[:, :WIDE]).astype(bf16)
    in_sent = down(0, gin.at[0], gin_got.at[0])
    near = {}
    for k in (1, 2, 3, 0):
        q = lax.rem(chip + k, CHIPS)
        at = pl.ds(pl.multiple_of(q * pair, pair), pair)
        part[k] = contract_cols(gj[at, :], w_in[...]).astype(bf16).reshape(2, count, D)
        near[k] = send(part.at[k, 1 - core], sib.at[k], near_s.at[k], near_r.at[k], twin)
    away = []
    for k in range(1, CHIPS):
        near[k].wait_recv()
        mix[k] = (part[k, core].astype(f32) + sib[k].astype(f32)).astype(bf16)
        away.append(
            send(mix.at[k], far.at[k], away_s.at[k], away_r.at[k], (z, lax.rem(p + 2 * k, PLANE)))
        )
    row[...] = jnp.zeros_like(row)
    row[0:STATE, :] = g_rate[...] * rate[...]
    for k in range(4):
        row[STATE + k : STATE + k + 1, :WIDE] = taps[k]
    row[STATE + 4 : STATE + 5, :WIDE] = conv_bias
    row[STATE + 5 : STATE + 6, :WIDE] = bias
    row[STATE + 6 : STATE + 7, :WIDE] = sums[3:4, :WIDE]
    side = row[...].T
    grad_sel_w = contract_rows(signal[...], gsel[...].reshape(rows, 128))
    for q in range(depth):
        cut = slice(q * ch, q * ch + ch)
        pack[q, :, :128] = grad_sel_w[cut].astype(bf16)
        pack[q, :, 128:256] = grad_step_w[cut].astype(bf16)
        pack[q, :, 256:] = side[cut].astype(bf16)
    pack_sent = down(1, pack, pack_got)
    near[0].wait_recv()
    total = part[0, core].astype(f32) + sib[0].astype(f32)
    for k in range(1, CHIPS):
        away[k - 1].wait_recv()
        total = total + far[k].astype(f32)
    values = tok[...].astype(f32)
    scale = lax.rsqrt(jnp.mean(values * values, axis=-1, keepdims=True) + epsilon)
    normed = values * scale
    grad_normed = total * gain[0:1]
    mean = jnp.mean(grad_normed * normed, axis=-1, keepdims=True)
    tokens_out[...] = (scale * (grad_normed - normed * mean) + grad_mid[...]).astype(bf16)
    stage.done("tokens_out")
    ours = jnp.concatenate(
        [jnp.sum(total * normed, axis=0, keepdims=True), sums[0:3, :], jnp.zeros((4, D), f32)], axis=0
    )
    for q in range(depth):
        sml[q] = ours[:, q * block : q * block + block]
    sml_sent = down(2, sml, sml_got)
    for h, copies in ((1, gate_sent), (0, in_sent)):
        for c in copies:
            c.wait_recv()
        total = gin[h, z].astype(f32)
        for k in range(1, depth):
            total = total + gin_got[h, k].astype(f32)
        for q in range(PLANE):
            own[q, :, h * WIDE : h * WIDE + WIDE] = total[q * rim : q * rim + rim].astype(bf16)
    across = []
    for k in range(1, PLANE):
        q = lax.rem(p + k, PLANE)
        across.append(send(own.at[q], in_out.at[p], cs.at[0, k], cr.at[0, k], (z, q)))
    in_out[p] = own[p]
    for c in sml_sent:
        c.wait_recv()
    total = sml[z]
    for k in range(1, depth):
        total = total + sml_got[k]
    sml_got[0] = total
    for k in range(1, PLANE):
        q = lax.rem(p + k, PLANE)
        across.append(send(sml_got.at[0], row_got.at[k], cs.at[1, k], cr.at[1, k], (z, q)))
    for c in pack_sent:
        c.wait_recv()
    total = pack[z].astype(f32)
    for k in range(1, depth):
        total = total + pack_got[k].astype(f32)
    sel_own[...] = total[:, :SEL]
    pack_out[...] = jnp.zeros_like(pack_out)
    pack_out[:ch, :] = total[:, 128:256]
    columns = pack_out[...].T
    step_own[...] = columns[:RANK, :ch]
    pack_out[:ch, :32] = total[:, 256:]
    columns = pack_out[...].T
    decay_own[...] = columns[:STATE, :ch]
    taps_own[...] = columns[STATE : STATE + 4, :ch]
    bias_own[...] = columns[STATE + 4 : STATE + 5, :ch]
    offset_own[...] = columns[STATE + 5 : STATE + 6, :ch]
    skip_own[...] = columns[STATE + 6 : STATE + 7, :ch]
    for c in ups_sent:
        c.wait()
    keep.wait()
    for q in range(PLANE):
        for i in range(EXPERTS * depth):
            start = ((i % depth) * PLANE + q) * fs
            up_own[:, i // depth, start : start + fs] = up_out[q, :, i * fs : i * fs + fs].astype(f32)
    stage.done("up_own")
    for c in across:
        c.wait()
    for q in range(PLANE):
        for i in range(2 * depth):
            start = (i // depth) * DI + ((i % depth) * PLANE + q) * ch
            in_own[:, start : start + ch] = in_out[q, :, i * ch : i * ch + ch].astype(f32)
    total = sml_got[0]
    for k in range(1, PLANE):
        total = total + row_got[k]
    for q in range(PLANE):

        @pl.when(p == q)
        def _():
            cut = total[:, q * rim : q * rim + rim]
            norm_own[...] = cut[0:1]
            moe_own[...] = cut[1:2]
            router_own[...] = cut[2:4]

    for c in list(near.values()) + away + gate_sent + in_sent + pack_sent + sml_sent:
        c.wait_send()


def back_part(cid, depth, rim, ch, **ins):
    count = ins["tok"].shape[0]
    rows = PLANE * count
    block = D // depth
    outs = dict(
        tokens_out=made(count, D, dtype=bf16),
        in_own=made(rim, 2 * DI),
        up_own=made(rim, EXPERTS, FF),
        sel_own=made(ch, SEL),
        step_own=made(RANK, ch),
        decay_own=made(STATE, ch),
        taps_own=made(4, ch),
        bias_own=made(1, ch),
        offset_own=made(1, ch),
        skip_own=made(1, ch),
        norm_own=made(1, rim),
        moe_own=made(1, rim),
        router_own=made(2, rim),
    )
    scratch = (
        [
            pltpu.VMEM((PLANE, rim, 2 * WIDE), bf16),
            pltpu.VMEM((PLANE, rim, EXPERTS * HID), bf16),
            pltpu.VMEM((128, 128), f32),
            pltpu.VMEM((PLANE, count, 128), f32),
            pltpu.VMEM((PLANE, count, 128), f32),
            pltpu.VMEM((PLANE, count, 128), bf16),
            pltpu.VMEM((rows, WIDE), bf16),
            pltpu.VMEM((rows + BLK, WIDE), f32),
            pltpu.VMEM((BLK, WIDE), f32),
            pltpu.VMEM((rows + BLK, WIDE), f32),
            pltpu.VMEM((rows, 2 * WIDE), bf16),
            pltpu.VMEM((CHIPS, 2, count, D), bf16),
            pltpu.VMEM((CHIPS, count, D), bf16),
            pltpu.VMEM((CHIPS, count, D), bf16),
            pltpu.VMEM((CHIPS, count, D), bf16),
            pltpu.VMEM((2, depth, block, WIDE), bf16),
            pltpu.VMEM((2, depth, block, WIDE), bf16),
            pltpu.VMEM((PLANE, rim, 2 * WIDE), bf16),
            pltpu.VMEM((depth, ch, 288), bf16),
            pltpu.VMEM((depth, ch, 288), bf16),
            pltpu.VMEM((2 * STATE, WIDE + PAD), f32),
            pltpu.VMEM((PLANE, 8, block), f32),
            pltpu.VMEM((depth, 8, block), f32),
            pltpu.VMEM((depth, 8, block), f32),
            DMA((2,)),
        ]
        + [DMA((PLANE,))] * 4
        + [DMA((CHIPS,))] * 4
        + [DMA((4, depth))] * 2
        + [DMA((2, PLANE))] * 2
        + [DMA((PLANE,))] * 2
        + [DMA]
    )
    late = (
        "normed_in", "gate_grad", "g_mixes", "w_step", "g_step", "g_push", "signal", "step_pre", "selected", "inner",
        "gup", "mixed_grad", "conv", "same", "w_sel", "w_in", "tok", "grad_mid",
    )
    return staged_call(
        functools.partial(back_kernel, depth), "back_part", cid, 70, ins, outs, scratch,
        late=late, early=("tokens_out", "up_own"),
    )


def middle_kernel(
    depth, stage,
    scanned, signal, gate_in, skip, w_out, tok, cot_all, up_early, up_rows, down0, down1, w_router, rows_in, picks,
    output, grad_mid, mixed_grad, gate_grad, grad_out, grad_up, down_own, sums,
    gated, part, sib, mix, far, routed_all, marks_all, hidden_all, pre_all, slot_all, back_all,
    up_late, w_up, wide, grad_down, down_got,
    near_s, near_r, away_s, away_r, gs, gr, zs, zr, ds, dr, ls,
):
    z, p = here()
    core = lax.rem(p, 2)
    chip = lax.div(p, 2)
    twin = (z, p + 1 - 2 * core)
    count = tok.shape[0]
    pair = 2 * count

    def chip_at(k):
        return lax.rem(chip + k, CHIPS)

    def rows_of(q):
        return pl.ds(pl.multiple_of(q * pair, pair), pair)

    def near(i, k):
        return remote(part.at[i, k, 1 - core], sib.at[i, k], near_s.at[i, k], near_r.at[i, k], twin)

    def away(i, k):
        return remote(
            mix.at[i, k], far.at[i, k], away_s.at[i, k], away_r.at[i, k], (z, lax.rem(p + 2 * k, PLANE))
        )

    def pass_away(i, k):
        near(i, k).wait_recv()
        mix[i, k] = (part[i, k, core].astype(f32) + sib[i, k].astype(f32)).astype(bf16)
        away(i, k).start()

    def gathered(i):
        near(i, 0).wait_recv()
        total = part[i, 0, core].astype(f32) + sib[i, 0].astype(f32)
        for k in range(1, CHIPS):
            away(i, k).wait_recv()
            total = total + far[i, k].astype(f32)
        return total

    def shared(i, ref, k):
        return remote(ref.at[p], ref.at[p], gs.at[i, k], gr.at[i, k], (z, lax.rem(p + 2 * k, PLANE)))

    def onward(i, ref, k):
        src = lax.rem(p + 2 * k, PLANE)
        return remote(ref.at[src], ref.at[src], gs.at[i, CHIPS + k], gr.at[i, CHIPS + k], twin)

    def arrived(k, refs):
        @pl.when(k == 0)
        def _():
            for i, ref in refs:
                remote(ref.at[p], ref.at[p], gs.at[i, 0], gr.at[i, 0], twin).wait_recv()

        @pl.when(k > 0)
        def _():
            for i, ref in refs:
                shared(i, ref, CHIPS - k).wait_recv()
                onward(i, ref, k).start()
            for i, ref in refs:
                onward(i, ref, k).wait_recv()

    greet(True, depth)
    stage.need("up_rows")
    local = pltpu.make_async_copy(up_rows.at[LATE], up_late.at[z], ls)
    local.start()
    column_start(depth, up_rows.at[LATE], up_late, zs, zr)
    stage.need("w_out", "scanned", "signal", "gate_in")
    @pl.loop(0, CHIPS)
    def _(turn):
        k = lax.rem(turn + 1, CHIPS)
        q = chip_at(k)
        at = rows_of(q)
        pre = scanned[at, :WIDE] + skip[6:7] * signal[at, :].astype(f32)
        inward = gate_in[at, :].astype(f32)
        gated[at, :] = (pre * (inward * jax.nn.sigmoid(inward))).astype(bf16)
        part[0, k] = mm(gated[at, :], w_out[...]).astype(bf16).reshape(2, count, D)
        near(0, k).start()

    for k in range(1, CHIPS):
        pass_away(0, k)
    branch = gathered(0)

    stage.need("tok", "w_router", "up_early", "cot_all", "down0", "down1")
    gain, router0, router1 = rows_in[1:2], rows_in[2:3], rows_in[3:4]
    middle = tok[...].astype(f32) + branch
    scale = lax.rsqrt(jnp.mean(middle * middle, axis=-1, keepdims=True) + epsilon)
    normed = middle * scale
    routed = (normed * gain).astype(bf16)
    routed_all[p] = routed
    logits = mm(routed, w_router[...])
    l0, l1 = logits[:, 66:67], logits[:, 67:68]
    top = jnp.maximum(l0, l1)
    e0, e1 = jnp.exp(l0 - top), jnp.exp(l1 - top)
    p0, p1 = e0 / (e0 + e1), e1 / (e0 + e1)
    taken = jnp.broadcast_to(picks[...].astype(f32), (count, count)).T[:, 0:1]
    c0 = (taken == 0).astype(f32)
    c1 = (taken == 1).astype(f32)
    chosen = jnp.where(lax.broadcasted_iota(jnp.int32, (count, 128), 1) == 0, c0, c1).astype(bf16)
    before = lax.broadcasted_iota(jnp.int32, (count, count), 0) >= lax.broadcasted_iota(
        jnp.int32, (count, count), 1
    )
    places = mm(before.astype(f32).astype(bf16), chosen)
    s0 = c0 * (places[:, 0:1] <= CAP).astype(f32)
    s1 = c1 * (places[:, 1:2] <= CAP).astype(f32)
    gate = p0 * c0 + p1 * c1
    kept = s0 + s1
    weight = gate * kept
    lane = lax.broadcasted_iota(jnp.int32, (count, 128), 1)
    marks_all[p] = jnp.where(lane == 0, weight, jnp.where(lane == 1, s0, s1))
    share_start(routed_all.at[p], routed_all, gs.at[0], gr.at[0])
    share_start(marks_all.at[p], marks_all, gs.at[1], gr.at[1])
    local.wait()
    column_forward(depth, up_late, zs, zr)
    column_finish(depth, up_rows.at[LATE], up_late, zs, zr)
    rim = up_rows.shape[1]
    block = PLANE * rim
    for k in range(depth):
        for q in range(PLANE):
            source = up_early[k, q] if q < EARLY.stop else up_late[k, q - EARLY.stop]
            wide[q * rim : q * rim + rim, :] = source.astype(f32)
        w_up[k * block : k * block + block, :] = wide[...].astype(bf16)

    odd = lax.broadcasted_iota(jnp.int32, (1, EXPERTS * HID), 1) >= HID

    @pl.loop(0, CHIPS)
    def _(k):
        q = chip_at(k)
        arrived(k, ((0, routed_all), (1, marks_all)))
        both = pl.ds(2 * q, 2)
        marks = marks_all[both].reshape(pair, 128)
        mask = jnp.where(odd, marks[:, 2:3], marks[:, 1:2])
        hidden = mm(routed_all[both].reshape(pair, D), w_up[...])
        slot = (cot_all[rows_of(q), :].astype(f32) * marks[:, 0:1]).astype(bf16)
        slot_all[q] = slot
        square = hidden * hidden
        bend = jnp.tanh(GELU * hidden * (1.0 + 0.044715 * square))
        units = (0.5 * hidden * (1.0 + bend) * mask).astype(bf16)
        hidden_all[q] = units
        slope = 0.5 * (1.0 + bend) + 0.5 * GELU * hidden * (1.0 - bend * bend) * (1.0 + 3 * 0.044715 * square)
        grad = jnp.concatenate([contract_cols(slot, down0[...]), contract_cols(slot, down1[...])], axis=1)
        grad = (slope * grad * mask).astype(bf16)
        pre_all[q] = grad
        made = mm(units[:, :HID], down0[...]) + mm(units[:, HID:], down1[...])
        part[1, k] = made.astype(bf16).reshape(2, count, D)
        near(1, k).start()
        part[2, k] = contract_cols(grad, w_up[...]).astype(bf16).reshape(2, count, D)
        near(2, k).start()

        @pl.when(k > 1)
        def _():
            pass_away(1, k - 1)
            pass_away(2, k - 1)

    pass_away(1, CHIPS - 1)
    pass_away(2, CHIPS - 1)
    every = CHIPS * pair
    fs = HID // depth
    for c in range(0, D, 384):
        for e in range(EXPERTS):
            made = contract_rows(
                hidden_all[:, :, e * HID : e * HID + HID].reshape(every, HID),
                slot_all[:, :, c : c + 384].reshape(every, 384),
            )
            for k in range(depth):
                grad_down[k, e, :, c : c + 384] = made[k * fs : k * fs + fs].astype(bf16)
    down = []
    for k in range(1, depth):
        q = lax.rem(z + k, depth)
        down.append(send(grad_down.at[q], down_got.at[k], ds.at[k], dr.at[k], (q, p)))
    expert_tok = gathered(1)
    slot_back = gathered(2)

    up = cot_all[pl.ds(pl.multiple_of(p * count, count), count), :].astype(f32)
    output[...] = (middle + weight * expert_tok).astype(bf16)
    stage.done("output")
    pull = jnp.sum(up * expert_tok, axis=-1, keepdims=True) * kept * gate
    g0, g1 = pull * (c0 - p0), pull * (c1 - p1)
    grad_routed = slot_back + g0 * router0 + g1 * router1
    routed = routed.astype(f32)
    sum0 = jnp.sum(grad_routed * normed, axis=0, keepdims=True)
    sum1 = jnp.sum(routed * g0, axis=0, keepdims=True)
    sum2 = jnp.sum(routed * g1, axis=0, keepdims=True)
    grad_normed = grad_routed * gain
    inner = jnp.mean(grad_normed * normed, axis=-1, keepdims=True)
    total = scale * (grad_normed - normed * inner) + up
    grad_mid[...] = total
    stage.done("grad_mid")
    back_all[p] = total.astype(bf16)
    share_start(back_all.at[p], back_all, gs.at[2], gr.at[2])
    for c in range(0, D, 384):
        grad_up[c : c + 384, :] = contract_rows(
            routed_all[:, :, c : c + 384].reshape(every, 384), pre_all[...].reshape(every, EXPERTS * HID)
        ).astype(bf16)
    stage.done("grad_up")

    sums[...] = jnp.zeros_like(sums)
    sums[0:1], sums[1:2], sums[2:3] = sum0, sum1, sum2

    @pl.loop(0, CHIPS)
    def _(k):
        q = chip_at(k)
        arrived(k, ((2, back_all),))
        at = rows_of(q)
        grad = contract_cols(back_all[pl.ds(2 * q, 2)].reshape(pair, D), w_out[...])
        inward = gate_in[at, :].astype(f32)
        sig = jax.nn.sigmoid(inward)
        act = inward * sig
        through = grad * act
        sums[3:4, :WIDE] += jnp.sum(through * signal[at, :].astype(f32), axis=0, keepdims=True)
        mixed_grad[at, :WIDE] = through
        mixed_grad[at, WIDE:] = jnp.zeros((pair, PAD), f32)
        pre = scanned[at, :WIDE] + skip[6:7] * signal[at, :].astype(f32)
        gate_grad[at, :] = (grad * pre * (sig * (1.0 + inward * (1.0 - sig)))).astype(bf16)
    stage.done("mixed_grad", "gate_grad")
    for c in range(0, D, 384):
        grad_out[:, c : c + 384] = contract_rows(
            gated[...], back_all[:, :, c : c + 384].reshape(every, 384)
        ).astype(bf16)
    for c in down:
        c.wait_recv()
    total = grad_down[z].astype(f32)
    for k in range(1, depth):
        total = total + down_got[k].astype(f32)
    down_own[...] = total
    for c in down:
        c.wait_send()
    for i in range(3):
        for k in range(CHIPS):
            near(i, k).wait_send()
            if k:
                away(i, k).wait_send()
    for i, ref in ((0, routed_all), (1, marks_all), (2, back_all)):
        remote(ref.at[p], ref.at[p], gs.at[i, 0], gr.at[i, 0], twin).wait_send()
        for k in range(1, CHIPS):
            shared(i, ref, k).wait_send()
            onward(i, ref, k).wait_send()


def middle_part(cid, depth, **ins):
    count, rows, rim = ins["tok"].shape[0], ins["cot_all"].shape[0], ins["up_rows"].shape[1]
    wide = EXPERTS * HID
    block = (CHIPS, count, D)
    outs = dict(
        output=made(count, D, dtype=bf16),
        grad_mid=made(count, D),
        mixed_grad=made(rows, WIDE + PAD),
        gate_grad=made(rows, WIDE, dtype=bf16),
        grad_out=made(WIDE, D, dtype=bf16),
        grad_up=made(D, wide, dtype=bf16),
        down_own=made(EXPERTS, HID // depth, D),
        sums=made(8, D),
    )
    scratch = (
        [
            pltpu.VMEM((rows, WIDE), bf16),
            pltpu.VMEM((3, CHIPS, 2, count, D), bf16),
            pltpu.VMEM((3,) + block, bf16),
            pltpu.VMEM((3,) + block, bf16),
            pltpu.VMEM((3,) + block, bf16),
            pltpu.VMEM((PLANE, count, D), bf16),
            pltpu.VMEM((PLANE, count, 128), f32),
            pltpu.VMEM((CHIPS, 2 * count, wide), bf16),
            pltpu.VMEM((CHIPS, 2 * count, wide), bf16),
            pltpu.VMEM((CHIPS, 2 * count, D), bf16),
            pltpu.VMEM((PLANE, count, D), bf16),
            pltpu.VMEM((depth, LATE.stop - LATE.start, rim, wide), bf16),
            pltpu.VMEM((D, wide), bf16),
            pltpu.VMEM((PLANE * rim, wide), f32),
            pltpu.VMEM((depth, EXPERTS, HID // depth, D), bf16),
            pltpu.VMEM((depth, EXPERTS, HID // depth, D), bf16),
        ]
        + [DMA((3, CHIPS))] * 4
        + [DMA((3, PLANE))] * 2
        + [DMA((depth,))] * 4
        + [DMA]
    )
    late = (
        "up_rows", "w_out", "scanned", "signal", "gate_in", "tok", "w_router", "up_early", "cot_all", "down0", "down1",
    )
    return staged_call(
        functools.partial(middle_kernel, depth), "middle_part", cid, 75, ins, outs, scratch,
        late=late, early=("output", "grad_mid", "grad_up", "mixed_grad", "gate_grad"),
    )


def tree(parts):
    row = lax.broadcasted_iota(jnp.int32, parts[0].shape, 0)
    for step in (1, 2, 4):
        low = (row // step) % 2 == 0
        parts = [
            jnp.where(low, a, b) + pltpu.roll(jnp.where(low, b, a), step, 0)
            for a, b in zip(parts[::2], parts[1::2])
        ]
    return parts[0]


def lane_tiles(x):
    total = x[:, :128]
    for k in range(128, x.shape[1], 128):
        total = total + x[:, k : k + 128]
    return total


def spread(ref, i):
    return jnp.broadcast_to(ref[pl.ds(i, 1), :], (8, ref.shape[1]))


HALVES = (slice(0, 8), slice(8, 16))


def ends_loop(dk, push, sel, slope):
    def block(b, carry):
        hidden, acc = list(carry[:2]), carry[2]
        base = pl.multiple_of(b * BLK, BLK)
        w = sel[b, :STATE]
        for t in range(BLK):
            d, u = spread(dk, base + t), spread(push, base + t)
            for k, h in enumerate(HALVES):
                hidden[k] = jnp.exp2(d * slope[k]) * hidden[k] + w[h, t : t + 1] * u
            acc = acc + d
        return hidden[0], hidden[1], acc

    zero = jnp.zeros(slope[0].shape, f32)
    return lax.fori_loop(0, dk.shape[0] // BLK, block, (zero, zero, zero))


def scan_kernel(
    depth,
    dk, push, sel, rate, up_rows, cot, w_down,
    out, states, ends, up_all, cot_all, down_all,
    slots, gs, gr, es, er, zs, zr, ks, ls,
):
    z, p = here()
    tile = slots.shape[1]
    tiles = dk.shape[0] // tile
    local = [
        pltpu.make_async_copy(up_rows.at[EARLY], up_all.at[z], ls.at[0]),
        pltpu.make_async_copy(cot, cot_all.at[p], ls.at[1]),
        pltpu.make_async_copy(w_down.at[1], down_all.at[z], ls.at[2]),
    ]
    for c in local:
        c.start()
    greet(True, depth)
    column_start(depth, up_rows.at[EARLY], up_all, zs.at[0], zr.at[0])
    first = share_start(cot, cot_all, gs, gr)
    slope = [rate[h, :] * LOG2E for h in HALVES]
    one, two, acc = ends_loop(dk, push, sel, slope)
    ends[z, :8], ends[z, 8:16], ends[z, 16:] = one, two, acc
    mine = []
    for k in range(1, depth):
        mine.append(send(ends.at[z], ends.at[z], es.at[k], er.at[k], (lax.rem(z + k, depth), p)))
    column_start(depth, w_down.at[1], down_all, zs.at[1], zr.at[1])
    second = share_forward(cot_all, first, gs, gr)
    for c in local:
        c.wait()
    column_forward(depth, up_all, zs.at[0], zr.at[0])
    for c in mine:
        c.wait_recv()
    hidden = [jnp.zeros(slope[0].shape, f32)] * 2
    for k in range(depth - 1):
        for i, h in enumerate(HALVES):
            hidden[i] = jnp.where(k < z, jnp.exp2(ends[k, 16:] * slope[i]) * hidden[i] + ends[k, h], hidden[i])

    def stored(i, slot):
        return pltpu.make_async_copy(
            slots.at[slot], states.at[pl.ds(pl.multiple_of(i * tile, tile), tile)], ks.at[slot]
        )

    def piece(i, carry):
        slot = lax.rem(i, 2)

        @pl.when(i >= 2)
        def _():
            stored(i - 2, slot).wait()

        def block(j, carry):
            hidden = list(carry)
            b = i * (tile // BLK) + j
            base = pl.multiple_of(b * BLK, BLK)
            inside = j * BLK
            w, r = sel[b, :STATE], sel[b, STATE:]
            parts = []
            for t in range(BLK):
                d, u = spread(dk, base + t), spread(push, base + t)
                line = None
                for k, h in enumerate(HALVES):
                    hidden[k] = jnp.exp2(d * slope[k]) * hidden[k] + w[h, t : t + 1] * u
                    slots[slot, inside + t, h] = hidden[k]
                    y = r[h, t : t + 1] * hidden[k]
                    line = y if line is None else line + y
                parts.append(line)
                if len(parts) == 8:
                    out[pl.ds(pl.multiple_of(base + t - 7, 8), 8), :] = tree(parts)
                    parts = []
            return tuple(hidden)

        carry = lax.fori_loop(0, tile // BLK, block, carry)
        stored(i, slot).start()
        return carry

    carry = lax.fori_loop(0, tiles - 2, piece, tuple(hidden))
    column_forward(depth, down_all, zs.at[1], zr.at[1])
    lax.fori_loop(tiles - 2, tiles, piece, carry)
    for i in (tiles - 2, tiles - 1):
        stored(i, i % 2).wait()
    share_finish(first, second)
    column_finish(depth, up_rows.at[EARLY], up_all, zs.at[0], zr.at[0])
    column_finish(depth, w_down.at[1], down_all, zs.at[1], zr.at[1])
    for c in mine:
        c.wait_send()


def scan_part(cid, depth, dk, push, sel, rate, up_rows, cot, w_down):
    rows, wide = dk.shape
    tile = cot.shape[0]
    return pl.pallas_call(
        functools.partial(scan_kernel, depth),
        out_shape=[
            jax.ShapeDtypeStruct((rows, wide), f32),
            jax.ShapeDtypeStruct((rows, STATE, wide), f32),
            jax.ShapeDtypeStruct((depth, STATE + 8, wide), f32),
            jax.ShapeDtypeStruct((depth, EARLY.stop) + up_rows.shape[1:], bf16),
            jax.ShapeDtypeStruct((PLANE,) + cot.shape, bf16),
            jax.ShapeDtypeStruct((depth,) + w_down.shape[1:], bf16),
        ],
        in_specs=[VM] * 7,
        out_specs=[VM, ANY, VM, ANY, ANY, ANY],
        scratch_shapes=[pltpu.VMEM((2, tile, STATE, wide), f32)]
        + [DMA((PLANE,))] * 2
        + [DMA((depth,))] * 2
        + [DMA((2, depth))] * 2
        + [DMA((2,)), DMA((3,))],
        compiler_params=params(cid),
        cost_estimate=cost(40),
        name="scan_part",
    )(dk, push, sel, rate, up_rows, cot, w_down)


def message_loop(dk, grad, sel, slope):
    blocks = dk.shape[0] // BLK

    def block(i, carry):
        message = list(carry)
        b = blocks - 1 - i
        base = pl.multiple_of(b * BLK, BLK)
        r = sel[b, STATE:]
        for t in reversed(range(BLK)):
            d, g = spread(dk, base + t), spread(grad, base + t)
            for k, h in enumerate(HALVES):
                message[k] = jnp.exp2(d * slope[k]) * (r[h, t : t + 1] * g + message[k])
        return tuple(message)

    zero = jnp.zeros(slope[0].shape, f32)
    return lax.fori_loop(0, blocks, block, (zero, zero))


def adjoint_kernel(
    depth, stage,
    dk, push, grad, sel, states, rate, ends, gup, gout,
    g_push, g_step, g_sel, g_rate, up_own, out_own,
    slots, notes, up_got, out_got, es, er, zs, zr, ks,
):
    z, p = here()
    tile = slots.shape[1]
    tiles = dk.shape[0] // tile
    per = tile // BLK

    def fetch(i, slot):
        return pltpu.make_async_copy(
            states.at[pl.ds(pl.multiple_of(i * tile, tile), tile)], slots.at[slot], ks.at[slot]
        )

    fetch(tiles - 1, 0).start()
    fetch(tiles - 2, 1).start()
    greet(False, depth)
    stage.need("sel", "dk", "grad", "gout")
    down = []
    for k in range(1, depth):
        q = lax.rem(z + k, depth)
        down.append(send(gout.at[q], out_got.at[k], zs.at[1, k], zr.at[1, k], (q, p)))
    slope = [rate[h, :] * LOG2E for h in HALVES]
    notes[z, :8], notes[z, 8:] = message_loop(dk, grad, sel, slope)
    mine = []
    for k in range(1, depth):
        mine.append(send(notes.at[z], notes.at[z], es.at[k], er.at[k], (lax.rem(z + k, depth), p)))
    stage.need("gup", "push")
    for k in range(1, depth):
        q = lax.rem(z + k, depth)
        down.append(send(gup.at[q], up_got.at[k], zs.at[0, k], zr.at[0, k], (q, p)))
    for c in mine:
        c.wait_recv()
    message = [jnp.zeros(slope[0].shape, f32)] * 2
    for k in range(depth - 1, 0, -1):
        for i, h in enumerate(HALVES):
            message[i] = jnp.where(k > z, notes[k, h] + jnp.exp2(ends[k, 16:] * slope[i]) * message[i], message[i])
    lane = lax.broadcasted_iota(jnp.int32, (STATE, 128), 1)
    ones = jnp.ones((128, 128), bf16)

    def piece(n, carry):
        i = tiles - 1 - n
        slot = lax.rem(n, 2)
        fetch(i, slot).wait()

        def block(m, carry):
            message, acc = list(carry[:2]), list(carry[2:])
            j = per - 1 - m
            b = i * per + j
            base = pl.multiple_of(b * BLK, BLK)
            inside = j * BLK
            w, r = sel[b, :STATE], sel[b, STATE:]
            pushes, steps = [], []
            reads, writes = [None] * (2 * BLK), [None] * (2 * BLK)
            for t in reversed(range(BLK)):
                d, u, g = spread(dk, base + t), spread(push, base + t), spread(grad, base + t)
                plain = jnp.where(d < RESET, d, 0.0)
                to_push = to_step = None
                for k, h in enumerate(HALVES):
                    wt = w[h, t : t + 1]
                    hidden = slots[slot, inside + t, h]
                    total = r[h, t : t + 1] * g + message[k]
                    reads[2 * t + k] = lane_tiles(hidden * g)
                    writes[2 * t + k] = lane_tiles(total * u)
                    x = total * wt
                    carried = total * (hidden - wt * u)
                    y = carried * slope[k]
                    to_push = x if k == 0 else to_push + x
                    to_step = y if k == 0 else to_step + y
                    acc[k] = acc[k] + carried * plain
                    message[k] = jnp.exp2(d * slope[k]) * total
                pushes.insert(0, to_push)
                steps.insert(0, to_step)
                if len(pushes) == 8:
                    at = pl.ds(pl.multiple_of(base + t, 8), 8)
                    g_push[at, :] = tree(pushes)
                    g_step[at, :] = tree(steps)
                    pushes, steps = [], []
            for j2, quantity in enumerate((writes, reads)):
                x = jnp.concatenate(quantity, axis=0)
                high = x.astype(bf16)
                low = (x - high.astype(f32)).astype(bf16)
                sums = jnp.dot(high, ones, preferred_element_type=f32)
                sums = sums + jnp.dot(low, ones, preferred_element_type=f32)
                kept = jnp.zeros((STATE, 128), f32)
                for t in range(BLK):
                    kept = jnp.where(lane == t, sums[STATE * t : STATE * t + STATE], kept)
                g_sel[b, STATE * j2 : STATE * j2 + STATE] = kept[:, :BLK]
            return message[0], message[1], acc[0], acc[1]

        carry = lax.fori_loop(0, per, block, carry)

        @pl.when(n + 2 < tiles)
        def _():
            fetch(i - 2, slot).start()

        return carry

    zero = jnp.zeros(slope[0].shape, f32)
    done = lax.fori_loop(0, tiles, piece, (message[0], message[1], zero, zero))
    g_rate[:8], g_rate[8:] = done[2], done[3]
    stage.done("g_push", "g_step", "g_sel")
    for c in down:
        c.wait_recv()
    total = gup[z].astype(f32)
    for k in range(1, depth):
        total = total + up_got[k].astype(f32)
    rim = up_own.shape[1]
    for q in range(PLANE):
        up_own[q] = total[q * rim : q * rim + rim].astype(bf16)
    total = gout[z].astype(f32)
    for k in range(1, depth):
        total = total + out_got[k].astype(f32)
    out_own[...] = total
    for c in mine + down:
        c.wait_send()


def adjoint_part(cid, depth, tile, **ins):
    rows, wide = ins["dk"].shape
    gup, gout = ins["gup"], ins["gout"]
    outs = dict(
        g_push=made(rows, wide),
        g_step=made(rows, wide),
        g_sel=made(*ins["sel"].shape),
        g_rate=made(STATE, wide),
        up_own=made(PLANE, gup.shape[1] // PLANE, gup.shape[2], dtype=bf16),
        out_own=made(*gout.shape[1:]),
    )
    scratch = (
        [
            pltpu.VMEM((2, tile, STATE, wide), f32),
            pltpu.VMEM((depth, STATE, wide), f32),
            pltpu.VMEM(gup.shape, bf16),
            pltpu.VMEM(gout.shape, bf16),
        ]
        + [DMA((depth,))] * 2
        + [DMA((2, depth))] * 2
        + [DMA((2,))]
    )
    return staged_call(
        functools.partial(adjoint_kernel, depth), "adjoint_part", cid, 60, ins, outs, scratch,
        late=("sel", "dk", "grad", "gout", "gup", "push"), early=("g_push", "g_step", "g_sel"), away=(), raw=("states",),
    )


def last_kernel(count, *refs):
    ins, outs, held = refs[:count], refs[count : 2 * count], refs[2 * count : 3 * count]
    in_sem, out_sem = refs[3 * count :]
    arriving = [pltpu.make_async_copy(ins[i], held[i], in_sem.at[i]) for i in range(count)]
    for c in arriving:
        c.start()
    leaving = [pltpu.make_async_copy(held[i], outs[i], out_sem.at[i]) for i in range(count)]
    for a, b in zip(arriving, leaving):
        a.wait()
        b.start()
    for c in leaving:
        c.wait()


def last_part(*results):
    count = len(results)
    return pl.pallas_call(
        functools.partial(last_kernel, count),
        out_shape=[jax.ShapeDtypeStruct(r.shape, r.dtype) for r in results],
        in_specs=[ANY] * count,
        out_specs=[ANY] * count,
        scratch_shapes=[pltpu.VMEM(r.shape, r.dtype) for r in results] + [DMA((count,))] * 2,
        compiler_params=params(),
        cost_estimate=cost(5),
        name="last_part",
    )(*results)


def body(
    depth,
    tokens,
    segments,
    routes,
    norm_gain,
    in_proj,
    conv_taps,
    conv_bias,
    select_proj,
    step_proj,
    step_bias,
    decay_log,
    skip_gain,
    out_proj,
    moe_gain,
    router,
    expert_up,
    expert_down,
    cotangent,
):
    count = tokens.shape[0]
    rows = PLANE * count
    rim = norm_gain.shape[0]
    ch = conv_bias.shape[0]
    fs = expert_down.shape[1]
    z, p = here()

    ids = jnp.concatenate([jnp.full((3,), -1, jnp.int32), segments, jnp.full((BLK,), -2, jnp.int32)])
    local_ids = lax.dynamic_slice_in_dim(ids, z * rows, rows + 3 + BLK)
    own_ids = local_ids[3:]
    inside = own_ids >= 0
    same = jnp.stack(
        [(local_ids[k : k + rows + BLK] == own_ids) & inside for k in range(4)], axis=1
    ).astype(f32)
    same = jnp.pad(same, ((0, 0), (0, 124)))
    (
        normed_in,
        w_in,
        w_route,
        small,
        w_sel,
        w_step,
        vecs,
        rate,
        inner,
        gate_in,
        conv,
        signal,
        selected,
        mixes,
        step_pre,
        dk,
        push,
        up_rows,
        down0,
        out_all,
    ) = front_part(
        1,
        depth,
        tok=tokens,
        in_proj=in_proj,
        norm_gain=norm_gain[None],
        moe_gain=moe_gain[None],
        router=router.T,
        expert_up=expert_up.transpose(1, 0, 2),
        select=select_proj,
        step=step_proj,
        decay=decay_log,
        taps=conv_taps,
        bias=conv_bias[None],
        offset=step_bias[None],
        skip=skip_gain[None],
        w_down=expert_down,
        w_out=out_proj,
        same=same,
    )
    scanned, states, ends, up_early, cot_all, down1 = scan_part(
        2, depth, dk, push, mixes, rate, up_rows, cotangent, expert_down
    )
    w_out = out_all.reshape(WIDE, D)
    output, grad_mid, mixed_wide, grad_gate_in, grad_out_w, grad_up, grad_down_own, sums = middle_part(
        3,
        depth,
        scanned=scanned,
        signal=signal,
        gate_in=gate_in,
        skip=vecs,
        w_out=w_out,
        tok=tokens,
        cot_all=cot_all.reshape(rows, D),
        up_early=up_early,
        up_rows=up_rows,
        down0=down0.reshape(HID, D),
        down1=down1.reshape(HID, D),
        w_router=w_route,
        rows_in=small,
        picks=routes.T,
    )
    grad_push, grad_scaled, grad_mixes, grad_rate, grad_up_rows, grad_out_own = adjoint_part(
        4,
        depth,
        count,
        dk=dk,
        push=push,
        grad=mixed_wide,
        sel=mixes,
        states=states,
        rate=rate,
        ends=ends,
        gup=grad_up.reshape(depth, D // depth, EXPERTS * HID),
        gout=grad_out_w.reshape(depth, ch, D),
    )
    (
        grad_tokens,
        grad_in,
        grad_up_own,
        grad_sel,
        grad_step,
        grad_decay,
        grad_taps,
        grad_bias,
        grad_offset,
        grad_skip,
        grad_norm,
        grad_moe,
        grad_router,
    ) = back_part(
        5,
        depth,
        rim,
        ch,
        g_push=grad_push,
        g_step=grad_scaled,
        g_mixes=grad_mixes,
        g_rate=grad_rate,
        step_pre=step_pre,
        signal=signal,
        conv=conv,
        inner=inner,
        same=same,
        vecs=vecs,
        rate=rate,
        selected=selected,
        w_sel=w_sel,
        w_step=w_step,
        mixed_grad=mixed_wide,
        gate_grad=grad_gate_in,
        w_in=w_in,
        normed_in=normed_in,
        tok=tokens,
        gain=small,
        grad_mid=grad_mid,
        sums=sums,
        gup=grad_up_rows,
    )
    (
        output,
        grad_tokens,
        grad_norm,
        grad_in,
        grad_taps,
        grad_bias,
        grad_sel,
        grad_step,
        grad_offset,
        grad_decay,
        grad_skip,
        grad_out_own,
        grad_moe,
        grad_router,
        grad_up_own,
        grad_down_own,
    ) = last_part(
        output,
        grad_tokens,
        grad_norm,
        grad_in,
        grad_taps,
        grad_bias,
        grad_sel,
        grad_step,
        grad_offset,
        grad_decay,
        grad_skip,
        grad_out_own,
        grad_moe,
        grad_router,
        grad_up_own,
        grad_down_own,
    )
    return (
        output,
        grad_tokens,
        grad_norm[0],
        grad_in,
        grad_taps,
        grad_bias[0],
        grad_sel,
        grad_step,
        grad_offset[0],
        grad_decay,
        grad_skip[0],
        grad_out_own,
        grad_moe[0],
        grad_router.T,
        grad_up_own.transpose(1, 0, 2),
        grad_down_own,
    )


def solution(mesh):
    planes = Mesh(mesh.devices.reshape(-1, PLANE), ("z", "p"))
    every = ("z", "p")
    rows, flat, cols, third = P(every, None), P(every), P(None, every), P(None, every, None)
    return jax.shard_map(
        functools.partial(body, planes.shape["z"]),
        mesh=planes,
        in_specs=(
            rows, P(), rows, flat, rows, cols, flat, rows, cols,
            flat, cols, flat, rows, flat, rows, third, third, rows,
        ),
        out_specs=(
            rows, rows, flat, rows, cols, flat, rows, cols,
            flat, cols, flat, rows, flat, rows, third, third,
        ),
        check_vma=False,
    )
```

```python
import functools

import jax
import jax.numpy as jnp
from jax import lax
from jax.experimental import pallas as pl
from jax.experimental.pallas import tpu as pltpu
from jax.sharding import Mesh, PartitionSpec as P

D = 1152
DI = 2304
FF = 3072
RANK = 72
STATE = 16
EXPERTS = 2
CAP = 68
SEL = RANK + 2 * STATE

PLANE = 8
CHIPS = PLANE // 2
WIDE = DI // PLANE
PAD = -WIDE % 128
HID = FF // PLANE
BLK = 16
LOG2E = 1.4426950408889634
GELU = 0.7978845608028654
RESET = 1e5
EARLY, LATE = slice(0, 2), slice(2, PLANE)
epsilon = 1e-05

MESH = pl.DeviceIdType.MESH
ANY = pl.BlockSpec(memory_space=pl.ANY)
VM = pl.BlockSpec(memory_space=pltpu.VMEM)
bf16 = jnp.bfloat16
f32 = jnp.float32
DMA = pltpu.SemaphoreType.DMA


def params(cid=None, grid=None):
    extra = {} if cid is None else {"collective_id": cid, "has_side_effects": True}
    if grid is not None:
        extra["dimension_semantics"] = grid
    return pltpu.CompilerParams(vmem_limit_bytes=60 * 1024 * 1024, **extra)


def cost(us):
    return pl.CostEstimate(flops=int(us * 1e9), bytes_accessed=int(us * 3e6), transcendentals=0)


def mm(left, right):
    return jnp.dot(left, right, preferred_element_type=f32)


def contract_rows(left, right):
    return lax.dot_general(left, right, (((0,), (0,)), ((), ())), preferred_element_type=f32)


def contract_cols(left, right):
    return lax.dot_general(left, right, (((1,), (1,)), ((), ())), preferred_element_type=f32)


class Stage:
    def __init__(self, fetches, flushes):
        self.fetches, self.flushes, self.going = fetches, flushes, []
        for copy in fetches.values():
            copy.start()

    def need(self, *names):
        for name in names:
            self.fetches.pop(name).wait()

    def done(self, *names):
        for name in names:
            self.flushes[name].start()
            self.going.append(self.flushes[name])

    def end(self):
        self.need(*tuple(self.fetches))
        for copy in self.going:
            copy.wait()


def staged_call(kernel, name, cid, us, ins, outs, scratch, late=(), early=(), away=(), raw=()):
    inside = [n for n in outs if n not in away]
    early = [n for n in inside if n in early]

    def body(*refs):
        refs = list(refs)
        take = lambda names: dict(zip(names, [refs.pop(0) for _ in names]))
        source, target = take(ins), take(outs)
        buffers, results = take(late), take(early)
        in_sem, out_sem = refs.pop(0), refs.pop(0)
        stage = Stage(
            {n: pltpu.make_async_copy(source[n], buffers[n], in_sem.at[i]) for i, n in enumerate(late)},
            {n: pltpu.make_async_copy(results[n], target[n], out_sem.at[i]) for i, n in enumerate(early)},
        )
        kernel(
            stage,
            *[buffers.get(n, source[n]) for n in ins],
            *[results.get(n, target[n]) for n in outs],
            *refs,
        )
        stage.end()

    return pl.pallas_call(
        body,
        out_shape=list(outs.values()),
        in_specs=[ANY if n in late or n in raw else VM for n in ins],
        out_specs=[ANY if n in early or n in away else VM for n in outs],
        scratch_shapes=[pltpu.VMEM(ins[n].shape, ins[n].dtype) for n in late]
        + [pltpu.VMEM(outs[n].shape, outs[n].dtype) for n in early]
        + [DMA((max(len(late), 1),)), DMA((max(len(early), 1),))]
        + scratch,
        compiler_params=params(cid),
        cost_estimate=cost(us),
        name=name,
    )(*ins.values())


def made(*shape, dtype=None):
    return jax.ShapeDtypeStruct(shape, dtype or f32)


def remote(src, dst, ss, rs, to):
    return pltpu.make_async_remote_copy(
        src_ref=src, dst_ref=dst, send_sem=ss, recv_sem=rs, device_id=to, device_id_type=MESH
    )


def send(src, dst, ss, rs, to):
    copy = remote(src, dst, ss, rs, to)
    copy.start()
    return copy


def here():
    return lax.axis_index("z"), lax.axis_index("p")


def greet(plane=True, depth=0):
    z, p = here()
    barrier = pltpu.get_barrier_semaphore()
    count = 0
    if plane:
        for k in range(1, PLANE):
            pl.semaphore_signal(
                barrier, inc=1, device_id=(z, lax.rem(p + k, PLANE)), device_id_type=MESH
            )
            count += 1
    for k in range(1, depth):
        pl.semaphore_signal(barrier, inc=1, device_id=(lax.rem(z + k, depth), p), device_id_type=MESH)
        count += 1
    pl.semaphore_wait(barrier, count)


def share_start(x, out, ss, rs):
    z, p = here()
    core = lax.rem(p, 2)
    copies = [send(x, out.at[p], ss.at[0], rs.at[0], (z, p + 1 - 2 * core))]
    for k in range(1, CHIPS):
        copies.append(send(x, out.at[p], ss.at[k], rs.at[k], (z, lax.rem(p + 2 * k, PLANE))))
    return copies


def share_forward(out, copies, ss, rs):
    z, p = here()
    core = lax.rem(p, 2)
    onward = []
    for k in range(1, CHIPS):
        copies[k].wait_recv()
        src = lax.rem(p + PLANE - 2 * k, PLANE)
        onward.append(
            send(out.at[src], out.at[src], ss.at[CHIPS + k], rs.at[CHIPS + k], (z, p + 1 - 2 * core))
        )
    return onward


def share_finish(copies, onward):
    copies[0].wait_recv()
    for c in copies:
        c.wait_send()
    for c in onward:
        c.wait()


def column_copy(src, out, ss, rs, frm, to, part=None):
    dst = out.at[frm] if part is None else out.at[frm, part]
    return pltpu.make_async_remote_copy(
        src_ref=dst if src is None else src,
        dst_ref=dst,
        send_sem=ss.at[to],
        recv_sem=rs.at[frm],
        device_id=(to, lax.axis_index("p")),
        device_id_type=MESH,
    )


def column_each(depth, act):
    z = lax.axis_index("z")
    for t in range(depth):
        far = abs(t - z) == depth - 1 if depth == 4 else t == z
        pl.when(jnp.logical_not((t == z) | far))(functools.partial(act, t))


def column_start(depth, src, out, ss, rs, part=None):
    z = lax.axis_index("z")
    column_each(depth, lambda t: column_copy(src, out, ss, rs, z, t, part).start())


def column_forward(depth, out, ss, rs, part=None):
    if depth != 4:
        return
    z = lax.axis_index("z")
    for me, frm, to in ((2, 0, 3), (1, 3, 0)):

        @pl.when(z == me)
        def _():
            copy = column_copy(None, out, ss, rs, frm, to, part)
            copy.wait_recv()
            copy.start()


def column_finish(depth, src, out, ss, rs, part=None):
    z = lax.axis_index("z")
    for s in range(depth):
        ahead = ((z == 2) & (s == 0)) | ((z == 1) & (s == 3)) if depth == 4 else s == z

        @pl.when(jnp.logical_not((s == z) | ahead))
        def _():
            column_copy(src, out, ss, rs, s, s, part).wait_recv()

    column_each(depth, lambda t: column_copy(src, out, ss, rs, z, t, part).wait_send())
    if depth == 4:
        for me, frm, to in ((2, 0, 3), (1, 3, 0)):

            @pl.when(z == me)
            def _():
                column_copy(None, out, ss, rs, frm, to, part).wait_send()


def softplus(x):
    return jnp.maximum(x, 0.0) + jnp.log1p(jnp.exp(-jnp.abs(x)))


def total_start(x, got, ss, rs):
    z, p = here()
    copies = []
    for k in range(1, PLANE):
        q = lax.rem(p + k, PLANE)
        copies.append(send(x.at[q], got.at[k], ss.at[k], rs.at[k], (z, q)))
    return copies


def total_share(x, got, copies, out, ts, us):
    z, p = here()
    total = x[p]
    for k in range(1, PLANE):
        copies[k - 1].wait_recv()
        total = total + got[k]
    out[p] = total.astype(bf16)
    after = [
        send(out.at[p], out.at[p], ts.at[k], us.at[k], (z, lax.rem(p + k, PLANE))) for k in range(1, PLANE)
    ]
    for c in copies:
        c.wait_send()
    return after


def front_kernel(
    depth, stage,
    tok, in_proj, norm_gain, moe_gain, router, expert_up, select, step, decay, taps, bias, offset, skip,
    w_down, w_out, same,
    normed_in, w_in, w_route, small, w_sel, w_step, vecs, rate, inner, gate_in, conv, signal, selected, mixes,
    step_pre, dk, push, up_rows, down_all, out_all,
    tok_all, win_all, pack_all, wide, thin, near, halo, x, got, sel_all, win, wup, pack, square,
    gs, gr, ws, wr, vs, vr, zs, zr, hs, ss, rs, ts, us, ls,
):
    z, p = here()
    count = tok.shape[0]
    rim = in_proj.shape[0]
    ch = select.shape[0]
    pair = 2 * count
    rows = PLANE * count
    fs = expert_up.shape[2] // (depth * PLANE)
    local = [
        pltpu.make_async_copy(tok, tok_all.at[p], ls.at[0]),
        pltpu.make_async_copy(win.at[p], win_all.at[z, p], ls.at[1]),
        pltpu.make_async_copy(wup.at[p], up_rows.at[p], ls.at[2]),
        pltpu.make_async_copy(pack, pack_all.at[z], ls.at[3]),
        pltpu.make_async_copy(w_down.at[0], down_all.at[z], ls.at[4]),
        pltpu.make_async_copy(w_out, out_all.at[z], ls.at[5]),
    ]
    for i in (0, 4, 5):
        local[i].start()
    square[...] = jnp.zeros_like(square)
    square[0:1, :rim] = norm_gain[...].astype(f32)
    square[1:2, :rim] = moe_gain[...].astype(f32)
    square[2:4, :rim] = router[...].astype(f32)
    columns = square[...].T
    square[...] = columns
    for q in range(PLANE):
        for i in range(2 * depth):
            start = (i // depth) * DI + ((i % depth) * PLANE + q) * ch
            win[q, :, i * ch : i * ch + ch] = in_proj[:, start : start + ch]
        win[q, :, 2 * WIDE :] = square[:rim, :64].astype(bf16)
    local[1].start()
    greet(True, depth)
    across = []
    for k in range(1, PLANE):
        q = lax.rem(p + k, PLANE)
        across.append(send(win.at[q], win_all.at[z, p], ws.at[k], wr.at[k], (z, q)))
    first = share_start(tok, tok_all, gs, gr)
    square[...] = jnp.zeros_like(square)
    square[0:STATE, :ch] = decay[...].astype(f32)
    square[STATE : STATE + 4, :ch] = taps[...].astype(f32)
    for i, ref in enumerate((bias, offset, skip)):
        square[STATE + 4 + i : STATE + 5 + i, :ch] = ref[...].astype(f32)
    columns = square[...].T
    pack[:, 256:] = columns[:ch].astype(bf16)
    square[...] = jnp.zeros_like(square)
    square[:RANK, :ch] = step[...].astype(f32)
    columns = square[...].T
    pack[:, 128:256] = columns[:ch].astype(bf16)
    pack[:, :128] = jnp.zeros((ch, 128), bf16)
    pack[:, :SEL] = select[...]
    column_start(depth, pack, pack_all, zs.at[0], zr.at[0])
    local[3].start()
    for q in range(PLANE):
        for i in range(EXPERTS * depth):
            start = ((i % depth) * PLANE + q) * fs
            wup[q, :, i * fs : i * fs + fs] = expert_up[:, i // depth, start : start + fs]
    local[2].start()
    local[1].wait()
    for c in across:
        c.wait_recv()
    column_start(depth, win_all.at[z], win_all, zs.at[1], zr.at[1])
    second = share_forward(tok_all, first, gs, gr)
    more = []
    for k in range(1, PLANE):
        q = lax.rem(p + k, PLANE)
        more.append(send(wup.at[q], up_rows.at[p], vs.at[k], vr.at[k], (z, q)))
    local[3].wait()
    column_forward(depth, pack_all, zs.at[0], zr.at[0])
    column_finish(depth, pack, pack_all, zs.at[0], zr.at[0])
    for k in range(depth):
        thin[k * ch : k * ch + ch, :] = pack_all[k].astype(f32)
    w_sel[...] = thin[:, :128].astype(bf16)
    w_step[...] = thin[:, 128:256].astype(bf16)
    side = thin[:, 256:].T
    rate[:, :WIDE] = -jnp.exp(side[:STATE])
    rate[:, WIDE:] = jnp.zeros((STATE, PAD), f32)
    vecs[...] = side[STATE : STATE + 8]
    column_forward(depth, win_all, zs.at[1], zr.at[1])
    local[0].wait()
    share_finish(first, second)
    column_finish(depth, win_all.at[z], win_all, zs.at[1], zr.at[1])
    for k in range(depth):
        for q in range(PLANE):
            at = (k * PLANE + q) * rim
            wide[at : at + rim, :] = win_all[k, q].astype(f32)
    w_in[...] = wide[:, : 2 * WIDE].astype(bf16)
    w_route[...] = wide[:, 512:].astype(bf16)
    small[...] = wide[:, 512:].T[64:72]
    gain = small[0:1]
    for b in (3, 0, 1, 2):
        at = slice(pair * b, pair * b + pair)
        values = tok_all[2 * b : 2 * b + 2].reshape(pair, D).astype(f32)
        scale = lax.rsqrt(jnp.mean(values * values, axis=-1, keepdims=True) + epsilon)
        normed = (values * scale * gain).astype(bf16)
        normed_in[at, :] = normed
        joined = mm(normed, w_in[...]).astype(bf16)
        near[BLK + pair * b : BLK + pair * b + pair, :] = joined[:, :WIDE].astype(f32)
        gate_in[at, :] = joined[:, WIDE:]
        if b == 3:
            edge = send(near.at[pl.ds(rows, BLK)], halo, hs.at[0], hs.at[1], (lax.rem(z + 1, depth), p))
            column_start(depth, w_out, out_all, zs.at[2], zr.at[2])
            column_start(depth, w_down.at[0], down_all, zs.at[3], zr.at[3])
    stage.done("w_in", "normed_in", "gate_in")
    stage.need("same")
    for b in (1, 2, 3, 0):
        if b == 0:
            edge.wait()
            near[:BLK, :] = halo[...]
        base = pair * b
        at = slice(base, base + pair)
        total = vecs[4:5] + vecs[0:1] * near[base + 13 : base + 13 + pair, :] * same[at, 0:1]
        for k in range(1, 4):
            total = total + vecs[k : k + 1] * near[base + 13 + k : base + 13 + k + pair, :] * same[at, k : k + 1]
        conv[at, :] = total
        value = (total * jax.nn.sigmoid(total)).astype(bf16)
        signal[at, :] = value
        x[2 * b : 2 * b + 2] = mm(value, w_sel[...]).reshape(2, count, 128)
    third = total_start(x, got, ss, rs)
    inner[...] = near[...].astype(bf16)
    stage.done("conv", "signal", "inner")
    fourth = total_share(x, got, third, sel_all, ts, us)
    local[5].wait()
    column_forward(depth, out_all, zs.at[2], zr.at[2])
    for c in fourth:
        c.wait()
    for b in range(CHIPS):
        at = slice(pair * b, pair * b + pair)
        chosen = sel_all[2 * b : 2 * b + 2].reshape(pair, 128)
        selected[at, :] = chosen
        step = contract_cols(chosen, w_step[...]) + vecs[5:6]
        step_pre[at, :] = step
        delta = softplus(step)
        dk[at, :WIDE] = delta + (1.0 - same[at, 2:3]) * RESET
        push[at, :WIDE] = delta * signal[at, :].astype(f32)
        dk[at, WIDE:] = jnp.zeros((pair, PAD), f32)
        push[at, WIDE:] = jnp.zeros((pair, PAD), f32)
        full = chosen.astype(f32)
        for i in range(pair // BLK):
            flipped = full[i * BLK : i * BLK + BLK].T
            mixes[b * (pair // BLK) + i] = flipped[RANK:SEL]
    stage.done("dk", "push", "step_pre", "mixes", "selected")
    local[2].wait()
    for c in across:
        c.wait_send()
    for c in more:
        c.wait()

    def onward():
        local[4].wait()
        column_forward(depth, down_all, zs.at[3], zr.at[3])

    def finish():
        column_finish(depth, w_out, out_all, zs.at[2], zr.at[2])
        column_finish(depth, w_down.at[0], down_all, zs.at[3], zr.at[3])

    return onward, finish


def front_part(cid, depth, **ins):
    count, rim, ch = ins["tok"].shape[0], ins["in_proj"].shape[0], ins["select"].shape[0]
    low = ins["w_down"].shape[1]
    rows = PLANE * count
    outs = dict(
        normed_in=made(rows, D, dtype=bf16),
        w_in=made(D, 2 * WIDE, dtype=bf16),
        w_route=made(D, 128, dtype=bf16),
        small=made(8, D),
        w_sel=made(WIDE, 128, dtype=bf16),
        w_step=made(WIDE, 128, dtype=bf16),
        vecs=made(8, WIDE),
        rate=made(STATE, WIDE + PAD),
        inner=made(rows + BLK, WIDE, dtype=bf16),
        gate_in=made(rows, WIDE, dtype=bf16),
        conv=made(rows, WIDE),
        signal=made(rows, WIDE, dtype=bf16),
        selected=made(rows, 128, dtype=bf16),
        mixes=made(rows // BLK, 2 * STATE, BLK),
        step_pre=made(rows, WIDE),
        dk=made(rows, WIDE + PAD),
        push=made(rows, WIDE + PAD),
        up_rows=made(PLANE, rim, EXPERTS * HID, dtype=bf16),
        down_all=made(depth, low, D, dtype=bf16),
        out_all=made(depth, ch, D, dtype=bf16),
    )
    scratch = (
        [
            pltpu.VMEM((PLANE, count, D), bf16),
            pltpu.VMEM((depth, PLANE, rim, 640), bf16),
            pltpu.VMEM((depth, ch, 384), bf16),
            pltpu.VMEM((D, 640), f32),
            pltpu.VMEM((WIDE, 384), f32),
            pltpu.VMEM((BLK + rows, WIDE), f32),
            pltpu.VMEM((BLK, WIDE), f32),
            pltpu.VMEM((PLANE, count, 128), f32),
            pltpu.VMEM((PLANE, count, 128), f32),
            pltpu.VMEM((PLANE, count, 128), bf16),
            pltpu.VMEM((PLANE, rim, 640), bf16),
            pltpu.VMEM((PLANE, rim, EXPERTS * HID), bf16),
            pltpu.VMEM((ch, 384), bf16),
            pltpu.VMEM((128, 128), f32),
        ]
        + [DMA((PLANE,))] * 6
        + [DMA((4, depth))] * 2
        + [DMA((2,))]
        + [DMA((PLANE,))] * 4
        + [DMA((6,))]
    )
    early = (
        "normed_in", "w_in", "inner", "gate_in", "conv", "signal", "selected", "mixes", "step_pre", "dk", "push",
    )
    up_rows, cot = outs["up_rows"], ins["cot"]
    outs.update(
        scanned=made(rows, WIDE + PAD),
        states=made(rows, STATE, WIDE + PAD),
        ends=made(depth, STATE + 8, WIDE + PAD),
        up_early=made(depth, EARLY.stop, *up_rows.shape[1:], dtype=bf16),
        cot_all=made(PLANE, *cot.shape, dtype=bf16),
        down1=made(depth, low, D, dtype=bf16),
    )
    mine = len(scratch)
    scratch = (
        scratch
        + [pltpu.VMEM((2, count, STATE, WIDE + PAD), f32)]
        + [DMA((PLANE,))] * 2
        + [DMA((depth,))] * 2
        + [DMA((2, depth))] * 2
        + [DMA((2,)), DMA((3,))]
    )
    names = tuple(ins) + tuple(outs)

    def kernel(stage, *refs):
        ref = dict(zip(names, refs))
        held = refs[len(names) :]
        first = [ref[n] for n in names if n != "cot"][: len(ins) - 1 + 20]
        onward, finish = front_kernel(depth, stage, *first, *held[:mine])
        scan_kernel(
            depth,
            stage,
            onward,
            *(ref[n] for n in ("dk", "push", "mixes", "rate", "up_rows", "cot", "w_down")),
            *(ref[n] for n in ("scanned", "states", "ends", "up_early", "cot_all", "down1")),
            *held[mine:],
        )
        finish()

    return staged_call(
        kernel, "front_part", cid, 110, ins, outs, scratch,
        late=("same", "cot"), early=early + ("scanned",),
        away=("down_all", "out_all", "states", "up_early", "cot_all", "down1"),
    )


def folded(x):
    half = x.shape[0] // 2
    return jnp.concatenate([x[:half], x[half:]], axis=1).astype(bf16)


def back_kernel(
    depth, stage,
    g_push, g_step, g_mixes, g_rate, step_pre, signal, conv, inner, same, vecs, rate, selected, w_sel, w_step,
    mixed_grad, gate_grad, w_in, normed_in, tok, gain, grad_mid, sums, gup,
    tokens_out, in_own, up_own, sel_own, step_own, decay_own, taps_own, bias_own, offset_own, skip_own,
    norm_own, moe_own, router_own,
    in_out, up_out, pack_out, x, got, gsel, low, gc, halo, nearf, gj, part, sib, mix, far, gin, gin_got, own, pack, pack_got, row, row_got, sml, sml_got,
    hs, ss, rs, ts, us, near_s, near_r, away_s, away_r, zs, zr, cs, cr, ups, upr, ls,
):
    z, p = here()
    core = lax.rem(p, 2)
    chip = lax.div(p, 2)
    twin = (z, p + 1 - 2 * core)
    count = tok.shape[0]
    pair = 2 * count
    rows = PLANE * count
    ch = sel_own.shape[0]
    rim = in_own.shape[0]
    fs = up_own.shape[2] // (depth * PLANE)
    sent = []

    def down(i, src, dst):
        copies = []
        for k in range(1, depth):
            q = lax.rem(z + k, depth)
            copies.append(send(src.at[q], dst.at[k], zs.at[i, k], zr.at[i, k], (q, p)))
        return copies

    block = D // depth
    stage.need("normed_in", "gate_grad")
    for q in range(depth):
        gin[1, q] = folded(contract_rows(normed_in[:, q * block : q * block + block], gate_grad[...]))
    gate_sent = down(3, gin.at[1], gin_got.at[1])
    stage.need("w_step", "signal", "step_pre")
    bias = jnp.zeros((1, WIDE), f32)
    for b in range(CHIPS):
        at = slice(pair * b, pair * b + pair)
        value = signal[at, :].astype(f32)
        grad = g_step[at, :WIDE] * (1.0 / LOG2E) + g_push[at, :WIDE] * value
        grad = grad * jax.nn.sigmoid(step_pre[at, :])
        bias = bias + jnp.sum(grad, axis=0, keepdims=True)
        low[at, :] = grad.astype(bf16)
        ranks = mm(low[at, :], w_step[...])
        for i in range(pair // BLK):
            mixed = g_mixes[b * (pair // BLK) + i]
            wide = jnp.concatenate(
                [jnp.zeros((RANK, BLK), f32), mixed, jnp.zeros((128 - SEL, BLK), f32)], axis=0
            ).T
            t = i * BLK
            x[2 * b + t // count, t % count : t % count + BLK, :] = ranks[t : t + BLK] + wide
    first = total_start(x, got, ss, rs)
    stage.need("selected", "inner")
    keep = pltpu.make_async_copy(gup.at[p], up_out.at[p], ls)
    keep.start()
    grad_step_w = contract_rows(low[...], selected[...])
    nearf[...] = inner[...].astype(f32)
    second = total_share(x, got, first, gsel, ts, us)
    ups_sent = []
    for k in range(1, PLANE):
        q = lax.rem(p + k, PLANE)
        ups_sent.append(send(gup.at[q], up_out.at[p], ups.at[k], upr.at[k], (z, q)))
    for c in second:
        c.wait()
    stage.need("conv", "same", "w_sel")
    taps = [jnp.zeros((1, WIDE), f32)] * 4
    conv_bias = jnp.zeros((1, WIDE), f32)
    for b in range(CHIPS):
        base = pair * b
        at = slice(base, base + pair)
        delta = softplus(step_pre[at, :])
        grad = mixed_grad[at, :WIDE] * vecs[6:7] + g_push[at, :WIDE] * delta
        grad = grad + contract_cols(gsel[2 * b : 2 * b + 2].reshape(pair, 128), w_sel[...])
        c = conv[at, :]
        sig = jax.nn.sigmoid(c)
        grad = grad * (sig * (1.0 + c * (1.0 - sig)))
        gc[at, :] = grad
        if b == 0:
            edge = send(gc.at[pl.ds(0, BLK)], halo, hs.at[0], hs.at[1], (lax.rem(z + depth - 1, depth), p))
        conv_bias = conv_bias + jnp.sum(grad, axis=0, keepdims=True)
        for k in range(4):
            taps[k] = taps[k] + jnp.sum(
                grad * nearf[base + 13 + k : base + 13 + k + pair, :] * same[at, k : k + 1], axis=0, keepdims=True
            )
    stage.need("w_in", "tok", "grad_mid")
    for b in range(CHIPS):
        base = pair * b
        if b == CHIPS - 1:
            edge.wait()
            gc[rows : rows + BLK, :] = halo[...]
        total = jnp.zeros((pair, WIDE), f32)
        for k in range(4):
            off = slice(base + 3 - k, base + 3 - k + pair)
            total = total + gc[off, :] * vecs[k : k + 1] * same[off, k : k + 1]
        gj[base : base + pair, :WIDE] = total.astype(bf16)
        gj[base : base + pair, WIDE:] = gate_grad[base : base + pair, :]
    for q in range(depth):
        gin[0, q] = folded(contract_rows(normed_in[:, q * block : q * block + block], gj[:, :WIDE]))
    in_sent = down(0, gin.at[0], gin_got.at[0])
    near = {}
    for k in (1, 2, 3, 0):
        q = lax.rem(chip + k, CHIPS)
        at = pl.ds(pl.multiple_of(q * pair, pair), pair)
        part[k] = contract_cols(gj[at, :], w_in[...]).astype(bf16).reshape(2, count, D)
        near[k] = send(part.at[k, 1 - core], sib.at[k], near_s.at[k], near_r.at[k], twin)
    away = []
    for k in range(1, CHIPS):
        near[k].wait_recv()
        mix[k] = (part[k, core].astype(f32) + sib[k].astype(f32)).astype(bf16)
        away.append(
            send(mix.at[k], far.at[k], away_s.at[k], away_r.at[k], (z, lax.rem(p + 2 * k, PLANE)))
        )
    row[...] = jnp.zeros_like(row)
    row[0:STATE, :] = g_rate[...] * rate[...]
    for k in range(4):
        row[STATE + k : STATE + k + 1, :WIDE] = taps[k]
    row[STATE + 4 : STATE + 5, :WIDE] = conv_bias
    row[STATE + 5 : STATE + 6, :WIDE] = bias
    row[STATE + 6 : STATE + 7, :WIDE] = sums[3:4, :WIDE]
    side = row[...].T
    grad_sel_w = contract_rows(signal[...], gsel[...].reshape(rows, 128))
    for q in range(depth):
        cut = slice(q * ch, q * ch + ch)
        pack[q, :, :128] = grad_sel_w[cut].astype(bf16)
        pack[q, :, 128:256] = grad_step_w[cut].astype(bf16)
        pack[q, :, 256:] = side[cut].astype(bf16)
    pack_sent = down(1, pack, pack_got)
    near[0].wait_recv()
    total = part[0, core].astype(f32) + sib[0].astype(f32)
    for k in range(1, CHIPS):
        away[k - 1].wait_recv()
        total = total + far[k].astype(f32)
    values = tok[...].astype(f32)
    scale = lax.rsqrt(jnp.mean(values * values, axis=-1, keepdims=True) + epsilon)
    normed = values * scale
    grad_normed = total * gain[0:1]
    mean = jnp.mean(grad_normed * normed, axis=-1, keepdims=True)
    tokens_out[...] = (scale * (grad_normed - normed * mean) + grad_mid[...]).astype(bf16)
    stage.done("tokens_out")
    ours = jnp.concatenate(
        [jnp.sum(total * normed, axis=0, keepdims=True), sums[0:3, :], jnp.zeros((4, D), f32)], axis=0
    )
    for q in range(depth):
        sml[q] = ours[:, q * block : q * block + block]
    sml_sent = down(2, sml, sml_got)
    for h, copies in ((1, gate_sent), (0, in_sent)):
        for c in copies:
            c.wait_recv()
        total = gin[h, z].astype(f32)
        for k in range(1, depth):
            total = total + gin_got[h, k].astype(f32)
        total = jnp.concatenate([total[:, :WIDE], total[:, WIDE:]], axis=0)
        for q in range(PLANE):
            own[q, :, h * WIDE : h * WIDE + WIDE] = total[q * rim : q * rim + rim].astype(bf16)
    across = []
    for k in range(1, PLANE):
        q = lax.rem(p + k, PLANE)
        across.append(send(own.at[q], in_out.at[p], cs.at[0, k], cr.at[0, k], (z, q)))
    in_out[p] = own[p]
    for c in sml_sent:
        c.wait_recv()
    total = sml[z]
    for k in range(1, depth):
        total = total + sml_got[k]
    sml_got[0] = total
    for k in range(1, PLANE):
        q = lax.rem(p + k, PLANE)
        across.append(send(sml_got.at[0], row_got.at[k], cs.at[1, k], cr.at[1, k], (z, q)))
    for c in pack_sent:
        c.wait_recv()
    total = pack[z].astype(f32)
    for k in range(1, depth):
        total = total + pack_got[k].astype(f32)
    sel_own[...] = total[:, :SEL]
    pack_out[...] = jnp.zeros_like(pack_out)
    pack_out[:ch, :] = total[:, 128:256]
    columns = pack_out[...].T
    step_own[...] = columns[:RANK, :ch]
    pack_out[:ch, :32] = total[:, 256:]
    columns = pack_out[...].T
    decay_own[...] = columns[:STATE, :ch]
    taps_own[...] = columns[STATE : STATE + 4, :ch]
    bias_own[...] = columns[STATE + 4 : STATE + 5, :ch]
    offset_own[...] = columns[STATE + 5 : STATE + 6, :ch]
    skip_own[...] = columns[STATE + 6 : STATE + 7, :ch]
    for c in ups_sent:
        c.wait()
    keep.wait()
    for q in range(PLANE):
        for i in range(EXPERTS * depth):
            start = ((i % depth) * PLANE + q) * fs
            up_own[:, i // depth, start : start + fs] = up_out[q, :, i * fs : i * fs + fs].astype(f32)
    stage.done("up_own")
    for c in across:
        c.wait()
    for q in range(PLANE):
        for i in range(2 * depth):
            start = (i // depth) * DI + ((i % depth) * PLANE + q) * ch
            in_own[:, start : start + ch] = in_out[q, :, i * ch : i * ch + ch].astype(f32)
    total = sml_got[0]
    for k in range(1, PLANE):
        total = total + row_got[k]
    for q in range(PLANE):

        @pl.when(p == q)
        def _():
            cut = total[:, q * rim : q * rim + rim]
            norm_own[...] = cut[0:1]
            moe_own[...] = cut[1:2]
            router_own[...] = cut[2:4]

    for c in list(near.values()) + away + gate_sent + in_sent + pack_sent + sml_sent:
        c.wait_send()


def back_part(cid, depth, rim, ch, **ins):
    count = ins["tok"].shape[0]
    rows, wide = ins["dk"].shape
    block = D // depth
    gup, gout = ins["gup"], ins["gout"]
    outs = dict(
        tokens_out=made(count, D, dtype=bf16),
        in_own=made(rim, 2 * DI),
        up_own=made(rim, EXPERTS, FF),
        sel_own=made(ch, SEL),
        step_own=made(RANK, ch),
        decay_own=made(STATE, ch),
        taps_own=made(4, ch),
        bias_own=made(1, ch),
        offset_own=made(1, ch),
        skip_own=made(1, ch),
        norm_own=made(1, rim),
        moe_own=made(1, rim),
        router_own=made(2, rim),
        out_own=made(*gout.shape[1:]),
    )
    scratch = (
        [
            pltpu.VMEM((PLANE, rim, 2 * WIDE), bf16),
            pltpu.VMEM((PLANE, rim, EXPERTS * HID), bf16),
            pltpu.VMEM((128, 128), f32),
            pltpu.VMEM((PLANE, count, 128), f32),
            pltpu.VMEM((PLANE, count, 128), f32),
            pltpu.VMEM((PLANE, count, 128), bf16),
            pltpu.VMEM((rows, WIDE), bf16),
            pltpu.VMEM((rows + BLK, WIDE), f32),
            pltpu.VMEM((BLK, WIDE), f32),
            pltpu.VMEM((rows + BLK, WIDE), f32),
            pltpu.VMEM((rows, 2 * WIDE), bf16),
            pltpu.VMEM((CHIPS, 2, count, D), bf16),
            pltpu.VMEM((CHIPS, count, D), bf16),
            pltpu.VMEM((CHIPS, count, D), bf16),
            pltpu.VMEM((CHIPS, count, D), bf16),
            pltpu.VMEM((2, depth, block // 2, 2 * WIDE), bf16),
            pltpu.VMEM((2, depth, block // 2, 2 * WIDE), bf16),
            pltpu.VMEM((PLANE, rim, 2 * WIDE), bf16),
            pltpu.VMEM((depth, ch, 288), bf16),
            pltpu.VMEM((depth, ch, 288), bf16),
            pltpu.VMEM((2 * STATE, WIDE + PAD), f32),
            pltpu.VMEM((PLANE, 8, block), f32),
            pltpu.VMEM((depth, 8, block), f32),
            pltpu.VMEM((depth, 8, block), f32),
            DMA((2,)),
        ]
        + [DMA((PLANE,))] * 4
        + [DMA((CHIPS,))] * 4
        + [DMA((4, depth))] * 2
        + [DMA((2, PLANE))] * 2
        + [DMA((PLANE,))] * 2
        + [DMA]
    )
    mine = len(scratch)
    scratch = (
        scratch
        + [
            pltpu.VMEM((2, count, STATE, wide), f32),
            pltpu.VMEM((depth, STATE, wide), f32),
            pltpu.VMEM(gup.shape, bf16),
            pltpu.VMEM(gout.shape, bf16),
        ]
        + [DMA((depth,))] * 2
        + [DMA((3, depth))] * 2
        + [DMA((2,))]
        + [
            pltpu.VMEM((rows, wide), f32),
            pltpu.VMEM((rows, wide), f32),
            pltpu.VMEM(ins["sel"].shape, f32),
            pltpu.VMEM((STATE, wide), f32),
            pltpu.VMEM((PLANE, rim, EXPERTS * HID), bf16),
        ]
    )
    names = tuple(ins) + tuple(outs)

    def kernel(stage, *refs):
        ref = dict(zip(names, refs))
        held = refs[len(names) :]
        g_push, g_step, g_sel, g_rate, up_part = held[-5:]
        finish = adjoint_kernel(
            depth,
            stage,
            lambda: None,
            *(ref[n] for n in ("dk", "push", "grad", "sel", "states", "rate", "ends", "gup", "gout")),
            g_push,
            g_step,
            g_sel,
            g_rate,
            up_part,
            ref["out_own"],
            *held[mine:-5],
        )
        back_kernel(
            depth,
            stage,
            g_push,
            g_step,
            g_sel,
            g_rate,
            *(
                ref[n]
                for n in (
                    "step_pre", "signal", "conv", "inner", "same", "vecs", "rate", "selected", "w_sel", "w_step",
                    "grad", "gate_grad", "w_in", "normed_in", "tok", "gain", "grad_mid", "sums",
                )
            ),
            up_part,
            *(ref[n] for n in outs if n != "out_own"),
            *held[:mine],
        )
        finish()

    late = (
        "gup", "sel", "dk", "grad", "push", "gout", "normed_in", "gate_grad", "w_step", "signal", "step_pre",
        "selected", "inner", "conv", "same", "w_sel", "w_in", "tok", "grad_mid",
    )
    return staged_call(
        kernel, "back_part", cid, 120, ins, outs, scratch,
        late=late, early=("tokens_out", "up_own"), raw=("states",),
    )


def middle_kernel(
    depth, stage,
    scanned, signal, gate_in, skip, w_out, tok, cot_all, up_early, up_rows, down0, down1, w_router, rows_in, picks,
    output, grad_mid, mixed_grad, gate_grad, grad_out, grad_up, down_own, sums,
    gated, part, sib, mix, far, routed_all, marks_all, hidden_all, pre_all, slot_all, back_all,
    up_late, w_up, wide, grad_down, down_got,
    near_s, near_r, away_s, away_r, gs, gr, zs, zr, ds, dr, ls,
):
    z, p = here()
    core = lax.rem(p, 2)
    chip = lax.div(p, 2)
    twin = (z, p + 1 - 2 * core)
    count = tok.shape[0]
    pair = 2 * count

    def chip_at(k):
        return lax.rem(chip + k, CHIPS)

    def rows_of(q):
        return pl.ds(pl.multiple_of(q * pair, pair), pair)

    def near(i, k):
        return remote(part.at[i, k, 1 - core], sib.at[i, k], near_s.at[i, k], near_r.at[i, k], twin)

    def away(i, k):
        return remote(
            mix.at[i, k], far.at[i, k], away_s.at[i, k], away_r.at[i, k], (z, lax.rem(p + 2 * k, PLANE))
        )

    def pass_away(i, k):
        near(i, k).wait_recv()
        mix[i, k] = (part[i, k, core].astype(f32) + sib[i, k].astype(f32)).astype(bf16)
        away(i, k).start()

    def gathered(i):
        near(i, 0).wait_recv()
        total = part[i, 0, core].astype(f32) + sib[i, 0].astype(f32)
        for k in range(1, CHIPS):
            away(i, k).wait_recv()
            total = total + far[i, k].astype(f32)
        return total

    def shared(i, ref, k):
        return remote(ref.at[p], ref.at[p], gs.at[i, k], gr.at[i, k], (z, lax.rem(p + 2 * k, PLANE)))

    def onward(i, ref, k):
        src = lax.rem(p + 2 * k, PLANE)
        return remote(ref.at[src], ref.at[src], gs.at[i, CHIPS + k], gr.at[i, CHIPS + k], twin)

    def arrived(k, refs):
        @pl.when(k == 0)
        def _():
            for i, ref in refs:
                remote(ref.at[p], ref.at[p], gs.at[i, 0], gr.at[i, 0], twin).wait_recv()

        @pl.when(k > 0)
        def _():
            for i, ref in refs:
                shared(i, ref, CHIPS - k).wait_recv()
                onward(i, ref, k).start()
            for i, ref in refs:
                onward(i, ref, k).wait_recv()

    greet(True, depth)
    stage.need("up_rows")
    local = pltpu.make_async_copy(up_rows.at[LATE], up_late.at[z], ls)
    local.start()
    column_start(depth, up_rows.at[LATE], up_late, zs, zr)
    stage.need("w_out", "scanned", "signal", "gate_in")
    @pl.loop(0, CHIPS)
    def _(turn):
        k = lax.rem(turn + 1, CHIPS)
        q = chip_at(k)
        at = rows_of(q)
        pre = scanned[at, :WIDE] + skip[6:7] * signal[at, :].astype(f32)
        inward = gate_in[at, :].astype(f32)
        gated[at, :] = (pre * (inward * jax.nn.sigmoid(inward))).astype(bf16)
        part[0, k] = mm(gated[at, :], w_out[...]).astype(bf16).reshape(2, count, D)
        near(0, k).start()

    for k in range(1, CHIPS):
        pass_away(0, k)
    branch = gathered(0)

    stage.need("tok", "w_router", "up_early", "cot_all", "down0", "down1")
    gain, router0, router1 = rows_in[1:2], rows_in[2:3], rows_in[3:4]
    middle = tok[...].astype(f32) + branch
    scale = lax.rsqrt(jnp.mean(middle * middle, axis=-1, keepdims=True) + epsilon)
    normed = middle * scale
    routed = (normed * gain).astype(bf16)
    routed_all[p] = routed
    logits = mm(routed, w_router[...])
    l0, l1 = logits[:, 66:67], logits[:, 67:68]
    top = jnp.maximum(l0, l1)
    e0, e1 = jnp.exp(l0 - top), jnp.exp(l1 - top)
    p0, p1 = e0 / (e0 + e1), e1 / (e0 + e1)
    taken = jnp.broadcast_to(picks[...].astype(f32), (count, count)).T[:, 0:1]
    c0 = (taken == 0).astype(f32)
    c1 = (taken == 1).astype(f32)
    chosen = jnp.where(lax.broadcasted_iota(jnp.int32, (count, 128), 1) == 0, c0, c1).astype(bf16)
    before = lax.broadcasted_iota(jnp.int32, (count, count), 0) >= lax.broadcasted_iota(
        jnp.int32, (count, count), 1
    )
    places = mm(before.astype(f32).astype(bf16), chosen)
    s0 = c0 * (places[:, 0:1] <= CAP).astype(f32)
    s1 = c1 * (places[:, 1:2] <= CAP).astype(f32)
    gate = p0 * c0 + p1 * c1
    kept = s0 + s1
    weight = gate * kept
    lane = lax.broadcasted_iota(jnp.int32, (count, 128), 1)
    marks_all[p] = jnp.where(lane == 0, weight, jnp.where(lane == 1, s0, s1)).T[:8]
    share_start(routed_all.at[p], routed_all, gs.at[0], gr.at[0])
    share_start(marks_all.at[p], marks_all, gs.at[1], gr.at[1])
    local.wait()
    column_forward(depth, up_late, zs, zr)
    column_finish(depth, up_rows.at[LATE], up_late, zs, zr)
    rim = up_rows.shape[1]
    block = PLANE * rim
    for k in range(depth):
        for q in range(PLANE):
            source = up_early[k, q] if q < EARLY.stop else up_late[k, q - EARLY.stop]
            wide[q * rim : q * rim + rim, :] = source.astype(f32)
        w_up[k * block : k * block + block, :] = wide[...].astype(bf16)

    odd = lax.broadcasted_iota(jnp.int32, (1, EXPERTS * HID), 1) >= HID

    @pl.loop(0, CHIPS)
    def _(k):
        q = chip_at(k)
        arrived(k, ((0, routed_all), (1, marks_all)))
        both = pl.ds(2 * q, 2)
        marks = [
            jnp.concatenate([marks_all[2 * q + i], jnp.zeros((120, count), f32)], axis=0).T for i in range(2)
        ]
        marks = jnp.concatenate(marks, axis=0)
        mask = jnp.where(odd, marks[:, 2:3], marks[:, 1:2])
        hidden = mm(routed_all[both].reshape(pair, D), w_up[...])
        slot = (cot_all[rows_of(q), :].astype(f32) * marks[:, 0:1]).astype(bf16)
        slot_all[q] = slot
        square = hidden * hidden
        bend = jnp.tanh(GELU * hidden * (1.0 + 0.044715 * square))
        units = (0.5 * hidden * (1.0 + bend) * mask).astype(bf16)
        hidden_all[q] = units
        slope = 0.5 * (1.0 + bend) + 0.5 * GELU * hidden * (1.0 - bend * bend) * (1.0 + 3 * 0.044715 * square)
        grad = jnp.concatenate([contract_cols(slot, down0[...]), contract_cols(slot, down1[...])], axis=1)
        grad = (slope * grad * mask).astype(bf16)
        pre_all[q] = grad
        made = mm(units[:, :HID], down0[...]) + mm(units[:, HID:], down1[...])
        part[1, k] = made.astype(bf16).reshape(2, count, D)
        near(1, k).start()
        part[2, k] = contract_cols(grad, w_up[...]).astype(bf16).reshape(2, count, D)
        near(2, k).start()

        @pl.when(k > 1)
        def _():
            pass_away(1, k - 1)
            pass_away(2, k - 1)

    pass_away(1, CHIPS - 1)
    pass_away(2, CHIPS - 1)
    every = CHIPS * pair
    fs = HID // depth
    for c in range(0, D, 384):
        for e in range(EXPERTS):
            made = contract_rows(
                hidden_all[:, :, e * HID : e * HID + HID].reshape(every, HID),
                slot_all[:, :, c : c + 384].reshape(every, 384),
            )
            for k in range(depth):
                grad_down[k, e, :, c : c + 384] = made[k * fs : k * fs + fs].astype(bf16)
    down = []
    for k in range(1, depth):
        q = lax.rem(z + k, depth)
        down.append(send(grad_down.at[q], down_got.at[k], ds.at[k], dr.at[k], (q, p)))
    expert_tok = gathered(1)
    slot_back = gathered(2)

    up = cot_all[pl.ds(pl.multiple_of(p * count, count), count), :].astype(f32)
    output[...] = (middle + weight * expert_tok).astype(bf16)
    stage.done("output")
    pull = jnp.sum(up * expert_tok, axis=-1, keepdims=True) * kept * gate
    g0, g1 = pull * (c0 - p0), pull * (c1 - p1)
    grad_routed = slot_back + g0 * router0 + g1 * router1
    routed = routed.astype(f32)
    sum0 = jnp.sum(grad_routed * normed, axis=0, keepdims=True)
    sum1 = jnp.sum(routed * g0, axis=0, keepdims=True)
    sum2 = jnp.sum(routed * g1, axis=0, keepdims=True)
    grad_normed = grad_routed * gain
    inner = jnp.mean(grad_normed * normed, axis=-1, keepdims=True)
    total = scale * (grad_normed - normed * inner) + up
    grad_mid[...] = total
    stage.done("grad_mid")
    back_all[p] = total.astype(bf16)
    share_start(back_all.at[p], back_all, gs.at[2], gr.at[2])
    for c in range(0, D, 384):
        grad_up[c : c + 384, :] = contract_rows(
            routed_all[:, :, c : c + 384].reshape(every, 384), pre_all[...].reshape(every, EXPERTS * HID)
        ).astype(bf16)
    stage.done("grad_up")

    sums[...] = jnp.zeros_like(sums)
    sums[0:1], sums[1:2], sums[2:3] = sum0, sum1, sum2

    @pl.loop(0, CHIPS)
    def _(k):
        q = chip_at(k)
        arrived(k, ((2, back_all),))
        at = rows_of(q)
        grad = contract_cols(back_all[pl.ds(2 * q, 2)].reshape(pair, D), w_out[...])
        inward = gate_in[at, :].astype(f32)
        sig = jax.nn.sigmoid(inward)
        act = inward * sig
        through = grad * act
        sums[3:4, :WIDE] += jnp.sum(through * signal[at, :].astype(f32), axis=0, keepdims=True)
        mixed_grad[at, :WIDE] = through
        mixed_grad[at, WIDE:] = jnp.zeros((pair, PAD), f32)
        pre = scanned[at, :WIDE] + skip[6:7] * signal[at, :].astype(f32)
        gate_grad[at, :] = (grad * pre * (sig * (1.0 + inward * (1.0 - sig)))).astype(bf16)
    stage.done("mixed_grad", "gate_grad")
    for c in range(0, D, 384):
        grad_out[:, c : c + 384] = contract_rows(
            gated[...], back_all[:, :, c : c + 384].reshape(every, 384)
        ).astype(bf16)
    for c in down:
        c.wait_recv()
    total = grad_down[z].astype(f32)
    for k in range(1, depth):
        total = total + down_got[k].astype(f32)
    down_own[...] = total
    for c in down:
        c.wait_send()
    for i in range(3):
        for k in range(CHIPS):
            near(i, k).wait_send()
            if k:
                away(i, k).wait_send()
    for i, ref in ((0, routed_all), (1, marks_all), (2, back_all)):
        remote(ref.at[p], ref.at[p], gs.at[i, 0], gr.at[i, 0], twin).wait_send()
        for k in range(1, CHIPS):
            shared(i, ref, k).wait_send()
            onward(i, ref, k).wait_send()


def middle_part(cid, depth, **ins):
    count, rows, rim = ins["tok"].shape[0], ins["cot_all"].shape[0], ins["up_rows"].shape[1]
    wide = EXPERTS * HID
    block = (CHIPS, count, D)
    outs = dict(
        output=made(count, D, dtype=bf16),
        grad_mid=made(count, D),
        mixed_grad=made(rows, WIDE + PAD),
        gate_grad=made(rows, WIDE, dtype=bf16),
        grad_out=made(WIDE, D, dtype=bf16),
        grad_up=made(D, wide, dtype=bf16),
        down_own=made(EXPERTS, HID // depth, D),
        sums=made(8, D),
    )
    scratch = (
        [
            pltpu.VMEM((rows, WIDE), bf16),
            pltpu.VMEM((3, CHIPS, 2, count, D), bf16),
            pltpu.VMEM((3,) + block, bf16),
            pltpu.VMEM((3,) + block, bf16),
            pltpu.VMEM((3,) + block, bf16),
            pltpu.VMEM((PLANE, count, D), bf16),
            pltpu.VMEM((PLANE, 8, count), f32),
            pltpu.VMEM((CHIPS, 2 * count, wide), bf16),
            pltpu.VMEM((CHIPS, 2 * count, wide), bf16),
            pltpu.VMEM((CHIPS, 2 * count, D), bf16),
            pltpu.VMEM((PLANE, count, D), bf16),
            pltpu.VMEM((depth, LATE.stop - LATE.start, rim, wide), bf16),
            pltpu.VMEM((D, wide), bf16),
            pltpu.VMEM((PLANE * rim, wide), f32),
            pltpu.VMEM((depth, EXPERTS, HID // depth, D), bf16),
            pltpu.VMEM((depth, EXPERTS, HID // depth, D), bf16),
        ]
        + [DMA((3, CHIPS))] * 4
        + [DMA((3, PLANE))] * 2
        + [DMA((depth,))] * 4
        + [DMA]
    )
    late = (
        "up_rows", "w_out", "scanned", "signal", "gate_in", "tok", "w_router", "up_early", "cot_all", "down0", "down1",
    )
    return staged_call(
        functools.partial(middle_kernel, depth), "middle_part", cid, 75, ins, outs, scratch,
        late=late, early=("output", "grad_mid", "grad_up", "mixed_grad", "gate_grad"),
    )


def tree(parts):
    row = lax.broadcasted_iota(jnp.int32, parts[0].shape, 0)
    for step in (1, 2, 4):
        low = (row // step) % 2 == 0
        parts = [
            jnp.where(low, a, b) + pltpu.roll(jnp.where(low, b, a), step, 0)
            for a, b in zip(parts[::2], parts[1::2])
        ]
    return parts[0]


def lane_tiles(x):
    total = x[:, :128]
    for k in range(128, x.shape[1], 128):
        total = total + x[:, k : k + 128]
    return total


def spread(ref, i):
    return jnp.broadcast_to(ref[pl.ds(i, 1), :], (8, ref.shape[1]))


HALVES = (slice(0, 8), slice(8, 16))


def ends_loop(dk, push, sel, slope):
    def block(b, carry):
        hidden, acc = list(carry[:2]), carry[2]
        base = pl.multiple_of(b * BLK, BLK)
        w = sel[b, :STATE]
        for t in range(BLK):
            d, u = spread(dk, base + t), spread(push, base + t)
            for k, h in enumerate(HALVES):
                hidden[k] = jnp.exp2(d * slope[k]) * hidden[k] + w[h, t : t + 1] * u
            acc = acc + d
        return hidden[0], hidden[1], acc

    zero = jnp.zeros(slope[0].shape, f32)
    return lax.fori_loop(0, dk.shape[0] // BLK, block, (zero, zero, zero))


def scan_kernel(
    depth, stage, onward,
    dk, push, sel, rate, up_rows, cot, w_down,
    out, states, ends, up_all, cot_all, down_all,
    slots, gs, gr, es, er, zs, zr, ks, ls,
):
    z, p = here()
    tile = slots.shape[1]
    tiles = dk.shape[0] // tile
    local = [
        pltpu.make_async_copy(up_rows.at[EARLY], up_all.at[z], ls.at[0]),
        pltpu.make_async_copy(cot, cot_all.at[p], ls.at[1]),
        pltpu.make_async_copy(w_down.at[1], down_all.at[z], ls.at[2]),
    ]
    stage.need("cot")
    for c in local:
        c.start()
    first = share_start(cot, cot_all, gs, gr)
    slope = [rate[h, :] * LOG2E for h in HALVES]
    one, two, acc = ends_loop(dk, push, sel, slope)
    ends[z, :8], ends[z, 8:16], ends[z, 16:] = one, two, acc
    mine = []
    for k in range(1, depth):
        mine.append(send(ends.at[z], ends.at[z], es.at[k], er.at[k], (lax.rem(z + k, depth), p)))
    column_start(depth, up_rows.at[EARLY], up_all, zs.at[0], zr.at[0])
    column_start(depth, w_down.at[1], down_all, zs.at[1], zr.at[1])
    onward()
    second = share_forward(cot_all, first, gs, gr)
    for c in local:
        c.wait()
    for c in mine:
        c.wait_recv()
    hidden = [jnp.zeros(slope[0].shape, f32)] * 2
    for k in range(depth - 1):
        for i, h in enumerate(HALVES):
            hidden[i] = jnp.where(k < z, jnp.exp2(ends[k, 16:] * slope[i]) * hidden[i] + ends[k, h], hidden[i])

    def stored(i, slot):
        return pltpu.make_async_copy(
            slots.at[slot], states.at[pl.ds(pl.multiple_of(i * tile, tile), tile)], ks.at[slot]
        )

    def piece(i, carry):
        slot = lax.rem(i, 2)

        @pl.when(i >= 2)
        def _():
            stored(i - 2, slot).wait()

        def block(j, carry):
            hidden = list(carry)
            b = i * (tile // BLK) + j
            base = pl.multiple_of(b * BLK, BLK)
            inside = j * BLK
            w, r = sel[b, :STATE], sel[b, STATE:]
            parts = []
            for t in range(BLK):
                d, u = spread(dk, base + t), spread(push, base + t)
                line = None
                for k, h in enumerate(HALVES):
                    hidden[k] = jnp.exp2(d * slope[k]) * hidden[k] + w[h, t : t + 1] * u
                    slots[slot, inside + t, h] = hidden[k]
                    y = r[h, t : t + 1] * hidden[k]
                    line = y if line is None else line + y
                parts.append(line)
                if len(parts) == 8:
                    out[pl.ds(pl.multiple_of(base + t - 7, 8), 8), :] = tree(parts)
                    parts = []
            return tuple(hidden)

        carry = lax.fori_loop(0, tile // BLK, block, carry)
        stored(i, slot).start()
        return carry

    carry = lax.fori_loop(0, tiles - 3, piece, tuple(hidden))
    column_forward(depth, up_all, zs.at[0], zr.at[0])
    lax.fori_loop(tiles - 3, tiles, piece, carry)
    stage.done("scanned")
    column_forward(depth, down_all, zs.at[1], zr.at[1])
    for i in (tiles - 2, tiles - 1):
        stored(i, i % 2).wait()
    share_finish(first, second)
    column_finish(depth, up_rows.at[EARLY], up_all, zs.at[0], zr.at[0])
    column_finish(depth, w_down.at[1], down_all, zs.at[1], zr.at[1])
    for c in mine:
        c.wait_send()


def message_loop(dk, grad, sel, slope):
    blocks = dk.shape[0] // BLK

    def block(i, carry):
        message = list(carry)
        b = blocks - 1 - i
        base = pl.multiple_of(b * BLK, BLK)
        r = sel[b, STATE:]
        for t in reversed(range(BLK)):
            d, g = spread(dk, base + t), spread(grad, base + t)
            for k, h in enumerate(HALVES):
                message[k] = jnp.exp2(d * slope[k]) * (r[h, t : t + 1] * g + message[k])
        return tuple(message)

    zero = jnp.zeros(slope[0].shape, f32)
    return lax.fori_loop(0, blocks, block, (zero, zero))


def adjoint_kernel(
    depth, stage, after,
    dk, push, grad, sel, states, rate, ends, gup, gout,
    g_push, g_step, g_sel, g_rate, up_own, out_own,
    slots, notes, up_got, out_got, es, er, zs, zr, ks,
):
    z, p = here()
    tile = slots.shape[1]
    tiles = dk.shape[0] // tile
    per = tile // BLK

    def fetch(i, slot):
        return pltpu.make_async_copy(
            states.at[pl.ds(pl.multiple_of(i * tile, tile), tile)], slots.at[slot], ks.at[slot]
        )

    fetch(tiles - 1, 0).start()
    fetch(tiles - 2, 1).start()
    greet(True, depth)
    first = gup.shape[1] // 64 * 16
    pieces = (pl.ds(0, first), pl.ds(first, gup.shape[1] - first))
    stage.need("gup")
    down = []
    for k in range(1, depth):
        q = lax.rem(z + k, depth)
        down.append(
            send(gup.at[q, pieces[0]], up_got.at[k, pieces[0]], zs.at[1, k], zr.at[1, k], (q, p))
        )
    stage.need("sel", "dk", "grad")
    slope = [rate[h, :] * LOG2E for h in HALVES]
    notes[z, :8], notes[z, 8:] = message_loop(dk, grad, sel, slope)
    mine = []
    for k in range(1, depth):
        mine.append(send(notes.at[z], notes.at[z], es.at[k], er.at[k], (lax.rem(z + k, depth), p)))
    stage.need("push")
    for k in range(1, depth):
        q = lax.rem(z + k, depth)
        down.append(
            send(gup.at[q, pieces[1]], up_got.at[k, pieces[1]], zs.at[0, k], zr.at[0, k], (q, p))
        )
    stage.need("gout")
    for k in range(1, depth):
        q = lax.rem(z + k, depth)
        down.append(send(gout.at[q], out_got.at[k], zs.at[2, k], zr.at[2, k], (q, p)))
    for c in mine:
        c.wait_recv()
    message = [jnp.zeros(slope[0].shape, f32)] * 2
    for k in range(depth - 1, 0, -1):
        for i, h in enumerate(HALVES):
            message[i] = jnp.where(k > z, notes[k, h] + jnp.exp2(ends[k, 16:] * slope[i]) * message[i], message[i])
    lane = lax.broadcasted_iota(jnp.int32, (STATE, 128), 1)
    ones = jnp.ones((128, 128), bf16)

    def piece(n, carry):
        i = tiles - 1 - n
        slot = lax.rem(n, 2)
        fetch(i, slot).wait()

        def block(m, carry):
            message, acc = list(carry[:2]), list(carry[2:])
            j = per - 1 - m
            b = i * per + j
            base = pl.multiple_of(b * BLK, BLK)
            inside = j * BLK
            w, r = sel[b, :STATE], sel[b, STATE:]
            pushes, steps = [], []
            reads, writes = [None] * (2 * BLK), [None] * (2 * BLK)
            for t in reversed(range(BLK)):
                d, u, g = spread(dk, base + t), spread(push, base + t), spread(grad, base + t)
                plain = jnp.where(d < RESET, d, 0.0)
                to_push = to_step = None
                for k, h in enumerate(HALVES):
                    wt = w[h, t : t + 1]
                    hidden = slots[slot, inside + t, h]
                    total = r[h, t : t + 1] * g + message[k]
                    reads[2 * t + k] = lane_tiles(hidden * g)
                    writes[2 * t + k] = lane_tiles(total * u)
                    x = total * wt
                    carried = total * (hidden - wt * u)
                    y = carried * slope[k]
                    to_push = x if k == 0 else to_push + x
                    to_step = y if k == 0 else to_step + y
                    acc[k] = acc[k] + carried * plain
                    message[k] = jnp.exp2(d * slope[k]) * total
                pushes.insert(0, to_push)
                steps.insert(0, to_step)
                if len(pushes) == 8:
                    at = pl.ds(pl.multiple_of(base + t, 8), 8)
                    g_push[at, :] = tree(pushes)
                    g_step[at, :] = tree(steps)
                    pushes, steps = [], []
            for j2, quantity in enumerate((writes, reads)):
                x = jnp.concatenate(quantity, axis=0)
                high = x.astype(bf16)
                low = (x - high.astype(f32)).astype(bf16)
                sums = jnp.dot(high, ones, preferred_element_type=f32)
                sums = sums + jnp.dot(low, ones, preferred_element_type=f32)
                kept = jnp.zeros((STATE, 128), f32)
                for t in range(BLK):
                    kept = jnp.where(lane == t, sums[STATE * t : STATE * t + STATE], kept)
                g_sel[b, STATE * j2 : STATE * j2 + STATE] = kept[:, :BLK]
            return message[0], message[1], acc[0], acc[1]

        carry = lax.fori_loop(0, per, block, carry)

        @pl.when(n + 2 < tiles)
        def _():
            fetch(i - 2, slot).start()

        return carry

    zero = jnp.zeros(slope[0].shape, f32)
    done = lax.fori_loop(0, tiles, piece, (message[0], message[1], zero, zero))
    g_rate[:8], g_rate[8:] = done[2], done[3]
    after()
    for c in down:
        c.wait_recv()
    total = gup[z].astype(f32)
    for k in range(1, depth):
        total = total + up_got[k].astype(f32)
    rim = up_own.shape[1]
    for q in range(PLANE):
        up_own[q] = total[q * rim : q * rim + rim].astype(bf16)
    total = gout[z].astype(f32)
    for k in range(1, depth):
        total = total + out_got[k].astype(f32)
    out_own[...] = total
    def finish():
        for c in mine + down:
            c.wait_send()

    return finish


def last_kernel(count, *refs):
    ins, outs, held = refs[:count], refs[count : 2 * count], refs[2 * count : 3 * count]
    in_sem, out_sem = refs[3 * count :]
    arriving = [pltpu.make_async_copy(ins[i], held[i], in_sem.at[i]) for i in range(count)]
    for c in arriving:
        c.start()
    leaving = [pltpu.make_async_copy(held[i], outs[i], out_sem.at[i]) for i in range(count)]
    for a, b in zip(arriving, leaving):
        a.wait()
        b.start()
    for c in leaving:
        c.wait()


def last_part(*results):
    count = len(results)
    return pl.pallas_call(
        functools.partial(last_kernel, count),
        out_shape=[jax.ShapeDtypeStruct(r.shape, r.dtype) for r in results],
        in_specs=[ANY] * count,
        out_specs=[ANY] * count,
        scratch_shapes=[pltpu.VMEM(r.shape, r.dtype) for r in results] + [DMA((count,))] * 2,
        compiler_params=params(),
        cost_estimate=cost(5),
        name="last_part",
    )(*results)


def body(
    depth,
    tokens,
    segments,
    routes,
    norm_gain,
    in_proj,
    conv_taps,
    conv_bias,
    select_proj,
    step_proj,
    step_bias,
    decay_log,
    skip_gain,
    out_proj,
    moe_gain,
    router,
    expert_up,
    expert_down,
    cotangent,
):
    count = tokens.shape[0]
    rows = PLANE * count
    rim = norm_gain.shape[0]
    ch = conv_bias.shape[0]
    fs = expert_down.shape[1]
    z, p = here()

    ids = jnp.concatenate([jnp.full((3,), -1, jnp.int32), segments, jnp.full((BLK,), -2, jnp.int32)])
    local_ids = lax.dynamic_slice_in_dim(ids, z * rows, rows + 3 + BLK)
    own_ids = local_ids[3:]
    inside = own_ids >= 0
    same = jnp.stack(
        [(local_ids[k : k + rows + BLK] == own_ids) & inside for k in range(4)], axis=1
    ).astype(f32)
    same = jnp.pad(same, ((0, 0), (0, 124)))
    (
        normed_in,
        w_in,
        w_route,
        small,
        w_sel,
        w_step,
        vecs,
        rate,
        inner,
        gate_in,
        conv,
        signal,
        selected,
        mixes,
        step_pre,
        dk,
        push,
        up_rows,
        down0,
        out_all,
        scanned,
        states,
        ends,
        up_early,
        cot_all,
        down1,
    ) = front_part(
        1,
        depth,
        tok=tokens,
        in_proj=in_proj,
        norm_gain=norm_gain[None],
        moe_gain=moe_gain[None],
        router=router.T,
        expert_up=expert_up.transpose(1, 0, 2),
        select=select_proj,
        step=step_proj,
        decay=decay_log,
        taps=conv_taps,
        bias=conv_bias[None],
        offset=step_bias[None],
        skip=skip_gain[None],
        w_down=expert_down,
        w_out=out_proj,
        same=same,
        cot=cotangent,
    )
    w_out = out_all.reshape(WIDE, D)
    output, grad_mid, mixed_wide, grad_gate_in, grad_out_w, grad_up, grad_down_own, sums = middle_part(
        3,
        depth,
        scanned=scanned,
        signal=signal,
        gate_in=gate_in,
        skip=vecs,
        w_out=w_out,
        tok=tokens,
        cot_all=cot_all.reshape(rows, D),
        up_early=up_early,
        up_rows=up_rows,
        down0=down0.reshape(HID, D),
        down1=down1.reshape(HID, D),
        w_router=w_route,
        rows_in=small,
        picks=routes.T,
    )
    (
        grad_tokens,
        grad_in,
        grad_up_own,
        grad_sel,
        grad_step,
        grad_decay,
        grad_taps,
        grad_bias,
        grad_offset,
        grad_skip,
        grad_norm,
        grad_moe,
        grad_router,
        grad_out_own,
    ) = back_part(
        5,
        depth,
        rim,
        ch,
        dk=dk,
        push=push,
        grad=mixed_wide,
        sel=mixes,
        states=states,
        ends=ends,
        gup=grad_up.reshape(depth, D // depth, EXPERTS * HID),
        gout=grad_out_w.reshape(depth, ch, D),
        step_pre=step_pre,
        signal=signal,
        conv=conv,
        inner=inner,
        same=same,
        vecs=vecs,
        rate=rate,
        selected=selected,
        w_sel=w_sel,
        w_step=w_step,
        gate_grad=grad_gate_in,
        w_in=w_in,
        normed_in=normed_in,
        tok=tokens,
        gain=small,
        grad_mid=grad_mid,
        sums=sums,
    )
    (
        output,
        grad_tokens,
        grad_norm,
        grad_in,
        grad_taps,
        grad_bias,
        grad_sel,
        grad_step,
        grad_offset,
        grad_decay,
        grad_skip,
        grad_out_own,
        grad_moe,
        grad_router,
        grad_up_own,
        grad_down_own,
    ) = last_part(
        output,
        grad_tokens,
        grad_norm,
        grad_in,
        grad_taps,
        grad_bias,
        grad_sel,
        grad_step,
        grad_offset,
        grad_decay,
        grad_skip,
        grad_out_own,
        grad_moe,
        grad_router,
        grad_up_own,
        grad_down_own,
    )
    return (
        output,
        grad_tokens,
        grad_norm[0],
        grad_in,
        grad_taps,
        grad_bias[0],
        grad_sel,
        grad_step,
        grad_offset[0],
        grad_decay,
        grad_skip[0],
        grad_out_own,
        grad_moe[0],
        grad_router.T,
        grad_up_own.transpose(1, 0, 2),
        grad_down_own,
    )


def solution(mesh):
    planes = Mesh(mesh.devices.reshape(-1, PLANE), ("z", "p"))
    every = ("z", "p")
    rows, flat, cols, third = P(every, None), P(every), P(None, every), P(None, every, None)
    return jax.shard_map(
        functools.partial(body, planes.shape["z"]),
        mesh=planes,
        in_specs=(
            rows, P(), rows, flat, rows, cols, flat, rows, cols,
            flat, cols, flat, rows, flat, rows, third, third, rows,
        ),
        out_specs=(
            rows, rows, flat, rows, cols, flat, rows, cols,
            flat, cols, flat, rows, flat, rows, third, third,
        ),
        check_vma=False,
    )
```

```python
import functools

import jax
import jax.numpy as jnp
from jax import lax
from jax.experimental import pallas as pl
from jax.experimental.pallas import tpu as pltpu
from jax.sharding import Mesh, PartitionSpec as P

D = 1152
DI = 2304
FF = 3072
RANK = 72
STATE = 16
EXPERTS = 2
CAP = 68
SEL = RANK + 2 * STATE

PLANE = 8
CHIPS = PLANE // 2
WIDE = DI // PLANE
PAD = -WIDE % 128
HID = FF // PLANE
BLK = 16
LOG2E = 1.4426950408889634
GELU = 0.7978845608028654
RESET = 1e5
EARLY, LATE = slice(0, 2), slice(2, PLANE)
epsilon = 1e-05

MESH = pl.DeviceIdType.MESH
ANY = pl.BlockSpec(memory_space=pl.ANY)
VM = pl.BlockSpec(memory_space=pltpu.VMEM)
bf16 = jnp.bfloat16
f32 = jnp.float32
DMA = pltpu.SemaphoreType.DMA


def params(cid=None, grid=None):
    extra = {} if cid is None else {"collective_id": cid, "has_side_effects": True}
    if grid is not None:
        extra["dimension_semantics"] = grid
    return pltpu.CompilerParams(vmem_limit_bytes=60 * 1024 * 1024, **extra)


def cost(us):
    return pl.CostEstimate(flops=int(us * 1e9), bytes_accessed=int(us * 3e6), transcendentals=0)


def mm(left, right):
    return jnp.dot(left, right, preferred_element_type=f32)


def contract_rows(left, right):
    return lax.dot_general(left, right, (((0,), (0,)), ((), ())), preferred_element_type=f32)


def contract_cols(left, right):
    return lax.dot_general(left, right, (((1,), (1,)), ((), ())), preferred_element_type=f32)


class Names:
    def __getattr__(self, name):
        return name


N = Names()


class Stage:
    def __init__(self, fetches, flushes):
        self.fetches, self.flushes, self.going = fetches, flushes, []
        for copy in fetches.values():
            copy.start()

    def need(self, *names):
        for name in names:
            self.fetches.pop(name).wait()

    def done(self, *names):
        for name in names:
            self.flushes[name].start()
            self.going.append(self.flushes[name])

    def end(self):
        self.need(*tuple(self.fetches))
        for copy in self.going:
            copy.wait()


def staged_call(kernel, name, cid, us, ins, outs, scratch, late=(), early=(), away=(), raw=()):
    inside = [n for n in outs if n not in away]
    early = [n for n in inside if n in early]

    def body(*refs):
        refs = list(refs)
        take = lambda names: dict(zip(names, [refs.pop(0) for _ in names]))
        source, target = take(ins), take(outs)
        buffers, results = take(late), take(early)
        in_sem, out_sem = refs.pop(0), refs.pop(0)
        stage = Stage(
            {n: pltpu.make_async_copy(source[n], buffers[n], in_sem.at[i]) for i, n in enumerate(late)},
            {n: pltpu.make_async_copy(results[n], target[n], out_sem.at[i]) for i, n in enumerate(early)},
        )
        kernel(
            stage,
            *[buffers.get(n, source[n]) for n in ins],
            *[results.get(n, target[n]) for n in outs],
            *refs,
        )
        stage.end()

    return pl.pallas_call(
        body,
        out_shape=list(outs.values()),
        in_specs=[ANY if n in late or n in raw else VM for n in ins],
        out_specs=[ANY if n in early or n in away else VM for n in outs],
        scratch_shapes=[pltpu.VMEM(ins[n].shape, ins[n].dtype) for n in late]
        + [pltpu.VMEM(outs[n].shape, outs[n].dtype) for n in early]
        + [DMA((max(len(late), 1),)), DMA((max(len(early), 1),))]
        + scratch,
        compiler_params=params(cid),
        cost_estimate=cost(us),
        name=name,
    )(*ins.values())


def made(*shape, dtype=None):
    return jax.ShapeDtypeStruct(shape, dtype or f32)


def remote(src, dst, ss, rs, to):
    return pltpu.make_async_remote_copy(
        src_ref=src, dst_ref=dst, send_sem=ss, recv_sem=rs, device_id=to, device_id_type=MESH
    )


def send(src, dst, ss, rs, to):
    copy = remote(src, dst, ss, rs, to)
    copy.start()
    return copy


def here():
    return lax.axis_index("z"), lax.axis_index("p")


def greet(plane=True, depth=0):
    z, p = here()
    barrier = pltpu.get_barrier_semaphore()
    count = 0
    if plane:
        for k in range(1, PLANE):
            pl.semaphore_signal(
                barrier, inc=1, device_id=(z, lax.rem(p + k, PLANE)), device_id_type=MESH
            )
            count += 1
    for k in range(1, depth):
        pl.semaphore_signal(barrier, inc=1, device_id=(lax.rem(z + k, depth), p), device_id_type=MESH)
        count += 1
    pl.semaphore_wait(barrier, count)


def share_start(x, out, ss, rs):
    z, p = here()
    core = lax.rem(p, 2)
    copies = [send(x, out.at[p], ss.at[0], rs.at[0], (z, p + 1 - 2 * core))]
    for k in range(1, CHIPS):
        copies.append(send(x, out.at[p], ss.at[k], rs.at[k], (z, lax.rem(p + 2 * k, PLANE))))
    return copies


def share_forward(out, copies, ss, rs):
    z, p = here()
    core = lax.rem(p, 2)
    onward = []
    for k in range(1, CHIPS):
        copies[k].wait_recv()
        src = lax.rem(p + PLANE - 2 * k, PLANE)
        onward.append(
            send(out.at[src], out.at[src], ss.at[CHIPS + k], rs.at[CHIPS + k], (z, p + 1 - 2 * core))
        )
    return onward


def share_finish(copies, onward):
    copies[0].wait_recv()
    for c in copies:
        c.wait_send()
    for c in onward:
        c.wait()


def column_copy(src, out, ss, rs, frm, to, part=None):
    dst = out.at[frm] if part is None else out.at[frm, part]
    return pltpu.make_async_remote_copy(
        src_ref=dst if src is None else src,
        dst_ref=dst,
        send_sem=ss.at[to],
        recv_sem=rs.at[frm],
        device_id=(to, lax.axis_index("p")),
        device_id_type=MESH,
    )


def column_each(depth, act):
    z = lax.axis_index("z")
    for t in range(depth):
        far = abs(t - z) == depth - 1 if depth == 4 else t == z
        pl.when(jnp.logical_not((t == z) | far))(functools.partial(act, t))


def column_start(depth, src, out, ss, rs, part=None):
    z = lax.axis_index("z")
    column_each(depth, lambda t: column_copy(src, out, ss, rs, z, t, part).start())


def column_forward(depth, out, ss, rs, part=None):
    if depth != 4:
        return
    z = lax.axis_index("z")
    for me, frm, to in ((2, 0, 3), (1, 3, 0)):

        @pl.when(z == me)
        def _():
            copy = column_copy(None, out, ss, rs, frm, to, part)
            copy.wait_recv()
            copy.start()


def column_finish(depth, src, out, ss, rs, part=None):
    z = lax.axis_index("z")
    for s in range(depth):
        ahead = ((z == 2) & (s == 0)) | ((z == 1) & (s == 3)) if depth == 4 else s == z

        @pl.when(jnp.logical_not((s == z) | ahead))
        def _():
            column_copy(src, out, ss, rs, s, s, part).wait_recv()

    column_each(depth, lambda t: column_copy(src, out, ss, rs, z, t, part).wait_send())
    if depth == 4:
        for me, frm, to in ((2, 0, 3), (1, 3, 0)):

            @pl.when(z == me)
            def _():
                column_copy(None, out, ss, rs, frm, to, part).wait_send()


def softplus(x):
    return jnp.maximum(x, 0.0) + jnp.log1p(jnp.exp(-jnp.abs(x)))


def total_start(x, got, ss, rs):
    z, p = here()
    copies = []
    for k in range(1, PLANE):
        q = lax.rem(p + k, PLANE)
        copies.append(send(x.at[q], got.at[k], ss.at[k], rs.at[k], (z, q)))
    return copies


def total_share(x, got, copies, out, ts, us):
    z, p = here()
    total = x[p]
    for k in range(1, PLANE):
        copies[k - 1].wait_recv()
        total = total + got[k]
    out[p] = total.astype(bf16)
    after = [
        send(out.at[p], out.at[p], ts.at[k], us.at[k], (z, lax.rem(p + k, PLANE))) for k in range(1, PLANE)
    ]
    for c in copies:
        c.wait_send()
    return after


def front_kernel(
    depth, stage,
    tok, in_proj, norm_gain, moe_gain, router, expert_up, select, step, decay, taps, bias, offset, skip,
    w_down, w_out, same,
    normed_in, w_in, w_route, small, w_sel, w_step, vecs, rate, inner, gate_in, conv, signal, selected, mixes,
    step_pre, dk, push, up_rows, down_all, out_all,
    tok_all, win_all, pack_all, wide, thin, near, halo, x, got, sel_all, win, wup, pack, square,
    gs, gr, ws, wr, vs, vr, zs, zr, hs, ss, rs, ts, us, ls,
):
    z, p = here()
    count = tok.shape[0]
    rim = in_proj.shape[0]
    ch = select.shape[0]
    pair = 2 * count
    rows = PLANE * count
    fs = expert_up.shape[2] // (depth * PLANE)
    local = [
        pltpu.make_async_copy(tok, tok_all.at[p], ls.at[0]),
        pltpu.make_async_copy(win.at[p], win_all.at[z, p], ls.at[1]),
        pltpu.make_async_copy(wup.at[p], up_rows.at[p], ls.at[2]),
        pltpu.make_async_copy(pack, pack_all.at[z], ls.at[3]),
        pltpu.make_async_copy(w_down.at[0], down_all.at[z], ls.at[4]),
        pltpu.make_async_copy(w_out, out_all.at[z], ls.at[5]),
    ]
    for i in (0, 4, 5):
        local[i].start()
    square[...] = jnp.zeros_like(square)
    square[0:1, :rim] = norm_gain[...].astype(f32)
    square[1:2, :rim] = moe_gain[...].astype(f32)
    square[2:4, :rim] = router[...].astype(f32)
    columns = square[...].T
    square[...] = columns
    for q in range(PLANE):
        for i in range(2 * depth):
            start = (i // depth) * DI + ((i % depth) * PLANE + q) * ch
            win[q, :, i * ch : i * ch + ch] = in_proj[:, start : start + ch]
        win[q, :, 2 * WIDE :] = square[:rim, :64].astype(bf16)
    local[1].start()
    greet(True, depth)
    across = []
    for k in range(1, PLANE):
        q = lax.rem(p + k, PLANE)
        across.append(send(win.at[q], win_all.at[z, p], ws.at[k], wr.at[k], (z, q)))
    first = share_start(tok, tok_all, gs, gr)
    square[...] = jnp.zeros_like(square)
    square[0:STATE, :ch] = decay[...].astype(f32)
    square[STATE : STATE + 4, :ch] = taps[...].astype(f32)
    for i, ref in enumerate((bias, offset, skip)):
        square[STATE + 4 + i : STATE + 5 + i, :ch] = ref[...].astype(f32)
    columns = square[...].T
    pack[:, 256:] = columns[:ch].astype(bf16)
    square[...] = jnp.zeros_like(square)
    square[:RANK, :ch] = step[...].astype(f32)
    columns = square[...].T
    pack[:, 128:256] = columns[:ch].astype(bf16)
    pack[:, :128] = jnp.zeros((ch, 128), bf16)
    pack[:, :SEL] = select[...]
    column_start(depth, pack, pack_all, zs.at[0], zr.at[0])
    local[3].start()
    for q in range(PLANE):
        for i in range(EXPERTS * depth):
            start = ((i % depth) * PLANE + q) * fs
            wup[q, :, i * fs : i * fs + fs] = expert_up[:, i // depth, start : start + fs]
    local[2].start()
    local[1].wait()
    for c in across:
        c.wait_recv()
    column_start(depth, win_all.at[z], win_all, zs.at[1], zr.at[1])
    second = share_forward(tok_all, first, gs, gr)
    more = []
    for k in range(1, PLANE):
        q = lax.rem(p + k, PLANE)
        more.append(send(wup.at[q], up_rows.at[p], vs.at[k], vr.at[k], (z, q)))
    local[3].wait()
    column_forward(depth, pack_all, zs.at[0], zr.at[0])
    column_finish(depth, pack, pack_all, zs.at[0], zr.at[0])
    for k in range(depth):
        thin[k * ch : k * ch + ch, :] = pack_all[k].astype(f32)
    w_sel[...] = thin[:, :128].astype(bf16)
    w_step[...] = thin[:, 128:256].astype(bf16)
    side = thin[:, 256:].T
    rate[:, :WIDE] = -jnp.exp(side[:STATE])
    rate[:, WIDE:] = jnp.zeros((STATE, PAD), f32)
    vecs[...] = side[STATE : STATE + 8]
    column_forward(depth, win_all, zs.at[1], zr.at[1])
    local[0].wait()
    share_finish(first, second)
    column_finish(depth, win_all.at[z], win_all, zs.at[1], zr.at[1])
    for k in range(depth):
        for q in range(PLANE):
            at = (k * PLANE + q) * rim
            wide[at : at + rim, :] = win_all[k, q].astype(f32)
    w_in[...] = wide[:, : 2 * WIDE].astype(bf16)
    w_route[...] = wide[:, 512:].astype(bf16)
    small[...] = wide[:, 512:].T[64:72]
    gain = small[0:1]
    for b in (3, 0, 1, 2):
        at = slice(pair * b, pair * b + pair)
        values = tok_all[2 * b : 2 * b + 2].reshape(pair, D).astype(f32)
        scale = lax.rsqrt(jnp.mean(values * values, axis=-1, keepdims=True) + epsilon)
        normed = (values * scale * gain).astype(bf16)
        normed_in[at, :] = normed
        joined = mm(normed, w_in[...]).astype(bf16)
        near[BLK + pair * b : BLK + pair * b + pair, :] = joined[:, :WIDE].astype(f32)
        gate_in[at, :] = joined[:, WIDE:]
        if b == 3:
            edge = send(near.at[pl.ds(rows, BLK)], halo, hs.at[0], hs.at[1], (lax.rem(z + 1, depth), p))
            column_start(depth, w_out, out_all, zs.at[2], zr.at[2])
            column_start(depth, w_down.at[0], down_all, zs.at[3], zr.at[3])
    stage.done(N.w_in, N.normed_in, N.gate_in)
    stage.need(N.same)
    for b in (1, 2, 3, 0):
        if b == 0:
            edge.wait()
            near[:BLK, :] = halo[...]
        base = pair * b
        at = slice(base, base + pair)
        total = vecs[4:5] + vecs[0:1] * near[base + 13 : base + 13 + pair, :] * same[at, 0:1]
        for k in range(1, 4):
            total = total + vecs[k : k + 1] * near[base + 13 + k : base + 13 + k + pair, :] * same[at, k : k + 1]
        conv[at, :] = total
        value = (total * jax.nn.sigmoid(total)).astype(bf16)
        signal[at, :] = value
        x[2 * b : 2 * b + 2] = mm(value, w_sel[...]).reshape(2, count, 128)
    third = total_start(x, got, ss, rs)
    inner[...] = near[...].astype(bf16)
    stage.done(N.conv, N.signal, N.inner)
    fourth = total_share(x, got, third, sel_all, ts, us)
    local[5].wait()
    column_forward(depth, out_all, zs.at[2], zr.at[2])
    for c in fourth:
        c.wait()
    for b in range(CHIPS):
        at = slice(pair * b, pair * b + pair)
        chosen = sel_all[2 * b : 2 * b + 2].reshape(pair, 128)
        selected[at, :] = chosen
        step = contract_cols(chosen, w_step[...]) + vecs[5:6]
        step_pre[at, :] = step
        delta = softplus(step)
        dk[at, :WIDE] = delta + (1.0 - same[at, 2:3]) * RESET
        push[at, :WIDE] = delta * signal[at, :].astype(f32)
        dk[at, WIDE:] = jnp.zeros((pair, PAD), f32)
        push[at, WIDE:] = jnp.zeros((pair, PAD), f32)
        full = chosen.astype(f32)
        for i in range(pair // BLK):
            flipped = full[i * BLK : i * BLK + BLK].T
            mixes[b * (pair // BLK) + i] = flipped[RANK:SEL]
    stage.done(N.dk, N.push, N.step_pre, N.mixes, N.selected)
    local[2].wait()
    for c in across:
        c.wait_send()
    for c in more:
        c.wait()

    def onward():
        local[4].wait()
        column_forward(depth, down_all, zs.at[3], zr.at[3])

    def finish():
        column_finish(depth, w_out, out_all, zs.at[2], zr.at[2])
        column_finish(depth, w_down.at[0], down_all, zs.at[3], zr.at[3])

    return onward, finish


def front_part(cid, depth, **ins):
    count, rim, ch = ins[N.tok].shape[0], ins[N.in_proj].shape[0], ins[N.select].shape[0]
    low = ins[N.w_down].shape[1]
    rows = PLANE * count
    outs = dict(
        normed_in=made(rows, D, dtype=bf16),
        w_in=made(D, 2 * WIDE, dtype=bf16),
        w_route=made(D, 128, dtype=bf16),
        small=made(8, D),
        w_sel=made(WIDE, 128, dtype=bf16),
        w_step=made(WIDE, 128, dtype=bf16),
        vecs=made(8, WIDE),
        rate=made(STATE, WIDE + PAD),
        inner=made(rows + BLK, WIDE, dtype=bf16),
        gate_in=made(rows, WIDE, dtype=bf16),
        conv=made(rows, WIDE),
        signal=made(rows, WIDE, dtype=bf16),
        selected=made(rows, 128, dtype=bf16),
        mixes=made(rows // BLK, 2 * STATE, BLK),
        step_pre=made(rows, WIDE),
        dk=made(rows, WIDE + PAD),
        push=made(rows, WIDE + PAD),
        up_rows=made(PLANE, rim, EXPERTS * HID, dtype=bf16),
        down_all=made(depth, low, D, dtype=bf16),
        out_all=made(depth, ch, D, dtype=bf16),
    )
    scratch = (
        [
            pltpu.VMEM((PLANE, count, D), bf16),
            pltpu.VMEM((depth, PLANE, rim, 640), bf16),
            pltpu.VMEM((depth, ch, 384), bf16),
            pltpu.VMEM((D, 640), f32),
            pltpu.VMEM((WIDE, 384), f32),
            pltpu.VMEM((BLK + rows, WIDE), f32),
            pltpu.VMEM((BLK, WIDE), f32),
            pltpu.VMEM((PLANE, count, 128), f32),
            pltpu.VMEM((PLANE, count, 128), f32),
            pltpu.VMEM((PLANE, count, 128), bf16),
            pltpu.VMEM((PLANE, rim, 640), bf16),
            pltpu.VMEM((PLANE, rim, EXPERTS * HID), bf16),
            pltpu.VMEM((ch, 384), bf16),
            pltpu.VMEM((128, 128), f32),
        ]
        + [DMA((PLANE,))] * 6
        + [DMA((4, depth))] * 2
        + [DMA((2,))]
        + [DMA((PLANE,))] * 4
        + [DMA((6,))]
    )
    early = (
        N.normed_in, N.w_in, N.inner, N.gate_in, N.conv, N.signal, N.selected, N.mixes, N.step_pre, N.dk, N.push,
    )
    up_rows, cot = outs[N.up_rows], ins[N.cot]
    outs.update(
        scanned=made(rows, WIDE + PAD),
        states=made(rows, STATE, WIDE + PAD),
        ends=made(depth, STATE + 8, WIDE + PAD),
        up_early=made(depth, EARLY.stop, *up_rows.shape[1:], dtype=bf16),
        cot_all=made(PLANE, *cot.shape, dtype=bf16),
        down1=made(depth, low, D, dtype=bf16),
    )
    mine = len(scratch)
    scratch = (
        scratch
        + [pltpu.VMEM((2, count, STATE, WIDE + PAD), f32)]
        + [DMA((PLANE,))] * 2
        + [DMA((depth,))] * 2
        + [DMA((2, depth))] * 2
        + [DMA((2,)), DMA((3,))]
    )
    names = tuple(ins) + tuple(outs)

    def kernel(stage, *refs):
        ref = dict(zip(names, refs))
        held = refs[len(names) :]
        first = [ref[n] for n in names if n != N.cot][: len(ins) - 1 + 20]
        onward, finish = front_kernel(depth, stage, *first, *held[:mine])
        scan_kernel(
            depth,
            stage,
            onward,
            *(ref[n] for n in (N.dk, N.push, N.mixes, N.rate, N.up_rows, N.cot, N.w_down)),
            *(ref[n] for n in (N.scanned, N.states, N.ends, N.up_early, N.cot_all, N.down1)),
            *held[mine:],
        )
        finish()

    return staged_call(
        kernel, "front_part", cid, 110, ins, outs, scratch,
        late=(N.same, N.cot), early=early + (N.scanned,),
        away=(N.down_all, N.out_all, N.states, N.up_early, N.cot_all, N.down1),
    )


def folded(x):
    half = x.shape[0] // 2
    return jnp.concatenate([x[:half], x[half:]], axis=1).astype(bf16)


def back_kernel(
    depth, stage,
    g_push, g_step, g_mixes, g_rate, step_pre, signal, conv, inner, same, vecs, rate, selected, w_sel, w_step,
    mixed_grad, gate_grad, w_in, normed_in, tok, gain, grad_mid, sums, gup,
    tokens_out, in_own, up_own, sel_own, step_own, decay_own, taps_own, bias_own, offset_own, skip_own,
    norm_own, moe_own, router_own,
    in_out, up_out, pack_out, x, got, gsel, low, gc, halo, nearf, gj, part, sib, mix, far, gin, gin_got, own, pack, pack_got, row, row_got, sml, sml_got,
    hs, ss, rs, ts, us, near_s, near_r, away_s, away_r, zs, zr, cs, cr, ups, upr, ls,
):
    z, p = here()
    core = lax.rem(p, 2)
    chip = lax.div(p, 2)
    twin = (z, p + 1 - 2 * core)
    count = tok.shape[0]
    pair = 2 * count
    rows = PLANE * count
    ch = sel_own.shape[0]
    rim = in_own.shape[0]
    fs = up_own.shape[2] // (depth * PLANE)
    sent = []

    def down(i, src, dst):
        copies = []
        for k in range(1, depth):
            q = lax.rem(z + k, depth)
            copies.append(send(src.at[q], dst.at[k], zs.at[i, k], zr.at[i, k], (q, p)))
        return copies

    block = D // depth
    stage.need(N.normed_in, N.gate_grad)
    for q in range(depth):
        gin[1, q] = folded(contract_rows(normed_in[:, q * block : q * block + block], gate_grad[...]))
    gate_sent = down(3, gin.at[1], gin_got.at[1])
    stage.need(N.w_step, N.signal, N.step_pre)
    bias = jnp.zeros((1, WIDE), f32)
    for b in range(CHIPS):
        at = slice(pair * b, pair * b + pair)
        value = signal[at, :].astype(f32)
        grad = g_step[at, :WIDE] * (1.0 / LOG2E) + g_push[at, :WIDE] * value
        grad = grad * jax.nn.sigmoid(step_pre[at, :])
        bias = bias + jnp.sum(grad, axis=0, keepdims=True)
        low[at, :] = grad.astype(bf16)
        ranks = mm(low[at, :], w_step[...])
        for i in range(pair // BLK):
            mixed = g_mixes[b * (pair // BLK) + i]
            wide = jnp.concatenate(
                [jnp.zeros((RANK, BLK), f32), mixed, jnp.zeros((128 - SEL, BLK), f32)], axis=0
            ).T
            t = i * BLK
            x[2 * b + t // count, t % count : t % count + BLK, :] = ranks[t : t + BLK] + wide
    first = total_start(x, got, ss, rs)
    stage.need(N.selected, N.inner)
    keep = pltpu.make_async_copy(gup.at[p], up_out.at[p], ls)
    keep.start()
    grad_step_w = contract_rows(low[...], selected[...])
    nearf[...] = inner[...].astype(f32)
    second = total_share(x, got, first, gsel, ts, us)
    ups_sent = []
    for k in range(1, PLANE):
        q = lax.rem(p + k, PLANE)
        ups_sent.append(send(gup.at[q], up_out.at[p], ups.at[k], upr.at[k], (z, q)))
    for c in second:
        c.wait()
    stage.need(N.conv, N.same, N.w_sel)
    taps = [jnp.zeros((1, WIDE), f32)] * 4
    conv_bias = jnp.zeros((1, WIDE), f32)
    for b in range(CHIPS):
        base = pair * b
        at = slice(base, base + pair)
        delta = softplus(step_pre[at, :])
        grad = mixed_grad[at, :WIDE] * vecs[6:7] + g_push[at, :WIDE] * delta
        grad = grad + contract_cols(gsel[2 * b : 2 * b + 2].reshape(pair, 128), w_sel[...])
        c = conv[at, :]
        sig = jax.nn.sigmoid(c)
        grad = grad * (sig * (1.0 + c * (1.0 - sig)))
        gc[at, :] = grad
        if b == 0:
            edge = send(gc.at[pl.ds(0, BLK)], halo, hs.at[0], hs.at[1], (lax.rem(z + depth - 1, depth), p))
        conv_bias = conv_bias + jnp.sum(grad, axis=0, keepdims=True)
        for k in range(4):
            taps[k] = taps[k] + jnp.sum(
                grad * nearf[base + 13 + k : base + 13 + k + pair, :] * same[at, k : k + 1], axis=0, keepdims=True
            )
    stage.need(N.w_in, N.tok, N.grad_mid)
    for b in range(CHIPS):
        base = pair * b
        if b == CHIPS - 1:
            edge.wait()
            gc[rows : rows + BLK, :] = halo[...]
        total = jnp.zeros((pair, WIDE), f32)
        for k in range(4):
            off = slice(base + 3 - k, base + 3 - k + pair)
            total = total + gc[off, :] * vecs[k : k + 1] * same[off, k : k + 1]
        gj[base : base + pair, :WIDE] = total.astype(bf16)
        gj[base : base + pair, WIDE:] = gate_grad[base : base + pair, :]
    for q in range(depth):
        gin[0, q] = folded(contract_rows(normed_in[:, q * block : q * block + block], gj[:, :WIDE]))
    in_sent = down(0, gin.at[0], gin_got.at[0])
    near = {}
    for k in (1, 2, 3, 0):
        q = lax.rem(chip + k, CHIPS)
        at = pl.ds(pl.multiple_of(q * pair, pair), pair)
        part[k] = contract_cols(gj[at, :], w_in[...]).astype(bf16).reshape(2, count, D)
        near[k] = send(part.at[k, 1 - core], sib.at[k], near_s.at[k], near_r.at[k], twin)
    away = []
    for k in range(1, CHIPS):
        near[k].wait_recv()
        mix[k] = (part[k, core].astype(f32) + sib[k].astype(f32)).astype(bf16)
        away.append(
            send(mix.at[k], far.at[k], away_s.at[k], away_r.at[k], (z, lax.rem(p + 2 * k, PLANE)))
        )
    row[...] = jnp.zeros_like(row)
    row[0:STATE, :] = g_rate[...] * rate[...]
    for k in range(4):
        row[STATE + k : STATE + k + 1, :WIDE] = taps[k]
    row[STATE + 4 : STATE + 5, :WIDE] = conv_bias
    row[STATE + 5 : STATE + 6, :WIDE] = bias
    row[STATE + 6 : STATE + 7, :WIDE] = sums[3:4, :WIDE]
    side = row[...].T
    grad_sel_w = contract_rows(signal[...], gsel[...].reshape(rows, 128))
    for q in range(depth):
        cut = slice(q * ch, q * ch + ch)
        pack[q, :, :128] = grad_sel_w[cut].astype(bf16)
        pack[q, :, 128:256] = grad_step_w[cut].astype(bf16)
        pack[q, :, 256:] = side[cut].astype(bf16)
    pack_sent = down(1, pack, pack_got)
    near[0].wait_recv()
    total = part[0, core].astype(f32) + sib[0].astype(f32)
    for k in range(1, CHIPS):
        away[k - 1].wait_recv()
        total = total + far[k].astype(f32)
    values = tok[...].astype(f32)
    scale = lax.rsqrt(jnp.mean(values * values, axis=-1, keepdims=True) + epsilon)
    normed = values * scale
    grad_normed = total * gain[0:1]
    mean = jnp.mean(grad_normed * normed, axis=-1, keepdims=True)
    tokens_out[...] = (scale * (grad_normed - normed * mean) + grad_mid[...]).astype(bf16)
    stage.done(N.tokens_out)
    ours = jnp.concatenate(
        [jnp.sum(total * normed, axis=0, keepdims=True), sums[0:3, :], jnp.zeros((4, D), f32)], axis=0
    )
    for q in range(depth):
        sml[q] = ours[:, q * block : q * block + block]
    sml_sent = down(2, sml, sml_got)
    for h, copies in ((1, gate_sent), (0, in_sent)):
        for c in copies:
            c.wait_recv()
        total = gin[h, z].astype(f32)
        for k in range(1, depth):
            total = total + gin_got[h, k].astype(f32)
        total = jnp.concatenate([total[:, :WIDE], total[:, WIDE:]], axis=0)
        for q in range(PLANE):
            own[q, :, h * WIDE : h * WIDE + WIDE] = total[q * rim : q * rim + rim].astype(bf16)
    across = []
    for k in range(1, PLANE):
        q = lax.rem(p + k, PLANE)
        across.append(send(own.at[q], in_out.at[p], cs.at[0, k], cr.at[0, k], (z, q)))
    in_out[p] = own[p]
    for c in sml_sent:
        c.wait_recv()
    total = sml[z]
    for k in range(1, depth):
        total = total + sml_got[k]
    sml_got[0] = total
    for k in range(1, PLANE):
        q = lax.rem(p + k, PLANE)
        across.append(send(sml_got.at[0], row_got.at[k], cs.at[1, k], cr.at[1, k], (z, q)))
    for c in pack_sent:
        c.wait_recv()
    total = pack[z].astype(f32)
    for k in range(1, depth):
        total = total + pack_got[k].astype(f32)
    sel_own[...] = total[:, :SEL]
    pack_out[...] = jnp.zeros_like(pack_out)
    pack_out[:ch, :] = total[:, 128:256]
    columns = pack_out[...].T
    step_own[...] = columns[:RANK, :ch]
    pack_out[:ch, :32] = total[:, 256:]
    columns = pack_out[...].T
    decay_own[...] = columns[:STATE, :ch]
    taps_own[...] = columns[STATE : STATE + 4, :ch]
    bias_own[...] = columns[STATE + 4 : STATE + 5, :ch]
    offset_own[...] = columns[STATE + 5 : STATE + 6, :ch]
    skip_own[...] = columns[STATE + 6 : STATE + 7, :ch]
    for c in ups_sent:
        c.wait()
    keep.wait()
    for q in range(PLANE):
        for i in range(EXPERTS * depth):
            start = ((i % depth) * PLANE + q) * fs
            up_own[:, i // depth, start : start + fs] = up_out[q, :, i * fs : i * fs + fs].astype(f32)
    stage.done(N.up_own)
    for c in across:
        c.wait()
    for q in range(PLANE):
        for i in range(2 * depth):
            start = (i // depth) * DI + ((i % depth) * PLANE + q) * ch
            in_own[:, start : start + ch] = in_out[q, :, i * ch : i * ch + ch].astype(f32)
    total = sml_got[0]
    for k in range(1, PLANE):
        total = total + row_got[k]
    for q in range(PLANE):

        @pl.when(p == q)
        def _():
            cut = total[:, q * rim : q * rim + rim]
            norm_own[...] = cut[0:1]
            moe_own[...] = cut[1:2]
            router_own[...] = cut[2:4]

    for c in list(near.values()) + away + gate_sent + in_sent + pack_sent + sml_sent:
        c.wait_send()


def back_part(cid, depth, rim, ch, **ins):
    count = ins[N.tok].shape[0]
    rows, wide = ins[N.dk].shape
    block = D // depth
    gup, gout = ins[N.gup], ins[N.gout]
    outs = dict(
        tokens_out=made(count, D, dtype=bf16),
        in_own=made(rim, 2 * DI),
        up_own=made(rim, EXPERTS, FF),
        sel_own=made(ch, SEL),
        step_own=made(RANK, ch),
        decay_own=made(STATE, ch),
        taps_own=made(4, ch),
        bias_own=made(1, ch),
        offset_own=made(1, ch),
        skip_own=made(1, ch),
        norm_own=made(1, rim),
        moe_own=made(1, rim),
        router_own=made(2, rim),
        out_own=made(*gout.shape[1:]),
    )
    scratch = (
        [
            pltpu.VMEM((PLANE, rim, 2 * WIDE), bf16),
            pltpu.VMEM((PLANE, rim, EXPERTS * HID), bf16),
            pltpu.VMEM((128, 128), f32),
            pltpu.VMEM((PLANE, count, 128), f32),
            pltpu.VMEM((PLANE, count, 128), f32),
            pltpu.VMEM((PLANE, count, 128), bf16),
            pltpu.VMEM((rows, WIDE), bf16),
            pltpu.VMEM((rows + BLK, WIDE), f32),
            pltpu.VMEM((BLK, WIDE), f32),
            pltpu.VMEM((rows + BLK, WIDE), f32),
            pltpu.VMEM((rows, 2 * WIDE), bf16),
            pltpu.VMEM((CHIPS, 2, count, D), bf16),
            pltpu.VMEM((CHIPS, count, D), bf16),
            pltpu.VMEM((CHIPS, count, D), bf16),
            pltpu.VMEM((CHIPS, count, D), bf16),
            pltpu.VMEM((2, depth, block // 2, 2 * WIDE), bf16),
            pltpu.VMEM((2, depth, block // 2, 2 * WIDE), bf16),
            pltpu.VMEM((PLANE, rim, 2 * WIDE), bf16),
            pltpu.VMEM((depth, ch, 288), bf16),
            pltpu.VMEM((depth, ch, 288), bf16),
            pltpu.VMEM((2 * STATE, WIDE + PAD), f32),
            pltpu.VMEM((PLANE, 8, block), f32),
            pltpu.VMEM((depth, 8, block), f32),
            pltpu.VMEM((depth, 8, block), f32),
            DMA((2,)),
        ]
        + [DMA((PLANE,))] * 4
        + [DMA((CHIPS,))] * 4
        + [DMA((4, depth))] * 2
        + [DMA((2, PLANE))] * 2
        + [DMA((PLANE,))] * 2
        + [DMA]
    )
    mine = len(scratch)
    scratch = (
        scratch
        + [
            pltpu.VMEM((2, count, STATE, wide), f32),
            pltpu.VMEM((depth, STATE, wide), f32),
            pltpu.VMEM(gup.shape, bf16),
            pltpu.VMEM(gout.shape, bf16),
        ]
        + [DMA((depth,))] * 2
        + [DMA((3, depth))] * 2
        + [DMA((2,))]
        + [
            pltpu.VMEM((rows, wide), f32),
            pltpu.VMEM((rows, wide), f32),
            pltpu.VMEM(ins[N.sel].shape, f32),
            pltpu.VMEM((STATE, wide), f32),
            pltpu.VMEM((PLANE, rim, EXPERTS * HID), bf16),
        ]
    )
    names = tuple(ins) + tuple(outs)

    def kernel(stage, *refs):
        ref = dict(zip(names, refs))
        held = refs[len(names) :]
        g_push, g_step, g_sel, g_rate, up_part = held[-5:]
        finish = adjoint_kernel(
            depth,
            stage,
            lambda: None,
            *(ref[n] for n in (N.dk, N.push, N.grad, N.sel, N.states, N.rate, N.ends, N.gup, N.gout)),
            g_push,
            g_step,
            g_sel,
            g_rate,
            up_part,
            ref[N.out_own],
            *held[mine:-5],
        )
        back_kernel(
            depth,
            stage,
            g_push,
            g_step,
            g_sel,
            g_rate,
            *(
                ref[n]
                for n in (
                    N.step_pre, N.signal, N.conv, N.inner, N.same, N.vecs, N.rate, N.selected, N.w_sel, N.w_step,
                    N.grad, N.gate_grad, N.w_in, N.normed_in, N.tok, N.gain, N.grad_mid, N.sums,
                )
            ),
            up_part,
            *(ref[n] for n in outs if n != N.out_own),
            *held[:mine],
        )
        finish()

    late = (
        N.gup, N.sel, N.dk, N.grad, N.push, N.gout, N.normed_in, N.gate_grad, N.w_step, N.signal, N.step_pre,
        N.selected, N.inner, N.conv, N.same, N.w_sel, N.w_in, N.tok, N.grad_mid,
    )
    return staged_call(
        kernel, "back_part", cid, 120, ins, outs, scratch,
        late=late, early=(N.tokens_out, N.up_own), raw=(N.states,),
    )


def middle_kernel(
    depth, stage,
    scanned, signal, gate_in, skip, w_out, tok, cot_all, up_early, up_rows, down0, down1, w_router, rows_in, picks,
    output, grad_mid, mixed_grad, gate_grad, grad_out, grad_up, down_own, sums,
    gated, part, sib, mix, far, routed_all, marks_all, hidden_all, pre_all, slot_all, back_all,
    up_late, w_up, wide, grad_down, down_got,
    near_s, near_r, away_s, away_r, gs, gr, zs, zr, ds, dr, ls,
):
    z, p = here()
    core = lax.rem(p, 2)
    chip = lax.div(p, 2)
    twin = (z, p + 1 - 2 * core)
    count = tok.shape[0]
    pair = 2 * count

    def chip_at(k):
        return lax.rem(chip + k, CHIPS)

    def rows_of(q):
        return pl.ds(pl.multiple_of(q * pair, pair), pair)

    def near(i, k):
        return remote(part.at[i, k, 1 - core], sib.at[i, k], near_s.at[i, k], near_r.at[i, k], twin)

    def away(i, k):
        return remote(
            mix.at[i, k], far.at[i, k], away_s.at[i, k], away_r.at[i, k], (z, lax.rem(p + 2 * k, PLANE))
        )

    def pass_away(i, k):
        near(i, k).wait_recv()
        mix[i, k] = (part[i, k, core].astype(f32) + sib[i, k].astype(f32)).astype(bf16)
        away(i, k).start()

    def gathered(i):
        near(i, 0).wait_recv()
        total = part[i, 0, core].astype(f32) + sib[i, 0].astype(f32)
        for k in range(1, CHIPS):
            away(i, k).wait_recv()
            total = total + far[i, k].astype(f32)
        return total

    def shared(i, ref, k):
        return remote(ref.at[p], ref.at[p], gs.at[i, k], gr.at[i, k], (z, lax.rem(p + 2 * k, PLANE)))

    def onward(i, ref, k):
        src = lax.rem(p + 2 * k, PLANE)
        return remote(ref.at[src], ref.at[src], gs.at[i, CHIPS + k], gr.at[i, CHIPS + k], twin)

    def arrived(k, refs):
        @pl.when(k == 0)
        def _():
            for i, ref in refs:
                remote(ref.at[p], ref.at[p], gs.at[i, 0], gr.at[i, 0], twin).wait_recv()

        @pl.when(k > 0)
        def _():
            for i, ref in refs:
                shared(i, ref, CHIPS - k).wait_recv()
                onward(i, ref, k).start()
            for i, ref in refs:
                onward(i, ref, k).wait_recv()

    greet(True, depth)
    stage.need(N.up_rows)
    local = pltpu.make_async_copy(up_rows.at[LATE], up_late.at[z], ls)
    local.start()
    column_start(depth, up_rows.at[LATE], up_late, zs, zr)
    stage.need(N.w_out, N.scanned, N.signal, N.gate_in)
    @pl.loop(0, CHIPS)
    def _(turn):
        k = lax.rem(turn + 1, CHIPS)
        q = chip_at(k)
        at = rows_of(q)
        pre = scanned[at, :WIDE] + skip[6:7] * signal[at, :].astype(f32)
        inward = gate_in[at, :].astype(f32)
        gated[at, :] = (pre * (inward * jax.nn.sigmoid(inward))).astype(bf16)
        part[0, k] = mm(gated[at, :], w_out[...]).astype(bf16).reshape(2, count, D)
        near(0, k).start()

    for k in range(1, CHIPS):
        pass_away(0, k)
    branch = gathered(0)

    stage.need(N.tok, N.w_router, N.up_early, N.cot_all, N.down0, N.down1)
    gain, router0, router1 = rows_in[1:2], rows_in[2:3], rows_in[3:4]
    middle = tok[...].astype(f32) + branch
    scale = lax.rsqrt(jnp.mean(middle * middle, axis=-1, keepdims=True) + epsilon)
    normed = middle * scale
    routed = (normed * gain).astype(bf16)
    routed_all[p] = routed
    logits = mm(routed, w_router[...])
    l0, l1 = logits[:, 66:67], logits[:, 67:68]
    top = jnp.maximum(l0, l1)
    e0, e1 = jnp.exp(l0 - top), jnp.exp(l1 - top)
    p0, p1 = e0 / (e0 + e1), e1 / (e0 + e1)
    taken = jnp.broadcast_to(picks[...].astype(f32), (count, count)).T[:, 0:1]
    c0 = (taken == 0).astype(f32)
    c1 = (taken == 1).astype(f32)
    chosen = jnp.where(lax.broadcasted_iota(jnp.int32, (count, 128), 1) == 0, c0, c1).astype(bf16)
    before = lax.broadcasted_iota(jnp.int32, (count, count), 0) >= lax.broadcasted_iota(
        jnp.int32, (count, count), 1
    )
    places = mm(before.astype(f32).astype(bf16), chosen)
    s0 = c0 * (places[:, 0:1] <= CAP).astype(f32)
    s1 = c1 * (places[:, 1:2] <= CAP).astype(f32)
    gate = p0 * c0 + p1 * c1
    kept = s0 + s1
    weight = gate * kept
    lane = lax.broadcasted_iota(jnp.int32, (count, 128), 1)
    marks_all[p] = jnp.where(lane == 0, weight, jnp.where(lane == 1, s0, s1)).T[:8]
    share_start(routed_all.at[p], routed_all, gs.at[0], gr.at[0])
    share_start(marks_all.at[p], marks_all, gs.at[1], gr.at[1])
    local.wait()
    column_forward(depth, up_late, zs, zr)
    column_finish(depth, up_rows.at[LATE], up_late, zs, zr)
    rim = up_rows.shape[1]
    block = PLANE * rim
    for k in range(depth):
        for q in range(PLANE):
            source = up_early[k, q] if q < EARLY.stop else up_late[k, q - EARLY.stop]
            wide[q * rim : q * rim + rim, :] = source.astype(f32)
        w_up[k * block : k * block + block, :] = wide[...].astype(bf16)

    odd = lax.broadcasted_iota(jnp.int32, (1, EXPERTS * HID), 1) >= HID

    @pl.loop(0, CHIPS)
    def _(k):
        q = chip_at(k)
        arrived(k, ((0, routed_all), (1, marks_all)))

        @pl.when(k > 1)
        def _():
            pass_away(1, k - 1)
            pass_away(2, k - 1)

        both = pl.ds(2 * q, 2)
        marks = [
            jnp.concatenate([marks_all[2 * q + i], jnp.zeros((120, count), f32)], axis=0).T for i in range(2)
        ]
        marks = jnp.concatenate(marks, axis=0)
        mask = jnp.where(odd, marks[:, 2:3], marks[:, 1:2])
        hidden = mm(routed_all[both].reshape(pair, D), w_up[...])
        slot = (cot_all[rows_of(q), :].astype(f32) * marks[:, 0:1]).astype(bf16)
        slot_all[q] = slot
        square = hidden * hidden
        bend = jnp.tanh(GELU * hidden * (1.0 + 0.044715 * square))
        units = (0.5 * hidden * (1.0 + bend) * mask).astype(bf16)
        hidden_all[q] = units
        slope = 0.5 * (1.0 + bend) + 0.5 * GELU * hidden * (1.0 - bend * bend) * (1.0 + 3 * 0.044715 * square)
        grad = jnp.concatenate([contract_cols(slot, down0[...]), contract_cols(slot, down1[...])], axis=1)
        grad = (slope * grad * mask).astype(bf16)
        pre_all[q] = grad
        made = mm(units[:, :HID], down0[...]) + mm(units[:, HID:], down1[...])
        part[1, k] = made.astype(bf16).reshape(2, count, D)
        near(1, k).start()
        part[2, k] = contract_cols(grad, w_up[...]).astype(bf16).reshape(2, count, D)
        near(2, k).start()

    pass_away(1, CHIPS - 1)
    pass_away(2, CHIPS - 1)
    every = CHIPS * pair
    fs = HID // depth
    for c in range(0, D, 384):
        for e in range(EXPERTS):
            made = contract_rows(
                hidden_all[:, :, e * HID : e * HID + HID].reshape(every, HID),
                slot_all[:, :, c : c + 384].reshape(every, 384),
            )
            for k in range(depth):
                grad_down[k, e, :, c : c + 384] = made[k * fs : k * fs + fs].astype(bf16)
    down = []
    for k in range(1, depth):
        q = lax.rem(z + k, depth)
        down.append(send(grad_down.at[q], down_got.at[k], ds.at[k], dr.at[k], (q, p)))
    expert_tok = gathered(1)
    slot_back = gathered(2)

    up = cot_all[pl.ds(pl.multiple_of(p * count, count), count), :].astype(f32)
    output[...] = (middle + weight * expert_tok).astype(bf16)
    stage.done(N.output)
    pull = jnp.sum(up * expert_tok, axis=-1, keepdims=True) * kept * gate
    g0, g1 = pull * (c0 - p0), pull * (c1 - p1)
    grad_routed = slot_back + g0 * router0 + g1 * router1
    routed = routed.astype(f32)
    sum0 = jnp.sum(grad_routed * normed, axis=0, keepdims=True)
    sum1 = jnp.sum(routed * g0, axis=0, keepdims=True)
    sum2 = jnp.sum(routed * g1, axis=0, keepdims=True)
    grad_normed = grad_routed * gain
    inner = jnp.mean(grad_normed * normed, axis=-1, keepdims=True)
    total = scale * (grad_normed - normed * inner) + up
    grad_mid[...] = total
    stage.done(N.grad_mid)
    back_all[p] = total.astype(bf16)
    share_start(back_all.at[p], back_all, gs.at[2], gr.at[2])
    for c in range(0, D, 384):
        grad_up[c : c + 384, :] = contract_rows(
            routed_all[:, :, c : c + 384].reshape(every, 384), pre_all[...].reshape(every, EXPERTS * HID)
        ).astype(bf16)
    stage.done(N.grad_up)

    sums[...] = jnp.zeros_like(sums)
    sums[0:1], sums[1:2], sums[2:3] = sum0, sum1, sum2

    @pl.loop(0, CHIPS)
    def _(k):
        q = chip_at(k)
        arrived(k, ((2, back_all),))
        at = rows_of(q)
        grad = contract_cols(back_all[pl.ds(2 * q, 2)].reshape(pair, D), w_out[...])
        inward = gate_in[at, :].astype(f32)
        sig = jax.nn.sigmoid(inward)
        act = inward * sig
        through = grad * act
        sums[3:4, :WIDE] += jnp.sum(through * signal[at, :].astype(f32), axis=0, keepdims=True)
        mixed_grad[at, :WIDE] = through
        mixed_grad[at, WIDE:] = jnp.zeros((pair, PAD), f32)
        pre = scanned[at, :WIDE] + skip[6:7] * signal[at, :].astype(f32)
        gate_grad[at, :] = (grad * pre * (sig * (1.0 + inward * (1.0 - sig)))).astype(bf16)
    stage.done(N.mixed_grad, N.gate_grad)
    for c in range(0, D, 384):
        grad_out[:, c : c + 384] = contract_rows(
            gated[...], back_all[:, :, c : c + 384].reshape(every, 384)
        ).astype(bf16)
    for c in down:
        c.wait_recv()
    total = grad_down[z].astype(f32)
    for k in range(1, depth):
        total = total + down_got[k].astype(f32)
    down_own[...] = total
    for c in down:
        c.wait_send()
    for i in range(3):
        for k in range(CHIPS):
            near(i, k).wait_send()
            if k:
                away(i, k).wait_send()
    for i, ref in ((0, routed_all), (1, marks_all), (2, back_all)):
        remote(ref.at[p], ref.at[p], gs.at[i, 0], gr.at[i, 0], twin).wait_send()
        for k in range(1, CHIPS):
            shared(i, ref, k).wait_send()
            onward(i, ref, k).wait_send()


def middle_part(cid, depth, **ins):
    count, rows, rim = ins[N.tok].shape[0], ins[N.cot_all].shape[0], ins[N.up_rows].shape[1]
    wide = EXPERTS * HID
    block = (CHIPS, count, D)
    outs = dict(
        output=made(count, D, dtype=bf16),
        grad_mid=made(count, D),
        mixed_grad=made(rows, WIDE + PAD),
        gate_grad=made(rows, WIDE, dtype=bf16),
        grad_out=made(WIDE, D, dtype=bf16),
        grad_up=made(D, wide, dtype=bf16),
        down_own=made(EXPERTS, HID // depth, D),
        sums=made(8, D),
    )
    scratch = (
        [
            pltpu.VMEM((rows, WIDE), bf16),
            pltpu.VMEM((3, CHIPS, 2, count, D), bf16),
            pltpu.VMEM((3,) + block, bf16),
            pltpu.VMEM((3,) + block, bf16),
            pltpu.VMEM((3,) + block, bf16),
            pltpu.VMEM((PLANE, count, D), bf16),
            pltpu.VMEM((PLANE, 8, count), f32),
            pltpu.VMEM((CHIPS, 2 * count, wide), bf16),
            pltpu.VMEM((CHIPS, 2 * count, wide), bf16),
            pltpu.VMEM((CHIPS, 2 * count, D), bf16),
            pltpu.VMEM((PLANE, count, D), bf16),
            pltpu.VMEM((depth, LATE.stop - LATE.start, rim, wide), bf16),
            pltpu.VMEM((D, wide), bf16),
            pltpu.VMEM((PLANE * rim, wide), f32),
            pltpu.VMEM((depth, EXPERTS, HID // depth, D), bf16),
            pltpu.VMEM((depth, EXPERTS, HID // depth, D), bf16),
        ]
        + [DMA((3, CHIPS))] * 4
        + [DMA((3, PLANE))] * 2
        + [DMA((depth,))] * 4
        + [DMA]
    )
    late = (
        N.up_rows, N.w_out, N.scanned, N.signal, N.gate_in, N.tok, N.w_router, N.up_early, N.cot_all, N.down0, N.down1,
    )
    return staged_call(
        functools.partial(middle_kernel, depth), "middle_part", cid, 75, ins, outs, scratch,
        late=late, early=(N.output, N.grad_mid, N.grad_up, N.mixed_grad, N.gate_grad),
    )


def tree(parts):
    row = lax.broadcasted_iota(jnp.int32, parts[0].shape, 0)
    for step in (1, 2, 4):
        low = (row // step) % 2 == 0
        parts = [
            jnp.where(low, a, b) + pltpu.roll(jnp.where(low, b, a), step, 0)
            for a, b in zip(parts[::2], parts[1::2])
        ]
    return parts[0]


def lane_tiles(x):
    total = x[:, :128]
    for k in range(128, x.shape[1], 128):
        total = total + x[:, k : k + 128]
    return total


def spread(ref, i):
    return jnp.broadcast_to(ref[pl.ds(i, 1), :], (8, ref.shape[1]))


HALVES = (slice(0, 8), slice(8, 16))


def ends_loop(dk, push, sel, slope):
    def block(b, carry):
        hidden, acc = list(carry[:2]), carry[2]
        base = pl.multiple_of(b * BLK, BLK)
        w = sel[b, :STATE]
        for t in range(BLK):
            d, u = spread(dk, base + t), spread(push, base + t)
            for k, h in enumerate(HALVES):
                hidden[k] = jnp.exp2(d * slope[k]) * hidden[k] + w[h, t : t + 1] * u
            acc = acc + d
        return hidden[0], hidden[1], acc

    zero = jnp.zeros(slope[0].shape, f32)
    return lax.fori_loop(0, dk.shape[0] // BLK, block, (zero, zero, zero))


def scan_kernel(
    depth, stage, onward,
    dk, push, sel, rate, up_rows, cot, w_down,
    out, states, ends, up_all, cot_all, down_all,
    slots, gs, gr, es, er, zs, zr, ks, ls,
):
    z, p = here()
    tile = slots.shape[1]
    tiles = dk.shape[0] // tile
    local = [
        pltpu.make_async_copy(up_rows.at[EARLY], up_all.at[z], ls.at[0]),
        pltpu.make_async_copy(cot, cot_all.at[p], ls.at[1]),
        pltpu.make_async_copy(w_down.at[1], down_all.at[z], ls.at[2]),
    ]
    stage.need(N.cot)
    for c in local:
        c.start()
    first = share_start(cot, cot_all, gs, gr)
    slope = [rate[h, :] * LOG2E for h in HALVES]
    one, two, acc = ends_loop(dk, push, sel, slope)
    ends[z, :8], ends[z, 8:16], ends[z, 16:] = one, two, acc
    mine = []
    for k in range(1, depth):
        mine.append(send(ends.at[z], ends.at[z], es.at[k], er.at[k], (lax.rem(z + k, depth), p)))
    column_start(depth, up_rows.at[EARLY], up_all, zs.at[0], zr.at[0])
    column_start(depth, w_down.at[1], down_all, zs.at[1], zr.at[1])
    onward()
    second = share_forward(cot_all, first, gs, gr)
    for c in local:
        c.wait()
    for c in mine:
        c.wait_recv()
    hidden = [jnp.zeros(slope[0].shape, f32)] * 2
    for k in range(depth - 1):
        for i, h in enumerate(HALVES):
            hidden[i] = jnp.where(k < z, jnp.exp2(ends[k, 16:] * slope[i]) * hidden[i] + ends[k, h], hidden[i])

    def stored(i, slot):
        return pltpu.make_async_copy(
            slots.at[slot], states.at[pl.ds(pl.multiple_of(i * tile, tile), tile)], ks.at[slot]
        )

    def piece(i, carry):
        slot = lax.rem(i, 2)

        @pl.when(i >= 2)
        def _():
            stored(i - 2, slot).wait()

        def block(j, carry):
            hidden = list(carry)
            b = i * (tile // BLK) + j
            base = pl.multiple_of(b * BLK, BLK)
            inside = j * BLK
            w, r = sel[b, :STATE], sel[b, STATE:]
            parts = []
            for t in range(BLK):
                d, u = spread(dk, base + t), spread(push, base + t)
                line = None
                for k, h in enumerate(HALVES):
                    hidden[k] = jnp.exp2(d * slope[k]) * hidden[k] + w[h, t : t + 1] * u
                    slots[slot, inside + t, h] = hidden[k]
                    y = r[h, t : t + 1] * hidden[k]
                    line = y if line is None else line + y
                parts.append(line)
                if len(parts) == 8:
                    out[pl.ds(pl.multiple_of(base + t - 7, 8), 8), :] = tree(parts)
                    parts = []
            return tuple(hidden)

        carry = lax.fori_loop(0, tile // BLK, block, carry)
        stored(i, slot).start()
        return carry

    carry = lax.fori_loop(0, tiles - 3, piece, tuple(hidden))
    column_forward(depth, up_all, zs.at[0], zr.at[0])
    lax.fori_loop(tiles - 3, tiles, piece, carry)
    stage.done(N.scanned)
    column_forward(depth, down_all, zs.at[1], zr.at[1])
    for i in (tiles - 2, tiles - 1):
        stored(i, i % 2).wait()
    share_finish(first, second)
    column_finish(depth, up_rows.at[EARLY], up_all, zs.at[0], zr.at[0])
    column_finish(depth, w_down.at[1], down_all, zs.at[1], zr.at[1])
    for c in mine:
        c.wait_send()


def message_loop(dk, grad, sel, slope):
    blocks = dk.shape[0] // BLK

    def block(i, carry):
        message = list(carry)
        b = blocks - 1 - i
        base = pl.multiple_of(b * BLK, BLK)
        r = sel[b, STATE:]
        for t in reversed(range(BLK)):
            d, g = spread(dk, base + t), spread(grad, base + t)
            for k, h in enumerate(HALVES):
                message[k] = jnp.exp2(d * slope[k]) * (r[h, t : t + 1] * g + message[k])
        return tuple(message)

    zero = jnp.zeros(slope[0].shape, f32)
    return lax.fori_loop(0, blocks, block, (zero, zero))


def adjoint_kernel(
    depth, stage, after,
    dk, push, grad, sel, states, rate, ends, gup, gout,
    g_push, g_step, g_sel, g_rate, up_own, out_own,
    slots, notes, up_got, out_got, es, er, zs, zr, ks,
):
    z, p = here()
    tile = slots.shape[1]
    tiles = dk.shape[0] // tile
    per = tile // BLK

    def fetch(i, slot):
        return pltpu.make_async_copy(
            states.at[pl.ds(pl.multiple_of(i * tile, tile), tile)], slots.at[slot], ks.at[slot]
        )

    fetch(tiles - 1, 0).start()
    fetch(tiles - 2, 1).start()
    greet(True, depth)
    first = gup.shape[1] // 64 * 16
    pieces = (pl.ds(0, first), pl.ds(first, gup.shape[1] - first))
    stage.need(N.gup)
    down = []
    for k in range(1, depth):
        q = lax.rem(z + k, depth)
        down.append(
            send(gup.at[q, pieces[0]], up_got.at[k, pieces[0]], zs.at[1, k], zr.at[1, k], (q, p))
        )
    stage.need(N.sel, N.dk, N.grad)
    slope = [rate[h, :] * LOG2E for h in HALVES]
    notes[z, :8], notes[z, 8:] = message_loop(dk, grad, sel, slope)
    mine = []
    for k in range(1, depth):
        mine.append(send(notes.at[z], notes.at[z], es.at[k], er.at[k], (lax.rem(z + k, depth), p)))
    stage.need(N.push)
    for k in range(1, depth):
        q = lax.rem(z + k, depth)
        down.append(
            send(gup.at[q, pieces[1]], up_got.at[k, pieces[1]], zs.at[0, k], zr.at[0, k], (q, p))
        )
    stage.need(N.gout)
    for k in range(1, depth):
        q = lax.rem(z + k, depth)
        down.append(send(gout.at[q], out_got.at[k], zs.at[2, k], zr.at[2, k], (q, p)))
    for c in mine:
        c.wait_recv()
    message = [jnp.zeros(slope[0].shape, f32)] * 2
    for k in range(depth - 1, 0, -1):
        for i, h in enumerate(HALVES):
            message[i] = jnp.where(k > z, notes[k, h] + jnp.exp2(ends[k, 16:] * slope[i]) * message[i], message[i])
    lane = lax.broadcasted_iota(jnp.int32, (STATE, 128), 1)
    ones = jnp.ones((128, 128), bf16)

    def piece(n, carry):
        i = tiles - 1 - n
        slot = lax.rem(n, 2)
        fetch(i, slot).wait()

        def block(m, carry):
            message, acc = list(carry[:2]), list(carry[2:])
            j = per - 1 - m
            b = i * per + j
            base = pl.multiple_of(b * BLK, BLK)
            inside = j * BLK
            w, r = sel[b, :STATE], sel[b, STATE:]
            pushes, steps = [], []
            reads, writes = [None] * (2 * BLK), [None] * (2 * BLK)
            for t in reversed(range(BLK)):
                d, u, g = spread(dk, base + t), spread(push, base + t), spread(grad, base + t)
                plain = jnp.where(d < RESET, d, 0.0)
                to_push = to_step = None
                for k, h in enumerate(HALVES):
                    wt = w[h, t : t + 1]
                    hidden = slots[slot, inside + t, h]
                    total = r[h, t : t + 1] * g + message[k]
                    reads[2 * t + k] = lane_tiles(hidden * g)
                    writes[2 * t + k] = lane_tiles(total * u)
                    x = total * wt
                    carried = total * (hidden - wt * u)
                    y = carried * slope[k]
                    to_push = x if k == 0 else to_push + x
                    to_step = y if k == 0 else to_step + y
                    acc[k] = acc[k] + carried * plain
                    message[k] = jnp.exp2(d * slope[k]) * total
                pushes.insert(0, to_push)
                steps.insert(0, to_step)
                if len(pushes) == 8:
                    at = pl.ds(pl.multiple_of(base + t, 8), 8)
                    g_push[at, :] = tree(pushes)
                    g_step[at, :] = tree(steps)
                    pushes, steps = [], []
            for j2, quantity in enumerate((writes, reads)):
                x = jnp.concatenate(quantity, axis=0)
                high = x.astype(bf16)
                low = (x - high.astype(f32)).astype(bf16)
                sums = jnp.dot(high, ones, preferred_element_type=f32)
                sums = sums + jnp.dot(low, ones, preferred_element_type=f32)
                kept = jnp.zeros((STATE, 128), f32)
                for t in range(BLK):
                    kept = jnp.where(lane == t, sums[STATE * t : STATE * t + STATE], kept)
                g_sel[b, STATE * j2 : STATE * j2 + STATE] = kept[:, :BLK]
            return message[0], message[1], acc[0], acc[1]

        carry = lax.fori_loop(0, per, block, carry)

        @pl.when(n + 2 < tiles)
        def _():
            fetch(i - 2, slot).start()

        return carry

    zero = jnp.zeros(slope[0].shape, f32)
    done = lax.fori_loop(0, tiles, piece, (message[0], message[1], zero, zero))
    g_rate[:8], g_rate[8:] = done[2], done[3]
    after()
    for c in down:
        c.wait_recv()
    total = gup[z].astype(f32)
    for k in range(1, depth):
        total = total + up_got[k].astype(f32)
    rim = up_own.shape[1]
    for q in range(PLANE):
        up_own[q] = total[q * rim : q * rim + rim].astype(bf16)
    total = gout[z].astype(f32)
    for k in range(1, depth):
        total = total + out_got[k].astype(f32)
    out_own[...] = total
    def finish():
        for c in mine + down:
            c.wait_send()

    return finish


def last_kernel(count, *refs):
    ins, outs, held = refs[:count], refs[count : 2 * count], refs[2 * count : 3 * count]
    in_sem, out_sem = refs[3 * count :]
    arriving = [pltpu.make_async_copy(ins[i], held[i], in_sem.at[i]) for i in range(count)]
    for c in arriving:
        c.start()
    leaving = [pltpu.make_async_copy(held[i], outs[i], out_sem.at[i]) for i in range(count)]
    for a, b in zip(arriving, leaving):
        a.wait()
        b.start()
    for c in leaving:
        c.wait()


def last_part(*results):
    count = len(results)
    return pl.pallas_call(
        functools.partial(last_kernel, count),
        out_shape=[jax.ShapeDtypeStruct(r.shape, r.dtype) for r in results],
        in_specs=[ANY] * count,
        out_specs=[ANY] * count,
        scratch_shapes=[pltpu.VMEM(r.shape, r.dtype) for r in results] + [DMA((count,))] * 2,
        compiler_params=params(),
        cost_estimate=cost(5),
        name="last_part",
    )(*results)


def body(
    depth,
    tokens,
    segments,
    routes,
    norm_gain,
    in_proj,
    conv_taps,
    conv_bias,
    select_proj,
    step_proj,
    step_bias,
    decay_log,
    skip_gain,
    out_proj,
    moe_gain,
    router,
    expert_up,
    expert_down,
    cotangent,
):
    count = tokens.shape[0]
    rows = PLANE * count
    rim = norm_gain.shape[0]
    ch = conv_bias.shape[0]
    fs = expert_down.shape[1]
    z, p = here()

    ids = jnp.concatenate([jnp.full((3,), -1, jnp.int32), segments, jnp.full((BLK,), -2, jnp.int32)])
    local_ids = lax.dynamic_slice_in_dim(ids, z * rows, rows + 3 + BLK)
    own_ids = local_ids[3:]
    inside = own_ids >= 0
    same = jnp.stack(
        [(local_ids[k : k + rows + BLK] == own_ids) & inside for k in range(4)], axis=1
    ).astype(f32)
    same = jnp.pad(same, ((0, 0), (0, 124)))
    (
        normed_in,
        w_in,
        w_route,
        small,
        w_sel,
        w_step,
        vecs,
        rate,
        inner,
        gate_in,
        conv,
        signal,
        selected,
        mixes,
        step_pre,
        dk,
        push,
        up_rows,
        down0,
        out_all,
        scanned,
        states,
        ends,
        up_early,
        cot_all,
        down1,
    ) = front_part(
        1,
        depth,
        tok=tokens,
        in_proj=in_proj,
        norm_gain=norm_gain[None],
        moe_gain=moe_gain[None],
        router=router.T,
        expert_up=expert_up.transpose(1, 0, 2),
        select=select_proj,
        step=step_proj,
        decay=decay_log,
        taps=conv_taps,
        bias=conv_bias[None],
        offset=step_bias[None],
        skip=skip_gain[None],
        w_down=expert_down,
        w_out=out_proj,
        same=same,
        cot=cotangent,
    )
    w_out = out_all.reshape(WIDE, D)
    output, grad_mid, mixed_wide, grad_gate_in, grad_out_w, grad_up, grad_down_own, sums = middle_part(
        3,
        depth,
        scanned=scanned,
        signal=signal,
        gate_in=gate_in,
        skip=vecs,
        w_out=w_out,
        tok=tokens,
        cot_all=cot_all.reshape(rows, D),
        up_early=up_early,
        up_rows=up_rows,
        down0=down0.reshape(HID, D),
        down1=down1.reshape(HID, D),
        w_router=w_route,
        rows_in=small,
        picks=routes.T,
    )
    (
        grad_tokens,
        grad_in,
        grad_up_own,
        grad_sel,
        grad_step,
        grad_decay,
        grad_taps,
        grad_bias,
        grad_offset,
        grad_skip,
        grad_norm,
        grad_moe,
        grad_router,
        grad_out_own,
    ) = back_part(
        5,
        depth,
        rim,
        ch,
        dk=dk,
        push=push,
        grad=mixed_wide,
        sel=mixes,
        states=states,
        ends=ends,
        gup=grad_up.reshape(depth, D // depth, EXPERTS * HID),
        gout=grad_out_w.reshape(depth, ch, D),
        step_pre=step_pre,
        signal=signal,
        conv=conv,
        inner=inner,
        same=same,
        vecs=vecs,
        rate=rate,
        selected=selected,
        w_sel=w_sel,
        w_step=w_step,
        gate_grad=grad_gate_in,
        w_in=w_in,
        normed_in=normed_in,
        tok=tokens,
        gain=small,
        grad_mid=grad_mid,
        sums=sums,
    )
    (
        output,
        grad_tokens,
        grad_norm,
        grad_in,
        grad_taps,
        grad_bias,
        grad_sel,
        grad_step,
        grad_offset,
        grad_decay,
        grad_skip,
        grad_out_own,
        grad_moe,
        grad_router,
        grad_up_own,
        grad_down_own,
    ) = last_part(
        output,
        grad_tokens,
        grad_norm,
        grad_in,
        grad_taps,
        grad_bias,
        grad_sel,
        grad_step,
        grad_offset,
        grad_decay,
        grad_skip,
        grad_out_own,
        grad_moe,
        grad_router,
        grad_up_own,
        grad_down_own,
    )
    return (
        output,
        grad_tokens,
        grad_norm[0],
        grad_in,
        grad_taps,
        grad_bias[0],
        grad_sel,
        grad_step,
        grad_offset[0],
        grad_decay,
        grad_skip[0],
        grad_out_own,
        grad_moe[0],
        grad_router.T,
        grad_up_own.transpose(1, 0, 2),
        grad_down_own,
    )


def solution(mesh):
    planes = Mesh(mesh.devices.reshape(-1, PLANE), ("z", "p"))
    every = ("z", "p")
    rows, flat, cols, third = P(every, None), P(every), P(None, every), P(None, every, None)
    return jax.shard_map(
        functools.partial(body, planes.shape["z"]),
        mesh=planes,
        in_specs=(
            rows, P(), rows, flat, rows, cols, flat, rows, cols,
            flat, cols, flat, rows, flat, rows, third, third, rows,
        ),
        out_specs=(
            rows, rows, flat, rows, cols, flat, rows, cols,
            flat, cols, flat, rows, flat, rows, third, third,
        ),
        check_vma=False,
    )
```

```python
import functools

import jax
import jax.numpy as jnp
from jax import lax
from jax.experimental import pallas as pl
from jax.experimental.pallas import tpu as pltpu
from jax.sharding import Mesh, PartitionSpec as P

D = 1152
DI = 2304
FF = 3072
RANK = 72
STATE = 16
EXPERTS = 2
CAP = 68
SEL = RANK + 2 * STATE

PLANE = 8
CHIPS = PLANE // 2
WIDE = DI // PLANE
PAD = -WIDE % 128
HID = FF // PLANE
BLK = 16
LOG2E = 1.4426950408889634
GELU = 0.7978845608028654
RESET = 1e5


def split_rows(rows):
    early = rows // 64 * 16
    return pl.ds(0, early), pl.ds(early, rows - early)


epsilon = 1e-05

MESH = pl.DeviceIdType.MESH
ANY = pl.BlockSpec(memory_space=pl.ANY)
VM = pl.BlockSpec(memory_space=pltpu.VMEM)
bf16 = jnp.bfloat16
f32 = jnp.float32
DMA = pltpu.SemaphoreType.DMA


def params(cid=None, grid=None):
    extra = {} if cid is None else {"collective_id": cid, "has_side_effects": True}
    if grid is not None:
        extra["dimension_semantics"] = grid
    return pltpu.CompilerParams(vmem_limit_bytes=60 * 1024 * 1024, **extra)


def cost(us):
    return pl.CostEstimate(flops=int(us * 1e9), bytes_accessed=int(us * 3e6), transcendentals=0)


def mm(left, right):
    return jnp.dot(left, right, preferred_element_type=f32)


def contract_rows(left, right):
    return lax.dot_general(left, right, (((0,), (0,)), ((), ())), preferred_element_type=f32)


def contract_cols(left, right):
    return lax.dot_general(left, right, (((1,), (1,)), ((), ())), preferred_element_type=f32)


class Names:
    def __getattr__(self, name):
        return name


N = Names()


class Stage:
    def __init__(self, fetches, flushes):
        self.fetches, self.flushes, self.going = fetches, flushes, []
        for copy in fetches.values():
            copy.start()

    def need(self, *names):
        for name in names:
            self.fetches.pop(name).wait()

    def done(self, *names):
        for name in names:
            self.flushes[name].start()
            self.going.append(self.flushes[name])

    def end(self):
        self.need(*tuple(self.fetches))
        for copy in self.going:
            copy.wait()


def staged_call(kernel, name, cid, us, ins, outs, scratch, late=(), early=(), away=(), raw=()):
    inside = [n for n in outs if n not in away]
    early = [n for n in inside if n in early]

    def body(*refs):
        refs = list(refs)
        take = lambda names: dict(zip(names, [refs.pop(0) for _ in names]))
        source, target = take(ins), take(outs)
        buffers, results = take(late), take(early)
        in_sem, out_sem = refs.pop(0), refs.pop(0)
        stage = Stage(
            {n: pltpu.make_async_copy(source[n], buffers[n], in_sem.at[i]) for i, n in enumerate(late)},
            {n: pltpu.make_async_copy(results[n], target[n], out_sem.at[i]) for i, n in enumerate(early)},
        )
        kernel(
            stage,
            *[buffers.get(n, source[n]) for n in ins],
            *[results.get(n, target[n]) for n in outs],
            *refs,
        )
        stage.end()

    return pl.pallas_call(
        body,
        out_shape=list(outs.values()),
        in_specs=[ANY if n in late or n in raw else VM for n in ins],
        out_specs=[ANY if n in early or n in away else VM for n in outs],
        scratch_shapes=[pltpu.VMEM(ins[n].shape, ins[n].dtype) for n in late]
        + [pltpu.VMEM(outs[n].shape, outs[n].dtype) for n in early]
        + [DMA((max(len(late), 1),)), DMA((max(len(early), 1),))]
        + scratch,
        compiler_params=params(cid),
        cost_estimate=cost(us),
        name=name,
    )(*ins.values())


def made(*shape, dtype=None):
    return jax.ShapeDtypeStruct(shape, dtype or f32)


def remote(src, dst, ss, rs, to):
    return pltpu.make_async_remote_copy(
        src_ref=src, dst_ref=dst, send_sem=ss, recv_sem=rs, device_id=to, device_id_type=MESH
    )


def send(src, dst, ss, rs, to):
    copy = remote(src, dst, ss, rs, to)
    copy.start()
    return copy


def here():
    return lax.axis_index("z"), lax.axis_index("p")


def greet(plane=True, depth=0):
    z, p = here()
    barrier = pltpu.get_barrier_semaphore()
    count = 0
    if plane:
        for k in range(1, PLANE):
            pl.semaphore_signal(
                barrier, inc=1, device_id=(z, lax.rem(p + k, PLANE)), device_id_type=MESH
            )
            count += 1
    for k in range(1, depth):
        pl.semaphore_signal(barrier, inc=1, device_id=(lax.rem(z + k, depth), p), device_id_type=MESH)
        count += 1
    pl.semaphore_wait(barrier, count)


def share_start(x, out, ss, rs):
    z, p = here()
    core = lax.rem(p, 2)
    copies = [send(x, out.at[p], ss.at[0], rs.at[0], (z, p + 1 - 2 * core))]
    for k in range(1, CHIPS):
        copies.append(send(x, out.at[p], ss.at[k], rs.at[k], (z, lax.rem(p + 2 * k, PLANE))))
    return copies


def share_forward(out, copies, ss, rs):
    z, p = here()
    core = lax.rem(p, 2)
    onward = []
    for k in range(1, CHIPS):
        copies[k].wait_recv()
        src = lax.rem(p + PLANE - 2 * k, PLANE)
        onward.append(
            send(out.at[src], out.at[src], ss.at[CHIPS + k], rs.at[CHIPS + k], (z, p + 1 - 2 * core))
        )
    return onward


def share_finish(copies, onward):
    copies[0].wait_recv()
    for c in copies:
        c.wait_send()
    for c in onward:
        c.wait()


def column_copy(src, out, ss, rs, frm, to, part=None):
    dst = out.at[frm] if part is None else out.at[frm, part]
    return pltpu.make_async_remote_copy(
        src_ref=dst if src is None else src,
        dst_ref=dst,
        send_sem=ss.at[to],
        recv_sem=rs.at[frm],
        device_id=(to, lax.axis_index("p")),
        device_id_type=MESH,
    )


def column_each(depth, act):
    z = lax.axis_index("z")
    for t in range(depth):
        far = abs(t - z) == depth - 1 if depth == 4 else t == z
        pl.when(jnp.logical_not((t == z) | far))(functools.partial(act, t))


def column_start(depth, src, out, ss, rs, part=None):
    z = lax.axis_index("z")
    column_each(depth, lambda t: column_copy(src, out, ss, rs, z, t, part).start())


def column_forward(depth, out, ss, rs, part=None):
    if depth != 4:
        return
    z = lax.axis_index("z")
    for me, frm, to in ((2, 0, 3), (1, 3, 0)):

        @pl.when(z == me)
        def _():
            copy = column_copy(None, out, ss, rs, frm, to, part)
            copy.wait_recv()
            copy.start()


def column_finish(depth, src, out, ss, rs, part=None):
    z = lax.axis_index("z")
    for s in range(depth):
        ahead = ((z == 2) & (s == 0)) | ((z == 1) & (s == 3)) if depth == 4 else s == z

        @pl.when(jnp.logical_not((s == z) | ahead))
        def _():
            column_copy(src, out, ss, rs, s, s, part).wait_recv()

    column_each(depth, lambda t: column_copy(src, out, ss, rs, z, t, part).wait_send())
    if depth == 4:
        for me, frm, to in ((2, 0, 3), (1, 3, 0)):

            @pl.when(z == me)
            def _():
                column_copy(None, out, ss, rs, frm, to, part).wait_send()


def softplus(x):
    return jnp.maximum(x, 0.0) + jnp.log1p(jnp.exp(-jnp.abs(x)))


def total_start(x, got, ss, rs):
    z, p = here()
    copies = []
    for k in range(1, PLANE):
        q = lax.rem(p + k, PLANE)
        copies.append(send(x.at[q], got.at[k], ss.at[k], rs.at[k], (z, q)))
    return copies


def total_share(x, got, copies, out, ts, us):
    z, p = here()
    total = x[p]
    for k in range(1, PLANE):
        copies[k - 1].wait_recv()
        total = total + got[k]
    out[p] = total.astype(bf16)
    after = [
        send(out.at[p], out.at[p], ts.at[k], us.at[k], (z, lax.rem(p + k, PLANE))) for k in range(1, PLANE)
    ]
    for c in copies:
        c.wait_send()
    return after


def front_kernel(
    depth, stage,
    tok, in_proj, norm_gain, moe_gain, router, expert_up, select, step, decay, taps, bias, offset, skip,
    w_down, w_out, same,
    normed_in, w_in, w_route, small, w_sel, w_step, vecs, rate, inner, gate_in, conv, signal, selected, mixes,
    step_pre, dk, push, up_rows, down_all, out_all,
    tok_all, win_all, pack_all, wide, thin, near, halo, x, got, sel_all, win, wup, pack, square, win_got, up_got, flat,
    gs, gr, ws, wr, vs, vr, zs, zr, hs, ss, rs, ts, us, ls,
):
    z, p = here()
    count = tok.shape[0]
    rim = in_proj.shape[0]
    ch = select.shape[0]
    pair = 2 * count
    rows = PLANE * count
    fs = expert_up.shape[2] // (depth * PLANE)
    local = [
        pltpu.make_async_copy(tok, tok_all.at[p], ls.at[0]),
        pltpu.make_async_copy(win.at[p], win_got.at[p], ls.at[1]),
        pltpu.make_async_copy(wup.at[p], up_got.at[p], ls.at[2]),
        pltpu.make_async_copy(pack, pack_all.at[z], ls.at[3]),
        pltpu.make_async_copy(w_down.at[0], down_all.at[z], ls.at[4]),
        pltpu.make_async_copy(w_out, out_all.at[z], ls.at[5]),
    ]
    for i in (0, 4, 5):
        local[i].start()
    square[...] = jnp.zeros_like(square)
    square[0:1, :rim] = norm_gain[...].astype(f32)
    square[1:2, :rim] = moe_gain[...].astype(f32)
    square[2:4, :rim] = router[...].astype(f32)
    columns = square[...].T
    square[...] = columns
    for q in range(PLANE):
        for i in range(2 * depth):
            start = (i // depth) * DI + ((i % depth) * PLANE + q) * ch
            win[q, :, i * ch : i * ch + ch] = in_proj[:, start : start + ch]
        win[q, :, 2 * WIDE :] = square[:rim, :64].astype(bf16)
    local[1].start()
    greet(True, depth)
    across = []
    for k in range(1, PLANE):
        q = lax.rem(p + k, PLANE)
        across.append(send(win.at[q], win_got.at[p], ws.at[k], wr.at[k], (z, q)))
    first = share_start(tok, tok_all, gs, gr)
    square[...] = jnp.zeros_like(square)
    square[0:STATE, :ch] = decay[...].astype(f32)
    square[STATE : STATE + 4, :ch] = taps[...].astype(f32)
    for i, ref in enumerate((bias, offset, skip)):
        square[STATE + 4 + i : STATE + 5 + i, :ch] = ref[...].astype(f32)
    columns = square[...].T
    pack[:, 256:] = columns[:ch].astype(bf16)
    square[...] = jnp.zeros_like(square)
    square[:RANK, :ch] = step[...].astype(f32)
    columns = square[...].T
    pack[:, 128:256] = columns[:ch].astype(bf16)
    pack[:, :128] = jnp.zeros((ch, 128), bf16)
    pack[:, :SEL] = select[...]
    column_start(depth, pack, pack_all, zs.at[0], zr.at[0])
    local[3].start()
    for q in range(PLANE):
        for i in range(EXPERTS * depth):
            start = ((i % depth) * PLANE + q) * fs
            wup[q, :, i * fs : i * fs + fs] = expert_up[:, i // depth, start : start + fs]
    local[2].start()
    local[1].wait()
    for c in across:
        c.wait_recv()
    for q in range(PLANE):
        flat[q * rim : q * rim + rim, :640] = win_got[q].astype(f32)
    win_all[z] = flat[:, :640].astype(bf16)
    column_start(depth, win_all.at[z], win_all, zs.at[1], zr.at[1])
    second = share_forward(tok_all, first, gs, gr)
    more = []
    for k in range(1, PLANE):
        q = lax.rem(p + k, PLANE)
        more.append(send(wup.at[q], up_got.at[p], vs.at[k], vr.at[k], (z, q)))
    local[3].wait()
    column_forward(depth, pack_all, zs.at[0], zr.at[0])
    column_finish(depth, pack, pack_all, zs.at[0], zr.at[0])
    for k in range(depth):
        thin[k * ch : k * ch + ch, :] = pack_all[k].astype(f32)
    w_sel[...] = thin[:, :128].astype(bf16)
    w_step[...] = thin[:, 128:256].astype(bf16)
    side = thin[:, 256:].T
    rate[:, :WIDE] = -jnp.exp(side[:STATE])
    rate[:, WIDE:] = jnp.zeros((STATE, PAD), f32)
    vecs[...] = side[STATE : STATE + 8]
    column_forward(depth, win_all, zs.at[1], zr.at[1])
    local[0].wait()
    share_finish(first, second)
    column_finish(depth, win_all.at[z], win_all, zs.at[1], zr.at[1])
    block = PLANE * rim
    for k in range(depth):
        w_in[k * block : k * block + block, :] = win_all[k, :, : 2 * WIDE]
        wide[k * block : k * block + block, :] = win_all[k, :, 512:].astype(f32)
    w_route[...] = wide[...].astype(bf16)
    small[...] = wide[...].T[64:72]
    gain = small[0:1]
    for b in (3, 0, 1, 2):
        at = slice(pair * b, pair * b + pair)
        values = tok_all[2 * b : 2 * b + 2].reshape(pair, D).astype(f32)
        scale = lax.rsqrt(jnp.mean(values * values, axis=-1, keepdims=True) + epsilon)
        normed = (values * scale * gain).astype(bf16)
        normed_in[at, :] = normed
        joined = mm(normed, w_in[...]).astype(bf16)
        near[BLK + pair * b : BLK + pair * b + pair, :] = joined[:, :WIDE].astype(f32)
        gate_in[at, :] = joined[:, WIDE:]
        if b == 3:
            edge = send(near.at[pl.ds(rows, BLK)], halo, hs.at[0], hs.at[1], (lax.rem(z + 1, depth), p))
            column_start(depth, w_out, out_all, zs.at[2], zr.at[2])
            column_start(depth, w_down.at[0], down_all, zs.at[3], zr.at[3])
    stage.done(N.w_in, N.normed_in, N.gate_in)
    stage.need(N.same)
    for b in (1, 2, 3, 0):
        if b == 0:
            edge.wait()
            near[:BLK, :] = halo[...]
        base = pair * b
        at = slice(base, base + pair)
        total = vecs[4:5] + vecs[0:1] * near[base + 13 : base + 13 + pair, :] * same[at, 0:1]
        for k in range(1, 4):
            total = total + vecs[k : k + 1] * near[base + 13 + k : base + 13 + k + pair, :] * same[at, k : k + 1]
        conv[at, :] = total
        value = (total * jax.nn.sigmoid(total)).astype(bf16)
        signal[at, :] = value
        x[2 * b : 2 * b + 2] = mm(value, w_sel[...]).reshape(2, count, 128)
    third = total_start(x, got, ss, rs)
    inner[...] = near[...].astype(bf16)
    stage.done(N.conv, N.signal, N.inner)
    fourth = total_share(x, got, third, sel_all, ts, us)
    local[5].wait()
    column_forward(depth, out_all, zs.at[2], zr.at[2])
    for c in fourth:
        c.wait()
    for b in range(CHIPS):
        at = slice(pair * b, pair * b + pair)
        chosen = sel_all[2 * b : 2 * b + 2].reshape(pair, 128)
        selected[at, :] = chosen
        step = contract_cols(chosen, w_step[...]) + vecs[5:6]
        step_pre[at, :] = step
        delta = softplus(step)
        dk[at, :WIDE] = delta + (1.0 - same[at, 2:3]) * RESET
        push[at, :WIDE] = delta * signal[at, :].astype(f32)
        dk[at, WIDE:] = jnp.zeros((pair, PAD), f32)
        push[at, WIDE:] = jnp.zeros((pair, PAD), f32)
        full = chosen.astype(f32)
        for i in range(pair // BLK):
            flipped = full[i * BLK : i * BLK + BLK].T
            mixes[b * (pair // BLK) + i] = flipped[RANK:SEL]
    stage.done(N.dk, N.push, N.step_pre, N.mixes, N.selected)
    local[2].wait()
    for c in across:
        c.wait_send()
    for c in more:
        c.wait()
    for q in range(PLANE):
        flat[q * rim : q * rim + rim, :] = up_got[q].astype(f32)
    up_rows[...] = flat[...].astype(bf16)

    def onward():
        local[4].wait()
        column_forward(depth, down_all, zs.at[3], zr.at[3])

    def finish():
        column_finish(depth, w_out, out_all, zs.at[2], zr.at[2])
        column_finish(depth, w_down.at[0], down_all, zs.at[3], zr.at[3])

    return onward, finish


def front_part(cid, depth, **ins):
    count, rim, ch = ins[N.tok].shape[0], ins[N.in_proj].shape[0], ins[N.select].shape[0]
    low = ins[N.w_down].shape[1]
    rows = PLANE * count
    outs = dict(
        normed_in=made(rows, D, dtype=bf16),
        w_in=made(D, 2 * WIDE, dtype=bf16),
        w_route=made(D, 128, dtype=bf16),
        small=made(8, D),
        w_sel=made(WIDE, 128, dtype=bf16),
        w_step=made(WIDE, 128, dtype=bf16),
        vecs=made(8, WIDE),
        rate=made(STATE, WIDE + PAD),
        inner=made(rows + BLK, WIDE, dtype=bf16),
        gate_in=made(rows, WIDE, dtype=bf16),
        conv=made(rows, WIDE),
        signal=made(rows, WIDE, dtype=bf16),
        selected=made(rows, 128, dtype=bf16),
        mixes=made(rows // BLK, 2 * STATE, BLK),
        step_pre=made(rows, WIDE),
        dk=made(rows, WIDE + PAD),
        push=made(rows, WIDE + PAD),
        up_rows=made(PLANE * rim, EXPERTS * HID, dtype=bf16),
        down_all=made(depth, low, D, dtype=bf16),
        out_all=made(depth, ch, D, dtype=bf16),
    )
    scratch = (
        [
            pltpu.VMEM((PLANE, count, D), bf16),
            pltpu.VMEM((depth, PLANE * rim, 640), bf16),
            pltpu.VMEM((depth, ch, 384), bf16),
            pltpu.VMEM((D, 128), f32),
            pltpu.VMEM((WIDE, 384), f32),
            pltpu.VMEM((BLK + rows, WIDE), f32),
            pltpu.VMEM((BLK, WIDE), f32),
            pltpu.VMEM((PLANE, count, 128), f32),
            pltpu.VMEM((PLANE, count, 128), f32),
            pltpu.VMEM((PLANE, count, 128), bf16),
            pltpu.VMEM((PLANE, rim, 640), bf16),
            pltpu.VMEM((PLANE, rim, EXPERTS * HID), bf16),
            pltpu.VMEM((ch, 384), bf16),
            pltpu.VMEM((128, 128), f32),
            pltpu.VMEM((PLANE, rim, 640), bf16),
            pltpu.VMEM((PLANE, rim, EXPERTS * HID), bf16),
            pltpu.VMEM((PLANE * rim, EXPERTS * HID), f32),
        ]
        + [DMA((PLANE,))] * 6
        + [DMA((4, depth))] * 2
        + [DMA((2,))]
        + [DMA((PLANE,))] * 4
        + [DMA((6,))]
    )
    early = (
        N.normed_in, N.w_in, N.inner, N.gate_in, N.conv, N.signal, N.selected, N.mixes, N.step_pre, N.dk, N.push,
    )
    up_rows, cot = outs[N.up_rows], ins[N.cot]
    outs.update(
        scanned=made(rows, WIDE + PAD),
        states=made(rows, STATE, WIDE + PAD),
        ends=made(depth, STATE + 8, WIDE + PAD),
        up_early=made(depth, split_rows(up_rows.shape[0])[0].size, up_rows.shape[1], dtype=bf16),
        cot_all=made(PLANE, *cot.shape, dtype=bf16),
        down1=made(depth, low, D, dtype=bf16),
    )
    mine = len(scratch)
    scratch = (
        scratch
        + [pltpu.VMEM((2, 2, count, STATE, WIDE + PAD), f32)]
        + [DMA((PLANE,))] * 2
        + [DMA((depth,))] * 2
        + [DMA((2, depth))] * 2
        + [DMA((2, 2)), DMA((3,))]
    )
    names = tuple(ins) + tuple(outs)

    def kernel(stage, *refs):
        ref = dict(zip(names, refs))
        held = refs[len(names) :]
        first = [ref[n] for n in names if n != N.cot][: len(ins) - 1 + 20]
        onward, finish = front_kernel(depth, stage, *first, *held[:mine])
        scan_kernel(
            depth,
            stage,
            onward,
            *(ref[n] for n in (N.dk, N.push, N.mixes, N.rate, N.up_rows, N.cot, N.w_down)),
            *(ref[n] for n in (N.scanned, N.states, N.ends, N.up_early, N.cot_all, N.down1)),
            *held[mine:],
        )
        finish()

    return staged_call(
        kernel, "front_part", cid, 110, ins, outs, scratch,
        late=(N.same, N.cot), early=early + (N.scanned,),
        away=(N.down_all, N.out_all, N.states, N.up_early, N.cot_all, N.down1),
    )


def folded(x):
    half = x.shape[0] // 2
    return jnp.concatenate([x[:half], x[half:]], axis=1).astype(bf16)


def back_kernel(
    depth, stage,
    g_push, g_step, g_mixes, g_rate, step_pre, signal, conv, inner, same, vecs, rate, selected, w_sel, w_step,
    mixed_grad, gate_grad, w_in, normed_in, tok, gain, grad_mid, sums, gup,
    tokens_out, in_own, up_own, sel_own, step_own, decay_own, taps_own, bias_own, offset_own, skip_own,
    norm_own, moe_own, router_own,
    in_out, up_out, pack_out, x, got, gsel, low, gc, halo, nearf, gj, part, sib, mix, far, gin, gin_got, own, pack, pack_got, row, row_got, sml, sml_got,
    hs, ss, rs, ts, us, near_s, near_r, away_s, away_r, zs, zr, cs, cr, ups, upr, ls,
):
    z, p = here()
    core = lax.rem(p, 2)
    chip = lax.div(p, 2)
    twin = (z, p + 1 - 2 * core)
    count = tok.shape[0]
    pair = 2 * count
    rows = PLANE * count
    ch = sel_own.shape[0]
    rim = in_own.shape[0]
    fs = up_own.shape[2] // (depth * PLANE)
    sent = []

    def down(i, src, dst):
        copies = []
        for k in range(1, depth):
            q = lax.rem(z + k, depth)
            copies.append(send(src.at[q], dst.at[k], zs.at[i, k], zr.at[i, k], (q, p)))
        return copies

    block = D // depth
    stage.need(N.normed_in, N.gate_grad)
    for q in range(depth):
        gin[1, q] = folded(contract_rows(normed_in[:, q * block : q * block + block], gate_grad[...]))
    gate_sent = down(3, gin.at[1], gin_got.at[1])
    stage.need(N.w_step, N.signal, N.step_pre)
    bias = jnp.zeros((1, WIDE), f32)
    for b in range(CHIPS):
        at = slice(pair * b, pair * b + pair)
        value = signal[at, :].astype(f32)
        grad = g_step[at, :WIDE] * (1.0 / LOG2E) + g_push[at, :WIDE] * value
        grad = grad * jax.nn.sigmoid(step_pre[at, :])
        bias = bias + jnp.sum(grad, axis=0, keepdims=True)
        low[at, :] = grad.astype(bf16)
        ranks = mm(low[at, :], w_step[...])
        for i in range(pair // BLK):
            mixed = g_mixes[b * (pair // BLK) + i]
            wide = jnp.concatenate(
                [jnp.zeros((RANK, BLK), f32), mixed, jnp.zeros((128 - SEL, BLK), f32)], axis=0
            ).T
            t = i * BLK
            x[2 * b + t // count, t % count : t % count + BLK, :] = ranks[t : t + BLK] + wide
    first = total_start(x, got, ss, rs)
    stage.need(N.selected, N.inner)
    keep = pltpu.make_async_copy(gup.at[p], up_out.at[p], ls)
    keep.start()
    grad_step_w = contract_rows(low[...], selected[...])
    nearf[...] = inner[...].astype(f32)
    second = total_share(x, got, first, gsel, ts, us)
    ups_sent = []
    for k in range(1, PLANE):
        q = lax.rem(p + k, PLANE)
        ups_sent.append(send(gup.at[q], up_out.at[p], ups.at[k], upr.at[k], (z, q)))
    for c in second:
        c.wait()
    stage.need(N.conv, N.same, N.w_sel)
    taps = [jnp.zeros((1, WIDE), f32)] * 4
    conv_bias = jnp.zeros((1, WIDE), f32)
    for b in range(CHIPS):
        base = pair * b
        at = slice(base, base + pair)
        delta = softplus(step_pre[at, :])
        grad = mixed_grad[at, :WIDE] * vecs[6:7] + g_push[at, :WIDE] * delta
        grad = grad + contract_cols(gsel[2 * b : 2 * b + 2].reshape(pair, 128), w_sel[...])
        c = conv[at, :]
        sig = jax.nn.sigmoid(c)
        grad = grad * (sig * (1.0 + c * (1.0 - sig)))
        gc[at, :] = grad
        if b == 0:
            edge = send(gc.at[pl.ds(0, BLK)], halo, hs.at[0], hs.at[1], (lax.rem(z + depth - 1, depth), p))
        conv_bias = conv_bias + jnp.sum(grad, axis=0, keepdims=True)
        for k in range(4):
            taps[k] = taps[k] + jnp.sum(
                grad * nearf[base + 13 + k : base + 13 + k + pair, :] * same[at, k : k + 1], axis=0, keepdims=True
            )
    stage.need(N.w_in, N.tok, N.grad_mid)
    for b in range(CHIPS):
        base = pair * b
        if b == CHIPS - 1:
            edge.wait()
            gc[rows : rows + BLK, :] = halo[...]
        total = jnp.zeros((pair, WIDE), f32)
        for k in range(4):
            off = slice(base + 3 - k, base + 3 - k + pair)
            total = total + gc[off, :] * vecs[k : k + 1] * same[off, k : k + 1]
        gj[base : base + pair, :WIDE] = total.astype(bf16)
        gj[base : base + pair, WIDE:] = gate_grad[base : base + pair, :]
    for q in range(depth):
        gin[0, q] = folded(contract_rows(normed_in[:, q * block : q * block + block], gj[:, :WIDE]))
    in_sent = down(0, gin.at[0], gin_got.at[0])
    near = {}
    for k in (1, 2, 3, 0):
        q = lax.rem(chip + k, CHIPS)
        at = pl.ds(pl.multiple_of(q * pair, pair), pair)
        part[k] = contract_cols(gj[at, :], w_in[...]).astype(bf16).reshape(2, count, D)
        near[k] = send(part.at[k, 1 - core], sib.at[k], near_s.at[k], near_r.at[k], twin)
    away = []
    for k in range(1, CHIPS):
        near[k].wait_recv()
        mix[k] = (part[k, core].astype(f32) + sib[k].astype(f32)).astype(bf16)
        away.append(
            send(mix.at[k], far.at[k], away_s.at[k], away_r.at[k], (z, lax.rem(p + 2 * k, PLANE)))
        )
    row[...] = jnp.zeros_like(row)
    row[0:STATE, :] = g_rate[...] * rate[...]
    for k in range(4):
        row[STATE + k : STATE + k + 1, :WIDE] = taps[k]
    row[STATE + 4 : STATE + 5, :WIDE] = conv_bias
    row[STATE + 5 : STATE + 6, :WIDE] = bias
    row[STATE + 6 : STATE + 7, :WIDE] = sums[3:4, :WIDE]
    side = row[...].T
    grad_sel_w = contract_rows(signal[...], gsel[...].reshape(rows, 128))
    for q in range(depth):
        cut = slice(q * ch, q * ch + ch)
        pack[q, :, :128] = grad_sel_w[cut].astype(bf16)
        pack[q, :, 128:256] = grad_step_w[cut].astype(bf16)
        pack[q, :, 256:] = side[cut].astype(bf16)
    pack_sent = down(1, pack, pack_got)
    near[0].wait_recv()
    total = part[0, core].astype(f32) + sib[0].astype(f32)
    for k in range(1, CHIPS):
        away[k - 1].wait_recv()
        total = total + far[k].astype(f32)
    values = tok[...].astype(f32)
    scale = lax.rsqrt(jnp.mean(values * values, axis=-1, keepdims=True) + epsilon)
    normed = values * scale
    grad_normed = total * gain[0:1]
    mean = jnp.mean(grad_normed * normed, axis=-1, keepdims=True)
    tokens_out[...] = (scale * (grad_normed - normed * mean) + grad_mid[...]).astype(bf16)
    stage.done(N.tokens_out)
    ours = jnp.concatenate(
        [jnp.sum(total * normed, axis=0, keepdims=True), sums[0:3, :], jnp.zeros((4, D), f32)], axis=0
    )
    for q in range(depth):
        sml[q] = ours[:, q * block : q * block + block]
    sml_sent = down(2, sml, sml_got)
    for h, copies in ((1, gate_sent), (0, in_sent)):
        for c in copies:
            c.wait_recv()
        total = gin[h, z].astype(f32)
        for k in range(1, depth):
            total = total + gin_got[h, k].astype(f32)
        total = jnp.concatenate([total[:, :WIDE], total[:, WIDE:]], axis=0)
        for q in range(PLANE):
            own[q, :, h * WIDE : h * WIDE + WIDE] = total[q * rim : q * rim + rim].astype(bf16)
    across = []
    for k in range(1, PLANE):
        q = lax.rem(p + k, PLANE)
        across.append(send(own.at[q], in_out.at[p], cs.at[0, k], cr.at[0, k], (z, q)))
    in_out[p] = own[p]
    for c in sml_sent:
        c.wait_recv()
    total = sml[z]
    for k in range(1, depth):
        total = total + sml_got[k]
    sml_got[0] = total
    for k in range(1, PLANE):
        q = lax.rem(p + k, PLANE)
        across.append(send(sml_got.at[0], row_got.at[k], cs.at[1, k], cr.at[1, k], (z, q)))
    for c in pack_sent:
        c.wait_recv()
    total = pack[z].astype(f32)
    for k in range(1, depth):
        total = total + pack_got[k].astype(f32)
    sel_own[...] = total[:, :SEL]
    pack_out[...] = jnp.zeros_like(pack_out)
    pack_out[:ch, :] = total[:, 128:256]
    columns = pack_out[...].T
    step_own[...] = columns[:RANK, :ch]
    pack_out[:ch, :32] = total[:, 256:]
    columns = pack_out[...].T
    decay_own[...] = columns[:STATE, :ch]
    taps_own[...] = columns[STATE : STATE + 4, :ch]
    bias_own[...] = columns[STATE + 4 : STATE + 5, :ch]
    offset_own[...] = columns[STATE + 5 : STATE + 6, :ch]
    skip_own[...] = columns[STATE + 6 : STATE + 7, :ch]
    for c in ups_sent:
        c.wait()
    keep.wait()
    for q in range(PLANE):
        for i in range(EXPERTS * depth):
            start = ((i % depth) * PLANE + q) * fs
            up_own[:, i // depth, start : start + fs] = up_out[q, :, i * fs : i * fs + fs].astype(f32)
    stage.done(N.up_own)
    for c in across:
        c.wait()
    for q in range(PLANE):
        for i in range(2 * depth):
            start = (i // depth) * DI + ((i % depth) * PLANE + q) * ch
            in_own[:, start : start + ch] = in_out[q, :, i * ch : i * ch + ch].astype(f32)
    total = sml_got[0]
    for k in range(1, PLANE):
        total = total + row_got[k]
    for q in range(PLANE):

        @pl.when(p == q)
        def _():
            cut = total[:, q * rim : q * rim + rim]
            norm_own[...] = cut[0:1]
            moe_own[...] = cut[1:2]
            router_own[...] = cut[2:4]

    for c in list(near.values()) + away + gate_sent + in_sent + pack_sent + sml_sent:
        c.wait_send()


def back_part(cid, depth, rim, ch, **ins):
    count = ins[N.tok].shape[0]
    rows, wide = ins[N.dk].shape
    block = D // depth
    gup, gout = ins[N.gup], ins[N.gout]
    outs = dict(
        tokens_out=made(count, D, dtype=bf16),
        in_own=made(rim, 2 * DI),
        up_own=made(rim, EXPERTS, FF),
        sel_own=made(ch, SEL),
        step_own=made(RANK, ch),
        decay_own=made(STATE, ch),
        taps_own=made(4, ch),
        bias_own=made(1, ch),
        offset_own=made(1, ch),
        skip_own=made(1, ch),
        norm_own=made(1, rim),
        moe_own=made(1, rim),
        router_own=made(2, rim),
        out_own=made(*gout.shape[1:]),
    )
    scratch = (
        [
            pltpu.VMEM((PLANE, rim, 2 * WIDE), bf16),
            pltpu.VMEM((PLANE, rim, EXPERTS * HID), bf16),
            pltpu.VMEM((128, 128), f32),
            pltpu.VMEM((PLANE, count, 128), f32),
            pltpu.VMEM((PLANE, count, 128), f32),
            pltpu.VMEM((PLANE, count, 128), bf16),
            pltpu.VMEM((rows, WIDE), bf16),
            pltpu.VMEM((rows + BLK, WIDE), f32),
            pltpu.VMEM((BLK, WIDE), f32),
            pltpu.VMEM((rows + BLK, WIDE), f32),
            pltpu.VMEM((rows, 2 * WIDE), bf16),
            pltpu.VMEM((CHIPS, 2, count, D), bf16),
            pltpu.VMEM((CHIPS, count, D), bf16),
            pltpu.VMEM((CHIPS, count, D), bf16),
            pltpu.VMEM((CHIPS, count, D), bf16),
            pltpu.VMEM((2, depth, block // 2, 2 * WIDE), bf16),
            pltpu.VMEM((2, depth, block // 2, 2 * WIDE), bf16),
            pltpu.VMEM((PLANE, rim, 2 * WIDE), bf16),
            pltpu.VMEM((depth, ch, 288), bf16),
            pltpu.VMEM((depth, ch, 288), bf16),
            pltpu.VMEM((2 * STATE, WIDE + PAD), f32),
            pltpu.VMEM((PLANE, 8, block), f32),
            pltpu.VMEM((depth, 8, block), f32),
            pltpu.VMEM((depth, 8, block), f32),
            DMA((2,)),
        ]
        + [DMA((PLANE,))] * 4
        + [DMA((CHIPS,))] * 4
        + [DMA((4, depth))] * 2
        + [DMA((2, PLANE))] * 2
        + [DMA((PLANE,))] * 2
        + [DMA]
    )
    mine = len(scratch)
    scratch = (
        scratch
        + [
            pltpu.VMEM((2, count, STATE, wide), f32),
            pltpu.VMEM((depth, STATE, wide), f32),
            pltpu.VMEM(gup.shape, bf16),
            pltpu.VMEM(gout.shape, bf16),
        ]
        + [DMA((depth,))] * 2
        + [DMA((3, depth))] * 2
        + [DMA((2,))]
        + [
            pltpu.VMEM((rows, wide), f32),
            pltpu.VMEM((rows, wide), f32),
            pltpu.VMEM(ins[N.sel].shape, f32),
            pltpu.VMEM((STATE, wide), f32),
            pltpu.VMEM((PLANE, rim, EXPERTS * HID), bf16),
        ]
    )
    names = tuple(ins) + tuple(outs)

    def kernel(stage, *refs):
        ref = dict(zip(names, refs))
        held = refs[len(names) :]
        g_push, g_step, g_sel, g_rate, up_part = held[-5:]
        finish = adjoint_kernel(
            depth,
            stage,
            lambda: None,
            *(ref[n] for n in (N.dk, N.push, N.grad, N.sel, N.states, N.rate, N.ends, N.gup, N.gout)),
            g_push,
            g_step,
            g_sel,
            g_rate,
            up_part,
            ref[N.out_own],
            *held[mine:-5],
        )
        back_kernel(
            depth,
            stage,
            g_push,
            g_step,
            g_sel,
            g_rate,
            *(
                ref[n]
                for n in (
                    N.step_pre, N.signal, N.conv, N.inner, N.same, N.vecs, N.rate, N.selected, N.w_sel, N.w_step,
                    N.grad, N.gate_grad, N.w_in, N.normed_in, N.tok, N.gain, N.grad_mid, N.sums,
                )
            ),
            up_part,
            *(ref[n] for n in outs if n != N.out_own),
            *held[:mine],
        )
        finish()

    late = (
        N.gup, N.sel, N.dk, N.grad, N.push, N.gout, N.normed_in, N.gate_grad, N.w_step, N.signal, N.step_pre,
        N.selected, N.inner, N.conv, N.same, N.w_sel, N.w_in, N.tok, N.grad_mid,
    )
    return staged_call(
        kernel, "back_part", cid, 120, ins, outs, scratch,
        late=late, early=(N.tokens_out, N.up_own), raw=(N.states,),
    )


def middle_kernel(
    depth, stage,
    scanned, signal, gate_in, skip, w_out, tok, cot_all, up_early, up_rows, down0, down1, w_router, rows_in, picks,
    output, grad_mid, mixed_grad, gate_grad, grad_out, grad_up, down_own, sums,
    gated, part, sib, mix, far, routed_all, marks_all, hidden_all, pre_all, slot_all, back_all,
    w_up, grad_down, down_got,
    near_s, near_r, away_s, away_r, gs, gr, zs, zr, ds, dr, ls,
):
    z, p = here()
    core = lax.rem(p, 2)
    chip = lax.div(p, 2)
    twin = (z, p + 1 - 2 * core)
    count = tok.shape[0]
    pair = 2 * count

    def chip_at(k):
        return lax.rem(chip + k, CHIPS)

    def rows_of(q):
        return pl.ds(pl.multiple_of(q * pair, pair), pair)

    def near(i, k):
        return remote(part.at[i, k, 1 - core], sib.at[i, k], near_s.at[i, k], near_r.at[i, k], twin)

    def away(i, k):
        return remote(
            mix.at[i, k], far.at[i, k], away_s.at[i, k], away_r.at[i, k], (z, lax.rem(p + 2 * k, PLANE))
        )

    def pass_away(i, k):
        near(i, k).wait_recv()
        mix[i, k] = (part[i, k, core].astype(f32) + sib[i, k].astype(f32)).astype(bf16)
        away(i, k).start()

    def gathered(i):
        near(i, 0).wait_recv()
        total = part[i, 0, core].astype(f32) + sib[i, 0].astype(f32)
        for k in range(1, CHIPS):
            away(i, k).wait_recv()
            total = total + far[i, k].astype(f32)
        return total

    def shared(i, ref, k):
        return remote(ref.at[p], ref.at[p], gs.at[i, k], gr.at[i, k], (z, lax.rem(p + 2 * k, PLANE)))

    def onward(i, ref, k):
        src = lax.rem(p + 2 * k, PLANE)
        return remote(ref.at[src], ref.at[src], gs.at[i, CHIPS + k], gr.at[i, CHIPS + k], twin)

    def arrived(k, refs):
        @pl.when(k == 0)
        def _():
            for i, ref in refs:
                remote(ref.at[p], ref.at[p], gs.at[i, 0], gr.at[i, 0], twin).wait_recv()

        @pl.when(k > 0)
        def _():
            for i, ref in refs:
                shared(i, ref, CHIPS - k).wait_recv()
                onward(i, ref, k).start()
            for i, ref in refs:
                onward(i, ref, k).wait_recv()

    greet(True, depth)
    stage.need(N.up_rows)
    early, late = split_rows(up_rows.shape[0])
    local = [
        pltpu.make_async_copy(up_rows.at[late], w_up.at[z, late], ls.at[0]),
        pltpu.make_async_copy(up_early, w_up.at[:, early], ls.at[1]),
    ]
    for c in local:
        c.start()
    column_start(depth, up_rows.at[late], w_up, zs, zr, late)
    stage.need(N.w_out, N.scanned, N.signal, N.gate_in)
    @pl.loop(0, CHIPS)
    def _(turn):
        k = lax.rem(turn + 1, CHIPS)
        q = chip_at(k)

        @pl.when(turn > 0)
        def _():
            pass_away(0, turn)

        at = rows_of(q)
        pre = scanned[at, :WIDE] + skip[6:7] * signal[at, :].astype(f32)
        inward = gate_in[at, :].astype(f32)
        gated[at, :] = (pre * (inward * jax.nn.sigmoid(inward))).astype(bf16)
        part[0, k] = mm(gated[at, :], w_out[...]).astype(bf16).reshape(2, count, D)
        near(0, k).start()

    branch = gathered(0)

    stage.need(N.tok, N.w_router, N.cot_all, N.down0, N.down1)
    gain, router0, router1 = rows_in[1:2], rows_in[2:3], rows_in[3:4]
    middle = tok[...].astype(f32) + branch
    scale = lax.rsqrt(jnp.mean(middle * middle, axis=-1, keepdims=True) + epsilon)
    normed = middle * scale
    routed = (normed * gain).astype(bf16)
    routed_all[p] = routed
    logits = mm(routed, w_router[...])
    l0, l1 = logits[:, 66:67], logits[:, 67:68]
    top = jnp.maximum(l0, l1)
    e0, e1 = jnp.exp(l0 - top), jnp.exp(l1 - top)
    p0, p1 = e0 / (e0 + e1), e1 / (e0 + e1)
    taken = jnp.broadcast_to(picks[...].astype(f32), (count, count)).T[:, 0:1]
    c0 = (taken == 0).astype(f32)
    c1 = (taken == 1).astype(f32)
    chosen = jnp.where(lax.broadcasted_iota(jnp.int32, (count, 128), 1) == 0, c0, c1).astype(bf16)
    before = lax.broadcasted_iota(jnp.int32, (count, count), 0) >= lax.broadcasted_iota(
        jnp.int32, (count, count), 1
    )
    places = mm(before.astype(f32).astype(bf16), chosen)
    s0 = c0 * (places[:, 0:1] <= CAP).astype(f32)
    s1 = c1 * (places[:, 1:2] <= CAP).astype(f32)
    gate = p0 * c0 + p1 * c1
    kept = s0 + s1
    weight = gate * kept
    lane = lax.broadcasted_iota(jnp.int32, (count, 128), 1)
    marks_all[p] = jnp.where(lane == 0, weight, jnp.where(lane == 1, s0, s1)).T[:8]
    share_start(routed_all.at[p], routed_all, gs.at[0], gr.at[0])
    share_start(marks_all.at[p], marks_all, gs.at[1], gr.at[1])
    for c in local:
        c.wait()
    column_forward(depth, w_up, zs, zr, late)
    column_finish(depth, up_rows.at[late], w_up, zs, zr, late)

    odd = lax.broadcasted_iota(jnp.int32, (1, EXPERTS * HID), 1) >= HID

    @pl.loop(0, CHIPS)
    def _(k):
        q = chip_at(k)
        arrived(k, ((0, routed_all), (1, marks_all)))

        @pl.when(k > 1)
        def _():
            pass_away(1, k - 1)
            pass_away(2, k - 1)

        both = pl.ds(2 * q, 2)
        marks = [
            jnp.concatenate([marks_all[2 * q + i], jnp.zeros((120, count), f32)], axis=0).T for i in range(2)
        ]
        marks = jnp.concatenate(marks, axis=0)
        mask = jnp.where(odd, marks[:, 2:3], marks[:, 1:2])
        hidden = mm(routed_all[both].reshape(pair, D), w_up[...].reshape(D, EXPERTS * HID))
        slot = (cot_all[rows_of(q), :].astype(f32) * marks[:, 0:1]).astype(bf16)
        slot_all[q] = slot
        square = hidden * hidden
        bend = jnp.tanh(GELU * hidden * (1.0 + 0.044715 * square))
        units = (0.5 * hidden * (1.0 + bend) * mask).astype(bf16)
        hidden_all[q] = units
        slope = 0.5 * (1.0 + bend) + 0.5 * GELU * hidden * (1.0 - bend * bend) * (1.0 + 3 * 0.044715 * square)
        grad = jnp.concatenate([contract_cols(slot, down0[...]), contract_cols(slot, down1[...])], axis=1)
        grad = (slope * grad * mask).astype(bf16)
        pre_all[q] = grad
        made = mm(units[:, :HID], down0[...]) + mm(units[:, HID:], down1[...])
        part[1, k] = made.astype(bf16).reshape(2, count, D)
        near(1, k).start()
        part[2, k] = contract_cols(grad, w_up[...].reshape(D, EXPERTS * HID)).astype(bf16).reshape(2, count, D)
        near(2, k).start()

    pass_away(1, CHIPS - 1)
    pass_away(2, CHIPS - 1)
    every = CHIPS * pair
    fs = HID // depth
    for c in range(0, D, 384):
        for e in range(EXPERTS):
            made = contract_rows(
                hidden_all[:, :, e * HID : e * HID + HID].reshape(every, HID),
                slot_all[:, :, c : c + 384].reshape(every, 384),
            )
            for k in range(depth):
                grad_down[k, e, :, c : c + 384] = made[k * fs : k * fs + fs].astype(bf16)
    down = []
    for k in range(1, depth):
        q = lax.rem(z + k, depth)
        down.append(send(grad_down.at[q], down_got.at[k], ds.at[k], dr.at[k], (q, p)))
    expert_tok = gathered(1)
    slot_back = gathered(2)

    up = cot_all[pl.ds(pl.multiple_of(p * count, count), count), :].astype(f32)
    output[...] = (middle + weight * expert_tok).astype(bf16)
    stage.done(N.output)
    pull = jnp.sum(up * expert_tok, axis=-1, keepdims=True) * kept * gate
    g0, g1 = pull * (c0 - p0), pull * (c1 - p1)
    grad_routed = slot_back + g0 * router0 + g1 * router1
    routed = routed.astype(f32)
    sum0 = jnp.sum(grad_routed * normed, axis=0, keepdims=True)
    sum1 = jnp.sum(routed * g0, axis=0, keepdims=True)
    sum2 = jnp.sum(routed * g1, axis=0, keepdims=True)
    grad_normed = grad_routed * gain
    inner = jnp.mean(grad_normed * normed, axis=-1, keepdims=True)
    total = scale * (grad_normed - normed * inner) + up
    grad_mid[...] = total
    stage.done(N.grad_mid)
    back_all[p] = total.astype(bf16)
    share_start(back_all.at[p], back_all, gs.at[2], gr.at[2])
    for c in range(0, D, 384):
        grad_up[c : c + 384, :] = contract_rows(
            routed_all[:, :, c : c + 384].reshape(every, 384), pre_all[...].reshape(every, EXPERTS * HID)
        ).astype(bf16)
    stage.done(N.grad_up)

    sums[...] = jnp.zeros_like(sums)
    sums[0:1], sums[1:2], sums[2:3] = sum0, sum1, sum2

    @pl.loop(0, CHIPS)
    def _(k):
        q = chip_at(k)
        arrived(k, ((2, back_all),))
        at = rows_of(q)
        grad = contract_cols(back_all[pl.ds(2 * q, 2)].reshape(pair, D), w_out[...])
        inward = gate_in[at, :].astype(f32)
        sig = jax.nn.sigmoid(inward)
        act = inward * sig
        through = grad * act
        sums[3:4, :WIDE] += jnp.sum(through * signal[at, :].astype(f32), axis=0, keepdims=True)
        mixed_grad[at, :WIDE] = through
        mixed_grad[at, WIDE:] = jnp.zeros((pair, PAD), f32)
        pre = scanned[at, :WIDE] + skip[6:7] * signal[at, :].astype(f32)
        gate_grad[at, :] = (grad * pre * (sig * (1.0 + inward * (1.0 - sig)))).astype(bf16)
    stage.done(N.mixed_grad, N.gate_grad)
    for c in range(0, D, 384):
        grad_out[:, c : c + 384] = contract_rows(
            gated[...], back_all[:, :, c : c + 384].reshape(every, 384)
        ).astype(bf16)
    for c in down:
        c.wait_recv()
    total = grad_down[z].astype(f32)
    for k in range(1, depth):
        total = total + down_got[k].astype(f32)
    down_own[...] = total
    for c in down:
        c.wait_send()
    for i in range(3):
        for k in range(CHIPS):
            near(i, k).wait_send()
            if k:
                away(i, k).wait_send()
    for i, ref in ((0, routed_all), (1, marks_all), (2, back_all)):
        remote(ref.at[p], ref.at[p], gs.at[i, 0], gr.at[i, 0], twin).wait_send()
        for k in range(1, CHIPS):
            shared(i, ref, k).wait_send()
            onward(i, ref, k).wait_send()


def middle_part(cid, depth, **ins):
    count, rows = ins[N.tok].shape[0], ins[N.cot_all].shape[0]
    wide = EXPERTS * HID
    block = (CHIPS, count, D)
    outs = dict(
        output=made(count, D, dtype=bf16),
        grad_mid=made(count, D),
        mixed_grad=made(rows, WIDE + PAD),
        gate_grad=made(rows, WIDE, dtype=bf16),
        grad_out=made(WIDE, D, dtype=bf16),
        grad_up=made(D, wide, dtype=bf16),
        down_own=made(EXPERTS, HID // depth, D),
        sums=made(8, D),
    )
    scratch = (
        [
            pltpu.VMEM((rows, WIDE), bf16),
            pltpu.VMEM((3, CHIPS, 2, count, D), bf16),
            pltpu.VMEM((3,) + block, bf16),
            pltpu.VMEM((3,) + block, bf16),
            pltpu.VMEM((3,) + block, bf16),
            pltpu.VMEM((PLANE, count, D), bf16),
            pltpu.VMEM((PLANE, 8, count), f32),
            pltpu.VMEM((CHIPS, 2 * count, wide), bf16),
            pltpu.VMEM((CHIPS, 2 * count, wide), bf16),
            pltpu.VMEM((CHIPS, 2 * count, D), bf16),
            pltpu.VMEM((PLANE, count, D), bf16),
            pltpu.VMEM((depth, D // depth, wide), bf16),
            pltpu.VMEM((depth, EXPERTS, HID // depth, D), bf16),
            pltpu.VMEM((depth, EXPERTS, HID // depth, D), bf16),
        ]
        + [DMA((3, CHIPS))] * 4
        + [DMA((3, PLANE))] * 2
        + [DMA((depth,))] * 4
        + [DMA((2,))]
    )
    late = (
        N.up_rows, N.w_out, N.scanned, N.signal, N.gate_in, N.tok, N.w_router, N.cot_all, N.down0, N.down1,
    )
    return staged_call(
        functools.partial(middle_kernel, depth), "middle_part", cid, 75, ins, outs, scratch,
        late=late, early=(N.output, N.grad_mid, N.grad_up, N.mixed_grad, N.gate_grad), raw=(N.up_early,),
    )


def tree(parts):
    row = lax.broadcasted_iota(jnp.int32, parts[0].shape, 0)
    for step in (1, 2, 4):
        low = (row // step) % 2 == 0
        parts = [
            jnp.where(low, a, b) + pltpu.roll(jnp.where(low, b, a), step, 0)
            for a, b in zip(parts[::2], parts[1::2])
        ]
    return parts[0]


def lane_tiles(x):
    total = x[:, :128]
    for k in range(128, x.shape[1], 128):
        total = total + x[:, k : k + 128]
    return total


def spread(ref, i):
    return jnp.broadcast_to(ref[pl.ds(i, 1), :], (8, ref.shape[1]))


HALVES = (slice(0, 8), slice(8, 16))


def ends_loop(dk, push, sel, slope):
    blocks = dk.shape[0] // BLK // 2

    def block(b, carry):
        hidden, acc = [list(carry[:2]), list(carry[2:4])], list(carry[4:])
        for t in range(BLK):
            for j in range(2):
                at = b + j * blocks
                base = pl.multiple_of(at * BLK, BLK)
                d, u = spread(dk, base + t), spread(push, base + t)
                for k, h in enumerate(HALVES):
                    hidden[j][k] = jnp.exp2(d * slope[k]) * hidden[j][k] + sel[at, h, t : t + 1] * u
                acc[j] = acc[j] + d
        return (*hidden[0], *hidden[1], *acc)

    zero = jnp.zeros(slope[0].shape, f32)
    done = lax.fori_loop(0, blocks, block, (zero,) * 6)
    return done[:2], done[2:4], done[4], done[5]


def scan_kernel(
    depth, stage, onward,
    dk, push, sel, rate, up_rows, cot, w_down,
    out, states, ends, up_all, cot_all, down_all,
    slots, gs, gr, es, er, zs, zr, ks, ls,
):
    z, p = here()
    tile = slots.shape[2]
    early = split_rows(up_rows.shape[0])[0]
    tiles = dk.shape[0] // tile
    local = [
        pltpu.make_async_copy(up_rows.at[early], up_all.at[z], ls.at[0]),
        pltpu.make_async_copy(cot, cot_all.at[p], ls.at[1]),
        pltpu.make_async_copy(w_down.at[1], down_all.at[z], ls.at[2]),
    ]
    stage.need(N.cot)
    for c in local:
        c.start()
    first = share_start(cot, cot_all, gs, gr)
    slope = [rate[h, :] * LOG2E for h in HALVES]
    one, two, span_one, span_two = ends_loop(dk, push, sel, slope)
    for i, h in enumerate(HALVES):
        ends[z, h] = jnp.exp2(span_two * slope[i]) * one[i] + two[i]
    ends[z, 16:] = span_one + span_two
    mine = []
    for k in range(1, depth):
        mine.append(send(ends.at[z], ends.at[z], es.at[k], er.at[k], (lax.rem(z + k, depth), p)))
    column_start(depth, up_rows.at[early], up_all, zs.at[0], zr.at[0])
    column_start(depth, w_down.at[1], down_all, zs.at[1], zr.at[1])
    onward()
    second = share_forward(cot_all, first, gs, gr)
    for c in local:
        c.wait()
    for c in mine:
        c.wait_recv()
    hidden = [jnp.zeros(slope[0].shape, f32)] * 2
    for k in range(depth - 1):
        for i, h in enumerate(HALVES):
            hidden[i] = jnp.where(k < z, jnp.exp2(ends[k, 16:] * slope[i]) * hidden[i] + ends[k, h], hidden[i])

    middle = [jnp.exp2(span_one * slope[i]) * hidden[i] + one[i] for i in range(2)]
    steps = tiles // 2

    def stored(i, slot, j):
        return pltpu.make_async_copy(
            slots.at[slot, j],
            states.at[pl.ds(pl.multiple_of((i + j * steps) * tile, tile), tile)],
            ks.at[slot, j],
        )

    def piece(i, carry):
        slot = lax.rem(i, 2)

        @pl.when(i >= 2)
        def _():
            for j in range(2):
                stored(i - 2, slot, j).wait()

        def block(m, carry):
            hidden = [list(carry[:2]), list(carry[2:])]
            inside = m * BLK
            parts = [[], []]
            for t in range(BLK):
                for j in range(2):
                    b = (i + j * steps) * (tile // BLK) + m
                    base = pl.multiple_of(b * BLK, BLK)
                    d, u = spread(dk, base + t), spread(push, base + t)
                    line = None
                    for k, h in enumerate(HALVES):
                        now = jnp.exp2(d * slope[k]) * hidden[j][k] + sel[b, h, t : t + 1] * u
                        hidden[j][k] = now
                        slots[slot, j, inside + t, h] = now
                        y = sel[b, STATE + 8 * k : STATE + 8 * k + 8, t : t + 1] * now
                        line = y if line is None else line + y
                    parts[j].append(line)
                    if len(parts[j]) == 8:
                        out[pl.ds(pl.multiple_of(base + t - 7, 8), 8), :] = tree(parts[j])
                        parts[j] = []
            return (*hidden[0], *hidden[1])

        carry = lax.fori_loop(0, tile // BLK, block, carry)
        for j in range(2):
            stored(i, slot, j).start()
        return carry

    carry = lax.fori_loop(0, steps // 2 + 1, piece, (*hidden, *middle))
    column_forward(depth, up_all, zs.at[0], zr.at[0])
    lax.fori_loop(steps // 2 + 1, steps, piece, carry)
    stage.done(N.scanned)
    column_forward(depth, down_all, zs.at[1], zr.at[1])
    for i in (steps - 2, steps - 1):
        for j in range(2):
            stored(i, i % 2, j).wait()
    share_finish(first, second)
    column_finish(depth, up_rows.at[early], up_all, zs.at[0], zr.at[0])
    column_finish(depth, w_down.at[1], down_all, zs.at[1], zr.at[1])
    for c in mine:
        c.wait_send()


def message_loop(dk, grad, sel, slope):
    blocks = dk.shape[0] // BLK // 2

    def block(i, carry):
        message, acc = [list(carry[:2]), list(carry[2:4])], carry[4]
        for t in reversed(range(BLK)):
            for j in range(2):
                b = blocks - 1 - i + j * blocks
                base = pl.multiple_of(b * BLK, BLK)
                d, g = spread(dk, base + t), spread(grad, base + t)
                for k, h in enumerate(HALVES):
                    r = sel[b, STATE + 8 * k : STATE + 8 * k + 8, t : t + 1]
                    message[j][k] = jnp.exp2(d * slope[k]) * (r * g + message[j][k])
                if j == 0:
                    acc = acc + d
        return (*message[0], *message[1], acc)

    zero = jnp.zeros(slope[0].shape, f32)
    done = lax.fori_loop(0, blocks, block, (zero,) * 5)
    return [done[k] + jnp.exp2(done[4] * slope[k]) * done[2 + k] for k in range(2)]


def adjoint_kernel(
    depth, stage, after,
    dk, push, grad, sel, states, rate, ends, gup, gout,
    g_push, g_step, g_sel, g_rate, up_own, out_own,
    slots, notes, up_got, out_got, es, er, zs, zr, ks,
):
    z, p = here()
    tile = slots.shape[1]
    tiles = dk.shape[0] // tile
    per = tile // BLK

    def fetch(i, slot):
        return pltpu.make_async_copy(
            states.at[pl.ds(pl.multiple_of(i * tile, tile), tile)], slots.at[slot], ks.at[slot]
        )

    fetch(tiles - 1, 0).start()
    fetch(tiles - 2, 1).start()
    greet(True, depth)
    first = gup.shape[1] // 64 * 16
    pieces = (pl.ds(0, first), pl.ds(first, gup.shape[1] - first))
    stage.need(N.gup)
    down = []
    for k in range(1, depth):
        q = lax.rem(z + k, depth)
        down.append(
            send(gup.at[q, pieces[0]], up_got.at[k, pieces[0]], zs.at[1, k], zr.at[1, k], (q, p))
        )
    stage.need(N.sel, N.dk, N.grad)
    slope = [rate[h, :] * LOG2E for h in HALVES]
    notes[z, :8], notes[z, 8:] = message_loop(dk, grad, sel, slope)
    mine = []
    for k in range(1, depth):
        mine.append(send(notes.at[z], notes.at[z], es.at[k], er.at[k], (lax.rem(z + k, depth), p)))
    stage.need(N.push)
    for k in range(1, depth):
        q = lax.rem(z + k, depth)
        down.append(
            send(gup.at[q, pieces[1]], up_got.at[k, pieces[1]], zs.at[0, k], zr.at[0, k], (q, p))
        )
    stage.need(N.gout)
    for k in range(1, depth):
        q = lax.rem(z + k, depth)
        down.append(send(gout.at[q], out_got.at[k], zs.at[2, k], zr.at[2, k], (q, p)))
    for c in mine:
        c.wait_recv()
    message = [jnp.zeros(slope[0].shape, f32)] * 2
    for k in range(depth - 1, 0, -1):
        for i, h in enumerate(HALVES):
            message[i] = jnp.where(k > z, notes[k, h] + jnp.exp2(ends[k, 16:] * slope[i]) * message[i], message[i])
    lane = lax.broadcasted_iota(jnp.int32, (STATE, 128), 1)
    ones = jnp.ones((128, 128), bf16)

    def piece(n, carry):
        i = tiles - 1 - n
        slot = lax.rem(n, 2)
        fetch(i, slot).wait()

        def block(m, carry):
            message, acc = list(carry[:2]), list(carry[2:])
            j = per - 1 - m
            b = i * per + j
            base = pl.multiple_of(b * BLK, BLK)
            inside = j * BLK
            w, r = sel[b, :STATE], sel[b, STATE:]
            pushes, steps = [], []
            reads, writes = [None] * (2 * BLK), [None] * (2 * BLK)
            for t in reversed(range(BLK)):
                d, u, g = spread(dk, base + t), spread(push, base + t), spread(grad, base + t)
                plain = jnp.where(d < RESET, d, 0.0)
                to_push = to_step = None
                for k, h in enumerate(HALVES):
                    wt = w[h, t : t + 1]
                    hidden = slots[slot, inside + t, h]
                    total = r[h, t : t + 1] * g + message[k]
                    reads[2 * t + k] = lane_tiles(hidden * g)
                    writes[2 * t + k] = lane_tiles(total * u)
                    x = total * wt
                    carried = total * (hidden - wt * u)
                    y = carried * slope[k]
                    to_push = x if k == 0 else to_push + x
                    to_step = y if k == 0 else to_step + y
                    acc[k] = acc[k] + carried * plain
                    message[k] = jnp.exp2(d * slope[k]) * total
                pushes.insert(0, to_push)
                steps.insert(0, to_step)
                if len(pushes) == 8:
                    at = pl.ds(pl.multiple_of(base + t, 8), 8)
                    g_push[at, :] = tree(pushes)
                    g_step[at, :] = tree(steps)
                    pushes, steps = [], []
            for j2, quantity in enumerate((writes, reads)):
                x = jnp.concatenate(quantity, axis=0)
                high = x.astype(bf16)
                low = (x - high.astype(f32)).astype(bf16)
                sums = jnp.dot(high, ones, preferred_element_type=f32)
                sums = sums + jnp.dot(low, ones, preferred_element_type=f32)
                kept = jnp.zeros((STATE, 128), f32)
                for t in range(BLK):
                    kept = jnp.where(lane == t, sums[STATE * t : STATE * t + STATE], kept)
                g_sel[b, STATE * j2 : STATE * j2 + STATE] = kept[:, :BLK]
            return message[0], message[1], acc[0], acc[1]

        carry = lax.fori_loop(0, per, block, carry)

        @pl.when(n + 2 < tiles)
        def _():
            fetch(i - 2, slot).start()

        return carry

    zero = jnp.zeros(slope[0].shape, f32)
    done = lax.fori_loop(0, tiles, piece, (message[0], message[1], zero, zero))
    g_rate[:8], g_rate[8:] = done[2], done[3]
    after()
    for c in down:
        c.wait_recv()
    total = gup[z].astype(f32)
    for k in range(1, depth):
        total = total + up_got[k].astype(f32)
    rim = up_own.shape[1]
    for q in range(PLANE):
        up_own[q] = total[q * rim : q * rim + rim].astype(bf16)
    total = gout[z].astype(f32)
    for k in range(1, depth):
        total = total + out_got[k].astype(f32)
    out_own[...] = total
    def finish():
        for c in mine + down:
            c.wait_send()

    return finish


def last_kernel(count, *refs):
    ins, outs, held = refs[:count], refs[count : 2 * count], refs[2 * count : 3 * count]
    in_sem, out_sem = refs[3 * count :]
    arriving = [pltpu.make_async_copy(ins[i], held[i], in_sem.at[i]) for i in range(count)]
    for c in arriving:
        c.start()
    leaving = [pltpu.make_async_copy(held[i], outs[i], out_sem.at[i]) for i in range(count)]
    for a, b in zip(arriving, leaving):
        a.wait()
        b.start()
    for c in leaving:
        c.wait()


def last_part(*results):
    count = len(results)
    return pl.pallas_call(
        functools.partial(last_kernel, count),
        out_shape=[jax.ShapeDtypeStruct(r.shape, r.dtype) for r in results],
        in_specs=[ANY] * count,
        out_specs=[ANY] * count,
        scratch_shapes=[pltpu.VMEM(r.shape, r.dtype) for r in results] + [DMA((count,))] * 2,
        compiler_params=params(),
        cost_estimate=cost(5),
        name="last_part",
    )(*results)


def body(
    depth,
    tokens,
    segments,
    routes,
    norm_gain,
    in_proj,
    conv_taps,
    conv_bias,
    select_proj,
    step_proj,
    step_bias,
    decay_log,
    skip_gain,
    out_proj,
    moe_gain,
    router,
    expert_up,
    expert_down,
    cotangent,
):
    count = tokens.shape[0]
    rows = PLANE * count
    rim = norm_gain.shape[0]
    ch = conv_bias.shape[0]
    fs = expert_down.shape[1]
    z, p = here()

    ids = jnp.concatenate([jnp.full((3,), -1, jnp.int32), segments, jnp.full((BLK,), -2, jnp.int32)])
    local_ids = lax.dynamic_slice_in_dim(ids, z * rows, rows + 3 + BLK)
    own_ids = local_ids[3:]
    inside = own_ids >= 0
    same = jnp.stack(
        [(local_ids[k : k + rows + BLK] == own_ids) & inside for k in range(4)], axis=1
    ).astype(f32)
    same = jnp.pad(same, ((0, 0), (0, 124)))
    (
        normed_in,
        w_in,
        w_route,
        small,
        w_sel,
        w_step,
        vecs,
        rate,
        inner,
        gate_in,
        conv,
        signal,
        selected,
        mixes,
        step_pre,
        dk,
        push,
        up_rows,
        down0,
        out_all,
        scanned,
        states,
        ends,
        up_early,
        cot_all,
        down1,
    ) = front_part(
        1,
        depth,
        tok=tokens,
        in_proj=in_proj,
        norm_gain=norm_gain[None],
        moe_gain=moe_gain[None],
        router=router.T,
        expert_up=expert_up.transpose(1, 0, 2),
        select=select_proj,
        step=step_proj,
        decay=decay_log,
        taps=conv_taps,
        bias=conv_bias[None],
        offset=step_bias[None],
        skip=skip_gain[None],
        w_down=expert_down,
        w_out=out_proj,
        same=same,
        cot=cotangent,
    )
    w_out = out_all.reshape(WIDE, D)
    output, grad_mid, mixed_wide, grad_gate_in, grad_out_w, grad_up, grad_down_own, sums = middle_part(
        3,
        depth,
        scanned=scanned,
        signal=signal,
        gate_in=gate_in,
        skip=vecs,
        w_out=w_out,
        tok=tokens,
        cot_all=cot_all.reshape(rows, D),
        up_early=up_early,
        up_rows=up_rows,
        down0=down0.reshape(HID, D),
        down1=down1.reshape(HID, D),
        w_router=w_route,
        rows_in=small,
        picks=routes.T,
    )
    (
        grad_tokens,
        grad_in,
        grad_up_own,
        grad_sel,
        grad_step,
        grad_decay,
        grad_taps,
        grad_bias,
        grad_offset,
        grad_skip,
        grad_norm,
        grad_moe,
        grad_router,
        grad_out_own,
    ) = back_part(
        5,
        depth,
        rim,
        ch,
        dk=dk,
        push=push,
        grad=mixed_wide,
        sel=mixes,
        states=states,
        ends=ends,
        gup=grad_up.reshape(depth, D // depth, EXPERTS * HID),
        gout=grad_out_w.reshape(depth, ch, D),
        step_pre=step_pre,
        signal=signal,
        conv=conv,
        inner=inner,
        same=same,
        vecs=vecs,
        rate=rate,
        selected=selected,
        w_sel=w_sel,
        w_step=w_step,
        gate_grad=grad_gate_in,
        w_in=w_in,
        normed_in=normed_in,
        tok=tokens,
        gain=small,
        grad_mid=grad_mid,
        sums=sums,
    )
    (
        output,
        grad_tokens,
        grad_norm,
        grad_in,
        grad_taps,
        grad_bias,
        grad_sel,
        grad_step,
        grad_offset,
        grad_decay,
        grad_skip,
        grad_out_own,
        grad_moe,
        grad_router,
        grad_up_own,
        grad_down_own,
    ) = last_part(
        output,
        grad_tokens,
        grad_norm,
        grad_in,
        grad_taps,
        grad_bias,
        grad_sel,
        grad_step,
        grad_offset,
        grad_decay,
        grad_skip,
        grad_out_own,
        grad_moe,
        grad_router,
        grad_up_own,
        grad_down_own,
    )
    return (
        output,
        grad_tokens,
        grad_norm[0],
        grad_in,
        grad_taps,
        grad_bias[0],
        grad_sel,
        grad_step,
        grad_offset[0],
        grad_decay,
        grad_skip[0],
        grad_out_own,
        grad_moe[0],
        grad_router.T,
        grad_up_own.transpose(1, 0, 2),
        grad_down_own,
    )


def solution(mesh):
    planes = Mesh(mesh.devices.reshape(-1, PLANE), ("z", "p"))
    every = ("z", "p")
    rows, flat, cols, third = P(every, None), P(every), P(None, every), P(None, every, None)
    return jax.shard_map(
        functools.partial(body, planes.shape["z"]),
        mesh=planes,
        in_specs=(
            rows, P(), rows, flat, rows, cols, flat, rows, cols,
            flat, cols, flat, rows, flat, rows, third, third, rows,
        ),
        out_specs=(
            rows, rows, flat, rows, cols, flat, rows, cols,
            flat, cols, flat, rows, flat, rows, third, third,
        ),
        check_vma=False,
    )
```

```python
import functools

import jax
import jax.numpy as jnp
from jax import lax
from jax.experimental import pallas as pl
from jax.experimental.pallas import tpu as pltpu
from jax.sharding import Mesh, PartitionSpec as P

D = 1152
DI = 2304
FF = 3072
RANK = 72
STATE = 16
EXPERTS = 2
CAP = 68
SEL = RANK + 2 * STATE

PLANE = 8
CHIPS = PLANE // 2
WIDE = DI // PLANE
PAD = -WIDE % 128
HID = FF // PLANE
BLK = 16
LOG2E = 1.4426950408889634
GELU = 0.7978845608028654
RESET = 1e5


def split_rows(rows):
    early = rows // 64 * 16
    return pl.ds(0, early), pl.ds(early, rows - early)


epsilon = 1e-05

MESH = pl.DeviceIdType.MESH
ANY = pl.BlockSpec(memory_space=pl.ANY)
VM = pl.BlockSpec(memory_space=pltpu.VMEM)
bf16 = jnp.bfloat16
f32 = jnp.float32
DMA = pltpu.SemaphoreType.DMA


def params(cid=None, grid=None):
    extra = {} if cid is None else {"collective_id": cid, "has_side_effects": True}
    if grid is not None:
        extra["dimension_semantics"] = grid
    return pltpu.CompilerParams(vmem_limit_bytes=60 * 1024 * 1024, **extra)


def cost(us):
    return pl.CostEstimate(flops=int(us * 1e9), bytes_accessed=int(us * 3e6), transcendentals=0)


def mm(left, right):
    return jnp.dot(left, right, preferred_element_type=f32)


def contract_rows(left, right):
    return lax.dot_general(left, right, (((0,), (0,)), ((), ())), preferred_element_type=f32)


def contract_cols(left, right):
    return lax.dot_general(left, right, (((1,), (1,)), ((), ())), preferred_element_type=f32)


class Names:
    def __getattr__(self, name):
        return name


N = Names()


class Stage:
    def __init__(self, fetches, flushes):
        self.fetches, self.flushes, self.going = fetches, flushes, []
        for copy in fetches.values():
            copy.start()

    def need(self, *names):
        for name in names:
            self.fetches.pop(name).wait()

    def done(self, *names):
        for name in names:
            self.flushes[name].start()
            self.going.append(self.flushes[name])

    def end(self):
        self.need(*tuple(self.fetches))
        for copy in self.going:
            copy.wait()


def staged_call(kernel, name, cid, us, ins, outs, scratch, late=(), early=(), away=(), raw=()):
    inside = [n for n in outs if n not in away]
    early = [n for n in inside if n in early]

    def body(*refs):
        refs = list(refs)
        take = lambda names: dict(zip(names, [refs.pop(0) for _ in names]))
        source, target = take(ins), take(outs)
        buffers, results = take(late), take(early)
        in_sem, out_sem = refs.pop(0), refs.pop(0)
        stage = Stage(
            {n: pltpu.make_async_copy(source[n], buffers[n], in_sem.at[i]) for i, n in enumerate(late)},
            {n: pltpu.make_async_copy(results[n], target[n], out_sem.at[i]) for i, n in enumerate(early)},
        )
        kernel(
            stage,
            *[buffers.get(n, source[n]) for n in ins],
            *[results.get(n, target[n]) for n in outs],
            *refs,
        )
        stage.end()

    return pl.pallas_call(
        body,
        out_shape=list(outs.values()),
        in_specs=[ANY if n in late or n in raw else VM for n in ins],
        out_specs=[ANY if n in early or n in away else VM for n in outs],
        scratch_shapes=[pltpu.VMEM(ins[n].shape, ins[n].dtype) for n in late]
        + [pltpu.VMEM(outs[n].shape, outs[n].dtype) for n in early]
        + [DMA((max(len(late), 1),)), DMA((max(len(early), 1),))]
        + scratch,
        compiler_params=params(cid),
        cost_estimate=cost(us),
        name=name,
    )(*ins.values())


def made(*shape, dtype=None):
    return jax.ShapeDtypeStruct(shape, dtype or f32)


def remote(src, dst, ss, rs, to):
    return pltpu.make_async_remote_copy(
        src_ref=src, dst_ref=dst, send_sem=ss, recv_sem=rs, device_id=to, device_id_type=MESH
    )


def send(src, dst, ss, rs, to):
    copy = remote(src, dst, ss, rs, to)
    copy.start()
    return copy


def here():
    return lax.axis_index("z"), lax.axis_index("p")


def greet(plane=True, depth=0):
    z, p = here()
    barrier = pltpu.get_barrier_semaphore()
    count = 0
    if plane:
        for k in range(1, PLANE):
            pl.semaphore_signal(
                barrier, inc=1, device_id=(z, lax.rem(p + k, PLANE)), device_id_type=MESH
            )
            count += 1
    for k in range(1, depth):
        pl.semaphore_signal(barrier, inc=1, device_id=(lax.rem(z + k, depth), p), device_id_type=MESH)
        count += 1
    pl.semaphore_wait(barrier, count)


def share_start(x, out, ss, rs):
    z, p = here()
    core = lax.rem(p, 2)
    copies = [send(x, out.at[p], ss.at[0], rs.at[0], (z, p + 1 - 2 * core))]
    for k in range(1, CHIPS):
        copies.append(send(x, out.at[p], ss.at[k], rs.at[k], (z, lax.rem(p + 2 * k, PLANE))))
    return copies


def share_forward(out, copies, ss, rs):
    z, p = here()
    core = lax.rem(p, 2)
    onward = []
    for k in range(1, CHIPS):
        copies[k].wait_recv()
        src = lax.rem(p + PLANE - 2 * k, PLANE)
        onward.append(
            send(out.at[src], out.at[src], ss.at[CHIPS + k], rs.at[CHIPS + k], (z, p + 1 - 2 * core))
        )
    return onward


def share_finish(copies, onward):
    copies[0].wait_recv()
    for c in copies:
        c.wait_send()
    for c in onward:
        c.wait()


def column_copy(src, out, ss, rs, frm, to, part=None):
    dst = out.at[frm] if part is None else out.at[frm, part]
    return pltpu.make_async_remote_copy(
        src_ref=dst if src is None else src,
        dst_ref=dst,
        send_sem=ss.at[to],
        recv_sem=rs.at[frm],
        device_id=(to, lax.axis_index("p")),
        device_id_type=MESH,
    )


def column_each(depth, act):
    z = lax.axis_index("z")
    for t in range(depth):
        far = abs(t - z) == depth - 1 if depth == 4 else t == z
        pl.when(jnp.logical_not((t == z) | far))(functools.partial(act, t))


def column_start(depth, src, out, ss, rs, part=None):
    z = lax.axis_index("z")
    column_each(depth, lambda t: column_copy(src, out, ss, rs, z, t, part).start())


def column_forward(depth, out, ss, rs, part=None):
    if depth != 4:
        return
    z = lax.axis_index("z")
    for me, frm, to in ((2, 0, 3), (1, 3, 0)):

        @pl.when(z == me)
        def _():
            copy = column_copy(None, out, ss, rs, frm, to, part)
            copy.wait_recv()
            copy.start()


def column_finish(depth, src, out, ss, rs, part=None):
    z = lax.axis_index("z")
    for s in range(depth):
        ahead = ((z == 2) & (s == 0)) | ((z == 1) & (s == 3)) if depth == 4 else s == z

        @pl.when(jnp.logical_not((s == z) | ahead))
        def _():
            column_copy(src, out, ss, rs, s, s, part).wait_recv()

    column_each(depth, lambda t: column_copy(src, out, ss, rs, z, t, part).wait_send())
    if depth == 4:
        for me, frm, to in ((2, 0, 3), (1, 3, 0)):

            @pl.when(z == me)
            def _():
                column_copy(None, out, ss, rs, frm, to, part).wait_send()


def softplus(x):
    return jnp.maximum(x, 0.0) + jnp.log1p(jnp.exp(-jnp.abs(x)))


def total_start(x, got, ss, rs):
    z, p = here()
    copies = []
    for k in range(1, PLANE):
        q = lax.rem(p + k, PLANE)
        copies.append(send(x.at[q], got.at[k], ss.at[k], rs.at[k], (z, q)))
    return copies


def total_share(x, got, copies, out, ts, us):
    z, p = here()
    total = x[p]
    for k in range(1, PLANE):
        copies[k - 1].wait_recv()
        total = total + got[k]
    out[p] = total.astype(bf16)
    after = [
        send(out.at[p], out.at[p], ts.at[k], us.at[k], (z, lax.rem(p + k, PLANE))) for k in range(1, PLANE)
    ]
    for c in copies:
        c.wait_send()
    return after


def front_kernel(
    depth, stage,
    tok, in_proj, norm_gain, moe_gain, router, expert_up, select, step, decay, taps, bias, offset, skip,
    w_down, w_out, same,
    normed_in, w_in, w_route, small, w_sel, w_step, vecs, rate, inner, gate_in, conv, signal, selected, mixes,
    step_pre, dk, push, up_rows, down_all, out_all,
    tok_all, win_all, pack_all, wide, thin, near, halo, x, got, sel_all, win, wup, pack, square, win_got, up_got, flat,
    gs, gr, ws, wr, vs, vr, zs, zr, hs, ss, rs, ts, us, ls,
):
    z, p = here()
    count = tok.shape[0]
    rim = in_proj.shape[0]
    ch = select.shape[0]
    pair = 2 * count
    rows = PLANE * count
    fs = expert_up.shape[2] // (depth * PLANE)
    local = [
        pltpu.make_async_copy(tok, tok_all.at[p], ls.at[0]),
        pltpu.make_async_copy(win.at[p], win_got.at[p], ls.at[1]),
        pltpu.make_async_copy(wup.at[p], up_got.at[p], ls.at[2]),
        pltpu.make_async_copy(pack, pack_all.at[z], ls.at[3]),
        pltpu.make_async_copy(w_down.at[0], down_all.at[z], ls.at[4]),
        pltpu.make_async_copy(w_out, out_all.at[z], ls.at[5]),
    ]
    for i in (0, 4, 5):
        local[i].start()
    square[...] = jnp.zeros_like(square)
    square[0:1, :rim] = norm_gain[...].astype(f32)
    square[1:2, :rim] = moe_gain[...].astype(f32)
    square[2:4, :rim] = router[...].astype(f32)
    columns = square[...].T
    square[...] = columns
    for q in range(PLANE):
        for i in range(2 * depth):
            start = (i // depth) * DI + ((i % depth) * PLANE + q) * ch
            win[q, :, i * ch : i * ch + ch] = in_proj[:, start : start + ch]
        win[q, :, 2 * WIDE :] = square[:rim, :64].astype(bf16)
    local[1].start()
    greet(True, depth)
    across = []
    for k in range(1, PLANE):
        q = lax.rem(p + k, PLANE)
        across.append(send(win.at[q], win_got.at[p], ws.at[k], wr.at[k], (z, q)))
    first = share_start(tok, tok_all, gs, gr)
    square[...] = jnp.zeros_like(square)
    square[0:STATE, :ch] = decay[...].astype(f32)
    square[STATE : STATE + 4, :ch] = taps[...].astype(f32)
    for i, ref in enumerate((bias, offset, skip)):
        square[STATE + 4 + i : STATE + 5 + i, :ch] = ref[...].astype(f32)
    columns = square[...].T
    pack[:, 256:] = columns[:ch].astype(bf16)
    square[...] = jnp.zeros_like(square)
    square[:RANK, :ch] = step[...].astype(f32)
    columns = square[...].T
    pack[:, 128:256] = columns[:ch].astype(bf16)
    pack[:, :128] = jnp.zeros((ch, 128), bf16)
    pack[:, :SEL] = select[...]
    column_start(depth, pack, pack_all, zs.at[0], zr.at[0])
    local[3].start()
    for q in range(PLANE):
        for i in range(EXPERTS * depth):
            start = ((i % depth) * PLANE + q) * fs
            wup[q, :, i * fs : i * fs + fs] = expert_up[:, i // depth, start : start + fs]
    local[2].start()
    local[1].wait()
    for c in across:
        c.wait_recv()
    for q in range(PLANE):
        flat[q * rim : q * rim + rim, :640] = win_got[q].astype(f32)
    win_all[z] = flat[:, :640].astype(bf16)
    column_start(depth, win_all.at[z], win_all, zs.at[1], zr.at[1])
    second = share_forward(tok_all, first, gs, gr)
    more = []
    for k in range(1, PLANE):
        q = lax.rem(p + k, PLANE)
        more.append(send(wup.at[q], up_got.at[p], vs.at[k], vr.at[k], (z, q)))
    local[3].wait()
    column_forward(depth, pack_all, zs.at[0], zr.at[0])
    column_finish(depth, pack, pack_all, zs.at[0], zr.at[0])
    for k in range(depth):
        thin[k * ch : k * ch + ch, :] = pack_all[k].astype(f32)
    w_sel[...] = thin[:, :128].astype(bf16)
    w_step[...] = thin[:, 128:256].astype(bf16)
    side = thin[:, 256:].T
    rate[:, :WIDE] = -jnp.exp(side[:STATE])
    rate[:, WIDE:] = jnp.zeros((STATE, PAD), f32)
    vecs[...] = side[STATE : STATE + 8]
    column_forward(depth, win_all, zs.at[1], zr.at[1])
    local[0].wait()
    share_finish(first, second)
    column_finish(depth, win_all.at[z], win_all, zs.at[1], zr.at[1])
    block = PLANE * rim
    for k in range(depth):
        w_in[k * block : k * block + block, :] = win_all[k, :, : 2 * WIDE]
        wide[k * block : k * block + block, :] = win_all[k, :, 512:].astype(f32)
    w_route[...] = wide[...].astype(bf16)
    small[...] = wide[...].T[64:72]
    gain = small[0:1]
    for b in (3, 0, 1, 2):
        at = slice(pair * b, pair * b + pair)
        values = tok_all[2 * b : 2 * b + 2].reshape(pair, D).astype(f32)
        scale = lax.rsqrt(jnp.mean(values * values, axis=-1, keepdims=True) + epsilon)
        normed = (values * scale * gain).astype(bf16)
        normed_in[at, :] = normed
        joined = mm(normed, w_in[...]).astype(bf16)
        near[BLK + pair * b : BLK + pair * b + pair, :] = joined[:, :WIDE].astype(f32)
        gate_in[at, :] = joined[:, WIDE:]
        if b == 3:
            edge = send(near.at[pl.ds(rows, BLK)], halo, hs.at[0], hs.at[1], (lax.rem(z + 1, depth), p))
            column_start(depth, w_out, out_all, zs.at[2], zr.at[2])
            column_start(depth, w_down.at[0], down_all, zs.at[3], zr.at[3])
    stage.done(N.w_in, N.normed_in, N.gate_in)
    stage.need(N.same)
    for b in (1, 2, 3, 0):
        if b == 0:
            edge.wait()
            near[:BLK, :] = halo[...]
        base = pair * b
        at = slice(base, base + pair)
        total = vecs[4:5] + vecs[0:1] * near[base + 13 : base + 13 + pair, :] * same[at, 0:1]
        for k in range(1, 4):
            total = total + vecs[k : k + 1] * near[base + 13 + k : base + 13 + k + pair, :] * same[at, k : k + 1]
        conv[at, :] = total
        value = (total * jax.nn.sigmoid(total)).astype(bf16)
        signal[at, :] = value
        x[2 * b : 2 * b + 2] = mm(value, w_sel[...]).reshape(2, count, 128)
    third = total_start(x, got, ss, rs)
    inner[...] = near[...].astype(bf16)
    stage.done(N.conv, N.signal, N.inner)
    fourth = total_share(x, got, third, sel_all, ts, us)
    local[5].wait()
    column_forward(depth, out_all, zs.at[2], zr.at[2])
    for c in fourth:
        c.wait()
    for b in range(CHIPS):
        at = slice(pair * b, pair * b + pair)
        chosen = sel_all[2 * b : 2 * b + 2].reshape(pair, 128)
        selected[at, :] = chosen
        step = contract_cols(chosen, w_step[...]) + vecs[5:6]
        step_pre[at, :] = step
        delta = softplus(step)
        dk[at, :WIDE] = delta + (1.0 - same[at, 2:3]) * RESET
        push[at, :WIDE] = delta * signal[at, :].astype(f32)
        dk[at, WIDE:] = jnp.zeros((pair, PAD), f32)
        push[at, WIDE:] = jnp.zeros((pair, PAD), f32)
        full = chosen.astype(f32)
        for i in range(pair // BLK):
            flipped = full[i * BLK : i * BLK + BLK].T
            mixes[b * (pair // BLK) + i] = flipped[RANK:SEL]
    stage.done(N.dk, N.push, N.step_pre, N.mixes, N.selected)
    local[2].wait()
    for c in across:
        c.wait_send()
    for c in more:
        c.wait()
    for q in range(PLANE):
        flat[q * rim : q * rim + rim, :] = up_got[q].astype(f32)
    up_rows[...] = flat[...].astype(bf16)

    def onward():
        local[4].wait()
        column_forward(depth, down_all, zs.at[3], zr.at[3])

    def finish():
        column_finish(depth, w_out, out_all, zs.at[2], zr.at[2])
        column_finish(depth, w_down.at[0], down_all, zs.at[3], zr.at[3])

    return onward, finish


def front_part(cid, depth, **ins):
    count, rim, ch = ins[N.tok].shape[0], ins[N.in_proj].shape[0], ins[N.select].shape[0]
    low = ins[N.w_down].shape[1]
    rows = PLANE * count
    outs = dict(
        normed_in=made(rows, D, dtype=bf16),
        w_in=made(D, 2 * WIDE, dtype=bf16),
        w_route=made(D, 128, dtype=bf16),
        small=made(8, D),
        w_sel=made(WIDE, 128, dtype=bf16),
        w_step=made(WIDE, 128, dtype=bf16),
        vecs=made(8, WIDE),
        rate=made(STATE, WIDE + PAD),
        inner=made(rows + BLK, WIDE, dtype=bf16),
        gate_in=made(rows, WIDE, dtype=bf16),
        conv=made(rows, WIDE),
        signal=made(rows, WIDE, dtype=bf16),
        selected=made(rows, 128, dtype=bf16),
        mixes=made(rows // BLK, 2 * STATE, BLK),
        step_pre=made(rows, WIDE),
        dk=made(rows, WIDE + PAD),
        push=made(rows, WIDE + PAD),
        up_rows=made(PLANE * rim, EXPERTS * HID, dtype=bf16),
        down_all=made(depth, low, D, dtype=bf16),
        out_all=made(depth, ch, D, dtype=bf16),
    )
    scratch = (
        [
            pltpu.VMEM((PLANE, count, D), bf16),
            pltpu.VMEM((depth, PLANE * rim, 640), bf16),
            pltpu.VMEM((depth, ch, 384), bf16),
            pltpu.VMEM((D, 128), f32),
            pltpu.VMEM((WIDE, 384), f32),
            pltpu.VMEM((BLK + rows, WIDE), f32),
            pltpu.VMEM((BLK, WIDE), f32),
            pltpu.VMEM((PLANE, count, 128), f32),
            pltpu.VMEM((PLANE, count, 128), f32),
            pltpu.VMEM((PLANE, count, 128), bf16),
            pltpu.VMEM((PLANE, rim, 640), bf16),
            pltpu.VMEM((PLANE, rim, EXPERTS * HID), bf16),
            pltpu.VMEM((ch, 384), bf16),
            pltpu.VMEM((128, 128), f32),
            pltpu.VMEM((PLANE, rim, 640), bf16),
            pltpu.VMEM((PLANE, rim, EXPERTS * HID), bf16),
            pltpu.VMEM((PLANE * rim, EXPERTS * HID), f32),
        ]
        + [DMA((PLANE,))] * 6
        + [DMA((4, depth))] * 2
        + [DMA((2,))]
        + [DMA((PLANE,))] * 4
        + [DMA((6,))]
    )
    early = (
        N.normed_in, N.w_in, N.inner, N.gate_in, N.conv, N.signal, N.selected, N.mixes, N.step_pre, N.dk, N.push,
    )
    up_rows, cot = outs[N.up_rows], ins[N.cot]
    outs.update(
        scanned=made(rows, WIDE + PAD),
        states=made(rows, STATE, WIDE + PAD),
        ends=made(depth, STATE + 8, WIDE + PAD),
        up_early=made(depth, split_rows(up_rows.shape[0])[0].size, up_rows.shape[1], dtype=bf16),
        cot_all=made(PLANE, *cot.shape, dtype=bf16),
        down1=made(depth, low, D, dtype=bf16),
    )
    mine = len(scratch)
    scratch = (
        scratch
        + [pltpu.VMEM((2, 2, count, STATE, WIDE + PAD), f32)]
        + [DMA((PLANE,))] * 2
        + [DMA((depth,))] * 2
        + [DMA((2, depth))] * 2
        + [DMA((2, 2)), DMA((3,))]
    )
    names = tuple(ins) + tuple(outs)

    def kernel(stage, *refs):
        ref = dict(zip(names, refs))
        held = refs[len(names) :]
        first = [ref[n] for n in names if n != N.cot][: len(ins) - 1 + 20]
        onward, finish = front_kernel(depth, stage, *first, *held[:mine])
        scan_kernel(
            depth,
            stage,
            onward,
            *(ref[n] for n in (N.dk, N.push, N.mixes, N.rate, N.up_rows, N.cot, N.w_down)),
            *(ref[n] for n in (N.scanned, N.states, N.ends, N.up_early, N.cot_all, N.down1)),
            *held[mine:],
        )
        finish()

    return staged_call(
        kernel, "front_part", cid, 110, ins, outs, scratch,
        late=(N.same, N.cot), early=early + (N.scanned,),
        away=(N.down_all, N.out_all, N.states, N.up_early, N.cot_all, N.down1),
    )


def folded(x):
    half = x.shape[0] // 2
    return jnp.concatenate([x[:half], x[half:]], axis=1).astype(bf16)


def back_kernel(
    depth, stage,
    g_push, g_step, g_mixes, g_rate, step_pre, signal, conv, inner, same, vecs, rate, selected, w_sel, w_step,
    mixed_grad, gate_grad, w_in, normed_in, tok, gain, grad_mid, sums, gup,
    tokens_out, in_own, up_own, sel_own, step_own, decay_own, taps_own, bias_own, offset_own, skip_own,
    norm_own, moe_own, router_own,
    in_out, up_out, pack_out, x, got, gsel, low, gc, halo, nearf, gj, part, sib, mix, far, gin, gin_got, own, pack, pack_got, row, row_got, sml, sml_got,
    hs, ss, rs, ts, us, near_s, near_r, away_s, away_r, zs, zr, cs, cr, ups, upr, ls,
):
    z, p = here()
    core = lax.rem(p, 2)
    chip = lax.div(p, 2)
    twin = (z, p + 1 - 2 * core)
    count = tok.shape[0]
    pair = 2 * count
    rows = PLANE * count
    ch = sel_own.shape[0]
    rim = in_own.shape[0]
    fs = up_own.shape[2] // (depth * PLANE)
    sent = []

    def down(i, src, dst):
        copies = []
        for k in range(1, depth):
            q = lax.rem(z + k, depth)
            copies.append(send(src.at[q], dst.at[k], zs.at[i, k], zr.at[i, k], (q, p)))
        return copies

    block = D // depth
    stage.need(N.normed_in, N.gate_grad)
    for q in range(depth):
        gin[1, q] = folded(contract_rows(normed_in[:, q * block : q * block + block], gate_grad[...]))
    gate_sent = down(3, gin.at[1], gin_got.at[1])
    stage.need(N.w_step, N.signal, N.step_pre)
    bias = jnp.zeros((1, WIDE), f32)
    for b in range(CHIPS):
        at = slice(pair * b, pair * b + pair)
        value = signal[at, :].astype(f32)
        grad = g_step[at, :WIDE] * (1.0 / LOG2E) + g_push[at, :WIDE] * value
        grad = grad * jax.nn.sigmoid(step_pre[at, :])
        bias = bias + jnp.sum(grad, axis=0, keepdims=True)
        low[at, :] = grad.astype(bf16)
        ranks = mm(low[at, :], w_step[...])
        for i in range(pair // BLK):
            mixed = g_mixes[b * (pair // BLK) + i]
            wide = jnp.concatenate(
                [jnp.zeros((RANK, BLK), f32), mixed, jnp.zeros((128 - SEL, BLK), f32)], axis=0
            ).T
            t = i * BLK
            x[2 * b + t // count, t % count : t % count + BLK, :] = ranks[t : t + BLK] + wide
    first = total_start(x, got, ss, rs)
    stage.need(N.selected, N.inner)
    keep = pltpu.make_async_copy(gup.at[p], up_out.at[p], ls)
    keep.start()
    grad_step_w = contract_rows(low[...], selected[...])
    nearf[...] = inner[...].astype(f32)
    second = total_share(x, got, first, gsel, ts, us)
    ups_sent = []
    for k in range(1, PLANE):
        q = lax.rem(p + k, PLANE)
        ups_sent.append(send(gup.at[q], up_out.at[p], ups.at[k], upr.at[k], (z, q)))
    for c in second:
        c.wait()
    stage.need(N.conv, N.same, N.w_sel)
    taps = [jnp.zeros((1, WIDE), f32)] * 4
    conv_bias = jnp.zeros((1, WIDE), f32)
    for b in range(CHIPS):
        base = pair * b
        at = slice(base, base + pair)
        delta = softplus(step_pre[at, :])
        grad = mixed_grad[at, :WIDE] * vecs[6:7] + g_push[at, :WIDE] * delta
        grad = grad + contract_cols(gsel[2 * b : 2 * b + 2].reshape(pair, 128), w_sel[...])
        c = conv[at, :]
        sig = jax.nn.sigmoid(c)
        grad = grad * (sig * (1.0 + c * (1.0 - sig)))
        gc[at, :] = grad
        if b == 0:
            edge = send(gc.at[pl.ds(0, BLK)], halo, hs.at[0], hs.at[1], (lax.rem(z + depth - 1, depth), p))
        conv_bias = conv_bias + jnp.sum(grad, axis=0, keepdims=True)
        for k in range(4):
            taps[k] = taps[k] + jnp.sum(
                grad * nearf[base + 13 + k : base + 13 + k + pair, :] * same[at, k : k + 1], axis=0, keepdims=True
            )
    stage.need(N.w_in, N.tok, N.grad_mid)
    for b in range(CHIPS):
        base = pair * b
        if b == CHIPS - 1:
            edge.wait()
            gc[rows : rows + BLK, :] = halo[...]
        total = jnp.zeros((pair, WIDE), f32)
        for k in range(4):
            off = slice(base + 3 - k, base + 3 - k + pair)
            total = total + gc[off, :] * vecs[k : k + 1] * same[off, k : k + 1]
        gj[base : base + pair, :WIDE] = total.astype(bf16)
        gj[base : base + pair, WIDE:] = gate_grad[base : base + pair, :]
    for q in range(depth):
        gin[0, q] = folded(contract_rows(normed_in[:, q * block : q * block + block], gj[:, :WIDE]))
    in_sent = down(0, gin.at[0], gin_got.at[0])
    near, away = {}, []
    order = (1, 2, 3, 0)
    for j, k in enumerate(order):
        q = lax.rem(chip + k, CHIPS)
        at = pl.ds(pl.multiple_of(q * pair, pair), pair)
        part[k] = contract_cols(gj[at, :], w_in[...]).astype(bf16).reshape(2, count, D)
        near[k] = send(part.at[k, 1 - core], sib.at[k], near_s.at[k], near_r.at[k], twin)
        if j > 0:
            k = order[j - 1]
            near[k].wait_recv()
            mix[k] = (part[k, core].astype(f32) + sib[k].astype(f32)).astype(bf16)
            away.append(
                send(mix.at[k], far.at[k], away_s.at[k], away_r.at[k], (z, lax.rem(p + 2 * k, PLANE)))
            )
    row[...] = jnp.zeros_like(row)
    row[0:STATE, :] = g_rate[...] * rate[...]
    for k in range(4):
        row[STATE + k : STATE + k + 1, :WIDE] = taps[k]
    row[STATE + 4 : STATE + 5, :WIDE] = conv_bias
    row[STATE + 5 : STATE + 6, :WIDE] = bias
    row[STATE + 6 : STATE + 7, :WIDE] = sums[3:4, :WIDE]
    side = row[...].T
    grad_sel_w = contract_rows(signal[...], gsel[...].reshape(rows, 128))
    for q in range(depth):
        cut = slice(q * ch, q * ch + ch)
        pack[q, :, :SEL] = grad_sel_w[cut, :SEL].astype(bf16)
        pack[q, :, SEL : SEL + RANK] = grad_step_w[cut, :RANK].astype(bf16)
        pack[q, :, SEL + RANK : SEL + RANK + 32] = side[cut].astype(bf16)
        pack[q, :, SEL + RANK + 32 :] = jnp.zeros((ch, 256 - SEL - RANK - 32), bf16)
    pack_sent = down(1, pack, pack_got)
    near[0].wait_recv()
    total = part[0, core].astype(f32) + sib[0].astype(f32)
    for k in range(1, CHIPS):
        away[k - 1].wait_recv()
        total = total + far[k].astype(f32)
    values = tok[...].astype(f32)
    scale = lax.rsqrt(jnp.mean(values * values, axis=-1, keepdims=True) + epsilon)
    normed = values * scale
    grad_normed = total * gain[0:1]
    mean = jnp.mean(grad_normed * normed, axis=-1, keepdims=True)
    tokens_out[...] = (scale * (grad_normed - normed * mean) + grad_mid[...]).astype(bf16)
    stage.done(N.tokens_out)
    ours = jnp.concatenate(
        [jnp.sum(total * normed, axis=0, keepdims=True), sums[0:3, :], jnp.zeros((4, D), f32)], axis=0
    )
    for q in range(depth):
        sml[q] = ours[:, q * block : q * block + block]
    sml_sent = down(2, sml, sml_got)
    for h, copies in ((1, gate_sent), (0, in_sent)):
        for c in copies:
            c.wait_recv()
        total = gin[h, z].astype(f32)
        for k in range(1, depth):
            total = total + gin_got[h, k].astype(f32)
        total = jnp.concatenate([total[:, :WIDE], total[:, WIDE:]], axis=0)
        for q in range(PLANE):
            own[q, :, h * WIDE : h * WIDE + WIDE] = total[q * rim : q * rim + rim].astype(bf16)
    across = []
    for k in range(1, PLANE):
        q = lax.rem(p + k, PLANE)
        across.append(send(own.at[q], in_out.at[p], cs.at[0, k], cr.at[0, k], (z, q)))
    in_out[p] = own[p]
    for c in sml_sent:
        c.wait_recv()
    total = sml[z]
    for k in range(1, depth):
        total = total + sml_got[k]
    sml_got[0] = total
    for k in range(1, PLANE):
        q = lax.rem(p + k, PLANE)
        across.append(send(sml_got.at[0], row_got.at[k], cs.at[1, k], cr.at[1, k], (z, q)))
    for c in pack_sent:
        c.wait_recv()
    total = pack[z].astype(f32)
    for k in range(1, depth):
        total = total + pack_got[k].astype(f32)
    sel_own[...] = total[:, :SEL]
    pack_out[...] = jnp.zeros_like(pack_out)
    pack_out[:ch, :RANK] = total[:, SEL : SEL + RANK]
    columns = pack_out[...].T
    step_own[...] = columns[:RANK, :ch]
    pack_out[:ch, :32] = total[:, SEL + RANK : SEL + RANK + 32]
    columns = pack_out[...].T
    decay_own[...] = columns[:STATE, :ch]
    taps_own[...] = columns[STATE : STATE + 4, :ch]
    bias_own[...] = columns[STATE + 4 : STATE + 5, :ch]
    offset_own[...] = columns[STATE + 5 : STATE + 6, :ch]
    skip_own[...] = columns[STATE + 6 : STATE + 7, :ch]
    for c in ups_sent:
        c.wait()
    keep.wait()
    for q in range(PLANE):
        for i in range(EXPERTS * depth):
            start = ((i % depth) * PLANE + q) * fs
            up_own[:, i // depth, start : start + fs] = up_out[q, :, i * fs : i * fs + fs].astype(f32)
    stage.done(N.up_own)
    for c in across:
        c.wait()
    for q in range(PLANE):
        for i in range(2 * depth):
            start = (i // depth) * DI + ((i % depth) * PLANE + q) * ch
            in_own[:, start : start + ch] = in_out[q, :, i * ch : i * ch + ch].astype(f32)
    total = sml_got[0]
    for k in range(1, PLANE):
        total = total + row_got[k]
    for q in range(PLANE):

        @pl.when(p == q)
        def _():
            cut = total[:, q * rim : q * rim + rim]
            norm_own[...] = cut[0:1]
            moe_own[...] = cut[1:2]
            router_own[...] = cut[2:4]

    for c in list(near.values()) + away + gate_sent + in_sent + pack_sent + sml_sent:
        c.wait_send()


def back_part(cid, depth, rim, ch, **ins):
    count = ins[N.tok].shape[0]
    rows, wide = ins[N.dk].shape
    block = D // depth
    gup, gout = ins[N.gup], ins[N.gout]
    outs = dict(
        tokens_out=made(count, D, dtype=bf16),
        in_own=made(rim, 2 * DI),
        up_own=made(rim, EXPERTS, FF),
        sel_own=made(ch, SEL),
        step_own=made(RANK, ch),
        decay_own=made(STATE, ch),
        taps_own=made(4, ch),
        bias_own=made(1, ch),
        offset_own=made(1, ch),
        skip_own=made(1, ch),
        norm_own=made(1, rim),
        moe_own=made(1, rim),
        router_own=made(2, rim),
        out_own=made(*gout.shape[1:]),
    )
    scratch = (
        [
            pltpu.VMEM((PLANE, rim, 2 * WIDE), bf16),
            pltpu.VMEM((PLANE, rim, EXPERTS * HID), bf16),
            pltpu.VMEM((128, 128), f32),
            pltpu.VMEM((PLANE, count, 128), f32),
            pltpu.VMEM((PLANE, count, 128), f32),
            pltpu.VMEM((PLANE, count, 128), bf16),
            pltpu.VMEM((rows, WIDE), bf16),
            pltpu.VMEM((rows + BLK, WIDE), f32),
            pltpu.VMEM((BLK, WIDE), f32),
            pltpu.VMEM((rows + BLK, WIDE), f32),
            pltpu.VMEM((rows, 2 * WIDE), bf16),
            pltpu.VMEM((CHIPS, 2, count, D), bf16),
            pltpu.VMEM((CHIPS, count, D), bf16),
            pltpu.VMEM((CHIPS, count, D), bf16),
            pltpu.VMEM((CHIPS, count, D), bf16),
            pltpu.VMEM((2, depth, block // 2, 2 * WIDE), bf16),
            pltpu.VMEM((2, depth, block // 2, 2 * WIDE), bf16),
            pltpu.VMEM((PLANE, rim, 2 * WIDE), bf16),
            pltpu.VMEM((depth, ch, 256), bf16),
            pltpu.VMEM((depth, ch, 256), bf16),
            pltpu.VMEM((2 * STATE, WIDE + PAD), f32),
            pltpu.VMEM((PLANE, 8, block), f32),
            pltpu.VMEM((depth, 8, block), f32),
            pltpu.VMEM((depth, 8, block), f32),
            DMA((2,)),
        ]
        + [DMA((PLANE,))] * 4
        + [DMA((CHIPS,))] * 4
        + [DMA((4, depth))] * 2
        + [DMA((2, PLANE))] * 2
        + [DMA((PLANE,))] * 2
        + [DMA]
    )
    mine = len(scratch)
    scratch = (
        scratch
        + [
            pltpu.VMEM((2, count, STATE, wide), f32),
            pltpu.VMEM((depth, STATE, wide), f32),
            pltpu.VMEM(gup.shape, bf16),
            pltpu.VMEM(gout.shape, bf16),
        ]
        + [DMA((depth,))] * 2
        + [DMA((3, depth))] * 2
        + [DMA((2,))]
        + [
            pltpu.VMEM((rows, wide), f32),
            pltpu.VMEM((rows, wide), f32),
            pltpu.VMEM(ins[N.sel].shape, f32),
            pltpu.VMEM((STATE, wide), f32),
            pltpu.VMEM((PLANE, rim, EXPERTS * HID), bf16),
        ]
    )
    names = tuple(ins) + tuple(outs)

    def kernel(stage, *refs):
        ref = dict(zip(names, refs))
        held = refs[len(names) :]
        g_push, g_step, g_sel, g_rate, up_part = held[-5:]
        finish = adjoint_kernel(
            depth,
            stage,
            lambda: None,
            *(ref[n] for n in (N.dk, N.push, N.grad, N.sel, N.states, N.rate, N.ends, N.gup, N.gout)),
            g_push,
            g_step,
            g_sel,
            g_rate,
            up_part,
            ref[N.out_own],
            *held[mine:-5],
        )
        back_kernel(
            depth,
            stage,
            g_push,
            g_step,
            g_sel,
            g_rate,
            *(
                ref[n]
                for n in (
                    N.step_pre, N.signal, N.conv, N.inner, N.same, N.vecs, N.rate, N.selected, N.w_sel, N.w_step,
                    N.grad, N.gate_grad, N.w_in, N.normed_in, N.tok, N.gain, N.grad_mid, N.sums,
                )
            ),
            up_part,
            *(ref[n] for n in outs if n != N.out_own),
            *held[:mine],
        )
        finish()

    late = (
        N.gup, N.sel, N.dk, N.grad, N.push, N.gout, N.normed_in, N.gate_grad, N.w_step, N.signal, N.step_pre,
        N.selected, N.inner, N.conv, N.same, N.w_sel, N.w_in, N.tok, N.grad_mid,
    )
    return staged_call(
        kernel, "back_part", cid, 120, ins, outs, scratch,
        late=late, early=(N.tokens_out, N.up_own), raw=(N.states,),
    )


def middle_kernel(
    depth, stage,
    scanned, signal, gate_in, skip, w_out, tok, cot_all, up_early, up_rows, down0, down1, w_router, rows_in, picks,
    output, grad_mid, mixed_grad, gate_grad, grad_out, grad_up, down_own, sums,
    gated, part, sib, mix, far, routed_all, marks_all, hidden_all, pre_all, slot_all, back_all,
    w_up, grad_down, down_got,
    near_s, near_r, away_s, away_r, gs, gr, zs, zr, ds, dr, ls,
):
    z, p = here()
    core = lax.rem(p, 2)
    chip = lax.div(p, 2)
    twin = (z, p + 1 - 2 * core)
    count = tok.shape[0]
    pair = 2 * count

    def chip_at(k):
        return lax.rem(chip + k, CHIPS)

    def rows_of(q):
        return pl.ds(pl.multiple_of(q * pair, pair), pair)

    def near(i, k):
        return remote(part.at[i, k, 1 - core], sib.at[i, k], near_s.at[i, k], near_r.at[i, k], twin)

    def away(i, k):
        return remote(
            mix.at[i, k], far.at[i, k], away_s.at[i, k], away_r.at[i, k], (z, lax.rem(p + 2 * k, PLANE))
        )

    def pass_away(i, k):
        near(i, k).wait_recv()
        mix[i, k] = (part[i, k, core].astype(f32) + sib[i, k].astype(f32)).astype(bf16)
        away(i, k).start()

    def gathered(i):
        near(i, 0).wait_recv()
        total = part[i, 0, core].astype(f32) + sib[i, 0].astype(f32)
        for k in range(1, CHIPS):
            away(i, k).wait_recv()
            total = total + far[i, k].astype(f32)
        return total

    def shared(i, ref, k):
        return remote(ref.at[p], ref.at[p], gs.at[i, k], gr.at[i, k], (z, lax.rem(p + 2 * k, PLANE)))

    def onward(i, ref, k):
        src = lax.rem(p + 2 * k, PLANE)
        return remote(ref.at[src], ref.at[src], gs.at[i, CHIPS + k], gr.at[i, CHIPS + k], twin)

    def arrived(k, refs):
        @pl.when(k == 0)
        def _():
            for i, ref in refs:
                remote(ref.at[p], ref.at[p], gs.at[i, 0], gr.at[i, 0], twin).wait_recv()

        @pl.when(k > 0)
        def _():
            for i, ref in refs:
                shared(i, ref, CHIPS - k).wait_recv()
                onward(i, ref, k).start()
            for i, ref in refs:
                onward(i, ref, k).wait_recv()

    greet(True, depth)
    stage.need(N.up_rows)
    early, late = split_rows(up_rows.shape[0])
    local = [
        pltpu.make_async_copy(up_rows.at[late], w_up.at[z, late], ls.at[0]),
        pltpu.make_async_copy(up_early, w_up.at[:, early], ls.at[1]),
    ]
    for c in local:
        c.start()
    column_start(depth, up_rows.at[late], w_up, zs, zr, late)
    stage.need(N.w_out, N.scanned, N.signal, N.gate_in)
    @pl.loop(0, CHIPS)
    def _(turn):
        k = lax.rem(turn + 1, CHIPS)
        q = chip_at(k)

        @pl.when(turn > 0)
        def _():
            pass_away(0, turn)

        at = rows_of(q)
        pre = scanned[at, :WIDE] + skip[6:7] * signal[at, :].astype(f32)
        inward = gate_in[at, :].astype(f32)
        gated[at, :] = (pre * (inward * jax.nn.sigmoid(inward))).astype(bf16)
        part[0, k] = mm(gated[at, :], w_out[...]).astype(bf16).reshape(2, count, D)
        near(0, k).start()

    branch = gathered(0)

    stage.need(N.tok, N.w_router, N.cot_all, N.down0, N.down1)
    gain, router0, router1 = rows_in[1:2], rows_in[2:3], rows_in[3:4]
    middle = tok[...].astype(f32) + branch
    scale = lax.rsqrt(jnp.mean(middle * middle, axis=-1, keepdims=True) + epsilon)
    normed = middle * scale
    routed = (normed * gain).astype(bf16)
    routed_all[p] = routed
    logits = mm(routed, w_router[...])
    l0, l1 = logits[:, 66:67], logits[:, 67:68]
    top = jnp.maximum(l0, l1)
    e0, e1 = jnp.exp(l0 - top), jnp.exp(l1 - top)
    p0, p1 = e0 / (e0 + e1), e1 / (e0 + e1)
    taken = jnp.broadcast_to(picks[...].astype(f32), (count, count)).T[:, 0:1]
    c0 = (taken == 0).astype(f32)
    c1 = (taken == 1).astype(f32)
    chosen = jnp.where(lax.broadcasted_iota(jnp.int32, (count, 128), 1) == 0, c0, c1).astype(bf16)
    before = lax.broadcasted_iota(jnp.int32, (count, count), 0) >= lax.broadcasted_iota(
        jnp.int32, (count, count), 1
    )
    places = mm(before.astype(f32).astype(bf16), chosen)
    s0 = c0 * (places[:, 0:1] <= CAP).astype(f32)
    s1 = c1 * (places[:, 1:2] <= CAP).astype(f32)
    gate = p0 * c0 + p1 * c1
    kept = s0 + s1
    weight = gate * kept
    lane = lax.broadcasted_iota(jnp.int32, (count, 128), 1)
    marks_all[p] = jnp.where(lane == 0, weight, jnp.where(lane == 1, s0, s1)).T[:8]
    share_start(routed_all.at[p], routed_all, gs.at[0], gr.at[0])
    share_start(marks_all.at[p], marks_all, gs.at[1], gr.at[1])
    for c in local:
        c.wait()
    column_forward(depth, w_up, zs, zr, late)
    column_finish(depth, up_rows.at[late], w_up, zs, zr, late)

    odd = lax.broadcasted_iota(jnp.int32, (1, EXPERTS * HID), 1) >= HID

    @pl.loop(0, CHIPS)
    def _(k):
        q = chip_at(k)
        arrived(k, ((0, routed_all), (1, marks_all)))

        @pl.when(k > 1)
        def _():
            pass_away(1, k - 1)
            pass_away(2, k - 1)

        both = pl.ds(2 * q, 2)
        marks = [
            jnp.concatenate([marks_all[2 * q + i], jnp.zeros((120, count), f32)], axis=0).T for i in range(2)
        ]
        marks = jnp.concatenate(marks, axis=0)
        mask = jnp.where(odd, marks[:, 2:3], marks[:, 1:2])
        hidden = mm(routed_all[both].reshape(pair, D), w_up[...].reshape(D, EXPERTS * HID))
        slot = (cot_all[rows_of(q), :].astype(f32) * marks[:, 0:1]).astype(bf16)
        slot_all[q] = slot
        square = hidden * hidden
        bend = jnp.tanh(GELU * hidden * (1.0 + 0.044715 * square))
        units = (0.5 * hidden * (1.0 + bend) * mask).astype(bf16)
        hidden_all[q] = units
        slope = 0.5 * (1.0 + bend) + 0.5 * GELU * hidden * (1.0 - bend * bend) * (1.0 + 3 * 0.044715 * square)
        grad = jnp.concatenate([contract_cols(slot, down0[...]), contract_cols(slot, down1[...])], axis=1)
        grad = (slope * grad * mask).astype(bf16)
        pre_all[q] = grad
        made = mm(units[:, :HID], down0[...]) + mm(units[:, HID:], down1[...])
        part[1, k] = made.astype(bf16).reshape(2, count, D)
        near(1, k).start()
        part[2, k] = contract_cols(grad, w_up[...].reshape(D, EXPERTS * HID)).astype(bf16).reshape(2, count, D)
        near(2, k).start()

    pass_away(1, CHIPS - 1)
    pass_away(2, CHIPS - 1)
    every = CHIPS * pair
    fs = HID // depth
    for c in range(0, D, 384):
        for e in range(EXPERTS):
            made = contract_rows(
                hidden_all[:, :, e * HID : e * HID + HID].reshape(every, HID),
                slot_all[:, :, c : c + 384].reshape(every, 384),
            )
            for k in range(depth):
                grad_down[k, e, :, c : c + 384] = made[k * fs : k * fs + fs].astype(bf16)
    down = []
    for k in range(1, depth):
        q = lax.rem(z + k, depth)
        down.append(send(grad_down.at[q], down_got.at[k], ds.at[k], dr.at[k], (q, p)))
    expert_tok = gathered(1)
    slot_back = gathered(2)

    up = cot_all[pl.ds(pl.multiple_of(p * count, count), count), :].astype(f32)
    output[...] = (middle + weight * expert_tok).astype(bf16)
    stage.done(N.output)
    pull = jnp.sum(up * expert_tok, axis=-1, keepdims=True) * kept * gate
    g0, g1 = pull * (c0 - p0), pull * (c1 - p1)
    grad_routed = slot_back + g0 * router0 + g1 * router1
    routed = routed.astype(f32)
    sum0 = jnp.sum(grad_routed * normed, axis=0, keepdims=True)
    sum1 = jnp.sum(routed * g0, axis=0, keepdims=True)
    sum2 = jnp.sum(routed * g1, axis=0, keepdims=True)
    grad_normed = grad_routed * gain
    inner = jnp.mean(grad_normed * normed, axis=-1, keepdims=True)
    total = scale * (grad_normed - normed * inner) + up
    grad_mid[...] = total
    stage.done(N.grad_mid)
    back_all[p] = total.astype(bf16)
    share_start(back_all.at[p], back_all, gs.at[2], gr.at[2])
    for c in range(0, D, 384):
        grad_up[c : c + 384, :] = contract_rows(
            routed_all[:, :, c : c + 384].reshape(every, 384), pre_all[...].reshape(every, EXPERTS * HID)
        ).astype(bf16)
    stage.done(N.grad_up)

    sums[...] = jnp.zeros_like(sums)
    sums[0:1], sums[1:2], sums[2:3] = sum0, sum1, sum2

    @pl.loop(0, CHIPS)
    def _(k):
        q = chip_at(k)
        arrived(k, ((2, back_all),))
        at = rows_of(q)
        grad = contract_cols(back_all[pl.ds(2 * q, 2)].reshape(pair, D), w_out[...])
        inward = gate_in[at, :].astype(f32)
        sig = jax.nn.sigmoid(inward)
        act = inward * sig
        through = grad * act
        sums[3:4, :WIDE] += jnp.sum(through * signal[at, :].astype(f32), axis=0, keepdims=True)
        mixed_grad[at, :WIDE] = through
        mixed_grad[at, WIDE:] = jnp.zeros((pair, PAD), f32)
        pre = scanned[at, :WIDE] + skip[6:7] * signal[at, :].astype(f32)
        gate_grad[at, :] = (grad * pre * (sig * (1.0 + inward * (1.0 - sig)))).astype(bf16)
    stage.done(N.mixed_grad, N.gate_grad)
    for c in range(0, D, 384):
        grad_out[:, c : c + 384] = contract_rows(
            gated[...], back_all[:, :, c : c + 384].reshape(every, 384)
        ).astype(bf16)
    for c in down:
        c.wait_recv()
    total = grad_down[z].astype(f32)
    for k in range(1, depth):
        total = total + down_got[k].astype(f32)
    down_own[...] = total
    for c in down:
        c.wait_send()
    for i in range(3):
        for k in range(CHIPS):
            near(i, k).wait_send()
            if k:
                away(i, k).wait_send()
    for i, ref in ((0, routed_all), (1, marks_all), (2, back_all)):
        remote(ref.at[p], ref.at[p], gs.at[i, 0], gr.at[i, 0], twin).wait_send()
        for k in range(1, CHIPS):
            shared(i, ref, k).wait_send()
            onward(i, ref, k).wait_send()


def middle_part(cid, depth, **ins):
    count, rows = ins[N.tok].shape[0], ins[N.cot_all].shape[0]
    wide = EXPERTS * HID
    block = (CHIPS, count, D)
    outs = dict(
        output=made(count, D, dtype=bf16),
        grad_mid=made(count, D),
        mixed_grad=made(rows, WIDE + PAD),
        gate_grad=made(rows, WIDE, dtype=bf16),
        grad_out=made(WIDE, D, dtype=bf16),
        grad_up=made(D, wide, dtype=bf16),
        down_own=made(EXPERTS, HID // depth, D),
        sums=made(8, D),
    )
    scratch = (
        [
            pltpu.VMEM((rows, WIDE), bf16),
            pltpu.VMEM((3, CHIPS, 2, count, D), bf16),
            pltpu.VMEM((3,) + block, bf16),
            pltpu.VMEM((3,) + block, bf16),
            pltpu.VMEM((3,) + block, bf16),
            pltpu.VMEM((PLANE, count, D), bf16),
            pltpu.VMEM((PLANE, 8, count), f32),
            pltpu.VMEM((CHIPS, 2 * count, wide), bf16),
            pltpu.VMEM((CHIPS, 2 * count, wide), bf16),
            pltpu.VMEM((CHIPS, 2 * count, D), bf16),
            pltpu.VMEM((PLANE, count, D), bf16),
            pltpu.VMEM((depth, D // depth, wide), bf16),
            pltpu.VMEM((depth, EXPERTS, HID // depth, D), bf16),
            pltpu.VMEM((depth, EXPERTS, HID // depth, D), bf16),
        ]
        + [DMA((3, CHIPS))] * 4
        + [DMA((3, PLANE))] * 2
        + [DMA((depth,))] * 4
        + [DMA((2,))]
    )
    late = (
        N.up_rows, N.w_out, N.scanned, N.signal, N.gate_in, N.tok, N.w_router, N.cot_all, N.down0, N.down1,
    )
    return staged_call(
        functools.partial(middle_kernel, depth), "middle_part", cid, 75, ins, outs, scratch,
        late=late, early=(N.output, N.grad_mid, N.grad_up, N.mixed_grad, N.gate_grad), raw=(N.up_early,),
    )


def tree(parts):
    row = lax.broadcasted_iota(jnp.int32, parts[0].shape, 0)
    for step in (1, 2, 4):
        low = (row // step) % 2 == 0
        parts = [
            jnp.where(low, a, b) + pltpu.roll(jnp.where(low, b, a), step, 0)
            for a, b in zip(parts[::2], parts[1::2])
        ]
    return parts[0]


def lane_tiles(x):
    total = x[:, :128]
    for k in range(128, x.shape[1], 128):
        total = total + x[:, k : k + 128]
    return total


def spread(ref, i):
    return jnp.broadcast_to(ref[pl.ds(i, 1), :], (8, ref.shape[1]))


HALVES = (slice(0, 8), slice(8, 16))


def ends_loop(dk, push, sel, slope):
    blocks = dk.shape[0] // BLK // 2

    def block(b, carry):
        hidden, acc = [list(carry[:2]), list(carry[2:4])], list(carry[4:])
        for t in range(BLK):
            for j in range(2):
                at = b + j * blocks
                base = pl.multiple_of(at * BLK, BLK)
                d, u = spread(dk, base + t), spread(push, base + t)
                for k, h in enumerate(HALVES):
                    hidden[j][k] = jnp.exp2(d * slope[k]) * hidden[j][k] + sel[at, h, t : t + 1] * u
                acc[j] = acc[j] + d
        return (*hidden[0], *hidden[1], *acc)

    zero = jnp.zeros(slope[0].shape, f32)
    done = lax.fori_loop(0, blocks, block, (zero,) * 6)
    return done[:2], done[2:4], done[4], done[5]


def scan_kernel(
    depth, stage, onward,
    dk, push, sel, rate, up_rows, cot, w_down,
    out, states, ends, up_all, cot_all, down_all,
    slots, gs, gr, es, er, zs, zr, ks, ls,
):
    z, p = here()
    tile = slots.shape[2]
    early = split_rows(up_rows.shape[0])[0]
    tiles = dk.shape[0] // tile
    local = [
        pltpu.make_async_copy(up_rows.at[early], up_all.at[z], ls.at[0]),
        pltpu.make_async_copy(cot, cot_all.at[p], ls.at[1]),
        pltpu.make_async_copy(w_down.at[1], down_all.at[z], ls.at[2]),
    ]
    stage.need(N.cot)
    for c in local:
        c.start()
    first = share_start(cot, cot_all, gs, gr)
    slope = [rate[h, :] * LOG2E for h in HALVES]
    one, two, span_one, span_two = ends_loop(dk, push, sel, slope)
    for i, h in enumerate(HALVES):
        ends[z, h] = jnp.exp2(span_two * slope[i]) * one[i] + two[i]
    ends[z, 16:] = span_one + span_two
    mine = []
    for k in range(1, depth):
        mine.append(send(ends.at[z], ends.at[z], es.at[k], er.at[k], (lax.rem(z + k, depth), p)))
    column_start(depth, up_rows.at[early], up_all, zs.at[0], zr.at[0])
    column_start(depth, w_down.at[1], down_all, zs.at[1], zr.at[1])
    onward()
    second = share_forward(cot_all, first, gs, gr)
    for c in local:
        c.wait()
    for c in mine:
        c.wait_recv()
    hidden = [jnp.zeros(slope[0].shape, f32)] * 2
    for k in range(depth - 1):
        for i, h in enumerate(HALVES):
            hidden[i] = jnp.where(k < z, jnp.exp2(ends[k, 16:] * slope[i]) * hidden[i] + ends[k, h], hidden[i])

    middle = [jnp.exp2(span_one * slope[i]) * hidden[i] + one[i] for i in range(2)]
    steps = tiles // 2

    def stored(i, slot, j):
        return pltpu.make_async_copy(
            slots.at[slot, j],
            states.at[pl.ds(pl.multiple_of((i + j * steps) * tile, tile), tile)],
            ks.at[slot, j],
        )

    def piece(i, carry):
        slot = lax.rem(i, 2)

        @pl.when(i >= 2)
        def _():
            for j in range(2):
                stored(i - 2, slot, j).wait()

        def block(m, carry):
            hidden = [list(carry[:2]), list(carry[2:])]
            inside = m * BLK
            parts = [[], []]
            for t in range(BLK):
                for j in range(2):
                    b = (i + j * steps) * (tile // BLK) + m
                    base = pl.multiple_of(b * BLK, BLK)
                    d, u = spread(dk, base + t), spread(push, base + t)
                    line = None
                    for k, h in enumerate(HALVES):
                        now = jnp.exp2(d * slope[k]) * hidden[j][k] + sel[b, h, t : t + 1] * u
                        hidden[j][k] = now
                        slots[slot, j, inside + t, h] = now
                        y = sel[b, STATE + 8 * k : STATE + 8 * k + 8, t : t + 1] * now
                        line = y if line is None else line + y
                    parts[j].append(line)
                    if len(parts[j]) == 8:
                        out[pl.ds(pl.multiple_of(base + t - 7, 8), 8), :] = tree(parts[j])
                        parts[j] = []
            return (*hidden[0], *hidden[1])

        carry = lax.fori_loop(0, tile // BLK, block, carry)
        for j in range(2):
            stored(i, slot, j).start()
        return carry

    carry = lax.fori_loop(0, steps // 2 + 1, piece, (*hidden, *middle))
    column_forward(depth, up_all, zs.at[0], zr.at[0])
    lax.fori_loop(steps // 2 + 1, steps, piece, carry)
    stage.done(N.scanned)
    column_forward(depth, down_all, zs.at[1], zr.at[1])
    for i in (steps - 2, steps - 1):
        for j in range(2):
            stored(i, i % 2, j).wait()
    share_finish(first, second)
    column_finish(depth, up_rows.at[early], up_all, zs.at[0], zr.at[0])
    column_finish(depth, w_down.at[1], down_all, zs.at[1], zr.at[1])
    for c in mine:
        c.wait_send()


def message_loop(dk, grad, sel, slope):
    blocks = dk.shape[0] // BLK // 2

    def block(i, carry):
        message, acc = [list(carry[:2]), list(carry[2:4])], carry[4]
        for t in reversed(range(BLK)):
            for j in range(2):
                b = blocks - 1 - i + j * blocks
                base = pl.multiple_of(b * BLK, BLK)
                d, g = spread(dk, base + t), spread(grad, base + t)
                for k, h in enumerate(HALVES):
                    r = sel[b, STATE + 8 * k : STATE + 8 * k + 8, t : t + 1]
                    message[j][k] = jnp.exp2(d * slope[k]) * (r * g + message[j][k])
                if j == 0:
                    acc = acc + d
        return (*message[0], *message[1], acc)

    zero = jnp.zeros(slope[0].shape, f32)
    done = lax.fori_loop(0, blocks, block, (zero,) * 5)
    return [done[k] + jnp.exp2(done[4] * slope[k]) * done[2 + k] for k in range(2)]


def adjoint_kernel(
    depth, stage, after,
    dk, push, grad, sel, states, rate, ends, gup, gout,
    g_push, g_step, g_sel, g_rate, up_own, out_own,
    slots, notes, up_got, out_got, es, er, zs, zr, ks,
):
    z, p = here()
    tile = slots.shape[1]
    tiles = dk.shape[0] // tile
    per = tile // BLK

    def fetch(i, slot):
        return pltpu.make_async_copy(
            states.at[pl.ds(pl.multiple_of(i * tile, tile), tile)], slots.at[slot], ks.at[slot]
        )

    fetch(tiles - 1, 0).start()
    fetch(tiles - 2, 1).start()
    greet(True, depth)
    first = gup.shape[1] // 64 * 16
    pieces = (pl.ds(0, first), pl.ds(first, gup.shape[1] - first))
    stage.need(N.gup)
    down = []
    for k in range(1, depth):
        q = lax.rem(z + k, depth)
        down.append(
            send(gup.at[q, pieces[0]], up_got.at[k, pieces[0]], zs.at[1, k], zr.at[1, k], (q, p))
        )
    stage.need(N.sel, N.dk, N.grad)
    slope = [rate[h, :] * LOG2E for h in HALVES]
    notes[z, :8], notes[z, 8:] = message_loop(dk, grad, sel, slope)
    mine = []
    for k in range(1, depth):
        mine.append(send(notes.at[z], notes.at[z], es.at[k], er.at[k], (lax.rem(z + k, depth), p)))
    stage.need(N.push)
    for k in range(1, depth):
        q = lax.rem(z + k, depth)
        down.append(
            send(gup.at[q, pieces[1]], up_got.at[k, pieces[1]], zs.at[0, k], zr.at[0, k], (q, p))
        )
    stage.need(N.gout)
    for k in range(1, depth):
        q = lax.rem(z + k, depth)
        down.append(send(gout.at[q], out_got.at[k], zs.at[2, k], zr.at[2, k], (q, p)))
    for c in mine:
        c.wait_recv()
    message = [jnp.zeros(slope[0].shape, f32)] * 2
    for k in range(depth - 1, 0, -1):
        for i, h in enumerate(HALVES):
            message[i] = jnp.where(k > z, notes[k, h] + jnp.exp2(ends[k, 16:] * slope[i]) * message[i], message[i])
    lane = lax.broadcasted_iota(jnp.int32, (STATE, 128), 1)
    ones = jnp.ones((128, 128), bf16)

    def piece(n, carry):
        i = tiles - 1 - n
        slot = lax.rem(n, 2)
        fetch(i, slot).wait()

        def block(m, carry):
            message, acc = list(carry[:2]), list(carry[2:])
            j = per - 1 - m
            b = i * per + j
            base = pl.multiple_of(b * BLK, BLK)
            inside = j * BLK
            w, r = sel[b, :STATE], sel[b, STATE:]
            pushes, steps = [], []
            reads, writes = [None] * (2 * BLK), [None] * (2 * BLK)
            for t in reversed(range(BLK)):
                d, u, g = spread(dk, base + t), spread(push, base + t), spread(grad, base + t)
                plain = jnp.where(d < RESET, d, 0.0)
                to_push = to_step = None
                for k, h in enumerate(HALVES):
                    wt = w[h, t : t + 1]
                    hidden = slots[slot, inside + t, h]
                    total = r[h, t : t + 1] * g + message[k]
                    reads[2 * t + k] = lane_tiles(hidden * g)
                    writes[2 * t + k] = lane_tiles(total * u)
                    x = total * wt
                    carried = total * (hidden - wt * u)
                    y = carried * slope[k]
                    to_push = x if k == 0 else to_push + x
                    to_step = y if k == 0 else to_step + y
                    acc[k] = acc[k] + carried * plain
                    message[k] = jnp.exp2(d * slope[k]) * total
                pushes.insert(0, to_push)
                steps.insert(0, to_step)
                if len(pushes) == 8:
                    at = pl.ds(pl.multiple_of(base + t, 8), 8)
                    g_push[at, :] = tree(pushes)
                    g_step[at, :] = tree(steps)
                    pushes, steps = [], []
            for j2, quantity in enumerate((writes, reads)):
                x = jnp.concatenate(quantity, axis=0)
                high = x.astype(bf16)
                low = (x - high.astype(f32)).astype(bf16)
                sums = jnp.dot(high, ones, preferred_element_type=f32)
                sums = sums + jnp.dot(low, ones, preferred_element_type=f32)
                kept = jnp.zeros((STATE, 128), f32)
                for t in range(BLK):
                    kept = jnp.where(lane == t, sums[STATE * t : STATE * t + STATE], kept)
                g_sel[b, STATE * j2 : STATE * j2 + STATE] = kept[:, :BLK]
            return message[0], message[1], acc[0], acc[1]

        carry = lax.fori_loop(0, per, block, carry)

        @pl.when(n + 2 < tiles)
        def _():
            fetch(i - 2, slot).start()

        return carry

    zero = jnp.zeros(slope[0].shape, f32)
    done = lax.fori_loop(0, tiles, piece, (message[0], message[1], zero, zero))
    g_rate[:8], g_rate[8:] = done[2], done[3]
    after()
    for c in down:
        c.wait_recv()
    total = gup[z].astype(f32)
    for k in range(1, depth):
        total = total + up_got[k].astype(f32)
    rim = up_own.shape[1]
    for q in range(PLANE):
        up_own[q] = total[q * rim : q * rim + rim].astype(bf16)
    total = gout[z].astype(f32)
    for k in range(1, depth):
        total = total + out_got[k].astype(f32)
    out_own[...] = total
    def finish():
        for c in mine + down:
            c.wait_send()

    return finish


def last_kernel(count, *refs):
    ins, outs, held = refs[:count], refs[count : 2 * count], refs[2 * count : 3 * count]
    in_sem, out_sem = refs[3 * count :]
    arriving = [pltpu.make_async_copy(ins[i], held[i], in_sem.at[i]) for i in range(count)]
    for c in arriving:
        c.start()
    leaving = [pltpu.make_async_copy(held[i], outs[i], out_sem.at[i]) for i in range(count)]
    for a, b in zip(arriving, leaving):
        a.wait()
        b.start()
    for c in leaving:
        c.wait()


def last_part(*results):
    count = len(results)
    return pl.pallas_call(
        functools.partial(last_kernel, count),
        out_shape=[jax.ShapeDtypeStruct(r.shape, r.dtype) for r in results],
        in_specs=[ANY] * count,
        out_specs=[ANY] * count,
        scratch_shapes=[pltpu.VMEM(r.shape, r.dtype) for r in results] + [DMA((count,))] * 2,
        compiler_params=params(),
        cost_estimate=cost(5),
        name="last_part",
    )(*results)


def body(
    depth,
    tokens,
    segments,
    routes,
    norm_gain,
    in_proj,
    conv_taps,
    conv_bias,
    select_proj,
    step_proj,
    step_bias,
    decay_log,
    skip_gain,
    out_proj,
    moe_gain,
    router,
    expert_up,
    expert_down,
    cotangent,
):
    count = tokens.shape[0]
    rows = PLANE * count
    rim = norm_gain.shape[0]
    ch = conv_bias.shape[0]
    fs = expert_down.shape[1]
    z, p = here()

    ids = jnp.concatenate([jnp.full((3,), -1, jnp.int32), segments, jnp.full((BLK,), -2, jnp.int32)])
    local_ids = lax.dynamic_slice_in_dim(ids, z * rows, rows + 3 + BLK)
    own_ids = local_ids[3:]
    inside = own_ids >= 0
    same = jnp.stack(
        [(local_ids[k : k + rows + BLK] == own_ids) & inside for k in range(4)], axis=1
    ).astype(f32)
    same = jnp.pad(same, ((0, 0), (0, 124)))
    (
        normed_in,
        w_in,
        w_route,
        small,
        w_sel,
        w_step,
        vecs,
        rate,
        inner,
        gate_in,
        conv,
        signal,
        selected,
        mixes,
        step_pre,
        dk,
        push,
        up_rows,
        down0,
        out_all,
        scanned,
        states,
        ends,
        up_early,
        cot_all,
        down1,
    ) = front_part(
        1,
        depth,
        tok=tokens,
        in_proj=in_proj,
        norm_gain=norm_gain[None],
        moe_gain=moe_gain[None],
        router=router.T,
        expert_up=expert_up.transpose(1, 0, 2),
        select=select_proj,
        step=step_proj,
        decay=decay_log,
        taps=conv_taps,
        bias=conv_bias[None],
        offset=step_bias[None],
        skip=skip_gain[None],
        w_down=expert_down,
        w_out=out_proj,
        same=same,
        cot=cotangent,
    )
    w_out = out_all.reshape(WIDE, D)
    output, grad_mid, mixed_wide, grad_gate_in, grad_out_w, grad_up, grad_down_own, sums = middle_part(
        3,
        depth,
        scanned=scanned,
        signal=signal,
        gate_in=gate_in,
        skip=vecs,
        w_out=w_out,
        tok=tokens,
        cot_all=cot_all.reshape(rows, D),
        up_early=up_early,
        up_rows=up_rows,
        down0=down0.reshape(HID, D),
        down1=down1.reshape(HID, D),
        w_router=w_route,
        rows_in=small,
        picks=routes.T,
    )
    (
        grad_tokens,
        grad_in,
        grad_up_own,
        grad_sel,
        grad_step,
        grad_decay,
        grad_taps,
        grad_bias,
        grad_offset,
        grad_skip,
        grad_norm,
        grad_moe,
        grad_router,
        grad_out_own,
    ) = back_part(
        5,
        depth,
        rim,
        ch,
        dk=dk,
        push=push,
        grad=mixed_wide,
        sel=mixes,
        states=states,
        ends=ends,
        gup=grad_up.reshape(depth, D // depth, EXPERTS * HID),
        gout=grad_out_w.reshape(depth, ch, D),
        step_pre=step_pre,
        signal=signal,
        conv=conv,
        inner=inner,
        same=same,
        vecs=vecs,
        rate=rate,
        selected=selected,
        w_sel=w_sel,
        w_step=w_step,
        gate_grad=grad_gate_in,
        w_in=w_in,
        normed_in=normed_in,
        tok=tokens,
        gain=small,
        grad_mid=grad_mid,
        sums=sums,
    )
    (
        output,
        grad_tokens,
        grad_norm,
        grad_in,
        grad_taps,
        grad_bias,
        grad_sel,
        grad_step,
        grad_offset,
        grad_decay,
        grad_skip,
        grad_out_own,
        grad_moe,
        grad_router,
        grad_up_own,
        grad_down_own,
    ) = last_part(
        output,
        grad_tokens,
        grad_norm,
        grad_in,
        grad_taps,
        grad_bias,
        grad_sel,
        grad_step,
        grad_offset,
        grad_decay,
        grad_skip,
        grad_out_own,
        grad_moe,
        grad_router,
        grad_up_own,
        grad_down_own,
    )
    return (
        output,
        grad_tokens,
        grad_norm[0],
        grad_in,
        grad_taps,
        grad_bias[0],
        grad_sel,
        grad_step,
        grad_offset[0],
        grad_decay,
        grad_skip[0],
        grad_out_own,
        grad_moe[0],
        grad_router.T,
        grad_up_own.transpose(1, 0, 2),
        grad_down_own,
    )


def solution(mesh):
    planes = Mesh(mesh.devices.reshape(-1, PLANE), ("z", "p"))
    every = ("z", "p")
    rows, flat, cols, third = P(every, None), P(every), P(None, every), P(None, every, None)
    return jax.shard_map(
        functools.partial(body, planes.shape["z"]),
        mesh=planes,
        in_specs=(
            rows, P(), rows, flat, rows, cols, flat, rows, cols,
            flat, cols, flat, rows, flat, rows, third, third, rows,
        ),
        out_specs=(
            rows, rows, flat, rows, cols, flat, rows, cols,
            flat, cols, flat, rows, flat, rows, third, third,
        ),
        check_vma=False,
    )
```
